128 devices in a mesh: lon: 8 (over y_lo, z), lat: 16 (over y_hi, x, core).
Axes of the slice: x: 4, y: 4 (y_hi: 2, y_lo: 2; y = y_hi * 2 + y_lo), z: 4, core: 2. Of those that a mesh axis runs over, the one named last changes fastest.
Arguments:
- costate: float32 [72, 8, 128, 2048], P(None, None, 'lat', 'lon'), may hold values from -6 to 6
- diffusion: float32 [2, 71, 128, 2048], P(None, None, 'lat', 'lon'), may hold values from 0.025 to 400
- east_courant: float32 [2, 128, 2048], P(None, 'lat', 'lon'), may hold values from 0.05 to 0.9
- north_courant: float32 [2, 128, 2048], P(None, 'lat', 'lon'), may hold values from 0.02 to 0.45
- south_courant: float32 [2, 128, 2048], P(None, 'lat', 'lon'), may hold values from 0.02 to 0.45
- polar_shift: int32 [2, 128], replicated, may hold values from -1024 to 1024
- owners: int32 [2, 163840, 1], P(None, ('lon', 'lat')), may hold values from 0 to 127; in each aligned block of 1280 rows (0 to 1279, 1280 to 2559, ..., all dimensions but the last counted through in order) at most 16 rows name the same one
- columns: int32 [2, 163840], P(None, ('lon', 'lat')), may hold values from 0 to 2047
- sounding_counts: int32 [2, 128], P(None, ('lon', 'lat')), may hold values from 640 to 1280, as said below
- kernels: float32 [2, 72, 163840], P(None, None, ('lon', 'lat')), may hold values from 0.1 to 2
- misfits: float32 [2, 8, 163840], P(None, None, ('lon', 'lat')), may hold values from -6 to 6
Outputs:
- adjoint_state: float32 [72, 8, 128, 2048], P(None, None, 'lat', 'lon')
- flux_gradient: float32 [8, 128, 2048], P(None, 'lat', 'lon')
The draws below stay inside these ranges and needn't reach their ends.
Inputs may be any that keep to these rules, and one draw needn't show every extreme that they name: `owners`: in every step no owner is named by more than 16 of one device's 1280 soundings, and in every step some owner is named by exactly 16 of some device's soundings. `sounding_counts`: in every step some device is full and some holds exactly 640 live soundings.
All inputs are finite; a program needn't handle non-finite values.
Results may differ from the reference program's by a relative error of at most 0.0001.
Values sent between devices are 32-bit elements; how exact they have to be, the bound alone decides.
No kernel may reach another device: no remote copies, remote signals or barrier semaphores. Data moves between devices by JAX's collectives and lax.ppermute only.
A program may use at most 128 MiB of HBM per device.

```python
import math
import jax
import jax.numpy as jnp
import numpy as np
from jax import lax

LONC = 256
LATC = 8
LEV = 72
TR = 8
STEPS = 2
SND_DEV = 1280
NLON = 2048
NLAT = 128
SOUND = 163840
CAP = 16
SHIFT_MAX = 1024
N_LAT = 16
DEVICES = 128


def draw_diffusion(key, part):
    low = math.log(0.05)
    high = math.log(200.0)
    base_draw = jax.random.uniform(jax.random.fold_in(key, 31), (1, 1, NLAT, NLON), jnp.float32)
    log_base = low + base_draw * (high - low)
    spread = math.log(2.0)
    rough = jax.random.uniform(jax.random.fold_in(key, 37), (STEPS, LEV - 1, NLAT, NLON), jnp.float32, -spread, spread)
    return jnp.exp(log_base + rough).astype(jnp.float32)


def draw_polar_shift(key, part):
    ends = jax.random.randint(jax.random.fold_in(key, 11), (STEPS, 2), -SHIFT_MAX, SHIFT_MAX + 1)
    ends = ends.at[0, 0].set(SHIFT_MAX).at[STEPS - 1, 1].set(-SHIFT_MAX)
    shifts = jnp.zeros((STEPS, NLAT), jnp.int32)
    shifts = shifts.at[:, 0].set(ends[:, 0]).at[:, NLAT - 1].set(ends[:, 1])
    return shifts.astype(jnp.int32)


def draw_sounding_counts(key, part):
    counts = jax.random.randint(jax.random.fold_in(key, 23), (STEPS, DEVICES), SND_DEV // 2, SND_DEV + 1)
    counts = counts.at[:, 0].set(SND_DEV).at[:, 1].set(SND_DEV // 2)
    return counts.astype(jnp.int32)


def with_ends(entries, key, smallest, largest):
    place = [jax.random.randint(jax.random.fold_in(key, axis), (), 0, length) for axis, length in enumerate(entries.shape)]
    longest = entries.shape.index(max(entries.shape))
    next_to = place[:longest] + [(place[longest] + 1) % entries.shape[longest]] + place[longest + 1:]
    return entries.at[tuple(place)].set(smallest).at[tuple(next_to)].set(largest)


def block_scale(key, extent, split, smallest, largest):
    def one(position, blocks):
        steps = jax.random.uniform(jax.random.fold_in(jax.random.fold_in(key, 6), position), (blocks,), jnp.float32, smallest / len(split), largest / len(split))
        return jnp.repeat(jnp.exp(steps), extent[position] // blocks).reshape((-1,) + (1,) * (len(extent) - position - 1))

    factor_of = one(*split[0])
    for cut in split[1:]:
        factor_of = factor_of * one(*cut)
    return factor_of


def assign_block(rng, own, number, rows, amount, top, reach, lean):
    ranking = jax.random.permutation(rng, amount)
    heavy_load, usual = portions_of(amount, rows * top, reach, lean, True), portions_of(amount, rows * top, reach, lean, False)
    places = jnp.arange(amount)

    def named(tallies, offset_by):
        used = int((tallies > 0).sum())
        fixed = max(1, used // 4)
        moved = fixed + (places - fixed + offset_by * (used - fixed)) % max(1, amount - fixed)
        return jnp.zeros((amount,), jnp.int32).at[ranking[jnp.where(places < fixed, places, moved)]].set(jnp.asarray(tallies, jnp.int32))

    tallies = jnp.where(number % 4 == 0, named(heavy_load, number // 4), named(usual, number - number // 4 - 1))
    mixed = jax.random.permutation(jax.random.fold_in(own, 3), amount)
    source_of, receiver = mixed[0:amount // 2 * 2:2], mixed[1:amount // 2 * 2:2]
    slack = jnp.minimum(tallies[source_of] - 1, reach - tallies[receiver]) // 2
    slack = jnp.where((source_of == ranking[0]) | (receiver == ranking[0]) | (tallies[receiver] == 0), 0, jnp.maximum(slack, 0))
    moved = jax.random.randint(jax.random.fold_in(own, 4), (amount // 2,), 0, 1 << 20) % (slack + 1)
    tallies = tallies.at[source_of].add(-moved).at[receiver].add(moved)
    members = jnp.searchsorted(jnp.cumsum(tallies), jnp.arange(rows * top), side="right").astype(jnp.int32)
    grid = members.reshape(top, rows).T
    grid = grid[jax.random.permutation(jax.random.fold_in(own, 1), rows)]
    offset_by = jax.random.randint(jax.random.fold_in(own, 2), (rows, 1), 0, top)
    return jnp.take_along_axis(grid, (jnp.arange(top)[None, :] + offset_by) % top, axis=1)


def portions_of(count, total, bound, lean, full):
    weights = [(1 << 20) // math.isqrt(rank ** lean) + 1 for rank in range(1, count + 1)]
    largest = bound if full else min(bound, max(-(-total // count), total * weights[0] // sum(weights)))
    least = 1 if total - largest >= count - 1 else 0
    holding, surplus = [largest] + [least] * (count - 1), total - largest - least * (count - 1)
    while surplus > 0:
        free = [i for i in range(1, count) if holding[i] < largest] or [i for i in range(1, count) if holding[i] < bound]
        mass, budget = sum([weights[i] for i in free]), surplus
        for i in free:
            extra = min(bound - holding[i], max(1, budget * weights[i] // mass), surplus)
            holding[i] = holding[i] + extra
            surplus = surplus - extra
    return np.array(holding)


def centred(key, dims, width, bound, pieces=(), held_as=jnp.bfloat16):
    entries = jax.random.normal(key, dims, jnp.float32) * width
    if len(pieces) > 0:
        entries = block_scale(key, dims, pieces, -0.22, 0.18) * entries
    return jnp.clip(entries, min=-bound, max=bound).astype(held_as)


def setup_inputs(seed: int = 0) -> dict:
    arg_keys = jax.random.split(jax.random.key(seed), 12)
    costate = centred(arg_keys[0], (LEV, TR, NLAT, NLON), 1.0, 6.0, ((2, 16), (3, 8)), jnp.float32)
    diffusion = draw_diffusion(jax.random.fold_in(arg_keys[11], 71), 0)
    east_courant = jnp.clip(0.05 + 0.84999998 * jax.random.uniform(arg_keys[2], (STEPS, NLAT, NLON), jnp.float32) ** block_scale(arg_keys[2], (STEPS, NLAT, NLON), ((1, 16), (2, 8)), -0.2, 0.2), 0.05, 0.9)
    north_courant = jnp.clip(0.02 + 0.42999999 * jax.random.uniform(arg_keys[3], (STEPS, NLAT, NLON), jnp.float32) ** block_scale(arg_keys[3], (STEPS, NLAT, NLON), ((1, 16), (2, 8)), -0.2, 0.2), 0.02, 0.45)
    south_courant = jnp.clip(0.02 + 0.42999999 * jax.random.uniform(arg_keys[4], (STEPS, NLAT, NLON), jnp.float32) ** block_scale(arg_keys[4], (STEPS, NLAT, NLON), ((1, 16), (2, 8)), -0.2, 0.2), 0.02, 0.45)
    polar_shift = draw_polar_shift(jax.random.fold_in(arg_keys[11], 71), 0)
    owners_keys = jax.random.split(jax.random.fold_in(arg_keys[6], 1), STEPS * SOUND // SND_DEV)
    owners_turns = jax.random.permutation(jax.random.fold_in(arg_keys[6], 3), STEPS * SOUND // SND_DEV)
    owners = jax.vmap(lambda own, number: assign_block(jax.random.fold_in(arg_keys[6], 2), own, number, SND_DEV, DEVICES, 1, CAP, 2))(owners_keys, owners_turns).reshape((STEPS, SOUND, 1))
    columns = with_ends(jax.random.randint(arg_keys[7], (STEPS, SOUND), 0, LATC * LONC), jax.random.fold_in(arg_keys[7], 1), 0, (LATC * LONC) - 1).astype(jnp.int32)
    sounding_counts = draw_sounding_counts(jax.random.fold_in(arg_keys[11], 71), 0)
    kernels = jnp.clip(jnp.exp(math.log(2.0) - 2.9957323 * jax.random.uniform(arg_keys[9], (STEPS, LEV, SOUND), jnp.float32) ** block_scale(arg_keys[9], (STEPS, LEV, SOUND), ((2, 128),), -0.2, 0.2)), 0.1, 2.0)
    misfits = centred(arg_keys[10], (STEPS, TR, SOUND), 1.0, 6.0, ((2, 128),), jnp.float32)
    return dict(costate=costate, diffusion=diffusion, east_courant=east_courant, north_courant=north_courant, south_courant=south_courant, polar_shift=polar_shift, owners=owners, columns=columns, sounding_counts=sounding_counts, kernels=kernels, misfits=misfits)


def column_solve(coeffs, values):
    zero_row = jnp.zeros_like(coeffs[:1])
    lower_coef = jnp.concatenate([zero_row, coeffs], axis=0)
    upper_coef = jnp.concatenate([coeffs, zero_row], axis=0)

    def eliminate(carry, items):
        prev_ratio, prev_value = carry
        below, above, right = items
        pivot = 1.0 + below + above + below * prev_ratio
        ratio = -above / pivot
        value = (right + below[None] * prev_value) / pivot[None]
        return (ratio, value), (ratio, value)

    start = (jnp.zeros(values.shape[2:], jnp.float32), jnp.zeros(values.shape[1:], jnp.float32))
    unused, (ratios, reduced) = lax.scan(eliminate, start, (lower_coef, upper_coef, values))

    def substitute(following, items):
        ratio, value = items
        solved = value - ratio[None] * following
        return solved, solved

    unused2, solved_all = lax.scan(substitute, jnp.zeros(values.shape[1:], jnp.float32), (ratios, reduced), reverse=True)
    return solved_all


def reference(costate, diffusion, east_courant, north_courant, south_courant, polar_shift, owners, columns, sounding_counts, kernels, misfits):
    state = costate
    gradient = jnp.zeros((TR, NLAT, NLON), jnp.float32)
    row_index = jnp.arange(NLAT)[:, None]
    slot_index = jnp.arange(SOUND)
    for step in reversed(range(STEPS)):
        diffused = column_solve(diffusion[step], state)
        zero_band = jnp.zeros_like(diffused[:, :, :1])
        next_row = jnp.concatenate([diffused[:, :, 1:], zero_band], axis=2)
        prev_row = jnp.concatenate([zero_band, diffused[:, :, :-1]], axis=2)
        meridional = diffused + north_courant[step] * (next_row - diffused) + south_courant[step] * (prev_row - diffused)
        east_cells = jnp.roll(meridional, -1, axis=3)
        zonal = meridional + east_courant[step] * (east_cells - meridional)
        source_cell = jnp.mod(jnp.arange(NLON)[None, :] + polar_shift[step][:, None], NLON)
        shifted = zonal[:, :, row_index, source_cell]
        source_dev = slot_index // SND_DEV
        live = (slot_index % SND_DEV) < sounding_counts[step][source_dev]
        owner = owners[step, :, 0]
        global_row = (owner % N_LAT) * LATC + columns[step] // LONC
        global_lon = (owner // N_LAT) * LONC + columns[step] % LONC
        flat_cell = (global_row * NLON + global_lon).astype(jnp.int32)
        weights = jnp.where(live, 1.0, 0.0).astype(jnp.float32)
        outer = kernels[step][:, None, :] * misfits[step][None, :, :] * weights[None, None, :]
        forcing = jnp.zeros((LEV, TR, NLAT * NLON), jnp.float32).at[:, :, flat_cell].add(outer)
        state = shifted + forcing.reshape(LEV, TR, NLAT, NLON)
        gradient = gradient + state[LEV - 1]
    return state, gradient
```

```python
import functools

import jax
import jax.numpy as jnp
from jax import lax
from jax.experimental import pallas as pl
from jax.experimental.pallas import tpu as pltpu
from jax.sharding import PartitionSpec as P

AXES = ("lon", "lat")
LANES = 128
CAP = 16
GROUP = 8
F32 = jnp.float32
BF16 = jnp.bfloat16
VMEM_LIMIT = 56 * 1024 * 1024


def vmem():
    return pl.BlockSpec(memory_space=pltpu.VMEM)


def smem():
    return pl.BlockSpec(memory_space=pltpu.SMEM)


def params():
    return pltpu.CompilerParams(vmem_limit_bytes=VMEM_LIMIT)


def dot(a, b, contract=((1,), (0,))):
    return lax.dot_general(a, b, (contract, ((), ())), preferred_element_type=F32)


def halves(x):
    high = x.astype(BF16)
    return high, (x - high.astype(F32)).astype(BF16)


def pack_kernel(step, counts, owners, columns, kernels, misfits, out, payload, target):
    held = owners.shape[2]
    owner = owners[step]
    live = lax.broadcasted_iota(jnp.int32, owner.shape, 1) < counts[step, 0]
    owner = jnp.where(live, owner, -1)
    shape = (LANES, LANES)
    device = lax.broadcasted_iota(jnp.int32, shape, 0)
    earlier = (device < lax.broadcasted_iota(jnp.int32, shape, 1)).astype(F32)
    table = jnp.concatenate([earlier, jnp.ones(shape, F32)], axis=1).astype(BF16)
    seen = jnp.zeros(shape, F32)
    for start in range(0, held, LANES):
        here = owner[:, start : start + LANES]
        hot = device == here
        counted = dot(jnp.where(hot, 1.0, 0.0).astype(BF16), table)
        rank = jnp.sum(
            jnp.where(hot, counted[:, :LANES] + seen, 0.0), axis=0, keepdims=True
        )
        seen = seen + counted[:, LANES:]
        target[:, start : start + LANES] = jnp.where(
            here >= 0, here * CAP + rank.astype(jnp.int32), -1
        )
    levels, tracers = kernels.shape[1], misfits.shape[1]
    fields = levels + tracers
    column = columns[step : step + 1, :].astype(F32) + 1.0
    column = jnp.where(lax.broadcasted_iota(jnp.int32, (8, held), 0) == 0, column, 0.0)
    rows = jnp.concatenate(
        [kernels[0], misfits[0], column, jnp.zeros((LANES - fields - 8, held), F32)], axis=0
    )
    high, low = halves(rows)
    payload[:LANES, :] = high
    payload[LANES:, :] = low
    block = 256

    def place(i, carry):
        slot = lax.broadcasted_iota(jnp.int32, (block, held), 0) + i * block
        hot = jnp.where(slot == target[...], 1.0, 0.0).astype(BF16)
        both = dot(hot, payload[...], ((1,), (1,)))
        out[pl.ds(pl.multiple_of(i * block, block), block), :] = (
            both[:, :LANES] + both[:, LANES:]
        )
        return carry

    lax.fori_loop(0, out.shape[0] // block, place, 0)


def packed(step, counts, owners, columns, kernels, misfits):
    levels, held = kernels.shape[1:]
    tracers = misfits.shape[1]
    devices = lax.axis_size("lon") * lax.axis_size("lat")
    return pl.pallas_call(
        functools.partial(pack_kernel, step),
        grid=(1,),
        out_shape=jax.ShapeDtypeStruct((devices * CAP, LANES), F32),
        in_specs=[
            smem(),
            pl.BlockSpec(owners.shape, lambda i: (0, 0, 0)),
            pl.BlockSpec(columns.shape, lambda i: (0, 0)),
            pl.BlockSpec((1, levels, held), lambda i: (step, 0, 0)),
            pl.BlockSpec((1, tracers, held), lambda i: (step, 0, 0)),
        ],
        out_specs=pl.BlockSpec((devices * CAP, LANES), lambda i: (0, 0)),
        scratch_shapes=[
            pltpu.VMEM((2 * LANES, held), BF16),
            pltpu.VMEM((1, held), jnp.int32),
        ],
        compiler_params=params(),
        name="pack",
    )(counts, owners, columns, kernels, misfits)


def forcing_kernel(received, out, high, low, cell):
    levels, rows, tracers, cells = out.shape
    slots = received.shape[0]

    def outer(i, carry):
        at = pl.multiple_of(i * LANES, LANES)
        block = received[pl.ds(at, LANES), :]
        turned = block.T
        cell[pl.ds(at, LANES), :] = jnp.broadcast_to(
            block[:, levels + tracers : levels + tracers + 1] - 1.0, (LANES, LANES)
        )
        product = turned[:levels][:, None, :] * turned[levels : levels + tracers][None]
        first, second = halves(product.reshape(levels * tracers, LANES))
        high[:, pl.ds(at, LANES)] = first
        low[:, pl.ds(at, LANES)] = second
        return carry

    lax.fori_loop(0, slots // LANES, outer, 0)

    def place(row, carry):
        lane = lax.broadcasted_iota(jnp.int32, (1, LANES), 1)
        first = (lane + row * cells).astype(F32)
        hot = jnp.concatenate(
            [
                jnp.where(cell[...] == first + float(part * LANES), 1.0, 0.0).astype(BF16)
                for part in range(cells // LANES)
            ],
            axis=1,
        )
        total = dot(high[...], hot) + dot(low[...], hot)
        out[:, pl.ds(row, 1), :, :] = total.reshape(levels, 1, tracers, cells)
        return carry

    lax.fori_loop(0, rows, place, 0)


def forcing(received, levels, tracers, rows, cells):
    slots = received.shape[0]
    return pl.pallas_call(
        forcing_kernel,
        out_shape=jax.ShapeDtypeStruct((levels, rows, tracers, cells), F32),
        in_specs=[vmem()],
        out_specs=vmem(),
        scratch_shapes=[
            pltpu.VMEM((levels * tracers, slots), BF16),
            pltpu.VMEM((levels * tracers, slots), BF16),
            pltpu.VMEM((slots, LANES), F32),
        ],
        compiler_params=params(),
        name="forcing",
    )(received)


def pivots(level, levels, diffusion, carry):
    below, ratio = carry
    above = diffusion[0, level] if level is not None else jnp.zeros_like(below)
    inverse = 1.0 / (1.0 + below + above + below * ratio)
    return inverse, below * inverse, above, -above * inverse


def spread(x, row, tracers):
    return jnp.broadcast_to(x[row : row + 1, :], (tracers, x.shape[1]))


def eliminate(level, above, carry, rights, ratios):
    below, ratio, values = carry
    if above is None:
        above = jnp.zeros_like(below)
    inverse = 1.0 / (1.0 + below + above + below * ratio)
    lower = below * inverse
    ratio = -above * inverse
    ratios[level] = ratio
    tracers = rights[0].shape[0]
    fresh = [
        spread(inverse, r, tracers) * rights[r] + spread(lower, r, tracers) * values[r]
        for r in range(len(rights))
    ]
    return (above, ratio, fresh)


def substitute(diffused, ratios, north, south, east, first, last, polar):
    levels, rows, tracers, cells = diffused.shape
    lat = lax.axis_index("lat")
    at_start = lat == 0
    row = jnp.where(at_start, 0, rows - 1)
    picked_north = jnp.where(at_start, north[0, 0:1, :], north[0, rows - 1 : rows, :])
    picked_south = jnp.where(at_start, south[0, 0:1, :], south[0, rows - 1 : rows, :])
    own = jnp.broadcast_to(1.0 - picked_north - picked_south, (tracers, cells))
    side = jnp.broadcast_to(jnp.where(at_start, picked_north, picked_south), (tracers, cells))
    picked_east = jnp.where(at_start, east[0, 0:1, :], east[0, rows - 1 : rows, :])
    polar[levels] = jnp.broadcast_to(picked_east, (tracers, cells))

    def one(level, solved):
        first[level] = solved[0]
        last[level] = solved[rows - 1]
        polar[level] = own * jnp.where(at_start, solved[0], solved[rows - 1]) + side * jnp.where(
            at_start, solved[1], solved[rows - 2]
        )

    solved = [diffused[levels - 1, r] for r in range(rows)]
    one(levels - 1, solved)

    def back(level, solved):
        ratio = ratios[level]
        fresh = []
        for r in range(rows):
            value = diffused[level, r] - spread(ratio, r, tracers) * solved[r]
            diffused[level, r] = value
            fresh.append(value)
        one(level, fresh)
        return fresh

    def steps(i, solved):
        for j in range(GROUP - 1):
            solved = back(levels - 2 - i * (GROUP - 1) - j, solved)
        return solved

    full = (levels - 1) // (GROUP - 1)
    solved = lax.fori_loop(0, full, steps, solved)
    for level in range(levels - 2 - full * (GROUP - 1), -1, -1):
        solved = back(level, solved)


def first_kernel(costate, diffusion, north, south, east, diffused, first, last, polar, ratios):
    levels, tracers, rows, cells = costate.shape
    zero = jnp.zeros((rows, cells), F32)
    carry = (zero, zero, [jnp.zeros((tracers, cells), F32)] * rows)

    def forward(level, above, carry):
        rights = [costate[level, :, r, :] for r in range(rows)]
        carry = eliminate(level, above, carry, rights, ratios)
        for r in range(rows):
            diffused[level, r] = carry[2][r]
        return carry

    def group(i, carry):
        for j in range(GROUP):
            level = i * GROUP + j
            carry = forward(level, diffusion[0, level], carry)
        return carry

    carry = lax.fori_loop(0, levels // GROUP - 1, group, carry)
    for level in range(levels - GROUP, levels):
        carry = forward(level, diffusion[0, level] if level < levels - 1 else None, carry)
    substitute(diffused, ratios, north, south, east, first, last, polar)


def meridional(level, row, diffused, after, before, coefs):
    rows = diffused.shape[1]
    own, north, south = coefs
    up = diffused[level, row + 1] if row < rows - 1 else after[level]
    down = diffused[level, row - 1] if row > 0 else before[level]
    return own * diffused[level, row] + north * up + south * down


def edge_kernel(diffused, after, before, north, south, edge):
    levels, rows, tracers, cells = diffused.shape
    shape = (tracers, LANES)
    lane = lax.broadcasted_iota(jnp.int32, shape, 1)
    coefs = []
    for r in range(rows):
        n = jnp.broadcast_to(north[0, r : r + 1, :LANES], shape)
        s = jnp.broadcast_to(south[0, r : r + 1, :LANES], shape)
        coefs.append((1.0 - n - s, n, s))

    def group(i, carry):
        packed_edge = jnp.zeros(shape, F32)
        for j in range(GROUP):
            level = i * GROUP + j
            values = [diffused[level, r, :, :LANES] for r in range(rows)]
            values = [before[level, :, :LANES]] + values + [after[level, :, :LANES]]
            for r in range(rows):
                own, n, s = coefs[r]
                value = own * values[r + 1] + n * values[r + 2] + s * values[r]
                at = j * rows + r
                packed_edge = jnp.where(
                    lane == at, pltpu.roll(value, at, 1) if at else value, packed_edge
                )
        edge[i] = packed_edge
        return carry

    lax.fori_loop(0, levels // GROUP, group, 0)


def prepare_stencil(shift, step, north, south, east, polars, coefs, turned):
    rows, cells = north.shape[1:]
    tracers = coefs.shape[2]
    for r in range(rows):
        n = north[0, r : r + 1, :]
        s = south[0, r : r + 1, :]
        coefs[0, r] = jnp.broadcast_to(1.0 - n - s, (tracers, cells))
        coefs[1, r] = jnp.broadcast_to(n, (tracers, cells))
        coefs[2, r] = jnp.broadcast_to(s, (tracers, cells))
        coefs[3, r] = jnp.broadcast_to(east[0, r : r + 1, :], (tracers, cells))
    levels = turned.shape[0]
    lat = lax.axis_index("lat")
    last_lat = lax.axis_size("lat") - 1
    last_row = rows * lax.axis_size("lat") - 1

    def turn(low, high, amount):
        inner = lax.rem(amount + 2 * 2048, 2048) & (cells - 1)
        back = 2 * cells - inner
        weight = jnp.concatenate([low[levels], high[levels]], axis=1)

        def one(level, carry):
            row = jnp.concatenate([low[level], high[level]], axis=1)
            moved = row + weight * (pltpu.roll(row, 2 * cells - 1, 1) - row)
            turned[level] = pltpu.roll(moved, back, 1)[:, :cells]
            return carry

        lax.fori_loop(0, levels, one, 0, unroll=4)

    @pl.when(lat == 0)
    def _():
        turn(polars[0], polars[1], shift[step, 0])

    @pl.when(lat == last_lat)
    def _():
        turn(polars[2], polars[3], shift[step, last_row])


def transported(level, lane_at, diffused, after, before, edge_row, coefs, turned):
    rows, tracers, cells = diffused.shape[1:]
    lat = lax.axis_index("lat")
    last = lax.broadcasted_iota(jnp.int32, (tracers, cells), 1) == cells - 1
    result = []
    for r in range(rows):
        mer = meridional(level, r, diffused, after, before, [coefs[k, r] for k in range(3)])
        arrived = pltpu.roll(edge_row, LANES - 1 - (lane_at * rows + r), 1)
        arrived = jnp.concatenate([arrived] * (cells // LANES), axis=1)
        following = jnp.where(last, arrived, pltpu.roll(mer, cells - 1, 1))
        result.append(mer + coefs[3, r] * (following - mer))
    result[0] = jnp.where(lat == 0, turned[level], result[0])
    result[rows - 1] = jnp.where(
        lat == lax.axis_size("lat") - 1, turned[level], result[rows - 1]
    )
    return result


def middle_kernel(
    step,
    shift,
    diffused,
    after,
    before,
    edge,
    low0,
    high0,
    low1,
    high1,
    north,
    south,
    east,
    forced,
    diffusion,
    next_north,
    next_south,
    next_east,
    solved,
    first,
    last,
    polar,
    surface,
    coefs,
    turned,
    ratios,
):
    levels, rows, tracers, cells = diffused.shape
    prepare_stencil(shift, step, north, south, east, (low0, high0, low1, high1), coefs, turned)
    zero = jnp.zeros((rows, cells), F32)
    carry = (zero, zero, [jnp.zeros((tracers, cells), F32)] * rows)

    def forward(level, j, above, edge_row, carry):
        rights = transported(level, j, diffused, after, before, edge_row, coefs, turned)
        rights = [rights[r] + forced[level, r] for r in range(rows)]
        if isinstance(level, int) and level == levels - 1:
            for r in range(rows):
                surface[r] = rights[r]
        carry = eliminate(level, above, carry, rights, ratios)
        for r in range(rows):
            solved[level, r] = carry[2][r]
        return carry

    def group(i, carry):
        edge_row = edge[i]
        for j in range(GROUP):
            level = i * GROUP + j
            carry = forward(level, j, diffusion[0, level], edge_row, carry)
        return carry

    groups = levels // GROUP
    carry = lax.fori_loop(0, groups - 1, group, carry)
    edge_row = edge[groups - 1]
    for j in range(GROUP):
        level = levels - GROUP + j
        above = diffusion[0, level] if level < levels - 1 else None
        carry = forward(level, j, above, edge_row, carry)
    substitute(solved, ratios, next_north, next_south, next_east, first, last, polar)


def last_kernel(
    step,
    shift,
    diffused,
    after,
    before,
    edge,
    low0,
    high0,
    low1,
    high1,
    north,
    south,
    east,
    forced,
    surface,
    state,
    gradient,
    coefs,
    turned,
):
    levels, rows, tracers, cells = diffused.shape
    prepare_stencil(shift, step, north, south, east, (low0, high0, low1, high1), coefs, turned)

    def group(i, carry):
        edge_row = edge[i]
        for j in range(GROUP):
            level = i * GROUP + j
            values = transported(level, j, diffused, after, before, edge_row, coefs, turned)
            for r in range(rows):
                state[level, :, r, :] = values[r] + forced[level, r]
        return carry

    lax.fori_loop(0, levels // GROUP, group, 0)
    for r in range(rows):
        gradient[:, r, :] = surface[r] + state[levels - 1, :, r, :]


def step_block(array, step):
    shape = (1,) + array.shape[1:]
    return pl.BlockSpec(shape, lambda i: (step,) + (0,) * (len(shape) - 1))


def whole(array):
    return pl.BlockSpec(array.shape, lambda i: (0,) * len(array.shape))


def exchange(diffused, first, last, polar, north, south, shift, step):
    lat_count = lax.axis_size("lat")
    lon_count = lax.axis_size("lon")
    up = [(i, i + 1) for i in range(lat_count - 1)]
    down = [(j, i) for i, j in up]
    after = lax.ppermute(first, "lat", down)
    before = lax.ppermute(last, "lat", up)
    cells = north.shape[2]
    circle = cells * lon_count

    def route(lat, hops, row):
        pairs = [
            (((j + hops) % lon_count) * lat_count + lat, j * lat_count + lat)
            for j in range(lon_count)
        ]
        return lax.ppermute(row, AXES, pairs)

    polars = []
    for lat, row in ((0, 0), (lat_count - 1, shift.shape[1] - 1)):
        hops = jnp.mod(shift[step, row], circle) // cells
        polars += lax.switch(
            hops,
            [
                functools.partial(
                    lambda k, lat, x: [route(lat, k, x), route(lat, k + 1, x)], k, lat
                )
                for k in range(lon_count)
            ],
            polar,
        )
    levels, rows, tracers = diffused.shape[:3]
    edge = pl.pallas_call(
        edge_kernel,
        grid=(1,),
        out_shape=jax.ShapeDtypeStruct((levels // GROUP, tracers, LANES), F32),
        in_specs=[whole(diffused), whole(after), whole(before)]
        + [step_block(north, step)] * 2,
        out_specs=pl.BlockSpec((levels // GROUP, tracers, LANES), lambda i: (0, 0, 0)),
        compiler_params=params(),
        name="edge",
    )(diffused, after, before, north, south)
    west = [(i, (i - 1) % lon_count) for i in range(lon_count)]
    return after, before, lax.ppermute(edge, "lon", west), polars


def per_device(
    costate,
    diffusion,
    east_courant,
    north_courant,
    south_courant,
    polar_shift,
    owners,
    columns,
    sounding_counts,
    kernels,
    misfits,
):
    levels, tracers, rows, cells = costate.shape
    devices = lax.axis_size("lon") * lax.axis_size("lat")
    owner_rows = owners.reshape(owners.shape[0], 1, owners.shape[1])
    couplings = [north_courant, south_courant, east_courant]

    def exchanged(step):
        sent = packed(step, sounding_counts, owner_rows, columns, kernels, misfits)
        sent = sent.reshape(devices, CAP, LANES)
        return lax.all_to_all(sent, AXES, 0, 0, tiled=True).reshape(devices * CAP, LANES)

    got = {step: exchanged(step) for step in (1, 0)}
    forced = {step: forcing(got[step], levels, tracers, rows, cells) for step in (1, 0)}

    solved_shapes = [
        jax.ShapeDtypeStruct((levels, rows, tracers, cells), F32),
        jax.ShapeDtypeStruct((levels, tracers, cells), F32),
        jax.ShapeDtypeStruct((levels, tracers, cells), F32),
        jax.ShapeDtypeStruct((levels + 1, tracers, cells), F32),
    ]
    ratio_scratch = pltpu.VMEM((levels, rows, cells), F32)
    stencil_scratch = [
        pltpu.VMEM((4, rows, tracers, cells), F32),
        pltpu.VMEM((levels, tracers, cells), F32),
    ]
    diffused, first, last, polar = pl.pallas_call(
        first_kernel,
        grid=(1,),
        out_shape=solved_shapes,
        in_specs=[whole(costate)] + [step_block(x, 1) for x in [diffusion] + couplings],
        out_specs=[whole(x) for x in solved_shapes],
        scratch_shapes=[ratio_scratch],
        compiler_params=params(),
        name="first",
    )(costate, diffusion, *couplings)
    after, before, edge, polars = exchange(
        diffused, first, last, polar, north_courant, south_courant, polar_shift, 1
    )
    surface_shape = jax.ShapeDtypeStruct((rows, tracers, cells), F32)
    operands = [diffused, after, before, edge, *polars]
    solved, first, last, polar, surface = pl.pallas_call(
        functools.partial(middle_kernel, 1),
        grid=(1,),
        out_shape=solved_shapes + [surface_shape],
        in_specs=[smem()]
        + [whole(x) for x in operands]
        + [step_block(x, 1) for x in couplings]
        + [whole(forced[1])]
        + [step_block(x, 0) for x in [diffusion] + couplings],
        out_specs=[whole(x) for x in solved_shapes + [surface_shape]],
        scratch_shapes=stencil_scratch + [ratio_scratch],
        compiler_params=params(),
        name="middle",
    )(polar_shift, *operands, *couplings, forced[1], diffusion, *couplings)
    after, before, edge, polars = exchange(
        solved, first, last, polar, north_courant, south_courant, polar_shift, 0
    )
    operands = [solved, after, before, edge, *polars]
    finals = [
        jax.ShapeDtypeStruct(costate.shape, F32),
        jax.ShapeDtypeStruct((tracers, rows, cells), F32),
    ]
    return tuple(
        pl.pallas_call(
            functools.partial(last_kernel, 0),
            grid=(1,),
            out_shape=finals,
            in_specs=[smem()]
            + [whole(x) for x in operands]
            + [step_block(x, 0) for x in couplings]
            + [whole(forced[0]), whole(surface)],
            out_specs=[whole(x) for x in finals],
            scratch_shapes=stencil_scratch,
            compiler_params=params(),
            name="last",
        )(polar_shift, *operands, *couplings, forced[0], surface)
    )


def solution(mesh):
    return jax.shard_map(
        per_device,
        mesh=mesh,
        in_specs=(
            P(None, None, "lat", "lon"),
            P(None, None, "lat", "lon"),
            P(None, "lat", "lon"),
            P(None, "lat", "lon"),
            P(None, "lat", "lon"),
            P(),
            P(None, ("lon", "lat"), None),
            P(None, ("lon", "lat")),
            P(None, ("lon", "lat")),
            P(None, None, ("lon", "lat")),
            P(None, None, ("lon", "lat")),
        ),
        out_specs=(P(None, None, "lat", "lon"), P(None, "lat", "lon")),
        check_vma=False,
    )
```

```python
import functools

import jax
import jax.numpy as jnp
from jax import lax
from jax.experimental import pallas as pl
from jax.experimental.pallas import tpu as pltpu
from jax.sharding import PartitionSpec as P

AXES = ("lon", "lat")
LANES = 128
CAP = 16
GROUP = 8
F32 = jnp.float32
BF16 = jnp.bfloat16
VMEM_LIMIT = 56 * 1024 * 1024


def vmem():
    return pl.BlockSpec(memory_space=pltpu.VMEM)


def smem():
    return pl.BlockSpec(memory_space=pltpu.SMEM)


def params():
    return pltpu.CompilerParams(vmem_limit_bytes=VMEM_LIMIT)


def dot(a, b, contract=((1,), (0,))):
    return lax.dot_general(a, b, (contract, ((), ())), preferred_element_type=F32)


def halves(x):
    high = x.astype(BF16)
    return high, (x - high.astype(F32)).astype(BF16)


def pack_kernel(counts, owners, columns, kernels, misfits, out, payload, target):
    steps, levels, held = kernels.shape
    tracers = misfits.shape[1]
    shape = (LANES, LANES)
    device = lax.broadcasted_iota(jnp.int32, shape, 0)
    table = counting_table()
    for step in range(steps):
        owner = owners[step]
        live = lax.broadcasted_iota(jnp.int32, owner.shape, 1) < counts[step, 0]
        owner = jnp.where(live, owner, -1)
        seen = jnp.zeros(shape, F32)
        for start in range(0, held, LANES):
            here = owner[:, start : start + LANES]
            hot = device == here
            counted = dot(jnp.where(hot, 1.0, 0.0).astype(BF16), table)
            rank = jnp.sum(
                jnp.where(hot, counted[:, :LANES] + seen, 0.0), axis=0, keepdims=True
            )
            seen = seen + counted[:, LANES:]
            target[:, start : start + LANES] = jnp.where(
                here >= 0, here * CAP + rank.astype(jnp.int32), -1
            )
        column = columns[step : step + 1, :].astype(F32) + 1.0
        column = jnp.where(lax.broadcasted_iota(jnp.int32, (8, held), 0) == 0, column, 0.0)
        unused = jnp.zeros((LANES - levels - tracers - 8, held), F32)
        high, low = halves(
            jnp.concatenate([kernels[step], misfits[step], column, unused], axis=0)
        )
        payload[:LANES, :] = high
        payload[LANES:, :] = low
        owned = 256 // CAP

        def place(i, carry):
            slot = lax.broadcasted_iota(jnp.int32, (owned * CAP, held), 0) + i * owned * CAP
            hot = jnp.where(slot == target[...], 1.0, 0.0).astype(BF16)
            both = dot(hot, payload[...], ((1,), (1,)))
            both = both[:, :LANES] + both[:, LANES:]
            out[pl.ds(i * owned, owned), step * CAP : (step + 1) * CAP, :] = both.reshape(
                owned, CAP, LANES
            )
            return carry

        lax.fori_loop(0, out.shape[0] // owned, place, 0)


def counting_table():
    shape = (LANES, LANES)
    earlier = lax.broadcasted_iota(jnp.int32, shape, 0) < lax.broadcasted_iota(
        jnp.int32, shape, 1
    )
    return jnp.concatenate(
        [jnp.where(earlier, 1.0, 0.0), jnp.ones(shape, F32)], axis=1
    ).astype(BF16)


def packed(counts, owners, columns, kernels, misfits):
    steps, held = columns.shape
    devices = lax.axis_size("lon") * lax.axis_size("lat")
    return pl.pallas_call(
        pack_kernel,
        out_shape=jax.ShapeDtypeStruct((devices, steps * CAP, LANES), F32),
        in_specs=[smem()] + [vmem()] * 4,
        out_specs=vmem(),
        scratch_shapes=[
            pltpu.VMEM((2 * LANES, held), BF16),
            pltpu.VMEM((1, held), jnp.int32),
        ],
        compiler_params=params(),
        name="pack",
    )(counts, owners, columns, kernels, misfits)


def forcing_kernel(step, received, out, fields, hots, place, ordered):
    levels, rows, tracers, cells = out.shape
    slots = received.shape[0] * CAP
    blocks = slots // LANES
    sources = LANES // CAP
    sub = lax.broadcasted_iota(jnp.int32, (rows, LANES), 0)
    at_column = levels + tracers
    for b in range(blocks):
        span = slice(b * LANES, (b + 1) * LANES)
        block = received[b * sources : (b + 1) * sources, step * CAP : (step + 1) * CAP, :]
        turned = block.reshape(LANES, LANES).T
        high, low = halves(turned)
        fields[:LANES, span] = high
        fields[LANES:, span] = low
        row = (turned[at_column : at_column + 1].astype(jnp.int32) - 1) >> 8
        hots[b * rows : (b + 1) * rows, :] = jnp.where(sub == row, 1.0, 0.0)
    counted = dot(hots[...].astype(BF16), counting_table())
    run = jnp.zeros((rows, LANES), F32)
    runs = []
    for b in range(blocks):
        runs.append(run)
        run = run + counted[b * rows : (b + 1) * rows, LANES:]
    filled = jnp.floor((run + (LANES - 1.0)) * (1.0 / LANES))
    start = jnp.zeros((rows, LANES), F32)
    for j in range(1, rows):
        start = start + jnp.where(sub >= j, pltpu.roll(filled, j, 0), 0.0)
    for b in range(blocks):
        hot = hots[b * rows : (b + 1) * rows, :]
        at = counted[b * rows : (b + 1) * rows, :LANES] + runs[b] + start * float(LANES)
        at = jnp.sum(hot * at, axis=0, keepdims=True)
        live = jnp.sum(hot, axis=0, keepdims=True) > 0.0
        place[:, b * LANES : (b + 1) * LANES] = jnp.where(live, at, -1.0)
    counts = [jnp.max(filled[r : r + 1, :]).astype(jnp.int32) for r in range(rows)]
    used = sum(counts)
    wide = 2 * LANES

    def sort(i, carry):
        slot = (lax.broadcasted_iota(jnp.int32, (wide, slots), 0) + i * wide).astype(F32)
        hot = jnp.where(slot == place[...], 1.0, 0.0).astype(BF16)
        both = dot(fields[...], hot, ((1,), (1,)))
        ordered[:, pl.ds(pl.multiple_of(i * wide, wide), wide)] = both[:LANES] + both[LANES:]
        return carry

    lax.fori_loop(0, (used + 1) // 2, sort, 0)
    out[...] = jnp.zeros_like(out)
    cell = lax.broadcasted_iota(jnp.int32, (cells, LANES), 0)
    first = jnp.int32(0)
    for r in range(rows):
        names = (cell + (r * cells + 1)).astype(F32)

        def add(p, carry):
            block = ordered[:, pl.ds(pl.multiple_of(p * LANES, LANES), LANES)]
            hot = jnp.where(names == block[at_column : at_column + 1], 1.0, 0.0).astype(BF16)
            product = block[:levels][:, None, :] * block[levels:at_column][None]
            high, low = halves(product.reshape(levels * tracers, LANES))
            total = dot(high, hot, ((1,), (1,))) + dot(low, hot, ((1,), (1,)))
            out[:, r, :, :] += total.reshape(levels, tracers, cells)
            return carry

        lax.fori_loop(first, first + counts[r], add, 0)
        first = first + counts[r]


def forcing(step, received, levels, tracers, rows, cells):
    slots = received.shape[0] * CAP
    return pl.pallas_call(
        functools.partial(forcing_kernel, step),
        out_shape=jax.ShapeDtypeStruct((levels, rows, tracers, cells), F32),
        in_specs=[vmem()],
        out_specs=vmem(),
        scratch_shapes=[
            pltpu.VMEM((2 * LANES, slots), BF16),
            pltpu.VMEM((slots // LANES * rows, LANES), F32),
            pltpu.VMEM((1, slots), F32),
            pltpu.VMEM((LANES, slots + rows * LANES), F32),
        ],
        compiler_params=params(),
        name="forcing",
    )(received)


def spread(x, row, tracers):
    return jnp.broadcast_to(x[row : row + 1, :], (tracers, x.shape[1]))


def eliminate(level, above, carry, rights, ratios):
    below, ratio, values = carry
    if above is None:
        above = jnp.zeros_like(below)
    inverse = 1.0 / (1.0 + below + above + below * ratio)
    lower = below * inverse
    ratio = -above * inverse
    ratios[level] = ratio
    tracers = rights[0].shape[0]
    fresh = [
        spread(inverse, r, tracers) * rights[r] + spread(lower, r, tracers) * values[r]
        for r in range(len(rights))
    ]
    return (above, ratio, fresh)


def substitute(diffused, ratios, north, south, east, first, last, polar, column):
    levels, rows, tracers, cells = diffused.shape
    lat = lax.axis_index("lat")
    at_start = lat == 0
    picked_north = jnp.where(at_start, north[0, 0:1, :], north[0, rows - 1 : rows, :])
    picked_south = jnp.where(at_start, south[0, 0:1, :], south[0, rows - 1 : rows, :])
    own = jnp.broadcast_to(1.0 - picked_north - picked_south, (tracers, cells))
    side = jnp.broadcast_to(jnp.where(at_start, picked_north, picked_south), (tracers, cells))
    picked_east = jnp.where(at_start, east[0, 0:1, :], east[0, rows - 1 : rows, :])
    groups = levels // GROUP
    polar[:, groups, 0, :] = jnp.broadcast_to(picked_east, (tracers, cells))
    lane = lax.broadcasted_iota(jnp.int32, (tracers, LANES), 1)

    def group(i, solved):
        at = groups - 1 - i
        west = jnp.zeros((tracers, LANES), F32)
        for j in range(GROUP - 1, -1, -1):
            level = at * GROUP + j
            ratio = ratios[level]
            fresh = []
            for r in range(rows):
                value = diffused[level, r] - spread(ratio, r, tracers) * solved[r]
                diffused[level, r] = value
                fresh.append(value)
                lanes = j * rows + r
                moved = pltpu.roll(value[:, :LANES], lanes, 1) if lanes else value[:, :LANES]
                west = jnp.where(lane == lanes, moved, west)
            solved = fresh
            first[level] = solved[0]
            last[level] = solved[rows - 1]
            polar[:, at, j, :] = own * jnp.where(
                at_start, solved[0], solved[rows - 1]
            ) + side * jnp.where(at_start, solved[1], solved[rows - 2])
        column[at] = west
        return solved

    lax.fori_loop(0, groups, group, [jnp.zeros((tracers, cells), F32)] * rows)


def first_kernel(
    costate, diffusion, north, south, east, diffused, first, last, polar, column, ratios
):
    levels, tracers, rows, cells = costate.shape
    zero = jnp.zeros((rows, cells), F32)
    carry = (zero, zero, [jnp.zeros((tracers, cells), F32)] * rows)

    def forward(level, above, carry):
        rights = [costate[level, :, r, :] for r in range(rows)]
        carry = eliminate(level, above, carry, rights, ratios)
        for r in range(rows):
            diffused[level, r] = carry[2][r]
        return carry

    def group(i, carry):
        for j in range(GROUP):
            level = i * GROUP + j
            carry = forward(level, diffusion[0, level], carry)
        return carry

    carry = lax.fori_loop(0, levels // GROUP - 1, group, carry)
    for level in range(levels - GROUP, levels):
        carry = forward(level, diffusion[0, level] if level < levels - 1 else None, carry)
    substitute(diffused, ratios, north, south, east, first, last, polar, column)


def meridional(level, row, diffused, after, before, coefs):
    rows = diffused.shape[1]
    own, north, south = coefs
    up = diffused[level, row + 1] if row < rows - 1 else after[level]
    down = diffused[level, row - 1] if row > 0 else before[level]
    return own * diffused[level, row] + north * up + south * down


def edge_kernel(column, after, before, north, south, edge):
    groups, tracers, lanes = column.shape
    rows = north.shape[1]
    lane = lax.broadcasted_iota(jnp.int32, (tracers, lanes), 1)

    def along_lanes(x):
        shape = (rows, lanes)
        own_lane = (lax.broadcasted_iota(jnp.int32, shape, 1) & (rows - 1)) == (
            lax.broadcasted_iota(jnp.int32, shape, 0)
        )
        picked = jnp.where(own_lane, jnp.broadcast_to(x[0, :, :1], shape), 0.0)
        return jnp.broadcast_to(jnp.sum(picked, axis=0, keepdims=True), (tracers, lanes))

    n, s = along_lanes(north), along_lanes(south)
    own = 1.0 - n - s

    def group(i, carry):
        here = column[i]
        up = pltpu.roll(here, lanes - 1, 1)
        down = pltpu.roll(here, 1, 1)
        for j in range(GROUP):
            level = i * GROUP + j
            bottom, top = j * rows, j * rows + rows - 1
            up = jnp.where(lane == top, pltpu.roll(after[level], top, 1), up)
            moved = pltpu.roll(before[level], bottom, 1) if bottom else before[level]
            down = jnp.where(lane == bottom, moved, down)
        edge[i] = own * here + n * up + s * down
        return carry

    lax.fori_loop(0, groups, group, 0)


def rotate_kernel(step, shift, circle, out, moved):
    parts, groups, group, cells = out.shape
    lat = lax.axis_index("lat")
    last_lat = lax.axis_size("lat") - 1
    rows = shift.shape[1] // lax.axis_size("lat")

    @pl.when((lat == 0) | (lat == last_lat))
    def _():
        amount = jnp.where(lat == 0, shift[step, 0], shift[step, rows * last_lat + rows - 1])
        amount = lax.rem(amount + 2 * parts * cells, parts * cells)
        hops = amount // cells
        inner = amount - hops * cells
        shape = (group, cells)
        lane = lax.broadcasted_iota(jnp.int32, shape, 1)
        back = lax.rem(cells - inner, cells)
        for part in range(parts):
            weight = jnp.broadcast_to(circle[part, groups, 0:1, :], shape)
            for g in range(groups):
                here = circle[part, g]
                following = jnp.where(
                    lane == cells - 1,
                    pltpu.roll(circle[(part + 1) % parts, g], cells - 1, 1),
                    pltpu.roll(here, cells - 1, 1),
                )
                moved[part, g] = pltpu.roll(here + weight * (following - here), back, 1)
        for part in range(parts):
            low = lax.rem(part + hops, parts)
            high = lax.rem(part + hops + 1, parts)
            for g in range(groups):
                out[part, g] = jnp.where(lane < cells - inner, moved[low, g], moved[high, g])


def prepare_stencil(north, south, east, coefs):
    rows, cells = north.shape[1:]
    tracers = coefs.shape[2]
    for r in range(rows):
        n = north[0, r : r + 1, :]
        s = south[0, r : r + 1, :]
        coefs[0, r] = jnp.broadcast_to(1.0 - n - s, (tracers, cells))
        coefs[1, r] = jnp.broadcast_to(n, (tracers, cells))
        coefs[2, r] = jnp.broadcast_to(s, (tracers, cells))
        coefs[3, r] = jnp.broadcast_to(east[0, r : r + 1, :], (tracers, cells))


def transported(group, lane_at, diffused, after, before, edge_row, coefs, turned):
    level = group * GROUP + lane_at
    rows, tracers, cells = diffused.shape[1:]
    lat = lax.axis_index("lat")
    last = lax.broadcasted_iota(jnp.int32, (tracers, cells), 1) == cells - 1
    result = []
    for r in range(rows):
        mer = meridional(level, r, diffused, after, before, [coefs[k, r] for k in range(3)])
        arrived = pltpu.roll(edge_row, LANES - 1 - (lane_at * rows + r), 1)
        arrived = jnp.concatenate([arrived] * (cells // LANES), axis=1)
        following = jnp.where(last, arrived, pltpu.roll(mer, cells - 1, 1))
        result.append(mer + coefs[3, r] * (following - mer))
    polar = turned[:, group, lane_at, :]
    result[0] = jnp.where(lat == 0, polar, result[0])
    result[rows - 1] = jnp.where(lat == lax.axis_size("lat") - 1, polar, result[rows - 1])
    return result


def middle_kernel(
    diffused,
    after,
    before,
    edge,
    turned,
    north,
    south,
    east,
    forced,
    diffusion,
    next_north,
    next_south,
    next_east,
    solved,
    first,
    last,
    polar,
    column,
    surface,
    coefs,
    ratios,
):
    levels, rows, tracers, cells = diffused.shape
    prepare_stencil(north, south, east, coefs)
    zero = jnp.zeros((rows, cells), F32)
    carry = (zero, zero, [jnp.zeros((tracers, cells), F32)] * rows)

    def forward(g, j, above, edge_row, carry):
        level = g * GROUP + j
        rights = transported(g, j, diffused, after, before, edge_row, coefs, turned)
        rights = [rights[r] + forced[level, r] for r in range(rows)]
        if above is None:
            for r in range(rows):
                surface[r] = rights[r]
        carry = eliminate(level, above, carry, rights, ratios)
        for r in range(rows):
            solved[level, r] = carry[2][r]
        return carry

    def group(i, carry):
        edge_row = edge[i]
        for j in range(GROUP):
            carry = forward(i, j, diffusion[0, i * GROUP + j], edge_row, carry)
        return carry

    groups = levels // GROUP
    carry = lax.fori_loop(0, groups - 1, group, carry)
    edge_row = edge[groups - 1]
    for j in range(GROUP):
        level = levels - GROUP + j
        above = diffusion[0, level] if level < levels - 1 else None
        carry = forward(groups - 1, j, above, edge_row, carry)
    substitute(
        solved, ratios, next_north, next_south, next_east, first, last, polar, column
    )


def last_kernel(
    diffused,
    after,
    before,
    edge,
    turned,
    north,
    south,
    east,
    forced,
    surface,
    state,
    gradient,
    coefs,
):
    levels, rows, tracers, cells = diffused.shape
    prepare_stencil(north, south, east, coefs)

    def group(i, carry):
        edge_row = edge[i]
        for j in range(GROUP):
            level = i * GROUP + j
            values = transported(i, j, diffused, after, before, edge_row, coefs, turned)
            for r in range(rows):
                state[level, :, r, :] = values[r] + forced[level, r]
        return carry

    lax.fori_loop(0, levels // GROUP, group, 0)
    for r in range(rows):
        gradient[:, r, :] = surface[r] + state[levels - 1, :, r, :]


def step_block(array, step):
    shape = (1,) + array.shape[1:]
    return pl.BlockSpec(shape, lambda i: (step,) + (0,) * (len(shape) - 1))


def whole(array):
    return pl.BlockSpec(array.shape, lambda i: (0,) * len(array.shape))


def exchange(first, last, polar, column, north, south, shift, step):
    lat_count = lax.axis_size("lat")
    lon_count = lax.axis_size("lon")
    up = [(i, i + 1) for i in range(lat_count - 1)]
    down = [(j, i) for i, j in up]
    circle = lax.all_to_all(polar, "lon", 0, 0, tiled=True)
    after = lax.ppermute(first, "lat", down)
    before = lax.ppermute(last, "lat", up)
    parts, groups, group, cells = polar.shape
    turned = pl.pallas_call(
        functools.partial(rotate_kernel, step),
        out_shape=jax.ShapeDtypeStruct((parts, groups - 1, group, cells), F32),
        in_specs=[smem(), vmem()],
        out_specs=vmem(),
        scratch_shapes=[pltpu.VMEM((parts, groups - 1, group, cells), F32)],
        compiler_params=params(),
        name="rotate",
    )(shift, circle)
    turned = lax.all_to_all(turned, "lon", 0, 0, tiled=True)
    tile = pl.BlockSpec(after.shape[:2] + (LANES,), lambda i: (0, 0, 0))
    edge = pl.pallas_call(
        edge_kernel,
        grid=(1,),
        out_shape=jax.ShapeDtypeStruct(column.shape, F32),
        in_specs=[whole(column), tile, tile] + [step_block(north, step)] * 2,
        out_specs=whole(column),
        compiler_params=params(),
        name="edge",
    )(column, after, before, north, south)
    west = [(i, (i - 1) % lon_count) for i in range(lon_count)]
    return after, before, lax.ppermute(edge, "lon", west), turned


def per_device(
    costate,
    diffusion,
    east_courant,
    north_courant,
    south_courant,
    polar_shift,
    owners,
    columns,
    sounding_counts,
    kernels,
    misfits,
):
    levels, tracers, rows, cells = costate.shape
    devices = lax.axis_size("lon") * lax.axis_size("lat")
    owner_rows = owners.reshape(owners.shape[0], 1, owners.shape[1])
    couplings = [north_courant, south_courant, east_courant]

    sent = packed(sounding_counts, owner_rows, columns, kernels, misfits)
    got = lax.all_to_all(sent, AXES, 0, 0, tiled=True)
    forced = {step: forcing(step, got, levels, tracers, rows, cells) for step in (1, 0)}

    solved_shapes = [
        jax.ShapeDtypeStruct((levels, rows, tracers, cells), F32),
        jax.ShapeDtypeStruct((levels, tracers, cells), F32),
        jax.ShapeDtypeStruct((levels, tracers, cells), F32),
        jax.ShapeDtypeStruct((tracers, levels // GROUP + 1, GROUP, cells), F32),
        jax.ShapeDtypeStruct((levels // GROUP, tracers, LANES), F32),
    ]
    ratio_scratch = pltpu.VMEM((levels, rows, cells), F32)
    stencil_scratch = [pltpu.VMEM((4, rows, tracers, cells), F32)]
    diffused, *boundary = pl.pallas_call(
        first_kernel,
        grid=(1,),
        out_shape=solved_shapes,
        in_specs=[whole(costate)] + [step_block(x, 1) for x in [diffusion] + couplings],
        out_specs=[whole(x) for x in solved_shapes],
        scratch_shapes=[ratio_scratch],
        compiler_params=params(),
        name="first",
    )(costate, diffusion, *couplings)
    incoming = exchange(*boundary, north_courant, south_courant, polar_shift, 1)
    surface_shape = jax.ShapeDtypeStruct((rows, tracers, cells), F32)
    operands = [diffused, *incoming]
    solved, *boundary, surface = pl.pallas_call(
        middle_kernel,
        grid=(1,),
        out_shape=solved_shapes + [surface_shape],
        in_specs=[whole(x) for x in operands]
        + [step_block(x, 1) for x in couplings]
        + [whole(forced[1])]
        + [step_block(x, 0) for x in [diffusion] + couplings],
        out_specs=[whole(x) for x in solved_shapes + [surface_shape]],
        scratch_shapes=stencil_scratch + [ratio_scratch],
        compiler_params=params(),
        name="middle",
    )(*operands, *couplings, forced[1], diffusion, *couplings)
    incoming = exchange(*boundary, north_courant, south_courant, polar_shift, 0)
    operands = [solved, *incoming]
    finals = [
        jax.ShapeDtypeStruct(costate.shape, F32),
        jax.ShapeDtypeStruct((tracers, rows, cells), F32),
    ]
    return tuple(
        pl.pallas_call(
            last_kernel,
            grid=(1,),
            out_shape=finals,
            in_specs=[whole(x) for x in operands]
            + [step_block(x, 0) for x in couplings]
            + [whole(forced[0]), whole(surface)],
            out_specs=[whole(x) for x in finals],
            scratch_shapes=stencil_scratch,
            compiler_params=params(),
            name="last",
        )(*operands, *couplings, forced[0], surface)
    )


def solution(mesh):
    return jax.shard_map(
        per_device,
        mesh=mesh,
        in_specs=(
            P(None, None, "lat", "lon"),
            P(None, None, "lat", "lon"),
            P(None, "lat", "lon"),
            P(None, "lat", "lon"),
            P(None, "lat", "lon"),
            P(),
            P(None, ("lon", "lat"), None),
            P(None, ("lon", "lat")),
            P(None, ("lon", "lat")),
            P(None, None, ("lon", "lat")),
            P(None, None, ("lon", "lat")),
        ),
        out_specs=(P(None, None, "lat", "lon"), P(None, "lat", "lon")),
        check_vma=False,
    )
```

```python
import functools

import jax
import jax.numpy as jnp
from jax import lax
from jax.experimental import pallas as pl
from jax.experimental.pallas import tpu as pltpu
from jax.sharding import PartitionSpec as P

AXES = ("lon", "lat")
LANES = 128
CAP = 16
GROUP = 8
F32 = jnp.float32
BF16 = jnp.bfloat16
MIB = 1024 * 1024


def vmem():
    return pl.BlockSpec(memory_space=pltpu.VMEM)


def smem():
    return pl.BlockSpec(memory_space=pltpu.SMEM)


def hbm():
    return pl.BlockSpec(memory_space=pltpu.HBM)


def params(limit):
    return pltpu.CompilerParams(vmem_limit_bytes=limit * MIB)


def held(x):
    return pltpu.with_memory_space_constraint(x, pltpu.VMEM)


def pinned(x):
    return pltpu.with_memory_space_constraint(x, pltpu.HBM)


def resident(*shape):
    return pltpu.VMEM(shape, F32)


def chunk(source, target, done, g):
    at = pl.ds(g * GROUP, GROUP)
    return pltpu.make_async_copy(source.at[at], target.at[at], done.at[g])


def start_all(source, target, done):
    for g in range(source.shape[0] // GROUP):
        chunk(source, target, done, g).start()


def wait_all(source, target, done):
    for g in range(source.shape[0] // GROUP):
        chunk(source, target, done, g).wait()


def dot(a, b, contract=((1,), (0,))):
    return lax.dot_general(a, b, (contract, ((), ())), preferred_element_type=F32)


def halves(x):
    high = x.astype(BF16)
    return high, (x - high.astype(F32)).astype(BF16)


def pack_kernel(counts, owners, columns, kernels, misfits, out, payload, target):
    steps, levels, held = kernels.shape
    tracers = misfits.shape[1]
    shape = (LANES, LANES)
    device = lax.broadcasted_iota(jnp.int32, shape, 0)
    table = counting_table()
    for step in range(steps):
        owner = owners[step]
        live = lax.broadcasted_iota(jnp.int32, owner.shape, 1) < counts[step, 0]
        owner = jnp.where(live, owner, -1)
        seen = jnp.zeros(shape, F32)
        for start in range(0, held, LANES):
            here = owner[:, start : start + LANES]
            hot = device == here
            counted = dot(jnp.where(hot, 1.0, 0.0).astype(BF16), table)
            rank = jnp.sum(
                jnp.where(hot, counted[:, :LANES] + seen, 0.0), axis=0, keepdims=True
            )
            seen = seen + counted[:, LANES:]
            target[:, start : start + LANES] = jnp.where(
                here >= 0, here * CAP + rank.astype(jnp.int32), -1
            )
        column = columns[step : step + 1, :].astype(F32) + 1.0
        column = jnp.where(lax.broadcasted_iota(jnp.int32, (8, held), 0) == 0, column, 0.0)
        unused = jnp.zeros((LANES - levels - tracers - 8, held), F32)
        high, low = halves(
            jnp.concatenate([kernels[step], misfits[step], column, unused], axis=0)
        )
        payload[:LANES, :] = high
        payload[LANES:, :] = low
        owned = 256 // CAP

        def place(i, carry):
            slot = lax.broadcasted_iota(jnp.int32, (owned * CAP, held), 0) + i * owned * CAP
            hot = jnp.where(slot == target[...], 1.0, 0.0).astype(BF16)
            both = dot(hot, payload[...], ((1,), (1,)))
            both = both[:, :LANES] + both[:, LANES:]
            out[pl.ds(i * owned, owned), step * CAP : (step + 1) * CAP, :] = both.reshape(
                owned, CAP, LANES
            )
            return carry

        lax.fori_loop(0, out.shape[0] // owned, place, 0)


def counting_table():
    shape = (LANES, LANES)
    earlier = lax.broadcasted_iota(jnp.int32, shape, 0) < lax.broadcasted_iota(
        jnp.int32, shape, 1
    )
    return jnp.concatenate(
        [jnp.where(earlier, 1.0, 0.0), jnp.ones(shape, F32)], axis=1
    ).astype(BF16)


def packed(counts, owners, columns, kernels, misfits):
    steps, slots = columns.shape
    devices = lax.axis_size("lon") * lax.axis_size("lat")
    return pl.pallas_call(
        pack_kernel,
        out_shape=jax.ShapeDtypeStruct((devices, steps * CAP, LANES), F32),
        in_specs=[smem()] + [vmem()] * 4,
        out_specs=vmem(),
        scratch_shapes=[
            pltpu.VMEM((2 * LANES, slots), BF16),
            pltpu.VMEM((1, slots), jnp.int32),
        ],
        compiler_params=params(8),
        name="pack",
    )(counts, held(owners), held(columns), held(kernels), held(misfits))


def forcing_kernel(step, received, result, out, fields, hots, place, ordered, done):
    levels, rows, tracers, cells = out.shape
    slots = received.shape[0] * CAP
    blocks = slots // LANES
    sources = LANES // CAP
    sub = lax.broadcasted_iota(jnp.int32, (rows, LANES), 0)
    at_column = levels + tracers
    for b in range(blocks):
        span = slice(b * LANES, (b + 1) * LANES)
        block = received[b * sources : (b + 1) * sources, step * CAP : (step + 1) * CAP, :]
        turned = block.reshape(LANES, LANES).T
        high, low = halves(turned)
        fields[:LANES, span] = high
        fields[LANES:, span] = low
        row = (turned[at_column : at_column + 1].astype(jnp.int32) - 1) >> 8
        hots[b * rows : (b + 1) * rows, :] = jnp.where(sub == row, 1.0, 0.0)
    counted = dot(hots[...].astype(BF16), counting_table())
    run = jnp.zeros((rows, LANES), F32)
    runs = []
    for b in range(blocks):
        runs.append(run)
        run = run + counted[b * rows : (b + 1) * rows, LANES:]
    filled = jnp.floor((run + (LANES - 1.0)) * (1.0 / LANES))
    start = jnp.zeros((rows, LANES), F32)
    for j in range(1, rows):
        start = start + jnp.where(sub >= j, pltpu.roll(filled, j, 0), 0.0)
    for b in range(blocks):
        hot = hots[b * rows : (b + 1) * rows, :]
        at = counted[b * rows : (b + 1) * rows, :LANES] + runs[b] + start * float(LANES)
        at = jnp.sum(hot * at, axis=0, keepdims=True)
        live = jnp.sum(hot, axis=0, keepdims=True) > 0.0
        place[:, b * LANES : (b + 1) * LANES] = jnp.where(live, at, -1.0)
    counts = [jnp.max(filled[r : r + 1, :]).astype(jnp.int32) for r in range(rows)]
    used = sum(counts)
    wide = 2 * LANES

    def sort(i, carry):
        slot = (lax.broadcasted_iota(jnp.int32, (wide, slots), 0) + i * wide).astype(F32)
        hot = jnp.where(slot == place[...], 1.0, 0.0).astype(BF16)
        both = dot(fields[...], hot, ((1,), (1,)))
        ordered[:, pl.ds(pl.multiple_of(i * wide, wide), wide)] = both[:LANES] + both[LANES:]
        return carry

    lax.fori_loop(0, (used + 1) // 2, sort, 0)
    out[...] = jnp.zeros_like(out)
    cell = lax.broadcasted_iota(jnp.int32, (cells, LANES), 0)
    first = jnp.int32(0)
    for r in range(rows):
        names = (cell + (r * cells + 1)).astype(F32)

        def add(p, carry):
            block = ordered[:, pl.ds(pl.multiple_of(p * LANES, LANES), LANES)]
            hot = jnp.where(names == block[at_column : at_column + 1], 1.0, 0.0).astype(BF16)
            product = block[:levels][:, None, :] * block[levels:at_column][None]
            high, low = halves(product.reshape(levels * tracers, LANES))
            total = dot(high, hot, ((1,), (1,))) + dot(low, hot, ((1,), (1,)))
            out[:, r, :, :] += total.reshape(levels, tracers, cells)
            return carry

        lax.fori_loop(first, first + counts[r], add, 0)
        first = first + counts[r]
        pltpu.make_async_copy(out.at[:, r], result.at[:, r], done.at[r]).start()
    for r in range(rows):
        pltpu.make_async_copy(out.at[:, r], result.at[:, r], done.at[r]).wait()


def forcing(step, received, levels, tracers, rows, cells):
    slots = received.shape[0] * CAP
    return pl.pallas_call(
        functools.partial(forcing_kernel, step),
        out_shape=pltpu.HBM((levels, rows, tracers, cells), F32),
        in_specs=[vmem()],
        out_specs=hbm(),
        scratch_shapes=[
            pltpu.VMEM((levels, rows, tracers, cells), F32),
            pltpu.VMEM((2 * LANES, slots), BF16),
            pltpu.VMEM((slots // LANES * rows, LANES), F32),
            pltpu.VMEM((1, slots), F32),
            pltpu.VMEM((LANES, slots + rows * LANES), F32),
            pltpu.SemaphoreType.DMA((rows,)),
        ],
        compiler_params=params(14),
        name="forcing",
    )(held(received))


def spread(x, row, tracers):
    return jnp.broadcast_to(x[row : row + 1, :], (tracers, x.shape[1]))


def eliminate(level, above, carry, rights, ratios):
    below, ratio, values = carry
    if above is None:
        above = jnp.zeros_like(below)
    inverse = 1.0 / (1.0 + below + above + below * ratio)
    lower = below * inverse
    ratio = -above * inverse
    ratios[level] = ratio
    tracers = rights[0].shape[0]
    fresh = [
        spread(inverse, r, tracers) * rights[r] + spread(lower, r, tracers) * values[r]
        for r in range(len(rights))
    ]
    return (above, ratio, fresh)


def substitute(step, diffused, ratios, couplings, result, first, last, polar, column, done):
    levels, rows, tracers, cells = diffused.shape
    lat = lax.axis_index("lat")
    at_start = lat == 0

    def picked(x):
        return jnp.where(at_start, x[step, 0:1, :], x[step, rows - 1 : rows, :])

    north, south, east = [picked(x) for x in couplings]
    own = jnp.broadcast_to(1.0 - north - south, (tracers, cells))
    side = jnp.broadcast_to(jnp.where(at_start, north, south), (tracers, cells))
    polar[levels] = jnp.broadcast_to(east, (tracers, cells))
    groups = levels // GROUP
    lane = lax.broadcasted_iota(jnp.int32, (tracers, LANES), 1)

    def group(i, solved):
        at = groups - 1 - i
        west = jnp.zeros((tracers, LANES), F32)
        for j in range(GROUP - 1, -1, -1):
            level = at * GROUP + j
            ratio = ratios[level]
            fresh = []
            for r in range(rows):
                value = diffused[level, r] - spread(ratio, r, tracers) * solved[r]
                diffused[level, r] = value
                fresh.append(value)
                lanes = j * rows + r
                moved = pltpu.roll(value[:, :LANES], lanes, 1) if lanes else value[:, :LANES]
                west = jnp.where(lane == lanes, moved, west)
            solved = fresh
            first[level] = solved[0]
            last[level] = solved[rows - 1]
            polar[level] = own * jnp.where(
                at_start, solved[0], solved[rows - 1]
            ) + side * jnp.where(at_start, solved[1], solved[rows - 2])
        column[at] = west
        chunk(diffused, result, done, at).start()
        return solved

    lax.fori_loop(0, groups, group, [jnp.zeros((tracers, cells), F32)] * rows)
    wait_all(diffused, result, done)


def forward_sweep(levels, rows, tracers, cells, diffusion, right_of):
    zero = jnp.zeros((rows, cells), F32)
    carry = (zero, zero, [jnp.zeros((tracers, cells), F32)] * rows)
    groups = levels // GROUP

    def one(g, j, above, carry):
        rights, ratios, store = right_of(g, j, above is None)
        carry = eliminate(g * GROUP + j, above, carry, rights, ratios)
        store(carry[2])
        return carry

    def group(g, carry):
        for j in range(GROUP):
            carry = one(g, j, diffusion(g * GROUP + j), carry)
        return carry

    carry = lax.fori_loop(0, groups - 1, group, carry)
    for j in range(GROUP):
        level = levels - GROUP + j
        carry = one(groups - 1, j, diffusion(level) if level < levels - 1 else None, carry)


def first_kernel(
    step,
    costate,
    diffusion,
    north,
    south,
    east,
    result,
    first,
    last,
    polar,
    column,
    staged,
    diffused,
    ratios,
    arrived,
    sent,
):
    levels, tracers, rows, cells = costate.shape
    start_all(costate, staged, arrived)

    def right_of(g, j, final):
        if j == 0:
            chunk(costate, staged, arrived, g).wait()
        level = g * GROUP + j
        rights = [staged[level, :, r, :] for r in range(rows)]

        def store(values):
            for r in range(rows):
                diffused[level, r] = values[r]

        return rights, ratios, store

    forward_sweep(levels, rows, tracers, cells, lambda level: diffusion[step, level], right_of)
    couplings = (north, south, east)
    substitute(step, diffused, ratios, couplings, result, first, last, polar, column, sent)


def meridional(level, row, diffused, after, before, coefs):
    rows = diffused.shape[1]
    own, north, south = coefs
    up = diffused[level, row + 1] if row < rows - 1 else after[level]
    down = diffused[level, row - 1] if row > 0 else before[level]
    return own * diffused[level, row] + north * up + south * down


def borders_kernel(
    step, shift, polar, nearby, column, after, before, north, south, turned, edge
):
    groups, tracers, lanes = column.shape
    rows, cells = north.shape[1:]
    lane = lax.broadcasted_iota(jnp.int32, (tracers, lanes), 1)

    def along_lanes(x):
        shape = (rows, lanes)
        own_lane = (lax.broadcasted_iota(jnp.int32, shape, 1) & (rows - 1)) == (
            lax.broadcasted_iota(jnp.int32, shape, 0)
        )
        picked = jnp.where(own_lane, jnp.broadcast_to(x[step, :, :1], shape), 0.0)
        return jnp.broadcast_to(jnp.sum(picked, axis=0, keepdims=True), (tracers, lanes))

    n, s = along_lanes(north), along_lanes(south)
    own = 1.0 - n - s

    def group(i, carry):
        here = column[i]
        up = pltpu.roll(here, lanes - 1, 1)
        down = pltpu.roll(here, 1, 1)
        for j in range(GROUP):
            level = i * GROUP + j
            bottom, top = j * rows, j * rows + rows - 1
            up = jnp.where(lane == top, pltpu.roll(after[level, :, :LANES], top, 1), up)
            moved = before[level, :, :LANES]
            moved = pltpu.roll(moved, bottom, 1) if bottom else moved
            down = jnp.where(lane == bottom, moved, down)
        edge[i] = own * here + n * up + s * down
        return carry

    lax.fori_loop(0, groups, group, 0)
    lat = lax.axis_index("lat")
    last_lat = lax.axis_size("lat") - 1

    @pl.when((lat == 0) | (lat == last_lat))
    def _():
        levels = turned.shape[0]
        circle = cells * lax.axis_size("lon")
        amount = jnp.where(lat == 0, shift[step, 0], shift[step, rows * last_lat + rows - 1])
        back = 2 * cells - (lax.rem(amount + 2 * circle, circle) & (cells - 1))
        weight = jnp.concatenate([polar[levels], nearby[levels]], axis=1)

        def one(i, carry):
            for j in range(4):
                level = i * 4 + j
                row = jnp.concatenate([polar[level], nearby[level]], axis=1)
                moved = row + weight * (pltpu.roll(row, 2 * cells - 1, 1) - row)
                turned[level] = pltpu.roll(moved, back, 1)[:, :cells]
            return carry

        lax.fori_loop(0, levels // 4, one, 0)


def prepare_stencil(step, north, south, east, coefs):
    rows, cells = north.shape[1:]
    tracers = coefs.shape[2]
    for r in range(rows):
        n = north[step, r : r + 1, :]
        s = south[step, r : r + 1, :]
        coefs[0, r] = jnp.broadcast_to(1.0 - n - s, (tracers, cells))
        coefs[1, r] = jnp.broadcast_to(n, (tracers, cells))
        coefs[2, r] = jnp.broadcast_to(s, (tracers, cells))
        coefs[3, r] = jnp.broadcast_to(east[step, r : r + 1, :], (tracers, cells))


def transported(level, lane_at, diffused, after, before, edge_row, coefs, south_pole, north_pole):
    rows, tracers, cells = diffused.shape[1:]
    lat = lax.axis_index("lat")
    last = lax.broadcasted_iota(jnp.int32, (tracers, cells), 1) == cells - 1
    result = []
    for r in range(rows):
        mer = meridional(level, r, diffused, after, before, [coefs[k, r] for k in range(3)])
        arrived = pltpu.roll(edge_row, LANES - 1 - (lane_at * rows + r), 1)
        arrived = jnp.concatenate([arrived] * (cells // LANES), axis=1)
        following = jnp.where(last, arrived, pltpu.roll(mer, cells - 1, 1))
        result.append(mer + coefs[3, r] * (following - mer))
    result[0] = jnp.where(lat == 0, south_pole[level], result[0])
    result[rows - 1] = jnp.where(
        lat == lax.axis_size("lat") - 1, north_pole[level], result[rows - 1]
    )
    return result


def start_pairs(diffused_in, diffused, arrived, forcing_in, forced, brought):
    for g in range(diffused.shape[0] // GROUP):
        chunk(diffused_in, diffused, arrived, g).start()
        chunk(forcing_in, forced, brought, g).start()


def middle_kernel(
    step,
    before_step,
    after,
    before,
    edge,
    south_pole,
    north_pole,
    forcing_in,
    diffusion,
    north,
    south,
    east,
    result,
    first,
    last,
    polar,
    column,
    surface,
    coefs,
    ratios,
    diffused,
    forced,
    solved,
    arrived,
    brought,
    sent,
):
    levels, rows, tracers, cells = diffused.shape
    start_pairs(before_step, diffused, arrived, forcing_in, forced, brought)
    prepare_stencil(step, north, south, east, coefs)

    def right_of(g, j, final):
        if j == 0:
            chunk(before_step, diffused, arrived, g).wait()
            chunk(forcing_in, forced, brought, g).wait()
        level = g * GROUP + j
        rights = transported(
            level, j, diffused, after, before, edge[g], coefs, south_pole, north_pole
        )
        rights = [rights[r] + forced[level, r] for r in range(rows)]
        if final:
            for r in range(rows):
                surface[r] = rights[r]

        def store(values):
            for r in range(rows):
                solved[level, r] = values[r]

        return rights, ratios, store

    forward_sweep(
        levels, rows, tracers, cells, lambda level: diffusion[step - 1, level], right_of
    )
    couplings = (north, south, east)
    substitute(step - 1, solved, ratios, couplings, result, first, last, polar, column, sent)


def last_kernel(
    step,
    before_step,
    after,
    before,
    edge,
    south_pole,
    north_pole,
    forcing_in,
    north,
    south,
    east,
    surface,
    state,
    gradient,
    coefs,
    diffused,
    forced,
    staged,
    arrived,
    brought,
    sent,
):
    levels, rows, tracers, cells = diffused.shape
    start_pairs(before_step, diffused, arrived, forcing_in, forced, brought)
    prepare_stencil(step, north, south, east, coefs)
    groups = levels // GROUP

    def group(g, carry):
        chunk(before_step, diffused, arrived, g).wait()
        chunk(forcing_in, forced, brought, g).wait()
        edge_row = edge[g]
        for j in range(GROUP):
            level = g * GROUP + j
            values = transported(
                level, j, diffused, after, before, edge_row, coefs, south_pole, north_pole
            )
            for r in range(rows):
                staged[level, :, r, :] = values[r] + forced[level, r]
        chunk(staged, state, sent, g).start()
        return carry

    lax.fori_loop(0, groups, group, 0)
    for r in range(rows):
        gradient[:, r, :] = surface[r] + staged[levels - 1, :, r, :]
    wait_all(staged, state, sent)


def exchange(first, last, polar, column, north, south, shift, step):
    lat_count = lax.axis_size("lat")
    lon_count = lax.axis_size("lon")
    up = [(i, i + 1) for i in range(lat_count - 1)]
    down = [(j, i) for i, j in up]
    poles = (0, lat_count - 1)

    def pairs(lats, hops):
        return [
            (((j + hops) % lon_count) * lat_count + lat, j * lat_count + lat)
            for lat in lats
            for j in range(lon_count)
        ]

    nearby = lax.ppermute(polar, AXES, pairs(poles, 1))
    after = lax.ppermute(first, "lat", down)
    before = lax.ppermute(last, "lat", up)
    levels, tracers, cells = first.shape
    turned, edge = pl.pallas_call(
        functools.partial(borders_kernel, step),
        out_shape=[resident(levels, tracers, cells), resident(*column.shape)],
        in_specs=[smem()] + [vmem()] * 7,
        out_specs=[vmem()] * 2,
        compiler_params=params(4),
        name="borders",
    )(shift, *[held(x) for x in (polar, nearby, column, after, before, north, south)])
    west = [(i, (i - 1) % lon_count) for i in range(lon_count)]
    edge = lax.ppermute(edge, "lon", west)
    moved = []
    for lat, row in zip(poles, (0, shift.shape[1] - 1)):
        hops = jnp.mod(shift[step, row], cells * lon_count) // cells
        moved.append(
            lax.switch(
                hops,
                [
                    functools.partial(
                        lambda k, lat, x: lax.ppermute(x, AXES, pairs((lat,), k)), k, lat
                    )
                    for k in range(lon_count)
                ],
                turned,
            )
        )
    return [held(x) for x in (after, before, edge, *moved)]


def per_device(
    costate,
    diffusion,
    east_courant,
    north_courant,
    south_courant,
    polar_shift,
    owners,
    columns,
    sounding_counts,
    kernels,
    misfits,
):
    levels, tracers, rows, cells = costate.shape
    owner_rows = owners.reshape(owners.shape[0], 1, owners.shape[1])
    couplings = [held(x) for x in (north_courant, south_courant, east_courant)]
    diffusion = held(diffusion)
    groups = levels // GROUP

    sent = packed(sounding_counts, owner_rows, columns, kernels, misfits)
    got = lax.all_to_all(sent, AXES, 0, 0, tiled=True)
    forced = {step: forcing(step, got, levels, tracers, rows, cells) for step in (1, 0)}

    solved_shapes = [
        pltpu.HBM((levels, rows, tracers, cells), F32),
        resident(levels, tracers, cells),
        resident(levels, tracers, cells),
        resident(levels + 1, tracers, cells),
        resident(groups, tracers, LANES),
    ]
    ratios = pltpu.VMEM((levels, rows, cells), F32)
    coefs = pltpu.VMEM((4, rows, tracers, cells), F32)
    field = pltpu.VMEM((levels, rows, tracers, cells), F32)
    output = pltpu.VMEM(costate.shape, F32)
    semaphores = pltpu.SemaphoreType.DMA((groups,))
    diffused, *boundary = pl.pallas_call(
        functools.partial(first_kernel, 1),
        out_shape=solved_shapes,
        in_specs=[hbm()] + [vmem()] * 4,
        out_specs=[hbm()] + [vmem()] * 4,
        scratch_shapes=[output, field, ratios] + [semaphores] * 2,
        compiler_params=params(14),
        name="first",
    )(pinned(costate), diffusion, *couplings)
    incoming = exchange(*boundary, *couplings[:2], polar_shift, 1)
    solved, *boundary, surface = pl.pallas_call(
        functools.partial(middle_kernel, 1),
        out_shape=solved_shapes + [resident(rows, tracers, cells)],
        in_specs=[hbm()] + [vmem()] * 5 + [hbm()] + [vmem()] * 4,
        out_specs=[hbm()] + [vmem()] * 5,
        scratch_shapes=[coefs, ratios] + [field] * 3 + [semaphores] * 3,
        compiler_params=params(20),
        name="middle",
    )(pinned(diffused), *incoming, pinned(forced[1]), diffusion, *couplings)
    incoming = exchange(*boundary, *couplings[:2], polar_shift, 0)
    return tuple(
        pl.pallas_call(
            functools.partial(last_kernel, 0),
            out_shape=[
                pltpu.HBM(costate.shape, F32),
                jax.ShapeDtypeStruct((tracers, rows, cells), F32),
            ],
            in_specs=[hbm()] + [vmem()] * 5 + [hbm()] + [vmem()] * 4,
            out_specs=[hbm(), vmem()],
            scratch_shapes=[coefs, field, field, output] + [semaphores] * 3,
            compiler_params=params(20),
            name="last",
        )(pinned(solved), *incoming, pinned(forced[0]), *couplings, surface)
    )


def solution(mesh):
    return jax.shard_map(
        per_device,
        mesh=mesh,
        in_specs=(
            P(None, None, "lat", "lon"),
            P(None, None, "lat", "lon"),
            P(None, "lat", "lon"),
            P(None, "lat", "lon"),
            P(None, "lat", "lon"),
            P(),
            P(None, ("lon", "lat"), None),
            P(None, ("lon", "lat")),
            P(None, ("lon", "lat")),
            P(None, None, ("lon", "lat")),
            P(None, None, ("lon", "lat")),
        ),
        out_specs=(P(None, None, "lat", "lon"), P(None, "lat", "lon")),
        check_vma=False,
    )
```

```python
import functools

import jax
import jax.numpy as jnp
from jax import lax
from jax.experimental import pallas as pl
from jax.experimental.pallas import tpu as pltpu
from jax.sharding import PartitionSpec as P

AXES = ("lon", "lat")
LANES = 128
CAP = 16
GROUP = 8
F32 = jnp.float32
BF16 = jnp.bfloat16
MIB = 1024 * 1024


def vmem():
    return pl.BlockSpec(memory_space=pltpu.VMEM)


def smem():
    return pl.BlockSpec(memory_space=pltpu.SMEM)


def hbm():
    return pl.BlockSpec(memory_space=pltpu.HBM)


def params(limit):
    return pltpu.CompilerParams(vmem_limit_bytes=limit * MIB)


def held(x):
    return pltpu.with_memory_space_constraint(x, pltpu.VMEM)


def pinned(x):
    return pltpu.with_memory_space_constraint(x, pltpu.HBM)


def resident(*shape):
    return pltpu.VMEM(shape, F32)


def chunk(source, target, done, g):
    at = pl.ds(g * GROUP, GROUP)
    return pltpu.make_async_copy(source.at[at], target.at[at], done.at[g])


def start_all(source, target, done):
    for g in range(source.shape[0] // GROUP):
        chunk(source, target, done, g).start()


def wait_all(source, target, done):
    for g in range(source.shape[0] // GROUP):
        chunk(source, target, done, g).wait()


def dot(a, b, contract=((1,), (0,))):
    return lax.dot_general(a, b, (contract, ((), ())), preferred_element_type=F32)


def halves(x):
    high = x.astype(BF16)
    return high, (x - high.astype(F32)).astype(BF16)


def pack_kernel(
    counts, owners, columns, kernels, misfits, out, payload, target, staged, done
):
    steps, levels, held = kernels.shape
    tracers = misfits.shape[1]
    shape = (LANES, LANES)
    device = lax.broadcasted_iota(jnp.int32, shape, 0)
    table = counting_table()
    for step in range(steps):
        owner = owners[step]
        live = lax.broadcasted_iota(jnp.int32, owner.shape, 1) < counts[step, 0]
        owner = jnp.where(live, owner, -1)
        seen = jnp.zeros(shape, F32)
        for start in range(0, held, LANES):
            here = owner[:, start : start + LANES]
            hot = device == here
            counted = dot(jnp.where(hot, 1.0, 0.0).astype(BF16), table)
            rank = jnp.sum(
                jnp.where(hot, counted[:, :LANES] + seen, 0.0), axis=0, keepdims=True
            )
            seen = seen + counted[:, LANES:]
            target[step : step + 1, start : start + LANES] = jnp.where(
                here >= 0, here * CAP + rank.astype(jnp.int32), -1
            )
        column = columns[step : step + 1, :].astype(F32) + 1.0
        column = jnp.where(lax.broadcasted_iota(jnp.int32, (8, held), 0) == 0, column, 0.0)
        unused = jnp.zeros((LANES - levels - tracers - 8, held), F32)
        high, low = halves(
            jnp.concatenate([kernels[step], misfits[step], column, unused], axis=0)
        )
        payload[step, :LANES, :] = high
        payload[step, LANES:, :] = low
    owned = 256 // CAP
    tiles = out.shape[0] // owned

    def copy(i):
        at = pl.ds(i * owned, owned)
        return pltpu.make_async_copy(staged.at[at], out.at[at], done.at[i])

    def place(i, carry):
        slot = lax.broadcasted_iota(jnp.int32, (owned * CAP, held), 0) + i * owned * CAP
        for step in range(steps):
            hot = jnp.where(slot == target[step : step + 1, :], 1.0, 0.0).astype(BF16)
            both = dot(hot, payload[step], ((1,), (1,)))
            both = both[:, :LANES] + both[:, LANES:]
            staged[pl.ds(i * owned, owned), step * CAP : (step + 1) * CAP, :] = both.reshape(
                owned, CAP, LANES
            )
        copy(i).start()
        return carry

    lax.fori_loop(0, tiles, place, 0)
    for i in range(tiles):
        copy(i).wait()


def counting_table():
    shape = (LANES, LANES)
    earlier = lax.broadcasted_iota(jnp.int32, shape, 0) < lax.broadcasted_iota(
        jnp.int32, shape, 1
    )
    return jnp.concatenate(
        [jnp.where(earlier, 1.0, 0.0), jnp.ones(shape, F32)], axis=1
    ).astype(BF16)


def packed(counts, owners, columns, kernels, misfits):
    steps, slots = columns.shape
    devices = lax.axis_size("lon") * lax.axis_size("lat")
    return pl.pallas_call(
        pack_kernel,
        out_shape=pltpu.HBM((devices, steps * CAP, LANES), F32),
        in_specs=[smem()] + [vmem()] * 4,
        out_specs=hbm(),
        scratch_shapes=[
            pltpu.VMEM((steps, 2 * LANES, slots), BF16),
            pltpu.VMEM((steps, slots), jnp.int32),
            pltpu.VMEM((devices, steps * CAP, LANES), F32),
            pltpu.SemaphoreType.DMA((devices * CAP // 256,)),
        ],
        compiler_params=params(8),
        name="pack",
    )(counts, held(owners), held(columns), held(kernels), held(misfits))


def forcing_kernel(step, received, result, out, fields, hots, place, ordered, done):
    levels, rows, tracers, cells = out.shape
    slots = received.shape[0] * CAP
    blocks = slots // LANES
    sources = LANES // CAP
    sub = lax.broadcasted_iota(jnp.int32, (rows, LANES), 0)
    at_column = levels + tracers
    for b in range(blocks):
        span = slice(b * LANES, (b + 1) * LANES)
        block = received[b * sources : (b + 1) * sources, step * CAP : (step + 1) * CAP, :]
        turned = block.reshape(LANES, LANES).T
        high, low = halves(turned)
        fields[:LANES, span] = high
        fields[LANES:, span] = low
        row = (turned[at_column : at_column + 1].astype(jnp.int32) - 1) >> 8
        hots[b * rows : (b + 1) * rows, :] = jnp.where(sub == row, 1.0, 0.0)
    counted = dot(hots[...].astype(BF16), counting_table())
    run = jnp.zeros((rows, LANES), F32)
    runs = []
    for b in range(blocks):
        runs.append(run)
        run = run + counted[b * rows : (b + 1) * rows, LANES:]
    filled = jnp.floor((run + (LANES - 1.0)) * (1.0 / LANES))
    start = jnp.zeros((rows, LANES), F32)
    for j in range(1, rows):
        start = start + jnp.where(sub >= j, pltpu.roll(filled, j, 0), 0.0)
    for b in range(blocks):
        hot = hots[b * rows : (b + 1) * rows, :]
        at = counted[b * rows : (b + 1) * rows, :LANES] + runs[b] + start * float(LANES)
        at = jnp.sum(hot * at, axis=0, keepdims=True)
        live = jnp.sum(hot, axis=0, keepdims=True) > 0.0
        place[:, b * LANES : (b + 1) * LANES] = jnp.where(live, at, -1.0)
    counts = [jnp.max(filled[r : r + 1, :]).astype(jnp.int32) for r in range(rows)]
    used = sum(counts)
    wide = 2 * LANES

    def sort(i, carry):
        slot = (lax.broadcasted_iota(jnp.int32, (wide, slots), 0) + i * wide).astype(F32)
        hot = jnp.where(slot == place[...], 1.0, 0.0).astype(BF16)
        both = dot(fields[...], hot, ((1,), (1,)))
        ordered[:, pl.ds(pl.multiple_of(i * wide, wide), wide)] = both[:LANES] + both[LANES:]
        return carry

    lax.fori_loop(0, (used + 1) // 2, sort, 0)
    out[...] = jnp.zeros_like(out)
    cell = lax.broadcasted_iota(jnp.int32, (cells, LANES), 0)
    first = jnp.int32(0)
    for r in range(rows):
        names = (cell + (r * cells + 1)).astype(F32)

        def add(p, carry):
            block = ordered[:, pl.ds(pl.multiple_of(p * LANES, LANES), LANES)]
            hot = jnp.where(names == block[at_column : at_column + 1], 1.0, 0.0).astype(BF16)
            product = block[:levels][:, None, :] * block[levels:at_column][None]
            high, low = halves(product.reshape(levels * tracers, LANES))
            total = dot(high, hot, ((1,), (1,))) + dot(low, hot, ((1,), (1,)))
            out[:, r, :, :] += total.reshape(levels, tracers, cells)
            return carry

        lax.fori_loop(first, first + counts[r], add, 0)
        first = first + counts[r]
        pltpu.make_async_copy(out.at[:, r], result.at[:, r], done.at[r]).start()
    for r in range(rows):
        pltpu.make_async_copy(out.at[:, r], result.at[:, r], done.at[r]).wait()


def forcing(step, received, levels, tracers, rows, cells):
    slots = received.shape[0] * CAP
    return pl.pallas_call(
        functools.partial(forcing_kernel, step),
        out_shape=pltpu.HBM((levels, rows, tracers, cells), F32),
        in_specs=[vmem()],
        out_specs=hbm(),
        scratch_shapes=[
            pltpu.VMEM((levels, rows, tracers, cells), F32),
            pltpu.VMEM((2 * LANES, slots), BF16),
            pltpu.VMEM((slots // LANES * rows, LANES), F32),
            pltpu.VMEM((1, slots), F32),
            pltpu.VMEM((LANES, slots + rows * LANES), F32),
            pltpu.SemaphoreType.DMA((rows,)),
        ],
        compiler_params=params(14),
        name="forcing",
    )(held(received))


def spread(x, row, tracers):
    return jnp.broadcast_to(x[row : row + 1, :], (tracers, x.shape[1]))


def eliminate(level, above, carry, rights, ratios):
    below, ratio, values = carry
    if above is None:
        above = jnp.zeros_like(below)
    inverse = 1.0 / (1.0 + below + above + below * ratio)
    lower = below * inverse
    ratio = -above * inverse
    ratios[level] = ratio
    tracers = rights[0].shape[0]
    fresh = [
        spread(inverse, r, tracers) * rights[r] + spread(lower, r, tracers) * values[r]
        for r in range(len(rights))
    ]
    return (above, ratio, fresh)


def substitute(step, ratios, couplings, column, fields, results, done):
    diffused, first, last, polar = fields
    levels, rows, tracers, cells = diffused.shape
    lat = lax.axis_index("lat")
    at_start = lat == 0

    def picked(x):
        return jnp.where(at_start, x[step, 0:1, :], x[step, rows - 1 : rows, :])

    north, south, east = [picked(x) for x in couplings]
    own = jnp.broadcast_to(1.0 - north - south, (tracers, cells))
    side = jnp.broadcast_to(jnp.where(at_start, north, south), (tracers, cells))
    polar[levels] = jnp.broadcast_to(east, (tracers, cells))
    groups = levels // GROUP
    top = pl.ds(levels, 1)
    weight = pltpu.make_async_copy(polar.at[top], results[3].at[top], done.at[3, groups])
    weight.start()
    lane = lax.broadcasted_iota(jnp.int32, (tracers, LANES), 1)

    def group(i, solved):
        at = groups - 1 - i
        west = jnp.zeros((tracers, LANES), F32)
        for j in range(GROUP - 1, -1, -1):
            level = at * GROUP + j
            ratio = ratios[level]
            fresh = []
            for r in range(rows):
                value = diffused[level, r] - spread(ratio, r, tracers) * solved[r]
                diffused[level, r] = value
                fresh.append(value)
                lanes = j * rows + r
                moved = pltpu.roll(value[:, :LANES], lanes, 1) if lanes else value[:, :LANES]
                west = jnp.where(lane == lanes, moved, west)
            solved = fresh
            first[level] = solved[0]
            last[level] = solved[rows - 1]
            polar[level] = own * jnp.where(
                at_start, solved[0], solved[rows - 1]
            ) + side * jnp.where(at_start, solved[1], solved[rows - 2])
        column[at] = west
        for k, (field, result) in enumerate(zip(fields, results)):
            chunk(field, result, done.at[k], at).start()
        return solved

    lax.fori_loop(0, groups, group, [jnp.zeros((tracers, cells), F32)] * rows)
    weight.wait()
    for k, (field, result) in enumerate(zip(fields, results)):
        for g in range(groups):
            chunk(field, result, done.at[k], g).wait()


def forward_sweep(levels, rows, tracers, cells, diffusion, right_of):
    zero = jnp.zeros((rows, cells), F32)
    carry = (zero, zero, [jnp.zeros((tracers, cells), F32)] * rows)
    groups = levels // GROUP

    def one(g, j, above, carry):
        rights, ratios, store = right_of(g, j, above is None)
        carry = eliminate(g * GROUP + j, above, carry, rights, ratios)
        store(carry[2])
        return carry

    def group(g, carry):
        for j in range(GROUP):
            carry = one(g, j, diffusion(g * GROUP + j), carry)
        return carry

    carry = lax.fori_loop(0, groups - 1, group, carry)
    for j in range(GROUP):
        level = levels - GROUP + j
        carry = one(groups - 1, j, diffusion(level) if level < levels - 1 else None, carry)


def first_kernel(
    step,
    costate,
    diffusion_in,
    north_in,
    south_in,
    east_in,
    result,
    first_out,
    last_out,
    polar_out,
    column,
    staged,
    ratios,
    diffused,
    first,
    last,
    polar,
    diffusion,
    couplings,
    arrived,
    sent,
    ready,
):
    levels, tracers, rows, cells = costate.shape
    small = [pltpu.make_async_copy(diffusion_in.at[step], diffusion, ready.at[0])]
    for k, coupling in enumerate((north_in, south_in, east_in)):
        small.append(pltpu.make_async_copy(coupling, couplings.at[k], ready.at[1 + k]))
    chunk(costate, staged, arrived, 0).start()
    for copy in small:
        copy.start()
    for g in range(1, levels // GROUP):
        chunk(costate, staged, arrived, g).start()
    for copy in small:
        copy.wait()

    def right_of(g, j, final):
        if j == 0:
            chunk(costate, staged, arrived, g).wait()
        level = g * GROUP + j
        rights = [staged[level, :, r, :] for r in range(rows)]

        def store(values):
            for r in range(rows):
                diffused[level, r] = values[r]

        return rights, ratios, store

    forward_sweep(levels, rows, tracers, cells, lambda level: diffusion[level], right_of)
    views = [couplings.at[k] for k in range(3)]
    fields = (diffused, first, last, polar)
    results = (result, first_out, last_out, polar_out)
    substitute(step, ratios, views, column, fields, results, sent)


def meridional(level, row, diffused, after, before, coefs):
    rows = diffused.shape[1]
    own, north, south = coefs
    up = diffused[level, row + 1] if row < rows - 1 else after[level]
    down = diffused[level, row - 1] if row > 0 else before[level]
    return own * diffused[level, row] + north * up + south * down


def borders_kernel(
    step,
    shift,
    column,
    north,
    south,
    nearby,
    after,
    before,
    polar_in,
    turned_out,
    edge,
    polar,
    turned,
    ready,
):
    groups, tracers, lanes = column.shape
    rows, cells = north.shape[1:]
    fetch = pltpu.make_async_copy(polar_in, polar, ready.at[0])
    lat = lax.axis_index("lat")
    last_lat = lax.axis_size("lat") - 1
    at_pole = (lat == 0) | (lat == last_lat)

    @pl.when(at_pole)
    def _():
        fetch.start()

    lane = lax.broadcasted_iota(jnp.int32, (tracers, lanes), 1)

    def along_lanes(x):
        shape = (rows, lanes)
        own_lane = (lax.broadcasted_iota(jnp.int32, shape, 1) & (rows - 1)) == (
            lax.broadcasted_iota(jnp.int32, shape, 0)
        )
        picked = jnp.where(own_lane, jnp.broadcast_to(x[step, :, :1], shape), 0.0)
        return jnp.broadcast_to(jnp.sum(picked, axis=0, keepdims=True), (tracers, lanes))

    n, s = along_lanes(north), along_lanes(south)
    own = 1.0 - n - s

    def group(i, carry):
        here = column[i]
        up = pltpu.roll(here, lanes - 1, 1)
        down = pltpu.roll(here, 1, 1)
        for j in range(GROUP):
            level = i * GROUP + j
            bottom, top = j * rows, j * rows + rows - 1
            up = jnp.where(lane == top, pltpu.roll(after[level, :, :LANES], top, 1), up)
            moved = before[level, :, :LANES]
            moved = pltpu.roll(moved, bottom, 1) if bottom else moved
            down = jnp.where(lane == bottom, moved, down)
        edge[i] = own * here + n * up + s * down
        return carry

    sending = pltpu.make_async_copy(turned, turned_out, ready.at[1])

    @pl.when(at_pole)
    def _():
        fetch.wait()
        levels = turned.shape[0]
        circle = cells * lax.axis_size("lon")
        amount = jnp.where(lat == 0, shift[step, 0], shift[step, rows * last_lat + rows - 1])
        back = 2 * cells - (lax.rem(amount + 2 * circle, circle) & (cells - 1))
        weight = jnp.concatenate([polar[levels], nearby[levels]], axis=1)

        def one(i, carry):
            for j in range(GROUP):
                level = i * GROUP + j
                row = jnp.concatenate([polar[level], nearby[level]], axis=1)
                moved = row + weight * (pltpu.roll(row, 2 * cells - 1, 1) - row)
                turned[level] = pltpu.roll(moved, back, 1)[:, :cells]
            return carry

        lax.fori_loop(0, groups, one, 0)
        sending.start()

    lax.fori_loop(0, groups, group, 0)

    @pl.when(at_pole)
    def _():
        sending.wait()


def prepare_stencil(step, north, south, east, coefs):
    rows, cells = north.shape[1:]
    tracers = coefs.shape[2]
    for r in range(rows):
        n = north[step, r : r + 1, :]
        s = south[step, r : r + 1, :]
        coefs[0, r] = jnp.broadcast_to(1.0 - n - s, (tracers, cells))
        coefs[1, r] = jnp.broadcast_to(n, (tracers, cells))
        coefs[2, r] = jnp.broadcast_to(s, (tracers, cells))
        coefs[3, r] = jnp.broadcast_to(east[step, r : r + 1, :], (tracers, cells))


def transported(level, lane_at, diffused, after, before, edge_row, coefs, pole):
    rows, tracers, cells = diffused.shape[1:]
    lat = lax.axis_index("lat")
    last = lax.broadcasted_iota(jnp.int32, (tracers, cells), 1) == cells - 1
    result = []
    for r in range(rows):
        mer = meridional(level, r, diffused, after, before, [coefs[k, r] for k in range(3)])
        arrived = pltpu.roll(edge_row, LANES - 1 - (lane_at * rows + r), 1)
        arrived = jnp.concatenate([arrived] * (cells // LANES), axis=1)
        following = jnp.where(last, arrived, pltpu.roll(mer, cells - 1, 1))
        result.append(mer + coefs[3, r] * (following - mer))
    polar = pole[level]
    result[0] = jnp.where(lat == 0, polar, result[0])
    result[rows - 1] = jnp.where(lat == lax.axis_size("lat") - 1, polar, result[rows - 1])
    return result


def streams(sources, south_pole, north_pole, targets, pole, done):
    lat = lax.axis_index("lat")
    last_lat = lax.axis_size("lat") - 1
    last = len(sources)
    groups = pole.shape[0] // GROUP
    for g in range(groups):
        for k, (source, target) in enumerate(zip(sources, targets)):
            chunk(source, target, done.at[k], g).start()

        @pl.when(lat == 0)
        def _():
            chunk(south_pole, pole, done.at[last], g).start()

        @pl.when(lat == last_lat)
        def _():
            chunk(north_pole, pole, done.at[last], g).start()

    def wait(g):
        for k, (source, target) in enumerate(zip(sources, targets)):
            chunk(source, target, done.at[k], g).wait()

        @pl.when((lat == 0) | (lat == last_lat))
        def _():
            chunk(south_pole, pole, done.at[last], g).wait()

    return wait


def middle_kernel(
    step,
    before_step,
    forcing_in,
    after_in,
    before_in,
    south_pole,
    north_pole,
    edge,
    diffusion,
    north,
    south,
    east,
    result,
    first_out,
    last_out,
    polar_out,
    column,
    surface,
    coefs,
    ratios,
    diffused,
    forced,
    after,
    before,
    pole,
    solved,
    first,
    last,
    polar,
    arrived,
    sent,
):
    levels, rows, tracers, cells = diffused.shape
    wait = streams(
        (before_step, forcing_in, after_in, before_in),
        south_pole,
        north_pole,
        (diffused, forced, after, before),
        pole,
        arrived,
    )
    prepare_stencil(step, north, south, east, coefs)

    def right_of(g, j, final):
        if j == 0:
            wait(g)
        level = g * GROUP + j
        rights = transported(level, j, diffused, after, before, edge[g], coefs, pole)
        rights = [rights[r] + forced[level, r] for r in range(rows)]
        if final:
            for r in range(rows):
                surface[r] = rights[r]

        def store(values):
            for r in range(rows):
                solved[level, r] = values[r]

        return rights, ratios, store

    forward_sweep(
        levels, rows, tracers, cells, lambda level: diffusion[step - 1, level], right_of
    )
    couplings = (north, south, east)
    fields = (solved, first, last, polar)
    results = (result, first_out, last_out, polar_out)
    substitute(step - 1, ratios, couplings, column, fields, results, sent)


def last_kernel(
    step,
    before_step,
    forcing_in,
    after_in,
    before_in,
    south_pole,
    north_pole,
    edge,
    north,
    south,
    east,
    surface,
    state,
    gradient,
    coefs,
    diffused,
    forced,
    after,
    before,
    pole,
    staged,
    arrived,
    sent,
):
    levels, rows, tracers, cells = diffused.shape
    wait = streams(
        (before_step, forcing_in, after_in, before_in),
        south_pole,
        north_pole,
        (diffused, forced, after, before),
        pole,
        arrived,
    )
    prepare_stencil(step, north, south, east, coefs)

    def group(g, carry):
        wait(g)
        edge_row = edge[g]
        for j in range(GROUP):
            level = g * GROUP + j
            values = transported(level, j, diffused, after, before, edge_row, coefs, pole)
            for r in range(rows):
                staged[level, :, r, :] = values[r] + forced[level, r]
        chunk(staged, state, sent, g).start()
        return carry

    lax.fori_loop(0, levels // GROUP, group, 0)
    for r in range(rows):
        gradient[:, r, :] = surface[r] + staged[levels - 1, :, r, :]
    wait_all(staged, state, sent)


def boundaries(first, last, polar):
    lat_count = lax.axis_size("lat")
    up = [(i, i + 1) for i in range(lat_count - 1)]
    down = [(j, i) for i, j in up]
    nearby = lax.ppermute(polar, AXES, circles((0, lat_count - 1), 1))
    return lax.ppermute(first, "lat", down), lax.ppermute(last, "lat", up), nearby


def circles(lats, hops):
    lat_count = lax.axis_size("lat")
    lon_count = lax.axis_size("lon")
    return [
        (((j + hops) % lon_count) * lat_count + lat, j * lat_count + lat)
        for lat in lats
        for j in range(lon_count)
    ]


def exchange(after, before, nearby, polar, column, north, south, shift, step):
    lat_count = lax.axis_size("lat")
    lon_count = lax.axis_size("lon")
    poles = (0, lat_count - 1)
    levels, tracers, cells = after.shape
    turned, edge = pl.pallas_call(
        functools.partial(borders_kernel, step),
        out_shape=[pltpu.HBM((levels, tracers, cells), F32), resident(*column.shape)],
        in_specs=[smem()] + [vmem()] * 6 + [hbm()],
        out_specs=[hbm(), vmem()],
        scratch_shapes=[
            pltpu.VMEM(polar.shape, F32),
            pltpu.VMEM((levels, tracers, cells), F32),
            pltpu.SemaphoreType.DMA((2,)),
        ],
        compiler_params=params(4),
        name="borders",
    )(shift, column, north, south, *[held(x) for x in (nearby, after, before)], pinned(polar))
    west = [(i, (i - 1) % lon_count) for i in range(lon_count)]
    edge = lax.ppermute(edge, "lon", west)
    moved = []
    for lat, row in zip(poles, (0, shift.shape[1] - 1)):
        hops = jnp.mod(shift[step, row], cells * lon_count) // cells
        moved.append(
            lax.switch(
                hops,
                [
                    functools.partial(
                        lambda k, lat, x: lax.ppermute(x, AXES, circles((lat,), k)), k, lat
                    )
                    for k in range(lon_count)
                ],
                turned,
            )
        )
    return pinned(after), pinned(before), pinned(moved[0]), pinned(moved[1]), held(edge)


def per_device(
    costate,
    diffusion,
    east_courant,
    north_courant,
    south_courant,
    polar_shift,
    owners,
    columns,
    sounding_counts,
    kernels,
    misfits,
):
    levels, tracers, rows, cells = costate.shape
    owner_rows = owners.reshape(owners.shape[0], 1, owners.shape[1])
    couplings = (north_courant, south_courant, east_courant)
    groups = levels // GROUP

    solved_shapes = [
        pltpu.HBM((levels, rows, tracers, cells), F32),
        pltpu.HBM((levels, tracers, cells), F32),
        pltpu.HBM((levels, tracers, cells), F32),
        pltpu.HBM((levels + 1, tracers, cells), F32),
        resident(groups, tracers, LANES),
    ]
    ratios = pltpu.VMEM((levels, rows, cells), F32)
    coefs = pltpu.VMEM((4, rows, tracers, cells), F32)
    field = pltpu.VMEM((levels, rows, tracers, cells), F32)
    line = pltpu.VMEM((levels, tracers, cells), F32)
    solved_scratch = [field, line, line, pltpu.VMEM((levels + 1, tracers, cells), F32)]
    solved_specs = [hbm()] * 4 + [vmem()]
    leaving = pltpu.SemaphoreType.DMA((4, groups + 1))
    output = pltpu.VMEM(costate.shape, F32)
    semaphores = pltpu.SemaphoreType.DMA((groups,))
    diffused, first, last, polar, column = pl.pallas_call(
        functools.partial(first_kernel, 1),
        out_shape=solved_shapes,
        in_specs=[hbm()] * 5,
        out_specs=solved_specs,
        scratch_shapes=[
            output,
            ratios,
            *solved_scratch,
            pltpu.VMEM(diffusion.shape[1:], F32),
            pltpu.VMEM((3,) + east_courant.shape, F32),
            semaphores,
            leaving,
            pltpu.SemaphoreType.DMA((4,)),
        ],
        compiler_params=params(16),
        name="first",
    )(*[pinned(x) for x in (costate, diffusion, *couplings)])
    couplings = [held(x) for x in couplings]
    diffusion = held(diffusion)
    counts, column = lax.optimization_barrier((sounding_counts, column))
    around = boundaries(first, last, polar)
    sent = packed(counts, owner_rows, columns, kernels, misfits)
    sent, *around = lax.optimization_barrier((sent, *around))
    got = lax.all_to_all(sent, AXES, 0, 0, tiled=True)
    forced = pinned(forcing(1, got, levels, tracers, rows, cells))
    around = exchange(*around, polar, column, *couplings[:2], polar_shift, 1)
    scratch = [field, field, line, line, line]
    transfers = pltpu.SemaphoreType.DMA((5, groups))
    solved, first, last, polar, column, surface = pl.pallas_call(
        functools.partial(middle_kernel, 1),
        out_shape=solved_shapes + [resident(rows, tracers, cells)],
        in_specs=[hbm()] * 6 + [vmem()] * 5,
        out_specs=solved_specs + [vmem()],
        scratch_shapes=[coefs, ratios, *scratch, *solved_scratch, transfers, leaving],
        compiler_params=params(26),
        name="middle",
    )(pinned(diffused), forced, *around, diffusion, *couplings)
    around = boundaries(first, last, polar)
    got, column = lax.optimization_barrier((got, column))
    forced = pinned(forcing(0, got, levels, tracers, rows, cells))
    forced, *around = lax.optimization_barrier((forced, *around))
    around = exchange(*around, polar, column, *couplings[:2], polar_shift, 0)
    return tuple(
        pl.pallas_call(
            functools.partial(last_kernel, 0),
            out_shape=[
                pltpu.HBM(costate.shape, F32),
                jax.ShapeDtypeStruct((tracers, rows, cells), F32),
            ],
            in_specs=[hbm()] * 6 + [vmem()] * 5,
            out_specs=[hbm(), vmem()],
            scratch_shapes=[coefs, *scratch, output, transfers, semaphores],
            compiler_params=params(22),
            name="last",
        )(pinned(solved), pinned(forced), *around, *couplings, surface)
    )


def solution(mesh):
    return jax.shard_map(
        per_device,
        mesh=mesh,
        in_specs=(
            P(None, None, "lat", "lon"),
            P(None, None, "lat", "lon"),
            P(None, "lat", "lon"),
            P(None, "lat", "lon"),
            P(None, "lat", "lon"),
            P(),
            P(None, ("lon", "lat"), None),
            P(None, ("lon", "lat")),
            P(None, ("lon", "lat")),
            P(None, None, ("lon", "lat")),
            P(None, None, ("lon", "lat")),
        ),
        out_specs=(P(None, None, "lat", "lon"), P(None, "lat", "lon")),
        check_vma=False,
    )
```

```python
import functools

import jax
import jax.numpy as jnp
from jax import lax
from jax.experimental import pallas as pl
from jax.experimental.pallas import tpu as pltpu
from jax.sharding import PartitionSpec as P

AXES = ("lon", "lat")
LANES = 128
CAP = 16
GROUP = 8
F32 = jnp.float32
BF16 = jnp.bfloat16
MIB = 1024 * 1024


def vmem():
    return pl.BlockSpec(memory_space=pltpu.VMEM)


def smem():
    return pl.BlockSpec(memory_space=pltpu.SMEM)


def hbm():
    return pl.BlockSpec(memory_space=pltpu.HBM)


def params(limit):
    return pltpu.CompilerParams(vmem_limit_bytes=limit * MIB)


def held(x):
    return pltpu.with_memory_space_constraint(x, pltpu.VMEM)


def anywhere():
    return pl.BlockSpec(memory_space=pl.ANY)


def pinned(x):
    return pltpu.with_memory_space_constraint(x, pltpu.HBM)


def resident(*shape):
    return pltpu.VMEM(shape, F32)


def chunk(source, target, done, g):
    at = pl.ds(g * GROUP, GROUP)
    return pltpu.make_async_copy(source.at[at], target.at[at], done.at[g])


def start_all(source, target, done):
    for g in range(source.shape[0] // GROUP):
        chunk(source, target, done, g).start()


def wait_all(source, target, done):
    for g in range(source.shape[0] // GROUP):
        chunk(source, target, done, g).wait()


def dot(a, b, contract=((1,), (0,))):
    return lax.dot_general(a, b, (contract, ((), ())), preferred_element_type=F32)


def halves(x):
    high = x.astype(BF16)
    return high, (x - high.astype(F32)).astype(BF16)


def pack_kernel(
    counts, owners, columns, kernels, misfits, out, payload, target, staged, done
):
    steps, levels, held = kernels.shape
    tracers = misfits.shape[1]
    shape = (LANES, LANES)
    device = lax.broadcasted_iota(jnp.int32, shape, 0)
    table = counting_table()
    for step in range(steps):
        owner = owners[step]
        live = lax.broadcasted_iota(jnp.int32, owner.shape, 1) < counts[step, 0]
        owner = jnp.where(live, owner, -1)
        seen = jnp.zeros(shape, F32)
        for start in range(0, held, LANES):
            here = owner[:, start : start + LANES]
            hot = device == here
            counted = dot(jnp.where(hot, 1.0, 0.0).astype(BF16), table)
            rank = jnp.sum(
                jnp.where(hot, counted[:, :LANES] + seen, 0.0), axis=0, keepdims=True
            )
            seen = seen + counted[:, LANES:]
            target[step : step + 1, start : start + LANES] = jnp.where(
                here >= 0, here * CAP + rank.astype(jnp.int32), -1
            )
        column = columns[step : step + 1, :].astype(F32) + 1.0
        column = jnp.where(lax.broadcasted_iota(jnp.int32, (8, held), 0) == 0, column, 0.0)
        unused = jnp.zeros((LANES - levels - tracers - 8, held), F32)
        high, low = halves(
            jnp.concatenate([kernels[step], misfits[step], column, unused], axis=0)
        )
        payload[step, :LANES, :] = high
        payload[step, LANES:, :] = low
    owned = 256 // CAP
    tiles = out.shape[0] // owned

    def copy(i):
        at = pl.ds(i * owned, owned)
        return pltpu.make_async_copy(staged.at[at], out.at[at], done.at[i])

    def place(i, carry):
        for step in range(steps):
            hot = one_hot(target[step : step + 1, :] - i * owned * CAP, owned * CAP)
            both = dot(hot, payload[step], ((1,), (1,)))
            both = both[:, :LANES] + both[:, LANES:]
            staged[pl.ds(i * owned, owned), step * CAP : (step + 1) * CAP, :] = both.reshape(
                owned, CAP, LANES
            )
        copy(i).start()
        return carry

    lax.fori_loop(0, tiles, place, 0)
    for i in range(tiles):
        copy(i).wait()


def one_hot(at, size):
    at = jnp.where((at >= 0) & (at < size), at, -1).astype(F32).astype(BF16)
    shape = (size, at.shape[1])
    row = lax.broadcasted_iota(jnp.int32, shape, 0).astype(F32).astype(BF16)
    return jnp.where(row == at, jnp.ones(shape, BF16), jnp.zeros(shape, BF16))


def counting_table():
    shape = (LANES, LANES)
    earlier = lax.broadcasted_iota(jnp.int32, shape, 0) < lax.broadcasted_iota(
        jnp.int32, shape, 1
    )
    return jnp.concatenate(
        [jnp.where(earlier, 1.0, 0.0), jnp.ones(shape, F32)], axis=1
    ).astype(BF16)


def packed(counts, owners, columns, kernels, misfits):
    steps, slots = columns.shape
    devices = lax.axis_size("lon") * lax.axis_size("lat")
    return pl.pallas_call(
        pack_kernel,
        out_shape=pltpu.HBM((devices, steps * CAP, LANES), F32),
        in_specs=[smem()] + [vmem()] * 4,
        out_specs=hbm(),
        scratch_shapes=[
            pltpu.VMEM((steps, 2 * LANES, slots), BF16),
            pltpu.VMEM((steps, slots), jnp.int32),
            pltpu.VMEM((devices, steps * CAP, LANES), F32),
            pltpu.SemaphoreType.DMA((devices * CAP // 256,)),
        ],
        compiler_params=params(8),
        name="pack",
    )(counts, held(owners), held(columns), held(kernels), held(misfits))


def forcing_kernel(step, received, result, out, fields, hots, place, ordered, done):
    levels, rows, tracers, cells = out.shape
    slots = received.shape[0] * CAP
    blocks = slots // LANES
    sources = LANES // CAP
    sub = lax.broadcasted_iota(jnp.int32, (rows, LANES), 0)
    at_column = levels + tracers
    for b in range(blocks):
        span = slice(b * LANES, (b + 1) * LANES)
        block = received[b * sources : (b + 1) * sources, step * CAP : (step + 1) * CAP, :]
        turned = block.reshape(LANES, LANES).T
        high, low = halves(turned)
        fields[:LANES, span] = high
        fields[LANES:, span] = low
        row = (turned[at_column : at_column + 1].astype(jnp.int32) - 1) >> 8
        hots[b * rows : (b + 1) * rows, :] = jnp.where(sub == row, 1.0, 0.0)
    counted = dot(hots[...].astype(BF16), counting_table())
    run = jnp.zeros((rows, LANES), F32)
    runs = []
    for b in range(blocks):
        runs.append(run)
        run = run + counted[b * rows : (b + 1) * rows, LANES:]
    filled = jnp.floor((run + (LANES - 1.0)) * (1.0 / LANES))
    start = jnp.zeros((rows, LANES), F32)
    for j in range(1, rows):
        start = start + jnp.where(sub >= j, pltpu.roll(filled, j, 0), 0.0)
    for b in range(blocks):
        hot = hots[b * rows : (b + 1) * rows, :]
        at = counted[b * rows : (b + 1) * rows, :LANES] + runs[b] + start * float(LANES)
        at = jnp.sum(hot * at, axis=0, keepdims=True)
        live = jnp.sum(hot, axis=0, keepdims=True) > 0.0
        place[:, b * LANES : (b + 1) * LANES] = jnp.where(live, at, -1.0)
    counts = [jnp.max(filled[r : r + 1, :]).astype(jnp.int32) for r in range(rows)]
    used = sum(counts)
    wide = 2 * LANES

    def sort(i, carry):
        hot = one_hot(place[...] - (i * wide).astype(F32), wide)
        both = dot(fields[...], hot, ((1,), (1,)))
        ordered[:, pl.ds(pl.multiple_of(i * wide, wide), wide)] = both[:LANES] + both[LANES:]
        return carry

    lax.fori_loop(0, (used + 1) // 2, sort, 0)
    out[...] = jnp.zeros_like(out)
    cell = lax.broadcasted_iota(jnp.int32, (cells, LANES), 0)
    first = jnp.int32(0)
    for r in range(rows):
        names = (cell + (r * cells + 1)).astype(F32)

        def add(p, carry):
            block = ordered[:, pl.ds(pl.multiple_of(p * LANES, LANES), LANES)]
            hot = jnp.where(names == block[at_column : at_column + 1], 1.0, 0.0).astype(BF16)
            product = block[:levels][:, None, :] * block[levels:at_column][None]
            high, low = halves(product.reshape(levels * tracers, LANES))
            total = dot(high, hot, ((1,), (1,))) + dot(low, hot, ((1,), (1,)))
            out[:, r, :, :] += total.reshape(levels, tracers, cells)
            return carry

        lax.fori_loop(first, first + counts[r], add, 0)
        first = first + counts[r]
        pltpu.make_async_copy(out.at[:, r], result.at[:, r], done.at[r]).start()
    for r in range(rows):
        pltpu.make_async_copy(out.at[:, r], result.at[:, r], done.at[r]).wait()


def forcing(step, received, levels, tracers, rows, cells):
    slots = received.shape[0] * CAP
    return pl.pallas_call(
        functools.partial(forcing_kernel, step),
        out_shape=pltpu.HBM((levels, rows, tracers, cells), F32),
        in_specs=[vmem()],
        out_specs=hbm(),
        scratch_shapes=[
            pltpu.VMEM((levels, rows, tracers, cells), F32),
            pltpu.VMEM((2 * LANES, slots), BF16),
            pltpu.VMEM((slots // LANES * rows, LANES), F32),
            pltpu.VMEM((1, slots), F32),
            pltpu.VMEM((LANES, slots + rows * LANES), F32),
            pltpu.SemaphoreType.DMA((rows,)),
        ],
        compiler_params=params(14),
        name="forcing",
    )(held(received))


def spread(x, row, tracers):
    return jnp.broadcast_to(x[row : row + 1, :], (tracers, x.shape[1]))


def eliminate(level, above, carry, rights, ratios):
    below, ratio, values = carry
    if above is None:
        above = jnp.zeros_like(below)
    inverse = 1.0 / (1.0 + below + above + below * ratio)
    lower = below * inverse
    ratio = -above * inverse
    ratios[level] = ratio
    tracers = rights[0].shape[0]
    fresh = [
        spread(inverse, r, tracers) * rights[r] + spread(lower, r, tracers) * values[r]
        for r in range(len(rights))
    ]
    return (above, ratio, fresh)


def substitute(step, ratios, couplings, column, fields, results, done):
    diffused, first, last, polar = fields
    levels, rows, tracers, cells = diffused.shape
    lat = lax.axis_index("lat")
    at_start = lat == 0

    def picked(x):
        return jnp.where(at_start, x[step, 0:1, :], x[step, rows - 1 : rows, :])

    north, south, east = [picked(x) for x in couplings]
    own = jnp.broadcast_to(1.0 - north - south, (tracers, cells))
    side = jnp.broadcast_to(jnp.where(at_start, north, south), (tracers, cells))
    groups = levels // GROUP
    by_tracer = len(polar.shape) == 4
    if by_tracer:
        polar[:, groups, 0, :] = jnp.broadcast_to(east, (tracers, cells))
    else:
        polar[levels] = jnp.broadcast_to(east, (tracers, cells))

    def polar_copy(g):
        if by_tracer:
            source, target = [x.at[:, g] for x in (polar, results[3])]
        else:
            at = pl.ds(g * GROUP, GROUP if not isinstance(g, int) else 1)
            source, target = [x.at[at] for x in (polar, results[3])]
        return pltpu.make_async_copy(source, target, done.at[3, g])

    polar_copy(groups).start()
    lane = lax.broadcasted_iota(jnp.int32, (tracers, LANES), 1)

    def group(i, solved):
        at = groups - 1 - i
        west = jnp.zeros((tracers, LANES), F32)
        for j in range(GROUP - 1, -1, -1):
            level = at * GROUP + j
            ratio = ratios[level]
            fresh = []
            for r in range(rows):
                value = diffused[level, r] - spread(ratio, r, tracers) * solved[r]
                diffused[level, r] = value
                fresh.append(value)
                lanes = j * rows + r
                moved = pltpu.roll(value[:, :LANES], lanes, 1) if lanes else value[:, :LANES]
                west = jnp.where(lane == lanes, moved, west)
            solved = fresh
            first[level] = solved[0]
            last[level] = solved[rows - 1]
            row = own * jnp.where(at_start, solved[0], solved[rows - 1]) + side * jnp.where(
                at_start, solved[1], solved[rows - 2]
            )
            if by_tracer:
                polar[:, at, j, :] = row
            else:
                polar[level] = row
        column[at] = west
        for k in range(3):
            chunk(fields[k], results[k], done.at[k], at).start()
        polar_copy(at).start()
        return solved

    lax.fori_loop(0, groups, group, [jnp.zeros((tracers, cells), F32)] * rows)
    polar_copy(groups).wait()
    for g in range(groups):
        for k in range(3):
            chunk(fields[k], results[k], done.at[k], g).wait()
        polar_copy(jnp.int32(g)).wait()


def forward_sweep(levels, rows, tracers, cells, diffusion, right_of):
    zero = jnp.zeros((rows, cells), F32)
    carry = (zero, zero, [jnp.zeros((tracers, cells), F32)] * rows)
    groups = levels // GROUP

    def one(g, j, above, carry):
        rights, ratios, store = right_of(g, j, above is None)
        carry = eliminate(g * GROUP + j, above, carry, rights, ratios)
        store(carry[2])
        return carry

    def group(g, carry):
        for j in range(GROUP):
            carry = one(g, j, diffusion(g * GROUP + j), carry)
        return carry

    carry = lax.fori_loop(0, groups - 1, group, carry)
    for j in range(GROUP):
        level = levels - GROUP + j
        carry = one(groups - 1, j, diffusion(level) if level < levels - 1 else None, carry)


def first_kernel(
    step,
    costate,
    diffusion_in,
    north_in,
    south_in,
    east_in,
    result,
    first_out,
    last_out,
    polar_out,
    column,
    staged,
    ratios,
    diffused,
    first,
    last,
    polar,
    diffusion,
    couplings,
    arrived,
    sent,
    ready,
):
    levels, tracers, rows, cells = costate.shape
    small = [pltpu.make_async_copy(diffusion_in.at[step], diffusion, ready.at[0])]
    for k, coupling in enumerate((north_in, south_in, east_in)):
        small.append(pltpu.make_async_copy(coupling, couplings.at[k], ready.at[1 + k]))
    chunk(costate, staged, arrived, 0).start()
    for copy in small:
        copy.start()
    for g in range(1, levels // GROUP):
        chunk(costate, staged, arrived, g).start()
    for copy in small:
        copy.wait()

    def right_of(g, j, final):
        if j == 0:
            chunk(costate, staged, arrived, g).wait()
        level = g * GROUP + j
        rights = [staged[level, :, r, :] for r in range(rows)]

        def store(values):
            for r in range(rows):
                diffused[level, r] = values[r]

        return rights, ratios, store

    forward_sweep(levels, rows, tracers, cells, lambda level: diffusion[level], right_of)
    views = [couplings.at[k] for k in range(3)]
    fields = (diffused, first, last, polar)
    results = (result, first_out, last_out, polar_out)
    substitute(step, ratios, views, column, fields, results, sent)


def meridional(level, row, diffused, after, before, coefs):
    rows = diffused.shape[1]
    own, north, south = coefs
    up = diffused[level, row + 1] if row < rows - 1 else after[level]
    down = diffused[level, row - 1] if row > 0 else before[level]
    return own * diffused[level, row] + north * up + south * down


def borders_kernel(
    step,
    shift,
    column,
    north,
    south,
    after_in,
    before_in,
    polar_in,
    nearby_in,
    edge,
    turned_out,
    after,
    before,
    polar,
    nearby,
    turned,
    ready,
):
    rows, cells = north.shape[1:]
    fetches = [
        pltpu.make_async_copy(source, target, ready.at[2 + k])
        for k, (source, target) in enumerate(((polar_in, polar), (nearby_in, nearby)))
    ]
    sending = pltpu.make_async_copy(turned, turned_out, ready.at[4])
    lat = lax.axis_index("lat")
    last_lat = lax.axis_size("lat") - 1
    at_pole = (lat == 0) | (lat == last_lat)

    @pl.when(at_pole)
    def _():
        for fetch in fetches:
            fetch.start()

    finish = west_column(step, column, north, south, after_in, before_in, edge, after, before, ready)

    @pl.when(at_pole)
    def _():
        for fetch in fetches:
            fetch.wait()
        levels = turned.shape[0]
        circle = cells * lax.axis_size("lon")
        amount = jnp.where(lat == 0, shift[step, 0], shift[step, rows * last_lat + rows - 1])
        back = 2 * cells - (lax.rem(amount + 2 * circle, circle) & (cells - 1))
        weight = jnp.concatenate([polar[levels], nearby[levels]], axis=1)

        def one(i, carry):
            for j in range(GROUP):
                level = i * GROUP + j
                row = jnp.concatenate([polar[level], nearby[level]], axis=1)
                moved = row + weight * (pltpu.roll(row, 2 * cells - 1, 1) - row)
                turned[level] = pltpu.roll(moved, back, 1)[:, :cells]
            return carry

        lax.fori_loop(0, levels // GROUP, one, 0)
        sending.start()

    finish()

    @pl.when(at_pole)
    def _():
        sending.wait()


def edge_kernel(
    step, column, north, south, after_in, before_in, edge, after, before, ready
):
    west_column(step, column, north, south, after_in, before_in, edge, after, before, ready)()


def west_column(step, column, north, south, after_in, before_in, edge, after, before, ready):
    groups, tracers, lanes = column.shape
    rows, cells = north.shape[1:]
    tiles = [
        pltpu.make_async_copy(source.at[:, :, pl.ds(0, lanes)], target, ready.at[k])
        for k, (source, target) in enumerate(((after_in, after), (before_in, before)))
    ]
    for tile in tiles:
        tile.start()
    lane = lax.broadcasted_iota(jnp.int32, (tracers, lanes), 1)

    def along_lanes(x):
        shape = (rows, lanes)
        own_lane = (lax.broadcasted_iota(jnp.int32, shape, 1) & (rows - 1)) == (
            lax.broadcasted_iota(jnp.int32, shape, 0)
        )
        picked = jnp.where(own_lane, jnp.broadcast_to(x[step, :, :1], shape), 0.0)
        return jnp.broadcast_to(jnp.sum(picked, axis=0, keepdims=True), (tracers, lanes))

    n, s = along_lanes(north), along_lanes(south)
    own = 1.0 - n - s

    def group(i, carry):
        here = column[i]
        up = pltpu.roll(here, lanes - 1, 1)
        down = pltpu.roll(here, 1, 1)
        for j in range(GROUP):
            level = i * GROUP + j
            bottom, top = j * rows, j * rows + rows - 1
            up = jnp.where(lane == top, pltpu.roll(after[level], top, 1), up)
            moved = before[level]
            moved = pltpu.roll(moved, bottom, 1) if bottom else moved
            down = jnp.where(lane == bottom, moved, down)
        edge[i] = own * here + n * up + s * down
        return carry

    def finish():
        for tile in tiles:
            tile.wait()
        lax.fori_loop(0, groups, group, 0)

    return finish


def rotate_kernel(step, shift, circle_in, out, circle, moved, turned, ready):
    parts, groups, group, cells = turned.shape
    lat = lax.axis_index("lat")
    last_lat = lax.axis_size("lat") - 1
    rows = shift.shape[1] // lax.axis_size("lat")

    @pl.when((lat == 0) | (lat == last_lat))
    def _():
        fetch = pltpu.make_async_copy(circle_in, circle, ready.at[0])
        fetch.start()
        amount = jnp.where(lat == 0, shift[step, 0], shift[step, rows * last_lat + rows - 1])
        amount = lax.rem(amount + 2 * parts * cells, parts * cells)
        hops = amount // cells
        inner = amount - hops * cells
        shape = (group, cells)
        lane = lax.broadcasted_iota(jnp.int32, shape, 1)
        back = lax.rem(cells - inner, cells)
        fetch.wait()
        for part in range(parts):
            weight = jnp.broadcast_to(circle[part, groups, 0:1, :], shape)
            for g in range(groups):
                here = circle[part, g]
                following = jnp.where(
                    lane == cells - 1,
                    pltpu.roll(circle[(part + 1) % parts, g], cells - 1, 1),
                    pltpu.roll(here, cells - 1, 1),
                )
                moved[part, g] = pltpu.roll(here + weight * (following - here), back, 1)
        for part in range(parts):
            low = lax.rem(part + hops, parts)
            high = lax.rem(part + hops + 1, parts)
            for g in range(groups):
                turned[part, g] = jnp.where(lane < cells - inner, moved[low, g], moved[high, g])
        send = pltpu.make_async_copy(turned, out, ready.at[1])
        send.start()
        send.wait()


def prepare_stencil(step, north, south, east, coefs):
    rows, cells = north.shape[1:]
    tracers = coefs.shape[2]
    for r in range(rows):
        n = north[step, r : r + 1, :]
        s = south[step, r : r + 1, :]
        coefs[0, r] = jnp.broadcast_to(1.0 - n - s, (tracers, cells))
        coefs[1, r] = jnp.broadcast_to(n, (tracers, cells))
        coefs[2, r] = jnp.broadcast_to(s, (tracers, cells))
        coefs[3, r] = jnp.broadcast_to(east[step, r : r + 1, :], (tracers, cells))


def transported(group, lane_at, diffused, after, before, edge_row, coefs, pole):
    level = group * GROUP + lane_at
    rows, tracers, cells = diffused.shape[1:]
    lat = lax.axis_index("lat")
    last = lax.broadcasted_iota(jnp.int32, (tracers, cells), 1) == cells - 1
    result = []
    for r in range(rows):
        mer = meridional(level, r, diffused, after, before, [coefs[k, r] for k in range(3)])
        arrived = pltpu.roll(edge_row, LANES - 1 - (lane_at * rows + r), 1)
        arrived = jnp.concatenate([arrived] * (cells // LANES), axis=1)
        following = jnp.where(last, arrived, pltpu.roll(mer, cells - 1, 1))
        result.append(mer + coefs[3, r] * (following - mer))
    polar = pole[:, group, lane_at, :] if len(pole.shape) == 4 else pole[level]
    result[0] = jnp.where(lat == 0, polar, result[0])
    result[rows - 1] = jnp.where(lat == lax.axis_size("lat") - 1, polar, result[rows - 1])
    return result


def streams(sources, targets, poles, pole, done):
    lat = lax.axis_index("lat")
    last_lat = lax.axis_size("lat") - 1
    last = len(sources)

    def polar_copy(source, g):
        if len(pole.shape) == 4:
            return pltpu.make_async_copy(source.at[:, g], pole.at[:, g], done.at[last, g])
        return chunk(source, pole, done.at[last], g)

    for g in range(targets[0].shape[0] // GROUP):
        for k, (source, target) in enumerate(zip(sources, targets)):
            chunk(source, target, done.at[k], g).start()

        @pl.when(lat == 0)
        def _():
            polar_copy(poles[0], g).start()

        @pl.when(lat == last_lat)
        def _():
            polar_copy(poles[-1], g).start()

    def wait(g):
        for k, (source, target) in enumerate(zip(sources, targets)):
            chunk(source, target, done.at[k], g).wait()

        @pl.when((lat == 0) | (lat == last_lat))
        def _():
            polar_copy(poles[0], g).wait()

    return wait


def middle_kernel(
    step,
    before_step,
    forcing_in,
    after_in,
    before_in,
    south_pole,
    north_pole,
    edge,
    diffusion,
    north,
    south,
    east,
    result,
    first_out,
    last_out,
    polar_out,
    column,
    surface,
    coefs,
    ratios,
    diffused,
    forced,
    after,
    before,
    pole,
    solved,
    first,
    last,
    polar,
    arrived,
    sent,
):
    levels, rows, tracers, cells = diffused.shape
    wait = streams(
        (before_step, forcing_in, after_in, before_in),
        (diffused, forced, after, before),
        (south_pole, north_pole),
        pole,
        arrived,
    )
    prepare_stencil(step, north, south, east, coefs)

    def right_of(g, j, final):
        if j == 0:
            wait(g)
        level = g * GROUP + j
        rights = transported(g, j, diffused, after, before, edge[g], coefs, pole)
        rights = [rights[r] + forced[level, r] for r in range(rows)]
        if final:
            for r in range(rows):
                surface[r] = rights[r]

        def store(values):
            for r in range(rows):
                solved[level, r] = values[r]

        return rights, ratios, store

    forward_sweep(
        levels, rows, tracers, cells, lambda level: diffusion[step - 1, level], right_of
    )
    couplings = (north, south, east)
    fields = (solved, first, last, polar)
    results = (result, first_out, last_out, polar_out)
    substitute(step - 1, ratios, couplings, column, fields, results, sent)


def last_kernel(
    step,
    before_step,
    forcing_in,
    after_in,
    before_in,
    pole_in,
    edge,
    north,
    south,
    east,
    surface,
    state,
    gradient,
    coefs,
    diffused,
    forced,
    after,
    before,
    pole,
    staged,
    arrived,
    sent,
):
    levels, rows, tracers, cells = diffused.shape
    wait = streams(
        (before_step, forcing_in, after_in, before_in),
        (diffused, forced, after, before),
        (pole_in,),
        pole,
        arrived,
    )
    prepare_stencil(step, north, south, east, coefs)

    def group(g, carry):
        wait(g)
        edge_row = edge[g]
        for j in range(GROUP):
            level = g * GROUP + j
            values = transported(g, j, diffused, after, before, edge_row, coefs, pole)
            for r in range(rows):
                staged[level, :, r, :] = values[r] + forced[level, r]
        chunk(staged, state, sent, g).start()
        return carry

    lax.fori_loop(0, levels // GROUP, group, 0)
    for r in range(rows):
        gradient[:, r, :] = surface[r] + staged[levels - 1, :, r, :]
    wait_all(staged, state, sent)


def boundary_rows(first, last):
    up = [(i, i + 1) for i in range(lax.axis_size("lat") - 1)]
    down = [(j, i) for i, j in up]
    return lax.ppermute(first, "lat", down), lax.ppermute(last, "lat", up)


def circles(lats, hops):
    lat_count = lax.axis_size("lat")
    lon_count = lax.axis_size("lon")
    return [
        (((j + hops) % lon_count) * lat_count + lat, j * lat_count + lat)
        for lat in lats
        for j in range(lon_count)
    ]


def westward(edge):
    count = lax.axis_size("lon")
    return held(lax.ppermute(edge, "lon", [(i, (i - 1) % count) for i in range(count)]))


def first_exchange(step, after, before, nearby, polar, column, north, south, shift, hops):
    poles = (0, lax.axis_size("lat") - 1)
    levels, tracers, cells = after.shape
    edge, turned = pl.pallas_call(
        functools.partial(borders_kernel, step),
        out_shape=[resident(*column.shape), pltpu.HBM((levels, tracers, cells), F32)],
        in_specs=[smem()] + [vmem()] * 3 + [anywhere()] * 4,
        out_specs=[vmem(), hbm()],
        scratch_shapes=[
            pltpu.VMEM((levels, tracers, LANES), F32),
            pltpu.VMEM((levels, tracers, LANES), F32),
            pltpu.VMEM(polar.shape, F32),
            pltpu.VMEM(polar.shape, F32),
            pltpu.VMEM((levels, tracers, cells), F32),
            pltpu.SemaphoreType.DMA((5,)),
        ],
        compiler_params=params(6),
        name="borders",
    )(shift, column, north, south, after, before, pinned(polar), nearby)
    edge = westward(edge)
    moved = []
    for lat, hop in zip(poles, hops):
        moved.append(
            lax.switch(
                hop,
                [
                    functools.partial(
                        lambda k, lat, x: lax.ppermute(x, AXES, circles((lat,), k)), k, lat
                    )
                    for k in range(lax.axis_size("lon"))
                ],
                turned,
            )
        )
    return after, before, pinned(moved[0]), pinned(moved[1]), edge


def last_exchange(step, after, before, circle, column, north, south, shift):
    levels, tracers, cells = after.shape
    parts, groups, group = circle.shape[:3]
    shape = (parts, groups - 1, group, cells)
    turned = pl.pallas_call(
        functools.partial(rotate_kernel, step),
        out_shape=pltpu.HBM(shape, F32),
        in_specs=[smem(), anywhere()],
        out_specs=hbm(),
        scratch_shapes=[
            pltpu.VMEM(circle.shape, F32),
            pltpu.VMEM(shape, F32),
            pltpu.VMEM(shape, F32),
            pltpu.SemaphoreType.DMA((2,)),
        ],
        compiler_params=params(6),
        name="rotate",
    )(shift, circle)
    pole = lax.all_to_all(turned, "lon", 0, 0, tiled=True)
    edge = pl.pallas_call(
        functools.partial(edge_kernel, step),
        out_shape=resident(*column.shape),
        in_specs=[vmem()] * 3 + [anywhere()] * 2,
        out_specs=vmem(),
        scratch_shapes=[
            pltpu.VMEM((levels, tracers, LANES), F32),
            pltpu.VMEM((levels, tracers, LANES), F32),
            pltpu.SemaphoreType.DMA((2,)),
        ],
        compiler_params=params(4),
        name="edge",
    )(column, north, south, after, before)
    return after, before, pole, westward(edge)


def per_device(
    costate,
    diffusion,
    east_courant,
    north_courant,
    south_courant,
    polar_shift,
    owners,
    columns,
    sounding_counts,
    kernels,
    misfits,
):
    levels, tracers, rows, cells = costate.shape
    owner_rows = owners.reshape(owners.shape[0], 1, owners.shape[1])
    couplings = (north_courant, south_courant, east_courant)
    groups = levels // GROUP

    solved_shapes = [
        pltpu.HBM((levels, rows, tracers, cells), F32),
        pltpu.HBM((levels, tracers, cells), F32),
        pltpu.HBM((levels, tracers, cells), F32),
        pltpu.HBM((levels + 1, tracers, cells), F32),
        resident(groups, tracers, LANES),
    ]
    ratios = pltpu.VMEM((levels, rows, cells), F32)
    coefs = pltpu.VMEM((4, rows, tracers, cells), F32)
    field = pltpu.VMEM((levels, rows, tracers, cells), F32)
    line = pltpu.VMEM((levels, tracers, cells), F32)
    solved_scratch = [field, line, line, pltpu.VMEM((levels + 1, tracers, cells), F32)]
    solved_specs = [hbm()] * 4 + [vmem()]
    leaving = pltpu.SemaphoreType.DMA((4, groups + 1))
    output = pltpu.VMEM(costate.shape, F32)
    semaphores = pltpu.SemaphoreType.DMA((groups,))
    diffused, first, last, polar, column = pl.pallas_call(
        functools.partial(first_kernel, 1),
        out_shape=solved_shapes,
        in_specs=[hbm()] * 5,
        out_specs=solved_specs,
        scratch_shapes=[
            output,
            ratios,
            *solved_scratch,
            pltpu.VMEM(diffusion.shape[1:], F32),
            pltpu.VMEM((3,) + east_courant.shape, F32),
            semaphores,
            leaving,
            pltpu.SemaphoreType.DMA((4,)),
        ],
        compiler_params=params(16),
        name="first",
    )(*[pinned(x) for x in (costate, diffusion, *couplings)])
    couplings = [held(x) for x in couplings]
    diffusion = held(diffusion)
    counts, column = lax.optimization_barrier((sounding_counts, column))
    lat_count, lon_count = lax.axis_size("lat"), lax.axis_size("lon")
    ends = jnp.stack([polar_shift[1, 0], polar_shift[1, -1]])
    hops = (ends & (cells * lon_count - 1)) >> (cells.bit_length() - 1)
    nearby = lax.ppermute(polar, AXES, circles((0, lat_count - 1), 1))
    around = (*boundary_rows(first, last), nearby)
    sent = packed(counts, owner_rows, columns, kernels, misfits)
    sent, *around = lax.optimization_barrier((sent, *around))
    around = [pinned(x) for x in around]
    got = lax.all_to_all(sent, AXES, 0, 0, tiled=True)
    forced = pinned(forcing(1, got, levels, tracers, rows, cells))
    around = first_exchange(1, *around, polar, column, *couplings[:2], polar_shift, hops)
    scratch = [field, field, line, line]
    transfers = pltpu.SemaphoreType.DMA((5, groups))
    solved, first, last, polar, column, surface = pl.pallas_call(
        functools.partial(middle_kernel, 1),
        out_shape=[
            *solved_shapes[:3],
            pltpu.HBM((tracers, groups + 1, GROUP, cells), F32),
            solved_shapes[4],
            resident(rows, tracers, cells),
        ],
        in_specs=[hbm()] * 2 + [anywhere()] * 2 + [hbm()] * 2 + [vmem()] * 5,
        out_specs=solved_specs + [vmem()],
        scratch_shapes=[
            coefs,
            ratios,
            *scratch,
            line,
            *solved_scratch[:3],
            pltpu.VMEM((tracers, groups + 1, GROUP, cells), F32),
            transfers,
            leaving,
        ],
        compiler_params=params(26),
        name="middle",
    )(pinned(diffused), forced, *around, diffusion, *couplings)
    around = (*boundary_rows(first, last), lax.all_to_all(polar, "lon", 0, 0, tiled=True))
    got, column = lax.optimization_barrier((got, column))
    forced = pinned(forcing(0, got, levels, tracers, rows, cells))
    forced, *around = lax.optimization_barrier((forced, *around))
    around = last_exchange(0, *around, column, *couplings[:2], polar_shift)
    return tuple(
        pl.pallas_call(
            functools.partial(last_kernel, 0),
            out_shape=[
                pltpu.HBM(costate.shape, F32),
                jax.ShapeDtypeStruct((tracers, rows, cells), F32),
            ],
            in_specs=[hbm()] * 2 + [anywhere()] * 3 + [vmem()] * 5,
            out_specs=[hbm(), vmem()],
            scratch_shapes=[
                coefs,
                *scratch,
                pltpu.VMEM((tracers, groups, GROUP, cells), F32),
                output,
                transfers,
                semaphores,
            ],
            compiler_params=params(22),
            name="last",
        )(pinned(solved), pinned(forced), *around, *couplings, surface)
    )


def solution(mesh):
    return jax.shard_map(
        per_device,
        mesh=mesh,
        in_specs=(
            P(None, None, "lat", "lon"),
            P(None, None, "lat", "lon"),
            P(None, "lat", "lon"),
            P(None, "lat", "lon"),
            P(None, "lat", "lon"),
            P(),
            P(None, ("lon", "lat"), None),
            P(None, ("lon", "lat")),
            P(None, ("lon", "lat")),
            P(None, None, ("lon", "lat")),
            P(None, None, ("lon", "lat")),
        ),
        out_specs=(P(None, None, "lat", "lon"), P(None, "lat", "lon")),
        check_vma=False,
    )
```

```python
import functools

import jax
import jax.numpy as jnp
from jax import lax
from jax.experimental import pallas as pl
from jax.experimental.pallas import tpu as pltpu
from jax.sharding import PartitionSpec as P

AXES = ("lon", "lat")
LANES = 128
CAP = 16
GROUP = 8
F32 = jnp.float32
BF16 = jnp.bfloat16
MIB = 1024 * 1024


def vmem():
    return pl.BlockSpec(memory_space=pltpu.VMEM)


def smem():
    return pl.BlockSpec(memory_space=pltpu.SMEM)


def hbm():
    return pl.BlockSpec(memory_space=pltpu.HBM)


def params(limit):
    return pltpu.CompilerParams(vmem_limit_bytes=limit * MIB)


def held(x):
    return pltpu.with_memory_space_constraint(x, pltpu.VMEM)


def anywhere():
    return pl.BlockSpec(memory_space=pl.ANY)


def pinned(x):
    return pltpu.with_memory_space_constraint(x, pltpu.HBM)


def resident(*shape):
    return pltpu.VMEM(shape, F32)


def chunk(source, target, done, g):
    at = pl.ds(g * GROUP, GROUP)
    return pltpu.make_async_copy(source.at[at], target.at[at], done.at[g])


def start_all(source, target, done):
    for g in range(source.shape[0] // GROUP):
        chunk(source, target, done, g).start()


def wait_all(source, target, done):
    for g in range(source.shape[0] // GROUP):
        chunk(source, target, done, g).wait()


def dot(a, b, contract=((1,), (0,))):
    return lax.dot_general(a, b, (contract, ((), ())), preferred_element_type=F32)


def halves(x):
    high = x.astype(BF16)
    return high, (x - high.astype(F32)).astype(BF16)


def pack_kernel(
    counts, owners, columns, kernels, misfits, out, payload, target, staged, done
):
    steps, levels, held = kernels.shape
    tracers = misfits.shape[1]
    shape = (LANES, LANES)
    device = lax.broadcasted_iota(jnp.int32, shape, 0)
    table = counting_table()
    for step in range(steps):
        owner = owners[step]
        live = lax.broadcasted_iota(jnp.int32, owner.shape, 1) < counts[step, 0]
        owner = jnp.where(live, owner, -1)
        seen = jnp.zeros(shape, F32)
        for start in range(0, held, LANES):
            here = owner[:, start : start + LANES]
            hot = device == here
            counted = dot(jnp.where(hot, 1.0, 0.0).astype(BF16), table)
            rank = jnp.sum(
                jnp.where(hot, counted[:, :LANES] + seen, 0.0), axis=0, keepdims=True
            )
            seen = seen + counted[:, LANES:]
            target[step : step + 1, start : start + LANES] = jnp.where(
                here >= 0, here * CAP + rank.astype(jnp.int32), -1
            )
        column = columns[step : step + 1, :].astype(F32) + 1.0
        column = jnp.where(lax.broadcasted_iota(jnp.int32, (8, held), 0) == 0, column, 0.0)
        unused = jnp.zeros((LANES - levels - tracers - 8, held), F32)
        high, low = halves(
            jnp.concatenate([kernels[step], misfits[step], column, unused], axis=0)
        )
        payload[step, :LANES, :] = high
        payload[step, LANES:, :] = low
    owned = 256 // CAP
    tiles = out.shape[0] // owned

    def copy(i):
        at = pl.ds(i * owned, owned)
        return pltpu.make_async_copy(staged.at[at], out.at[at], done.at[i])

    def place(i, carry):
        for step in range(steps):
            hot = one_hot(target[step : step + 1, :] - i * owned * CAP, owned * CAP)
            both = dot(hot, payload[step], ((1,), (1,)))
            both = both[:, :LANES] + both[:, LANES:]
            staged[pl.ds(i * owned, owned), step * CAP : (step + 1) * CAP, :] = both.reshape(
                owned, CAP, LANES
            )
        copy(i).start()
        return carry

    lax.fori_loop(0, tiles, place, 0)
    for i in range(tiles):
        copy(i).wait()


def one_hot(at, size):
    at = jnp.where((at >= 0) & (at < size), at, -1).astype(F32).astype(BF16)
    shape = (size, at.shape[1])
    row = lax.broadcasted_iota(jnp.int32, shape, 0).astype(F32).astype(BF16)
    return jnp.where(row == at, jnp.ones(shape, BF16), jnp.zeros(shape, BF16))


def counting_table():
    shape = (LANES, LANES)
    earlier = lax.broadcasted_iota(jnp.int32, shape, 0) < lax.broadcasted_iota(
        jnp.int32, shape, 1
    )
    return jnp.concatenate(
        [jnp.where(earlier, 1.0, 0.0), jnp.ones(shape, F32)], axis=1
    ).astype(BF16)


def packed(counts, owners, columns, kernels, misfits):
    steps, slots = columns.shape
    devices = lax.axis_size("lon") * lax.axis_size("lat")
    return pl.pallas_call(
        pack_kernel,
        out_shape=pltpu.HBM((devices, steps * CAP, LANES), F32),
        in_specs=[smem()] + [vmem()] * 4,
        out_specs=hbm(),
        scratch_shapes=[
            pltpu.VMEM((steps, 2 * LANES, slots), BF16),
            pltpu.VMEM((steps, slots), jnp.int32),
            pltpu.VMEM((devices, steps * CAP, LANES), F32),
            pltpu.SemaphoreType.DMA((devices * CAP // 256,)),
        ],
        compiler_params=params(8),
        name="pack",
    )(counts, held(owners), held(columns), held(kernels), held(misfits))


def streamed_forcing_kernel(step, received, result, out, *scratch):
    done = scratch[-1]

    def copy(r):
        return pltpu.make_async_copy(out.at[:, r], result.at[:, r], done.at[r])

    forcing_kernel(step, received, out, *scratch[:-1], finished=lambda r: copy(r).start())
    for r in range(out.shape[1]):
        copy(r).wait()


def forcing_kernel(
    step, received, out, fields, hots, place, ordered, finished=lambda r: None
):
    levels, rows, tracers, cells = out.shape
    sources = received.shape[0]
    slots = sources * CAP
    blocks = slots // LANES
    at_column = levels + tracers
    data = received[:, step * CAP : (step + 1) * CAP, :].reshape(slots, LANES)
    high, low = halves(data)
    fields[:, :LANES] = high
    fields[:, LANES:] = low
    shape = (8, 2 * LANES)
    pick = (lax.broadcasted_iota(jnp.int32, shape, 1) & (LANES - 1)) == at_column
    column = dot(jnp.where(pick, 1.0, 0.0).astype(BF16), fields[...], ((1,), (1,)))
    cell_row = (column.astype(jnp.int32) - 1) >> (cells.bit_length() - 1)
    sub = lax.broadcasted_iota(jnp.int32, (rows, LANES), 0)
    for b in range(blocks):
        row = cell_row[:, b * LANES : (b + 1) * LANES]
        hots[b * rows : (b + 1) * rows, :] = jnp.where(sub == row, 1.0, 0.0)
    counted = dot(hots[...].astype(BF16), counting_table())
    run = jnp.zeros((rows, LANES), F32)
    runs = []
    for b in range(blocks):
        runs.append(run)
        run = run + counted[b * rows : (b + 1) * rows, LANES:]
    filled = jnp.floor((run + (LANES - 1.0)) * (1.0 / LANES))
    start = jnp.zeros((rows, LANES), F32)
    for j in range(1, rows):
        start = start + jnp.where(sub >= j, pltpu.roll(filled, j, 0), 0.0)
    for b in range(blocks):
        hot = hots[b * rows : (b + 1) * rows, :]
        at = counted[b * rows : (b + 1) * rows, :LANES] + runs[b] + start * float(LANES)
        at = jnp.sum(hot * at, axis=0, keepdims=True)
        live = jnp.sum(hot, axis=0, keepdims=True) > 0.0
        place[:, b * LANES : (b + 1) * LANES] = jnp.where(live, at, -1.0)
    counts = [jnp.max(filled[r : r + 1, :]).astype(jnp.int32) for r in range(rows)]
    used = sum(counts)
    wide = 2 * LANES

    def sort(i, carry):
        hot = one_hot(place[...] - (i * wide).astype(F32), wide)
        both = dot(hot, fields[...])
        ordered[pl.ds(pl.multiple_of(i * wide, wide), wide), :] = both[:, :LANES] + both[:, LANES:]
        return carry

    lax.fori_loop(0, (used + 1) // 2, sort, 0)
    out[...] = jnp.zeros_like(out)
    name = lax.broadcasted_iota(jnp.int32, (LANES, cells), 1).astype(F32)
    first = jnp.int32(0)
    for r in range(rows):

        def add(p, carry):
            block = ordered[pl.ds(pl.multiple_of(p * LANES, LANES), LANES), :]
            own = jnp.broadcast_to(
                block[:, at_column : at_column + 1] - (r * cells + 1.0), (LANES, cells)
            )
            hot = jnp.where(name == own, 1.0, 0.0).astype(BF16)
            turned = block.T
            product = turned[:levels][:, None, :] * turned[levels:at_column][None]
            first_half, second_half = halves(product.reshape(levels * tracers, LANES))
            total = dot(first_half, hot) + dot(second_half, hot)
            out[:, r, :, :] += total.reshape(levels, tracers, cells)
            return carry

        lax.fori_loop(first, first + counts[r], add, 0)
        first = first + counts[r]
        finished(r)


def forcing(step, received, shape, streamed):
    slots = received.shape[0] * CAP
    scratch = [
        pltpu.VMEM((slots, 2 * LANES), BF16),
        pltpu.VMEM((slots // LANES * shape[1], LANES), F32),
        pltpu.VMEM((1, slots), F32),
        pltpu.VMEM((slots + shape[1] * LANES, LANES), F32),
    ]
    if streamed:
        scratch = [resident(*shape), *scratch, pltpu.SemaphoreType.DMA((shape[1],))]
    return pl.pallas_call(
        functools.partial(streamed_forcing_kernel if streamed else forcing_kernel, step),
        out_shape=pltpu.HBM(shape, F32) if streamed else resident(*shape),
        in_specs=[vmem()],
        out_specs=hbm() if streamed else vmem(),
        scratch_shapes=scratch,
        compiler_params=params(16 if streamed else 12),
        name="forcing",
    )(held(received))


def shift_matrix(inner, cells):
    shape = (2 * cells, cells)
    source = lax.broadcasted_iota(jnp.int32, shape, 0)
    target = lax.broadcasted_iota(jnp.int32, shape, 1) + inner
    picks = [jnp.where(source == target + k, 1.0, 0.0).astype(BF16) for k in range(2)]
    return jnp.concatenate(picks, axis=1)


def shifted(low, high, matrix):
    row = jnp.concatenate([low, high], axis=1)
    first, rest = row.astype(BF16), None
    rest = row - first.astype(F32)
    second, third = halves(rest)
    return dot(first, matrix) + dot(second, matrix) + dot(third, matrix)


def spread(x, row, tracers):
    return jnp.broadcast_to(x[row : row + 1, :], (tracers, x.shape[1]))


def eliminate(level, above, carry, rights, ratios):
    below, ratio, values = carry
    if above is None:
        above = jnp.zeros_like(below)
    inverse = 1.0 / (1.0 + below + above + below * ratio)
    lower = below * inverse
    ratio = -above * inverse
    ratios[level] = ratio
    tracers = rights[0].shape[0]
    fresh = [
        spread(inverse, r, tracers) * rights[r] + spread(lower, r, tracers) * values[r]
        for r in range(len(rights))
    ]
    return (above, ratio, fresh)


def substitute(step, ratios, couplings, column, fields, results, done):
    diffused, first, last, polar = fields
    levels, rows, tracers, cells = diffused.shape
    lat = lax.axis_index("lat")
    at_start = lat == 0

    def picked(x):
        return jnp.where(at_start, x[step, 0:1, :], x[step, rows - 1 : rows, :])

    north, south, east = [picked(x) for x in couplings]
    own = jnp.broadcast_to(1.0 - north - south, (tracers, cells))
    side = jnp.broadcast_to(jnp.where(at_start, north, south), (tracers, cells))
    groups = levels // GROUP
    by_tracer = len(polar.shape) == 4
    if by_tracer:
        polar[:, groups, 0, :] = jnp.broadcast_to(east, (tracers, cells))
    else:
        polar[levels] = jnp.broadcast_to(east, (tracers, cells))

    def polar_copy(g):
        if by_tracer:
            source, target = [x.at[:, g] for x in (polar, results[3])]
        else:
            at = pl.ds(g * GROUP, GROUP if not isinstance(g, int) else 1)
            source, target = [x.at[at] for x in (polar, results[3])]
        return pltpu.make_async_copy(source, target, done.at[3, g])

    polar_copy(groups).start()
    lane = lax.broadcasted_iota(jnp.int32, (tracers, LANES), 1)

    def group(i, solved):
        at = groups - 1 - i
        west = jnp.zeros((tracers, LANES), F32)
        for j in range(GROUP - 1, -1, -1):
            level = at * GROUP + j
            ratio = ratios[level]
            fresh = []
            for r in range(rows):
                value = diffused[level, r] - spread(ratio, r, tracers) * solved[r]
                diffused[level, r] = value
                fresh.append(value)
                lanes = j * rows + r
                moved = pltpu.roll(value[:, :LANES], lanes, 1) if lanes else value[:, :LANES]
                west = jnp.where(lane == lanes, moved, west)
            solved = fresh
            first[level] = solved[0]
            last[level] = solved[rows - 1]
            row = own * jnp.where(at_start, solved[0], solved[rows - 1]) + side * jnp.where(
                at_start, solved[1], solved[rows - 2]
            )
            if by_tracer:
                polar[:, at, j, :] = row
            else:
                polar[level] = row
        column[at] = west
        for k in range(3):
            chunk(fields[k], results[k], done.at[k], at).start()
        polar_copy(at).start()
        return solved

    lax.fori_loop(0, groups, group, [jnp.zeros((tracers, cells), F32)] * rows)
    polar_copy(groups).wait()
    for g in range(groups):
        for k in range(3):
            chunk(fields[k], results[k], done.at[k], g).wait()
        polar_copy(jnp.int32(g)).wait()


def forward_sweep(levels, rows, tracers, cells, diffusion, right_of):
    zero = jnp.zeros((rows, cells), F32)
    carry = (zero, zero, [jnp.zeros((tracers, cells), F32)] * rows)
    groups = levels // GROUP

    def one(g, j, above, carry):
        rights, ratios, store = right_of(g, j, above is None)
        carry = eliminate(g * GROUP + j, above, carry, rights, ratios)
        store(carry[2])
        return carry

    def group(g, carry):
        for j in range(GROUP):
            carry = one(g, j, diffusion(g * GROUP + j), carry)
        return carry

    carry = lax.fori_loop(0, groups - 1, group, carry)
    for j in range(GROUP):
        level = levels - GROUP + j
        carry = one(groups - 1, j, diffusion(level) if level < levels - 1 else None, carry)


def first_kernel(
    step,
    costate,
    diffusion_in,
    north_in,
    south_in,
    east_in,
    result,
    first_out,
    last_out,
    polar_out,
    column,
    staged,
    ratios,
    diffused,
    first,
    last,
    polar,
    diffusion,
    couplings,
    arrived,
    sent,
    ready,
):
    levels, tracers, rows, cells = costate.shape
    small = [pltpu.make_async_copy(diffusion_in.at[step], diffusion, ready.at[0])]
    for k, coupling in enumerate((north_in, south_in, east_in)):
        small.append(pltpu.make_async_copy(coupling, couplings.at[k], ready.at[1 + k]))
    chunk(costate, staged, arrived, 0).start()
    for copy in small:
        copy.start()
    for g in range(1, levels // GROUP):
        chunk(costate, staged, arrived, g).start()
    for copy in small:
        copy.wait()

    def right_of(g, j, final):
        if j == 0:
            chunk(costate, staged, arrived, g).wait()
        level = g * GROUP + j
        rights = [staged[level, :, r, :] for r in range(rows)]

        def store(values):
            for r in range(rows):
                diffused[level, r] = values[r]

        return rights, ratios, store

    forward_sweep(levels, rows, tracers, cells, lambda level: diffusion[level], right_of)
    views = [couplings.at[k] for k in range(3)]
    fields = (diffused, first, last, polar)
    results = (result, first_out, last_out, polar_out)
    substitute(step, ratios, views, column, fields, results, sent)


def meridional(level, row, diffused, after, before, coefs):
    rows = diffused.shape[1]
    own, north, south = coefs
    up = diffused[level, row + 1] if row < rows - 1 else after[level]
    down = diffused[level, row - 1] if row > 0 else before[level]
    return own * diffused[level, row] + north * up + south * down


def borders_kernel(
    step,
    shift,
    column,
    north,
    south,
    after_in,
    before_in,
    polar_in,
    nearby_in,
    edge,
    turned_out,
    after,
    before,
    polar,
    nearby,
    turned,
    ready,
):
    rows, cells = north.shape[1:]
    fetches = [
        pltpu.make_async_copy(source, target, ready.at[2 + k])
        for k, (source, target) in enumerate(((polar_in, polar), (nearby_in, nearby)))
    ]
    sending = pltpu.make_async_copy(turned, turned_out, ready.at[4])
    lat = lax.axis_index("lat")
    last_lat = lax.axis_size("lat") - 1
    at_pole = (lat == 0) | (lat == last_lat)

    @pl.when(at_pole)
    def _():
        for fetch in fetches:
            fetch.start()

    finish = west_column(step, column, north, south, after_in, before_in, edge, after, before, ready)

    @pl.when(at_pole)
    def _():
        for fetch in fetches:
            fetch.wait()
        levels = turned.shape[0]
        circle = cells * lax.axis_size("lon")
        amount = jnp.where(lat == 0, shift[step, 0], shift[step, rows * last_lat + rows - 1])
        matrix = shift_matrix(lax.rem(amount + 2 * circle, circle) & (cells - 1), cells)
        tracers = turned.shape[1]
        weight = shifted(polar[levels], nearby[levels], matrix)[:1, :cells]
        size = 3 * GROUP
        for i in range(levels // size):
            at = slice(i * size, (i + 1) * size)
            low, high = [x[at].reshape(size * tracers, cells) for x in (polar, nearby)]
            row = shifted(low, high, matrix)
            row = row[:, :cells] + weight * (row[:, cells:] - row[:, :cells])
            turned[at] = row.reshape(size, tracers, cells)
        sending.start()

    finish()

    @pl.when(at_pole)
    def _():
        sending.wait()


def edge_kernel(
    step, column, north, south, after_in, before_in, edge, after, before, ready
):
    west_column(step, column, north, south, after_in, before_in, edge, after, before, ready)()


def west_column(step, column, north, south, after_in, before_in, edge, after, before, ready):
    groups, tracers, lanes = column.shape
    rows, cells = north.shape[1:]
    tiles = [
        pltpu.make_async_copy(source.at[:, :, pl.ds(0, lanes)], target, ready.at[k])
        for k, (source, target) in enumerate(((after_in, after), (before_in, before)))
    ]
    for tile in tiles:
        tile.start()
    lane = lax.broadcasted_iota(jnp.int32, (tracers, lanes), 1)

    def along_lanes(x):
        shape = (rows, lanes)
        own_lane = (lax.broadcasted_iota(jnp.int32, shape, 1) & (rows - 1)) == (
            lax.broadcasted_iota(jnp.int32, shape, 0)
        )
        picked = jnp.where(own_lane, jnp.broadcast_to(x[step, :, :1], shape), 0.0)
        return jnp.broadcast_to(jnp.sum(picked, axis=0, keepdims=True), (tracers, lanes))

    n, s = along_lanes(north), along_lanes(south)
    own = 1.0 - n - s

    def group(i, carry):
        here = column[i]
        up = pltpu.roll(here, lanes - 1, 1)
        down = pltpu.roll(here, 1, 1)
        for j in range(GROUP):
            level = i * GROUP + j
            bottom, top = j * rows, j * rows + rows - 1
            up = jnp.where(lane == top, pltpu.roll(after[level], top, 1), up)
            moved = before[level]
            moved = pltpu.roll(moved, bottom, 1) if bottom else moved
            down = jnp.where(lane == bottom, moved, down)
        edge[i] = own * here + n * up + s * down
        return carry

    def finish():
        for tile in tiles:
            tile.wait()
        lax.fori_loop(0, groups, group, 0)

    return finish


def rotate_kernel(step, shift, circle_in, out, circle, turned, ready):
    parts, groups, group, cells = turned.shape
    lat = lax.axis_index("lat")
    last_lat = lax.axis_size("lat") - 1
    rows = shift.shape[1] // lax.axis_size("lat")

    @pl.when((lat == 0) | (lat == last_lat))
    def _():
        fetch = pltpu.make_async_copy(circle_in, circle, ready.at[0])
        fetch.start()
        amount = jnp.where(lat == 0, shift[step, 0], shift[step, rows * last_lat + rows - 1])
        amount = lax.rem(amount + 2 * parts * cells, parts * cells)
        hops = amount // cells
        matrix = shift_matrix(amount - hops * cells, cells)
        fetch.wait()
        for part in range(parts):
            near = lax.rem(part + hops, parts)
            far = lax.rem(part + hops + 1, parts)
            low, high = [
                circle[x].reshape((groups + 1) * group, cells) for x in (near, far)
            ]
            row = shifted(low, high, matrix)
            size = groups * group
            weight = row[size : size + 1, :cells]
            row = row[:size]
            row = row[:, :cells] + weight * (row[:, cells:] - row[:, :cells])
            turned[part] = row.reshape(groups, group, cells)
        send = pltpu.make_async_copy(turned, out, ready.at[1])
        send.start()
        send.wait()


def prepare_stencil(step, north, south, east, coefs):
    rows, cells = north.shape[1:]
    tracers = coefs.shape[2]
    for r in range(rows):
        n = north[step, r : r + 1, :]
        s = south[step, r : r + 1, :]
        coefs[0, r] = jnp.broadcast_to(1.0 - n - s, (tracers, cells))
        coefs[1, r] = jnp.broadcast_to(n, (tracers, cells))
        coefs[2, r] = jnp.broadcast_to(s, (tracers, cells))
        coefs[3, r] = jnp.broadcast_to(east[step, r : r + 1, :], (tracers, cells))


def transported(group, lane_at, diffused, after, before, edge_row, coefs, pole):
    level = group * GROUP + lane_at
    rows, tracers, cells = diffused.shape[1:]
    lat = lax.axis_index("lat")
    last = lax.broadcasted_iota(jnp.int32, (tracers, cells), 1) == cells - 1
    result = []
    for r in range(rows):
        mer = meridional(level, r, diffused, after, before, [coefs[k, r] for k in range(3)])
        arrived = pltpu.roll(edge_row, LANES - 1 - (lane_at * rows + r), 1)
        arrived = jnp.concatenate([arrived] * (cells // LANES), axis=1)
        following = jnp.where(last, arrived, pltpu.roll(mer, cells - 1, 1))
        result.append(mer + coefs[3, r] * (following - mer))
    polar = pole[:, group, lane_at, :] if len(pole.shape) == 4 else pole[level]
    result[0] = jnp.where(lat == 0, polar, result[0])
    result[rows - 1] = jnp.where(lat == lax.axis_size("lat") - 1, polar, result[rows - 1])
    return result


def streams(sources, targets, poles, pole, done):
    lat = lax.axis_index("lat")
    last_lat = lax.axis_size("lat") - 1
    last = len(sources)

    def polar_copy(source, g):
        if len(pole.shape) == 4:
            return pltpu.make_async_copy(source.at[:, g], pole.at[:, g], done.at[last, g])
        return chunk(source, pole, done.at[last], g)

    for g in range(targets[0].shape[0] // GROUP):
        for k, (source, target) in enumerate(zip(sources, targets)):
            chunk(source, target, done.at[k], g).start()

        @pl.when(lat == 0)
        def _():
            polar_copy(poles[0], g).start()

        @pl.when(lat == last_lat)
        def _():
            polar_copy(poles[-1], g).start()

    def wait(g):
        for k, (source, target) in enumerate(zip(sources, targets)):
            chunk(source, target, done.at[k], g).wait()

        @pl.when((lat == 0) | (lat == last_lat))
        def _():
            polar_copy(poles[0], g).wait()

    return wait


def middle_kernel(
    step,
    before_step,
    forced,
    after_in,
    before_in,
    south_pole,
    north_pole,
    edge,
    diffusion,
    north,
    south,
    east,
    result,
    first_out,
    last_out,
    polar_out,
    column,
    surface,
    coefs,
    ratios,
    diffused,
    after,
    before,
    pole,
    solved,
    first,
    last,
    polar,
    arrived,
    sent,
):
    levels, rows, tracers, cells = diffused.shape
    wait = streams(
        (before_step, after_in, before_in),
        (diffused, after, before),
        (south_pole, north_pole),
        pole,
        arrived,
    )
    prepare_stencil(step, north, south, east, coefs)

    def right_of(g, j, final):
        if j == 0:
            wait(g)
        level = g * GROUP + j
        rights = transported(g, j, diffused, after, before, edge[g], coefs, pole)
        rights = [rights[r] + forced[level, r] for r in range(rows)]
        if final:
            for r in range(rows):
                surface[r] = rights[r]

        def store(values):
            for r in range(rows):
                solved[level, r] = values[r]

        return rights, ratios, store

    forward_sweep(
        levels, rows, tracers, cells, lambda level: diffusion[step - 1, level], right_of
    )
    couplings = (north, south, east)
    fields = (solved, first, last, polar)
    results = (result, first_out, last_out, polar_out)
    substitute(step - 1, ratios, couplings, column, fields, results, sent)


def last_kernel(
    step,
    before_step,
    forcing_in,
    after_in,
    before_in,
    pole_in,
    edge,
    north,
    south,
    east,
    surface,
    state,
    gradient,
    coefs,
    diffused,
    forced,
    after,
    before,
    pole,
    staged,
    arrived,
    sent,
):
    levels, rows, tracers, cells = diffused.shape
    wait = streams(
        (before_step, forcing_in, after_in, before_in),
        (diffused, forced, after, before),
        (pole_in,),
        pole,
        arrived,
    )
    prepare_stencil(step, north, south, east, coefs)

    def group(g, carry):
        wait(g)
        edge_row = edge[g]
        for j in range(GROUP):
            level = g * GROUP + j
            values = transported(g, j, diffused, after, before, edge_row, coefs, pole)
            for r in range(rows):
                staged[level, :, r, :] = values[r] + forced[level, r]
        chunk(staged, state, sent, g).start()
        return carry

    lax.fori_loop(0, levels // GROUP, group, 0)
    for r in range(rows):
        gradient[:, r, :] = surface[r] + staged[levels - 1, :, r, :]
    wait_all(staged, state, sent)


def boundary_rows(first, last):
    up = [(i, i + 1) for i in range(lax.axis_size("lat") - 1)]
    down = [(j, i) for i, j in up]
    return lax.ppermute(first, "lat", down), lax.ppermute(last, "lat", up)


def circles(lats, hops):
    lat_count = lax.axis_size("lat")
    lon_count = lax.axis_size("lon")
    return [
        (((j + hops) % lon_count) * lat_count + lat, j * lat_count + lat)
        for lat in lats
        for j in range(lon_count)
    ]


def westward(edge):
    count = lax.axis_size("lon")
    return held(lax.ppermute(edge, "lon", [(i, (i - 1) % count) for i in range(count)]))


def first_exchange(step, after, before, nearby, polar, column, north, south, shift, hops):
    poles = (0, lax.axis_size("lat") - 1)
    levels, tracers, cells = after.shape
    edge, turned = pl.pallas_call(
        functools.partial(borders_kernel, step),
        out_shape=[resident(*column.shape), pltpu.HBM((levels, tracers, cells), F32)],
        in_specs=[smem()] + [vmem()] * 3 + [anywhere()] * 4,
        out_specs=[vmem(), hbm()],
        scratch_shapes=[
            pltpu.VMEM((levels, tracers, LANES), F32),
            pltpu.VMEM((levels, tracers, LANES), F32),
            pltpu.VMEM(polar.shape, F32),
            pltpu.VMEM(polar.shape, F32),
            pltpu.VMEM((levels, tracers, cells), F32),
            pltpu.SemaphoreType.DMA((5,)),
        ],
        compiler_params=params(8),
        name="borders",
    )(shift, column, north, south, after, before, pinned(polar), nearby)
    edge = westward(edge)
    moved = []
    for lat, hop in zip(poles, hops):
        moved.append(
            lax.switch(
                hop,
                [
                    functools.partial(
                        lambda k, lat, x: lax.ppermute(x, AXES, circles((lat,), k)), k, lat
                    )
                    for k in range(lax.axis_size("lon"))
                ],
                turned,
            )
        )
    return after, before, pinned(moved[0]), pinned(moved[1]), edge


def last_exchange(step, after, before, circle, column, north, south, shift):
    levels, tracers, cells = after.shape
    parts, groups, group = circle.shape[:3]
    shape = (parts, groups - 1, group, cells)
    turned = pl.pallas_call(
        functools.partial(rotate_kernel, step),
        out_shape=pltpu.HBM(shape, F32),
        in_specs=[smem(), anywhere()],
        out_specs=hbm(),
        scratch_shapes=[
            pltpu.VMEM(circle.shape, F32),
            pltpu.VMEM(shape, F32),
            pltpu.SemaphoreType.DMA((2,)),
        ],
        compiler_params=params(8),
        name="rotate",
    )(shift, circle)
    pole = lax.all_to_all(turned, "lon", 0, 0, tiled=True)
    edge = pl.pallas_call(
        functools.partial(edge_kernel, step),
        out_shape=resident(*column.shape),
        in_specs=[vmem()] * 3 + [anywhere()] * 2,
        out_specs=vmem(),
        scratch_shapes=[
            pltpu.VMEM((levels, tracers, LANES), F32),
            pltpu.VMEM((levels, tracers, LANES), F32),
            pltpu.SemaphoreType.DMA((2,)),
        ],
        compiler_params=params(4),
        name="edge",
    )(column, north, south, after, before)
    return after, before, pole, westward(edge)


def per_device(
    costate,
    diffusion,
    east_courant,
    north_courant,
    south_courant,
    polar_shift,
    owners,
    columns,
    sounding_counts,
    kernels,
    misfits,
):
    levels, tracers, rows, cells = costate.shape
    owner_rows = owners.reshape(owners.shape[0], 1, owners.shape[1])
    couplings = (north_courant, south_courant, east_courant)
    groups = levels // GROUP

    solved_shapes = [
        pltpu.HBM((levels, rows, tracers, cells), F32),
        pltpu.HBM((levels, tracers, cells), F32),
        pltpu.HBM((levels, tracers, cells), F32),
        pltpu.HBM((levels + 1, tracers, cells), F32),
        resident(groups, tracers, LANES),
    ]
    ratios = pltpu.VMEM((levels, rows, cells), F32)
    coefs = pltpu.VMEM((4, rows, tracers, cells), F32)
    field = pltpu.VMEM((levels, rows, tracers, cells), F32)
    line = pltpu.VMEM((levels, tracers, cells), F32)
    solved_scratch = [field, line, line, pltpu.VMEM((levels + 1, tracers, cells), F32)]
    solved_specs = [hbm()] * 4 + [vmem()]
    leaving = pltpu.SemaphoreType.DMA((4, groups + 1))
    output = pltpu.VMEM(costate.shape, F32)
    semaphores = pltpu.SemaphoreType.DMA((groups,))
    diffused, first, last, polar, column = pl.pallas_call(
        functools.partial(first_kernel, 1),
        out_shape=solved_shapes,
        in_specs=[hbm()] * 5,
        out_specs=solved_specs,
        scratch_shapes=[
            output,
            ratios,
            *solved_scratch,
            pltpu.VMEM(diffusion.shape[1:], F32),
            pltpu.VMEM((3,) + east_courant.shape, F32),
            semaphores,
            leaving,
            pltpu.SemaphoreType.DMA((4,)),
        ],
        compiler_params=params(16),
        name="first",
    )(*[pinned(x) for x in (costate, diffusion, *couplings)])
    couplings = [held(x) for x in couplings]
    diffusion = held(diffusion)
    counts, column = lax.optimization_barrier((sounding_counts, column))
    lat_count, lon_count = lax.axis_size("lat"), lax.axis_size("lon")
    ends = jnp.stack([polar_shift[1, 0], polar_shift[1, -1]])
    hops = (ends & (cells * lon_count - 1)) >> (cells.bit_length() - 1)
    nearby = lax.ppermute(polar, AXES, circles((0, lat_count - 1), 1))
    around = (*boundary_rows(first, last), nearby)
    sent = packed(counts, owner_rows, columns, kernels, misfits)
    sent, *around = lax.optimization_barrier((sent, *around))
    around = [pinned(x) for x in around]
    got = lax.all_to_all(sent, AXES, 0, 0, tiled=True)
    shape = (levels, rows, tracers, cells)
    forced = forcing(1, got, shape, False)
    around = first_exchange(1, *around, polar, column, *couplings[:2], polar_shift, hops)
    scratch = [field, line, line]
    transfers = pltpu.SemaphoreType.DMA((4, groups))
    solved, first, last, polar, column, surface = pl.pallas_call(
        functools.partial(middle_kernel, 1),
        out_shape=[
            *solved_shapes[:3],
            pltpu.HBM((tracers, groups + 1, GROUP, cells), F32),
            solved_shapes[4],
            resident(rows, tracers, cells),
        ],
        in_specs=[hbm(), vmem()] + [anywhere()] * 2 + [hbm()] * 2 + [vmem()] * 5,
        out_specs=solved_specs + [vmem()],
        scratch_shapes=[
            coefs,
            ratios,
            *scratch,
            line,
            *solved_scratch[:3],
            pltpu.VMEM((tracers, groups + 1, GROUP, cells), F32),
            transfers,
            leaving,
        ],
        compiler_params=params(20),
        name="middle",
    )(pinned(diffused), forced, *around, diffusion, *couplings)
    around = (*boundary_rows(first, last), lax.all_to_all(polar, "lon", 0, 0, tiled=True))
    got, column = lax.optimization_barrier((got, column))
    forced = forcing(0, got, shape, True)
    forced, *around = lax.optimization_barrier((forced, *around))
    around = last_exchange(0, *around, column, *couplings[:2], polar_shift)
    return tuple(
        pl.pallas_call(
            functools.partial(last_kernel, 0),
            out_shape=[
                pltpu.HBM(costate.shape, F32),
                jax.ShapeDtypeStruct((tracers, rows, cells), F32),
            ],
            in_specs=[hbm()] * 2 + [anywhere()] * 3 + [vmem()] * 5,
            out_specs=[hbm(), vmem()],
            scratch_shapes=[
                coefs,
                field,
                *scratch,
                pltpu.VMEM((tracers, groups, GROUP, cells), F32),
                output,
                pltpu.SemaphoreType.DMA((5, groups)),
                semaphores,
            ],
            compiler_params=params(22),
            name="last",
        )(pinned(solved), pinned(forced), *around, *couplings, surface)
    )


def solution(mesh):
    return jax.shard_map(
        per_device,
        mesh=mesh,
        in_specs=(
            P(None, None, "lat", "lon"),
            P(None, None, "lat", "lon"),
            P(None, "lat", "lon"),
            P(None, "lat", "lon"),
            P(None, "lat", "lon"),
            P(),
            P(None, ("lon", "lat"), None),
            P(None, ("lon", "lat")),
            P(None, ("lon", "lat")),
            P(None, None, ("lon", "lat")),
            P(None, None, ("lon", "lat")),
        ),
        out_specs=(P(None, None, "lat", "lon"), P(None, "lat", "lon")),
        check_vma=False,
    )
```

```python
import functools

import jax
import jax.numpy as jnp
from jax import lax
from jax.experimental import pallas as pl
from jax.experimental.pallas import tpu as pltpu
from jax.sharding import PartitionSpec as P

AXES = ("lon", "lat")
LANES = 128
CAP = 16
GROUP = 8
SPAN = 3
F32 = jnp.float32
BF16 = jnp.bfloat16
MIB = 1024 * 1024


def vmem():
    return pl.BlockSpec(memory_space=pltpu.VMEM)


def smem():
    return pl.BlockSpec(memory_space=pltpu.SMEM)


def hbm():
    return pl.BlockSpec(memory_space=pltpu.HBM)


def params(limit):
    return pltpu.CompilerParams(vmem_limit_bytes=limit * MIB)


def held(x):
    return pltpu.with_memory_space_constraint(x, pltpu.VMEM)


def anywhere():
    return pl.BlockSpec(memory_space=pl.ANY)


def pinned(x):
    return pltpu.with_memory_space_constraint(x, pltpu.HBM)


def resident(*shape):
    return pltpu.VMEM(shape, F32)


def chunk(source, target, done, c):
    at = pl.ds(c * GROUP * SPAN, GROUP * SPAN)
    return pltpu.make_async_copy(source.at[at], target.at[at], done.at[c])


def at_span(g, place, act):
    if isinstance(g, int):
        if g % SPAN == place:
            act(g // SPAN)
    else:
        pl.when(lax.rem(g, SPAN) == place)(lambda: act(lax.div(g, SPAN)))


def dot(a, b, contract=((1,), (0,))):
    return lax.dot_general(a, b, (contract, ((), ())), preferred_element_type=F32)


def halves(x):
    high = x.astype(BF16)
    return high, (x - high.astype(F32)).astype(BF16)


def spare_lane(levels, tracers):
    return levels + tracers + 8


def pack_kernel(
    counts, owners, columns, kernels, misfits, out, payload, target, staged, done
):
    steps, levels, held = kernels.shape
    tracers = misfits.shape[1]
    shape = (LANES, LANES)
    half = CAP // 2
    device = lax.broadcasted_iota(jnp.int32, shape, 0)
    table = counting_table()
    for step in range(steps):
        owner = owners[step]
        live = lax.broadcasted_iota(jnp.int32, owner.shape, 1) < counts[step, 0]
        owner = jnp.where(live, owner, -1)
        seen = jnp.zeros(shape, F32)
        for start in range(0, held, LANES):
            here = owner[:, start : start + LANES]
            hot = device == here
            counted = dot(jnp.where(hot, 1.0, 0.0).astype(BF16), table)
            rank = jnp.sum(
                jnp.where(hot, counted[:, :LANES] + seen, 0.0), axis=0, keepdims=True
            )
            seen = seen + counted[:, LANES:]
            target[step : step + 1, start : start + LANES] = jnp.where(
                here >= 0, here * CAP + rank.astype(jnp.int32), -1
            )
    spare = spare_lane(levels, tracers)
    main = LANES - spare

    def fill(k, part, pieces):
        rows = jnp.concatenate(
            [jnp.zeros((x, held), F32) if isinstance(x, int) else x for x in pieces], axis=0
        )
        high, low = halves(rows)
        payload[k, :LANES, part * held : (part + 1) * held] = high
        payload[k, LANES:, part * held : (part + 1) * held] = low

    def column(step):
        x = columns[step : step + 1, :].astype(F32) + 1.0
        return jnp.where(lax.broadcasted_iota(jnp.int32, (8, held), 0) == 0, x, 0.0)

    rest = [kernels[0, main:, :], misfits[0], column(0)]
    used = levels - main + tracers + 8
    fill(0, 0, [kernels[1], misfits[1], column(1), main])
    fill(0, 1, [spare, kernels[0, :main, :]])
    fill(1, 0, [*rest, LANES - used])
    fill(1, 1, [LANES // 2, *rest, LANES // 2 - used])
    slot = target[0:1, :] & (CAP - 1)
    owner = target[0:1, :] >> (CAP.bit_length() - 1)
    lower = jnp.where((target[0:1, :] >= 0) & (slot < half), owner * half + slot, -1)
    upper = jnp.where((target[0:1, :] >= 0) & (slot >= half), owner * half + slot - half, -1)
    owned = 256 // CAP
    tiles = out.shape[0] // owned

    def copy(i):
        at = pl.ds(i * owned, owned)
        return pltpu.make_async_copy(staged.at[at], out.at[at], done.at[i])

    def place(i, carry):
        for k, ats, size, rows in (
            (0, (target[1:2, :], target[0:1, :]), owned * CAP, slice(0, CAP)),
            (1, (lower, upper), owned * half, slice(CAP, CAP + half)),
        ):
            hot = jnp.concatenate([one_hot(at - i * size, size) for at in ats], axis=1)
            both = dot(hot, payload[k], ((1,), (1,)))
            both = both[:, :LANES] + both[:, LANES:]
            staged[pl.ds(i * owned, owned), rows, :] = both.reshape(owned, -1, LANES)
        copy(i).start()
        return carry

    lax.fori_loop(0, tiles, place, 0)
    for i in range(tiles):
        copy(i).wait()


def one_hot(at, size):
    at = jnp.where((at >= 0) & (at < size), at, -1).astype(F32).astype(BF16)
    shape = (size, at.shape[1])
    row = lax.broadcasted_iota(jnp.int32, shape, 0).astype(F32).astype(BF16)
    return jnp.where(row == at, jnp.ones(shape, BF16), jnp.zeros(shape, BF16))


def counting_table():
    shape = (LANES, LANES)
    earlier = lax.broadcasted_iota(jnp.int32, shape, 0) < lax.broadcasted_iota(
        jnp.int32, shape, 1
    )
    return jnp.concatenate(
        [jnp.where(earlier, 1.0, 0.0), jnp.ones(shape, F32)], axis=1
    ).astype(BF16)


def packed(counts, owners, columns, kernels, misfits):
    steps, slots = columns.shape
    devices = lax.axis_size("lon") * lax.axis_size("lat")
    return pl.pallas_call(
        pack_kernel,
        out_shape=pltpu.HBM((devices, CAP + CAP // 2, LANES), F32),
        in_specs=[smem()] + [vmem()] * 4,
        out_specs=hbm(),
        scratch_shapes=[
            pltpu.VMEM((2, 2 * LANES, 2 * slots), BF16),
            pltpu.VMEM((steps, slots), jnp.int32),
            pltpu.VMEM((devices, CAP + CAP // 2, LANES), F32),
            pltpu.SemaphoreType.DMA((devices * CAP // 256,)),
        ],
        compiler_params=params(12),
        name="pack",
    )(counts, held(owners), held(columns), held(kernels), held(misfits))


def streamed_forcing_kernel(step, received, result, out, *scratch):
    done = scratch[-1]

    def copy(r):
        return pltpu.make_async_copy(out.at[:, r], result.at[:, r], done.at[r])

    forcing_kernel(step, received, out, *scratch[:-1], finished=lambda r: copy(r).start())
    for r in range(out.shape[1]):
        copy(r).wait()


def forcing_kernel(
    step, received, out, fields, hots, place, ordered, finished=lambda r: None
):
    levels, rows, tracers, cells = out.shape
    sources = received.shape[0]
    slots = sources * CAP
    blocks = slots // LANES
    spare = spare_lane(levels, tracers)
    data = received[:, :CAP, :].reshape(slots, LANES)
    if step == 1:
        at_column = levels + tracers

        def profile(turned):
            return turned[:levels]

    else:
        at_column = levels - (LANES - spare) + tracers
        extra = received[:, CAP:, :]
        other = pltpu.roll(extra.reshape(slots // 2, LANES), LANES // 2, 1)
        extra = jnp.concatenate([extra, other.reshape(extra.shape)], axis=1)
        lane = lax.broadcasted_iota(jnp.int32, (slots, LANES), 1)
        data = jnp.where(lane < LANES // 2, extra.reshape(slots, LANES), data)

        def profile(turned):
            return jnp.concatenate([turned[spare:], turned[: at_column - tracers]], axis=0)

    high, low = halves(data)
    fields[:, :LANES] = high
    fields[:, LANES:] = low
    shape = (8, 2 * LANES)
    pick = (lax.broadcasted_iota(jnp.int32, shape, 1) & (LANES - 1)) == at_column
    column = dot(jnp.where(pick, 1.0, 0.0).astype(BF16), fields[...], ((1,), (1,)))
    cell_row = (column.astype(jnp.int32) - 1) >> (cells.bit_length() - 1)
    sub = lax.broadcasted_iota(jnp.int32, (rows, LANES), 0)
    for b in range(blocks):
        row = cell_row[:, b * LANES : (b + 1) * LANES]
        hots[b * rows : (b + 1) * rows, :] = jnp.where(sub == row, 1.0, 0.0)
    counted = dot(hots[...].astype(BF16), counting_table())
    run = jnp.zeros((rows, LANES), F32)
    runs = []
    for b in range(blocks):
        runs.append(run)
        run = run + counted[b * rows : (b + 1) * rows, LANES:]
    filled = jnp.floor((run + (LANES - 1.0)) * (1.0 / LANES))
    start = jnp.zeros((rows, LANES), F32)
    for j in range(1, rows):
        start = start + jnp.where(sub >= j, pltpu.roll(filled, j, 0), 0.0)
    for b in range(blocks):
        hot = hots[b * rows : (b + 1) * rows, :]
        at = counted[b * rows : (b + 1) * rows, :LANES] + runs[b] + start * float(LANES)
        at = jnp.sum(hot * at, axis=0, keepdims=True)
        live = jnp.sum(hot, axis=0, keepdims=True) > 0.0
        place[:, b * LANES : (b + 1) * LANES] = jnp.where(live, at, -1.0)
    counts = [jnp.max(filled[r : r + 1, :]).astype(jnp.int32) for r in range(rows)]
    used = sum(counts)
    wide = 2 * LANES

    def sort(i, carry):
        hot = one_hot(place[...] - (i * wide).astype(F32), wide)
        both = dot(hot, fields[...])
        ordered[pl.ds(pl.multiple_of(i * wide, wide), wide), :] = both[:, :LANES] + both[:, LANES:]
        return carry

    lax.fori_loop(0, (used + 1) // 2, sort, 0)
    out[...] = jnp.zeros_like(out)
    name = lax.broadcasted_iota(jnp.int32, (LANES, cells), 1).astype(F32)
    first = jnp.int32(0)
    for r in range(rows):

        def add(p, carry):
            block = ordered[pl.ds(pl.multiple_of(p * LANES, LANES), LANES), :]
            own = jnp.broadcast_to(
                block[:, at_column : at_column + 1] - (r * cells + 1.0), (LANES, cells)
            )
            hot = jnp.where(name == own, 1.0, 0.0).astype(BF16)
            turned = block.T
            product = profile(turned)[:, None, :] * turned[at_column - tracers : at_column][None]
            product = product.reshape(levels * tracers, LANES)
            total = dot(
                jnp.concatenate(halves(product), axis=1), jnp.concatenate([hot, hot], axis=0)
            )
            out[:, r, :, :] += total.reshape(levels, tracers, cells)
            return carry

        lax.fori_loop(first, first + counts[r], add, 0)
        first = first + counts[r]
        finished(r)


def forcing(step, received, shape, streamed):
    slots = received.shape[0] * CAP
    scratch = [
        pltpu.VMEM((slots, 2 * LANES), BF16),
        pltpu.VMEM((slots // LANES * shape[1], LANES), F32),
        pltpu.VMEM((1, slots), F32),
        pltpu.VMEM((slots + shape[1] * LANES, LANES), F32),
    ]
    if streamed:
        scratch = [resident(*shape), *scratch, pltpu.SemaphoreType.DMA((shape[1],))]
    return pl.pallas_call(
        functools.partial(streamed_forcing_kernel if streamed else forcing_kernel, step),
        out_shape=pltpu.HBM(shape, F32) if streamed else resident(*shape),
        in_specs=[vmem()],
        out_specs=hbm() if streamed else vmem(),
        scratch_shapes=scratch,
        compiler_params=params(16 if streamed else 12),
        name="forcing",
    )(held(received))


def shift_matrix(inner, cells):
    shape = (2 * cells, cells)
    source = lax.broadcasted_iota(jnp.int32, shape, 0)
    target = lax.broadcasted_iota(jnp.int32, shape, 1) + inner
    picks = [jnp.where(source == target + k, 1.0, 0.0).astype(BF16) for k in range(2)]
    return jnp.concatenate(picks, axis=1)


def shifted(low, high, matrix):
    row = jnp.concatenate([low, high], axis=1)
    first, rest = row.astype(BF16), None
    rest = row - first.astype(F32)
    second, third = halves(rest)
    return dot(first, matrix) + dot(second, matrix) + dot(third, matrix)


def spread(x, row, tracers):
    return jnp.broadcast_to(x[row : row + 1, :], (tracers, x.shape[1]))


def eliminate(level, above, carry, rights, ratios):
    below, ratio, values = carry
    if above is None:
        above = jnp.zeros_like(below)
    inverse = 1.0 / (1.0 + below + above + below * ratio)
    lower = below * inverse
    ratio = -above * inverse
    ratios[level] = ratio
    tracers = rights[0].shape[0]
    fresh = [
        spread(inverse, r, tracers) * rights[r] + spread(lower, r, tracers) * values[r]
        for r in range(len(rights))
    ]
    return (above, ratio, fresh)


def substitute(step, ratios, couplings, column, fields, results, done):
    diffused, first, last, polar = fields
    levels, rows, tracers, cells = diffused.shape
    lat = lax.axis_index("lat")
    at_start = lat == 0

    def picked(x):
        return jnp.where(at_start, x[step, 0:1, :], x[step, rows - 1 : rows, :])

    north, south, east = [picked(x) for x in couplings]
    own = jnp.broadcast_to(1.0 - north - south, (tracers, cells))
    side = jnp.broadcast_to(jnp.where(at_start, north, south), (tracers, cells))
    groups = levels // GROUP
    by_tracer = len(polar.shape) == 4
    if by_tracer:
        polar[:, groups, 0, :] = jnp.broadcast_to(east, (tracers, cells))
    else:
        polar[levels] = jnp.broadcast_to(east, (tracers, cells))

    chunks = groups // SPAN

    def polar_copy(at, c):
        if by_tracer:
            source, target = [x.at[:, at] for x in (polar, results[3])]
        else:
            source, target = [x.at[at] for x in (polar, results[3])]
        return pltpu.make_async_copy(source, target, done.at[3, c])

    def copies(c):
        size = SPAN if by_tracer else SPAN * GROUP
        moves = [chunk(fields[k], results[k], done.at[k], c) for k in range(3)]
        return [*moves, polar_copy(pl.ds(c * size, size), c)]

    def send(c):
        for copy in copies(c):
            copy.start()

    weight = polar_copy(pl.ds(groups if by_tracer else levels, 1), chunks)
    weight.start()
    lane = lax.broadcasted_iota(jnp.int32, (tracers, LANES), 1)

    def group(i, solved):
        at = groups - 1 - i
        west = jnp.zeros((tracers, LANES), F32)
        for j in range(GROUP - 1, -1, -1):
            level = at * GROUP + j
            ratio = ratios[level]
            fresh = []
            for r in range(rows):
                value = diffused[level, r] - spread(ratio, r, tracers) * solved[r]
                diffused[level, r] = value
                fresh.append(value)
                lanes = j * rows + r
                moved = pltpu.roll(value[:, :LANES], lanes, 1) if lanes else value[:, :LANES]
                west = jnp.where(lane == lanes, moved, west)
            solved = fresh
            first[level] = solved[0]
            last[level] = solved[rows - 1]
            row = own * jnp.where(at_start, solved[0], solved[rows - 1]) + side * jnp.where(
                at_start, solved[1], solved[rows - 2]
            )
            if by_tracer:
                polar[:, at, j, :] = row
            else:
                polar[level] = row
        column[at] = west
        at_span(at, 0, send)
        return solved

    lax.fori_loop(0, groups, group, [jnp.zeros((tracers, cells), F32)] * rows)
    weight.wait()
    for c in range(chunks):
        for copy in copies(c):
            copy.wait()


def forward_sweep(levels, rows, tracers, cells, diffusion, right_of):
    zero = jnp.zeros((rows, cells), F32)
    carry = (zero, zero, [jnp.zeros((tracers, cells), F32)] * rows)
    groups = levels // GROUP

    def one(g, j, above, carry):
        rights, ratios, store = right_of(g, j, above is None)
        carry = eliminate(g * GROUP + j, above, carry, rights, ratios)
        store(carry[2])
        return carry

    def group(g, carry):
        for j in range(GROUP):
            carry = one(g, j, diffusion(g * GROUP + j), carry)
        return carry

    carry = lax.fori_loop(0, groups - 1, group, carry)
    for j in range(GROUP):
        level = levels - GROUP + j
        carry = one(groups - 1, j, diffusion(level) if level < levels - 1 else None, carry)


def first_kernel(
    step,
    costate,
    diffusion_in,
    north_in,
    south_in,
    east_in,
    result,
    first_out,
    last_out,
    polar_out,
    column,
    staged,
    ratios,
    diffused,
    first,
    last,
    polar,
    diffusion,
    couplings,
    arrived,
    sent,
    ready,
):
    levels, tracers, rows, cells = costate.shape
    small = [pltpu.make_async_copy(diffusion_in.at[step], diffusion, ready.at[0])]
    for k, coupling in enumerate((north_in, south_in, east_in)):
        small.append(pltpu.make_async_copy(coupling, couplings.at[k], ready.at[1 + k]))
    chunk(costate, staged, arrived, 0).start()
    for copy in small:
        copy.start()
    for c in range(1, levels // (GROUP * SPAN)):
        chunk(costate, staged, arrived, c).start()
    for copy in small:
        copy.wait()

    def right_of(g, j, final):
        if j == 0:
            at_span(g, 0, lambda c: chunk(costate, staged, arrived, c).wait())
        level = g * GROUP + j
        rights = [staged[level, :, r, :] for r in range(rows)]

        def store(values):
            for r in range(rows):
                diffused[level, r] = values[r]

        return rights, ratios, store

    forward_sweep(levels, rows, tracers, cells, lambda level: diffusion[level], right_of)
    views = [couplings.at[k] for k in range(3)]
    fields = (diffused, first, last, polar)
    results = (result, first_out, last_out, polar_out)
    substitute(step, ratios, views, column, fields, results, sent)


def meridional(level, row, diffused, after, before, coefs):
    rows = diffused.shape[1]
    own, north, south = coefs
    up = diffused[level, row + 1] if row < rows - 1 else after[level]
    down = diffused[level, row - 1] if row > 0 else before[level]
    return own * diffused[level, row] + north * up + south * down


def borders_kernel(
    step,
    shift,
    column,
    north,
    south,
    after_in,
    before_in,
    polar_in,
    nearby_in,
    edge,
    turned_out,
    after,
    before,
    polar,
    nearby,
    turned,
    ready,
):
    rows, cells = north.shape[1:]
    fetches = [
        pltpu.make_async_copy(source, target, ready.at[2 + k])
        for k, (source, target) in enumerate(((polar_in, polar), (nearby_in, nearby)))
    ]
    sending = pltpu.make_async_copy(turned, turned_out, ready.at[4])
    lat = lax.axis_index("lat")
    last_lat = lax.axis_size("lat") - 1
    at_pole = (lat == 0) | (lat == last_lat)

    @pl.when(at_pole)
    def _():
        for fetch in fetches:
            fetch.start()

    finish = west_column(step, column, north, south, after_in, before_in, edge, after, before, ready)

    @pl.when(at_pole)
    def _():
        for fetch in fetches:
            fetch.wait()
        levels = turned.shape[0]
        circle = cells * lax.axis_size("lon")
        amount = jnp.where(lat == 0, shift[step, 0], shift[step, rows * last_lat + rows - 1])
        matrix = shift_matrix(lax.rem(amount + 2 * circle, circle) & (cells - 1), cells)
        tracers = turned.shape[1]
        weight = shifted(polar[levels], nearby[levels], matrix)[:1, :cells]
        size = 3 * GROUP
        for i in range(levels // size):
            at = slice(i * size, (i + 1) * size)
            low, high = [x[at].reshape(size * tracers, cells) for x in (polar, nearby)]
            row = shifted(low, high, matrix)
            row = row[:, :cells] + weight * (row[:, cells:] - row[:, :cells])
            turned[at] = row.reshape(size, tracers, cells)
        sending.start()

    finish()

    @pl.when(at_pole)
    def _():
        sending.wait()


def edge_kernel(
    step, column, north, south, after_in, before_in, edge, after, before, ready
):
    west_column(step, column, north, south, after_in, before_in, edge, after, before, ready)()


def west_column(step, column, north, south, after_in, before_in, edge, after, before, ready):
    groups, tracers, lanes = column.shape
    rows, cells = north.shape[1:]
    tiles = [
        pltpu.make_async_copy(source.at[:, :, pl.ds(0, lanes)], target, ready.at[k])
        for k, (source, target) in enumerate(((after_in, after), (before_in, before)))
    ]
    for tile in tiles:
        tile.start()
    lane = lax.broadcasted_iota(jnp.int32, (tracers, lanes), 1)

    def along_lanes(x):
        shape = (rows, lanes)
        own_lane = (lax.broadcasted_iota(jnp.int32, shape, 1) & (rows - 1)) == (
            lax.broadcasted_iota(jnp.int32, shape, 0)
        )
        picked = jnp.where(own_lane, jnp.broadcast_to(x[step, :, :1], shape), 0.0)
        return jnp.broadcast_to(jnp.sum(picked, axis=0, keepdims=True), (tracers, lanes))

    n, s = along_lanes(north), along_lanes(south)
    own = 1.0 - n - s

    def group(i, carry):
        here = column[i]
        up = pltpu.roll(here, lanes - 1, 1)
        down = pltpu.roll(here, 1, 1)
        for j in range(GROUP):
            level = i * GROUP + j
            bottom, top = j * rows, j * rows + rows - 1
            up = jnp.where(lane == top, pltpu.roll(after[level], top, 1), up)
            moved = before[level]
            moved = pltpu.roll(moved, bottom, 1) if bottom else moved
            down = jnp.where(lane == bottom, moved, down)
        edge[i] = own * here + n * up + s * down
        return carry

    def finish():
        for tile in tiles:
            tile.wait()
        lax.fori_loop(0, groups, group, 0)

    return finish


def rotate_kernel(step, shift, circle_in, out, circle, turned, ready):
    parts, groups, group, cells = turned.shape
    lat = lax.axis_index("lat")
    last_lat = lax.axis_size("lat") - 1
    rows = shift.shape[1] // lax.axis_size("lat")

    @pl.when((lat == 0) | (lat == last_lat))
    def _():
        fetch = pltpu.make_async_copy(circle_in, circle, ready.at[0])
        fetch.start()
        amount = jnp.where(lat == 0, shift[step, 0], shift[step, rows * last_lat + rows - 1])
        amount = lax.rem(amount + 2 * parts * cells, parts * cells)
        hops = amount // cells
        matrix = shift_matrix(amount - hops * cells, cells)
        fetch.wait()
        for part in range(parts):
            near = lax.rem(part + hops, parts)
            far = lax.rem(part + hops + 1, parts)
            low, high = [
                circle[x].reshape((groups + 1) * group, cells) for x in (near, far)
            ]
            row = shifted(low, high, matrix)
            size = groups * group
            weight = row[size : size + 1, :cells]
            row = row[:size]
            row = row[:, :cells] + weight * (row[:, cells:] - row[:, :cells])
            turned[part] = row.reshape(groups, group, cells)
        send = pltpu.make_async_copy(turned, out, ready.at[1])
        send.start()
        send.wait()


def prepare_stencil(step, north, south, east, coefs):
    rows, cells = north.shape[1:]
    tracers = coefs.shape[2]
    for r in range(rows):
        n = north[step, r : r + 1, :]
        s = south[step, r : r + 1, :]
        coefs[0, r] = jnp.broadcast_to(1.0 - n - s, (tracers, cells))
        coefs[1, r] = jnp.broadcast_to(n, (tracers, cells))
        coefs[2, r] = jnp.broadcast_to(s, (tracers, cells))
        coefs[3, r] = jnp.broadcast_to(east[step, r : r + 1, :], (tracers, cells))


def transported(group, lane_at, diffused, after, before, edge_row, coefs, pole):
    level = group * GROUP + lane_at
    rows, tracers, cells = diffused.shape[1:]
    lat = lax.axis_index("lat")
    last = lax.broadcasted_iota(jnp.int32, (tracers, cells), 1) == cells - 1
    result = []
    for r in range(rows):
        mer = meridional(level, r, diffused, after, before, [coefs[k, r] for k in range(3)])
        arrived = pltpu.roll(edge_row, LANES - 1 - (lane_at * rows + r), 1)
        arrived = jnp.concatenate([arrived] * (cells // LANES), axis=1)
        following = jnp.where(last, arrived, pltpu.roll(mer, cells - 1, 1))
        result.append(mer + coefs[3, r] * (following - mer))
    polar = pole[:, group, lane_at, :] if len(pole.shape) == 4 else pole[level]
    result[0] = jnp.where(lat == 0, polar, result[0])
    result[rows - 1] = jnp.where(lat == lax.axis_size("lat") - 1, polar, result[rows - 1])
    return result


def streams(sources, targets, poles, pole, done):
    lat = lax.axis_index("lat")
    last_lat = lax.axis_size("lat") - 1
    last = len(sources)

    def polar_copy(source, c):
        if len(pole.shape) == 4:
            at = pl.ds(c * SPAN, SPAN)
            return pltpu.make_async_copy(source.at[:, at], pole.at[:, at], done.at[last, c])
        return chunk(source, pole, done.at[last], c)

    for g in range(targets[0].shape[0] // (GROUP * SPAN)):
        for k, (source, target) in enumerate(zip(sources, targets)):
            chunk(source, target, done.at[k], g).start()

        @pl.when(lat == 0)
        def _():
            polar_copy(poles[0], g).start()

        @pl.when(lat == last_lat)
        def _():
            polar_copy(poles[-1], g).start()

    def wait(g):
        for k, (source, target) in enumerate(zip(sources, targets)):
            chunk(source, target, done.at[k], g).wait()

        @pl.when((lat == 0) | (lat == last_lat))
        def _():
            polar_copy(poles[0], g).wait()

    return wait


def middle_kernel(
    step,
    before_step,
    forced,
    after_in,
    before_in,
    south_pole,
    north_pole,
    edge,
    diffusion,
    north,
    south,
    east,
    result,
    first_out,
    last_out,
    polar_out,
    column,
    surface,
    coefs,
    ratios,
    diffused,
    after,
    before,
    pole,
    solved,
    first,
    last,
    polar,
    arrived,
    sent,
):
    levels, rows, tracers, cells = diffused.shape
    wait = streams(
        (before_step, after_in, before_in),
        (diffused, after, before),
        (south_pole, north_pole),
        pole,
        arrived,
    )
    prepare_stencil(step, north, south, east, coefs)

    def right_of(g, j, final):
        if j == 0:
            at_span(g, 0, wait)
        level = g * GROUP + j
        rights = transported(g, j, diffused, after, before, edge[g], coefs, pole)
        rights = [rights[r] + forced[level, r] for r in range(rows)]
        if final:
            for r in range(rows):
                surface[r] = rights[r]

        def store(values):
            for r in range(rows):
                solved[level, r] = values[r]

        return rights, ratios, store

    forward_sweep(
        levels, rows, tracers, cells, lambda level: diffusion[step - 1, level], right_of
    )
    couplings = (north, south, east)
    fields = (solved, first, last, polar)
    results = (result, first_out, last_out, polar_out)
    substitute(step - 1, ratios, couplings, column, fields, results, sent)


def last_kernel(
    step,
    before_step,
    forcing_in,
    after_in,
    before_in,
    pole_in,
    edge,
    north,
    south,
    east,
    surface,
    state,
    gradient,
    coefs,
    diffused,
    forced,
    after,
    before,
    pole,
    staged,
    arrived,
    sent,
):
    levels, rows, tracers, cells = diffused.shape
    wait = streams(
        (before_step, forcing_in, after_in, before_in),
        (diffused, forced, after, before),
        (pole_in,),
        pole,
        arrived,
    )
    prepare_stencil(step, north, south, east, coefs)

    def group(g, carry):
        at_span(g, 0, wait)
        edge_row = edge[g]
        for j in range(GROUP):
            level = g * GROUP + j
            values = transported(g, j, diffused, after, before, edge_row, coefs, pole)
            for r in range(rows):
                staged[level, :, r, :] = values[r] + forced[level, r]
        at_span(g, SPAN - 1, lambda c: chunk(staged, state, sent, c).start())
        return carry

    lax.fori_loop(0, levels // GROUP, group, 0)
    for r in range(rows):
        gradient[:, r, :] = surface[r] + staged[levels - 1, :, r, :]
    for c in range(levels // (GROUP * SPAN)):
        chunk(staged, state, sent, c).wait()


def boundary_rows(first, last):
    up = [(i, i + 1) for i in range(lax.axis_size("lat") - 1)]
    down = [(j, i) for i, j in up]
    return lax.ppermute(first, "lat", down), lax.ppermute(last, "lat", up)


def circles(lats, hops):
    lat_count = lax.axis_size("lat")
    lon_count = lax.axis_size("lon")
    return [
        (((j + hops) % lon_count) * lat_count + lat, j * lat_count + lat)
        for lat in lats
        for j in range(lon_count)
    ]


def westward(edge):
    count = lax.axis_size("lon")
    return held(lax.ppermute(edge, "lon", [(i, (i - 1) % count) for i in range(count)]))


def first_exchange(step, after, before, nearby, polar, column, north, south, shift, hops):
    poles = (0, lax.axis_size("lat") - 1)
    levels, tracers, cells = after.shape
    edge, turned = pl.pallas_call(
        functools.partial(borders_kernel, step),
        out_shape=[resident(*column.shape), pltpu.HBM((levels, tracers, cells), F32)],
        in_specs=[smem()] + [vmem()] * 3 + [anywhere()] * 4,
        out_specs=[vmem(), hbm()],
        scratch_shapes=[
            pltpu.VMEM((levels, tracers, LANES), F32),
            pltpu.VMEM((levels, tracers, LANES), F32),
            pltpu.VMEM(polar.shape, F32),
            pltpu.VMEM(polar.shape, F32),
            pltpu.VMEM((levels, tracers, cells), F32),
            pltpu.SemaphoreType.DMA((5,)),
        ],
        compiler_params=params(8),
        name="borders",
    )(shift, column, north, south, after, before, pinned(polar), nearby)
    edge = westward(edge)
    moved = []
    for lat, hop in zip(poles, hops):
        moved.append(
            lax.switch(
                hop,
                [
                    functools.partial(
                        lambda k, lat, x: lax.ppermute(x, AXES, circles((lat,), k)), k, lat
                    )
                    for k in range(lax.axis_size("lon"))
                ],
                turned,
            )
        )
    return after, before, pinned(moved[0]), pinned(moved[1]), edge


def last_exchange(step, after, before, circle, column, north, south, shift):
    levels, tracers, cells = after.shape
    parts, groups, group = circle.shape[:3]
    shape = (parts, groups - 1, group, cells)
    turned = pl.pallas_call(
        functools.partial(rotate_kernel, step),
        out_shape=pltpu.HBM(shape, F32),
        in_specs=[smem(), anywhere()],
        out_specs=hbm(),
        scratch_shapes=[
            pltpu.VMEM(circle.shape, F32),
            pltpu.VMEM(shape, F32),
            pltpu.SemaphoreType.DMA((2,)),
        ],
        compiler_params=params(8),
        name="rotate",
    )(shift, circle)
    pole = lax.all_to_all(turned, "lon", 0, 0, tiled=True)
    edge = pl.pallas_call(
        functools.partial(edge_kernel, step),
        out_shape=resident(*column.shape),
        in_specs=[vmem()] * 3 + [anywhere()] * 2,
        out_specs=vmem(),
        scratch_shapes=[
            pltpu.VMEM((levels, tracers, LANES), F32),
            pltpu.VMEM((levels, tracers, LANES), F32),
            pltpu.SemaphoreType.DMA((2,)),
        ],
        compiler_params=params(4),
        name="edge",
    )(column, north, south, after, before)
    return after, before, pole, westward(edge)


def per_device(
    costate,
    diffusion,
    east_courant,
    north_courant,
    south_courant,
    polar_shift,
    owners,
    columns,
    sounding_counts,
    kernels,
    misfits,
):
    levels, tracers, rows, cells = costate.shape
    owner_rows = owners.reshape(owners.shape[0], 1, owners.shape[1])
    couplings = (north_courant, south_courant, east_courant)
    groups = levels // GROUP

    solved_shapes = [
        pltpu.HBM((levels, rows, tracers, cells), F32),
        pltpu.HBM((levels, tracers, cells), F32),
        pltpu.HBM((levels, tracers, cells), F32),
        pltpu.HBM((levels + 1, tracers, cells), F32),
        resident(groups, tracers, LANES),
    ]
    ratios = pltpu.VMEM((levels, rows, cells), F32)
    coefs = pltpu.VMEM((4, rows, tracers, cells), F32)
    field = pltpu.VMEM((levels, rows, tracers, cells), F32)
    line = pltpu.VMEM((levels, tracers, cells), F32)
    solved_scratch = [field, line, line, pltpu.VMEM((levels + 1, tracers, cells), F32)]
    solved_specs = [hbm()] * 4 + [vmem()]
    leaving = pltpu.SemaphoreType.DMA((4, groups // SPAN + 1))
    output = pltpu.VMEM(costate.shape, F32)
    semaphores = pltpu.SemaphoreType.DMA((groups // SPAN,))
    diffused, first, last, polar, column = pl.pallas_call(
        functools.partial(first_kernel, 1),
        out_shape=solved_shapes,
        in_specs=[hbm()] * 5,
        out_specs=solved_specs,
        scratch_shapes=[
            output,
            ratios,
            *solved_scratch,
            pltpu.VMEM(diffusion.shape[1:], F32),
            pltpu.VMEM((3,) + east_courant.shape, F32),
            semaphores,
            leaving,
            pltpu.SemaphoreType.DMA((4,)),
        ],
        compiler_params=params(16),
        name="first",
    )(*[pinned(x) for x in (costate, diffusion, *couplings)])
    couplings = [held(x) for x in couplings]
    diffusion = held(diffusion)
    counts, column = lax.optimization_barrier((sounding_counts, column))
    lat_count, lon_count = lax.axis_size("lat"), lax.axis_size("lon")
    ends = jnp.stack([polar_shift[1, 0], polar_shift[1, -1]])
    hops = (ends & (cells * lon_count - 1)) >> (cells.bit_length() - 1)
    nearby = lax.ppermute(polar, AXES, circles((0, lat_count - 1), 1))
    around = (*boundary_rows(first, last), nearby)
    sent = packed(counts, owner_rows, columns, kernels, misfits)
    sent, *around = lax.optimization_barrier((sent, *around))
    around = [pinned(x) for x in around]
    got = lax.all_to_all(sent, AXES, 0, 0, tiled=True)
    shape = (levels, rows, tracers, cells)
    forced = forcing(1, got, shape, False)
    around = first_exchange(1, *around, polar, column, *couplings[:2], polar_shift, hops)
    scratch = [field, line, line]
    transfers = pltpu.SemaphoreType.DMA((4, groups // SPAN))
    solved, first, last, polar, column, surface = pl.pallas_call(
        functools.partial(middle_kernel, 1),
        out_shape=[
            *solved_shapes[:3],
            pltpu.HBM((tracers, groups + 1, GROUP, cells), F32),
            solved_shapes[4],
            resident(rows, tracers, cells),
        ],
        in_specs=[hbm(), vmem()] + [anywhere()] * 2 + [hbm()] * 2 + [vmem()] * 5,
        out_specs=solved_specs + [vmem()],
        scratch_shapes=[
            coefs,
            ratios,
            *scratch,
            line,
            *solved_scratch[:3],
            pltpu.VMEM((tracers, groups + 1, GROUP, cells), F32),
            transfers,
            leaving,
        ],
        compiler_params=params(20),
        name="middle",
    )(pinned(diffused), forced, *around, diffusion, *couplings)
    around = (*boundary_rows(first, last), lax.all_to_all(polar, "lon", 0, 0, tiled=True))
    got, column = lax.optimization_barrier((got, column))
    forced = forcing(0, got, shape, True)
    forced, *around = lax.optimization_barrier((forced, *around))
    around = last_exchange(0, *around, column, *couplings[:2], polar_shift)
    return tuple(
        pl.pallas_call(
            functools.partial(last_kernel, 0),
            out_shape=[
                pltpu.HBM(costate.shape, F32),
                jax.ShapeDtypeStruct((tracers, rows, cells), F32),
            ],
            in_specs=[hbm()] * 2 + [anywhere()] * 3 + [vmem()] * 5,
            out_specs=[hbm(), vmem()],
            scratch_shapes=[
                coefs,
                field,
                *scratch,
                pltpu.VMEM((tracers, groups, GROUP, cells), F32),
                output,
                pltpu.SemaphoreType.DMA((5, groups // SPAN)),
                semaphores,
            ],
            compiler_params=params(22),
            name="last",
        )(pinned(solved), pinned(forced), *around, *couplings, surface)
    )


def solution(mesh):
    return jax.shard_map(
        per_device,
        mesh=mesh,
        in_specs=(
            P(None, None, "lat", "lon"),
            P(None, None, "lat", "lon"),
            P(None, "lat", "lon"),
            P(None, "lat", "lon"),
            P(None, "lat", "lon"),
            P(),
            P(None, ("lon", "lat"), None),
            P(None, ("lon", "lat")),
            P(None, ("lon", "lat")),
            P(None, None, ("lon", "lat")),
            P(None, None, ("lon", "lat")),
        ),
        out_specs=(P(None, None, "lat", "lon"), P(None, "lat", "lon")),
        check_vma=False,
    )
```

```python
import functools

import jax
import jax.numpy as jnp
from jax import lax
from jax.experimental import pallas as pl
from jax.experimental.pallas import tpu as pltpu
from jax.sharding import PartitionSpec as P

AXES = ("lon", "lat")
LANES = 128
CAP = 16
GROUP = 8
SPAN = 3
F32 = jnp.float32
BF16 = jnp.bfloat16
MIB = 1024 * 1024


def vmem():
    return pl.BlockSpec(memory_space=pltpu.VMEM)


def smem():
    return pl.BlockSpec(memory_space=pltpu.SMEM)


def hbm():
    return pl.BlockSpec(memory_space=pltpu.HBM)


def params(limit):
    return pltpu.CompilerParams(vmem_limit_bytes=limit * MIB)


def held(x):
    return pltpu.with_memory_space_constraint(x, pltpu.VMEM)


def anywhere():
    return pl.BlockSpec(memory_space=pl.ANY)


def pinned(x):
    return pltpu.with_memory_space_constraint(x, pltpu.HBM)


def resident(*shape):
    return pltpu.VMEM(shape, F32)


def chunk(source, target, done, c):
    at = pl.ds(c * GROUP * SPAN, GROUP * SPAN)
    return pltpu.make_async_copy(source.at[at], target.at[at], done.at[c])


def at_span(g, place, act):
    if isinstance(g, int):
        if g % SPAN == place:
            act(g // SPAN)
    else:
        pl.when(lax.rem(g, SPAN) == place)(lambda: act(lax.div(g, SPAN)))


def dot(a, b, contract=((1,), (0,))):
    return lax.dot_general(a, b, (contract, ((), ())), preferred_element_type=F32)


def halves(x):
    high = x.astype(BF16)
    return high, (x - high.astype(F32)).astype(BF16)


def spare_lane(levels, tracers):
    return levels + tracers + 8


def pack_kernel(
    counts, owners, columns, kernels, misfits, out, payload, target, staged, done
):
    steps, levels, held = kernels.shape
    tracers = misfits.shape[1]
    shape = (LANES, LANES)
    half = CAP // 2
    device = lax.broadcasted_iota(jnp.int32, shape, 0)
    table = counting_table()
    for step in range(steps):
        owner = owners[step]
        live = lax.broadcasted_iota(jnp.int32, owner.shape, 1) < counts[step, 0]
        owner = jnp.where(live, owner, -1)
        seen = jnp.zeros(shape, F32)
        for start in range(0, held, LANES):
            here = owner[:, start : start + LANES]
            hot = device == here
            counted = dot(jnp.where(hot, 1.0, 0.0).astype(BF16), table)
            rank = jnp.sum(
                jnp.where(hot, counted[:, :LANES] + seen, 0.0), axis=0, keepdims=True
            )
            seen = seen + counted[:, LANES:]
            target[step : step + 1, start : start + LANES] = jnp.where(
                here >= 0, here * CAP + rank.astype(jnp.int32), -1
            )
    spare = spare_lane(levels, tracers)
    main = LANES - spare

    def fill(k, part, pieces):
        rows = jnp.concatenate(
            [jnp.zeros((x, held), F32) if isinstance(x, int) else x for x in pieces], axis=0
        )
        high, low = halves(rows)
        payload[k, :LANES, part * held : (part + 1) * held] = high
        payload[k, LANES:, part * held : (part + 1) * held] = low

    def column(step):
        x = columns[step : step + 1, :].astype(F32) + 1.0
        return jnp.where(lax.broadcasted_iota(jnp.int32, (8, held), 0) == 0, x, 0.0)

    rest = [kernels[0, main:, :], misfits[0], column(0)]
    used = levels - main + tracers + 8
    fill(0, 0, [kernels[1], misfits[1], column(1), main])
    fill(0, 1, [spare, kernels[0, :main, :]])
    fill(1, 0, [*rest, LANES - used])
    fill(1, 1, [LANES // 2, *rest, LANES // 2 - used])
    slot = target[0:1, :] & (CAP - 1)
    owner = target[0:1, :] >> (CAP.bit_length() - 1)
    lower = jnp.where((target[0:1, :] >= 0) & (slot < half), owner * half + slot, -1)
    upper = jnp.where((target[0:1, :] >= 0) & (slot >= half), owner * half + slot - half, -1)
    owned = 512 // CAP
    tiles = out.shape[0] // owned

    def copy(i):
        at = pl.ds(i * owned, owned)
        return pltpu.make_async_copy(staged.at[at], out.at[at], done.at[i])

    def place(i, carry):
        for k, ats, size, rows in (
            (0, (target[1:2, :], target[0:1, :]), owned * CAP, slice(0, CAP)),
            (1, (lower, upper), owned * half, slice(CAP, CAP + half)),
        ):
            hot = jnp.concatenate([tall_one_hot(at - i * size, size) for at in ats], axis=1)
            both = dot(hot, payload[k], ((1,), (1,)))
            both = both[:, :LANES] + both[:, LANES:]
            staged[pl.ds(i * owned, owned), rows, :] = both.reshape(owned, -1, LANES)
        copy(i).start()
        return carry

    lax.fori_loop(0, tiles, place, 0)
    for i in range(tiles):
        copy(i).wait()


def one_hot(at, size):
    at = jnp.where((at >= 0) & (at < size), at, -1).astype(F32).astype(BF16)
    shape = (size, at.shape[1])
    row = lax.broadcasted_iota(jnp.int32, shape, 0).astype(F32).astype(BF16)
    return jnp.where(row == at, jnp.ones(shape, BF16), jnp.zeros(shape, BF16))


def tall_one_hot(at, size):
    parts = [one_hot(at - start, 256) for start in range(0, size, 256)]
    return parts[0] if len(parts) == 1 else jnp.concatenate(parts, axis=0)


def counting_table():
    shape = (LANES, LANES)
    earlier = lax.broadcasted_iota(jnp.int32, shape, 0) < lax.broadcasted_iota(
        jnp.int32, shape, 1
    )
    return jnp.concatenate(
        [jnp.where(earlier, 1.0, 0.0), jnp.ones(shape, F32)], axis=1
    ).astype(BF16)


def packed(counts, owners, columns, kernels, misfits):
    steps, slots = columns.shape
    devices = lax.axis_size("lon") * lax.axis_size("lat")
    return pl.pallas_call(
        pack_kernel,
        out_shape=pltpu.HBM((devices, CAP + CAP // 2, LANES), F32),
        in_specs=[smem()] + [vmem()] * 4,
        out_specs=hbm(),
        scratch_shapes=[
            pltpu.VMEM((2, 2 * LANES, 2 * slots), BF16),
            pltpu.VMEM((steps, slots), jnp.int32),
            pltpu.VMEM((devices, CAP + CAP // 2, LANES), F32),
            pltpu.SemaphoreType.DMA((devices * CAP // 512,)),
        ],
        compiler_params=params(20),
        name="pack",
    )(counts, held(owners), held(columns), held(kernels), held(misfits))


def streamed_forcing_kernel(step, received, result, out, *scratch):
    done = scratch[-1]

    def copy(r):
        return pltpu.make_async_copy(out.at[:, r], result.at[:, r], done.at[r])

    forcing_kernel(step, received, out, *scratch[:-1], finished=lambda r: copy(r).start())
    for r in range(out.shape[1]):
        copy(r).wait()


def forcing_kernel(
    step, received, out, fields, hots, place, ordered, finished=lambda r: None
):
    levels, rows, tracers, cells = out.shape
    sources = received.shape[0]
    slots = sources * CAP
    blocks = slots // LANES
    spare = spare_lane(levels, tracers)
    data = received[:, :CAP, :].reshape(slots, LANES)
    if step == 1:
        at_column = levels + tracers

        def profile(turned):
            return turned[:levels]

    else:
        at_column = levels - (LANES - spare) + tracers
        extra = received[:, CAP:, :]
        other = pltpu.roll(extra.reshape(slots // 2, LANES), LANES // 2, 1)
        extra = jnp.concatenate([extra, other.reshape(extra.shape)], axis=1)
        lane = lax.broadcasted_iota(jnp.int32, (slots, LANES), 1)
        data = jnp.where(lane < LANES // 2, extra.reshape(slots, LANES), data)

        def profile(turned):
            return jnp.concatenate([turned[spare:], turned[: at_column - tracers]], axis=0)

    high, low = halves(data)
    fields[:, :LANES] = high
    fields[:, LANES:] = low
    shape = (8, 2 * LANES)
    pick = (lax.broadcasted_iota(jnp.int32, shape, 1) & (LANES - 1)) == at_column
    column = dot(jnp.where(pick, 1.0, 0.0).astype(BF16), fields[...], ((1,), (1,)))
    cell_row = (column.astype(jnp.int32) - 1) >> (cells.bit_length() - 1)
    sub = lax.broadcasted_iota(jnp.int32, (rows, LANES), 0)
    for b in range(blocks):
        row = cell_row[:, b * LANES : (b + 1) * LANES]
        hots[b * rows : (b + 1) * rows, :] = jnp.where(sub == row, 1.0, 0.0)
    counted = dot(hots[...].astype(BF16), counting_table())
    run = jnp.zeros((rows, LANES), F32)
    runs = []
    for b in range(blocks):
        runs.append(run)
        run = run + counted[b * rows : (b + 1) * rows, LANES:]
    filled = jnp.floor((run + (LANES - 1.0)) * (1.0 / LANES))
    start = jnp.zeros((rows, LANES), F32)
    for j in range(1, rows):
        start = start + jnp.where(sub >= j, pltpu.roll(filled, j, 0), 0.0)
    for b in range(blocks):
        hot = hots[b * rows : (b + 1) * rows, :]
        at = counted[b * rows : (b + 1) * rows, :LANES] + runs[b] + start * float(LANES)
        at = jnp.sum(hot * at, axis=0, keepdims=True)
        live = jnp.sum(hot, axis=0, keepdims=True) > 0.0
        place[:, b * LANES : (b + 1) * LANES] = jnp.where(live, at, -1.0)
    counts = [jnp.max(filled[r : r + 1, :]).astype(jnp.int32) for r in range(rows)]
    used = sum(counts)
    wide = 2 * LANES

    def sort(i, carry):
        hot = one_hot(place[...] - (i * wide).astype(F32), wide)
        both = dot(hot, fields[...])
        ordered[pl.ds(pl.multiple_of(i * wide, wide), wide), :] = both[:, :LANES] + both[:, LANES:]
        return carry

    lax.fori_loop(0, (used + 1) // 2, sort, 0)
    out[...] = jnp.zeros_like(out)
    name = lax.broadcasted_iota(jnp.int32, (LANES, cells), 1).astype(F32)
    first = jnp.int32(0)
    for r in range(rows):

        def add(p, carry):
            block = ordered[pl.ds(pl.multiple_of(p * LANES, LANES), LANES), :]
            own = jnp.broadcast_to(
                block[:, at_column : at_column + 1] - (r * cells + 1.0), (LANES, cells)
            )
            hot = jnp.where(name == own, 1.0, 0.0).astype(BF16)
            turned = block.T
            product = profile(turned)[:, None, :] * turned[at_column - tracers : at_column][None]
            product = product.reshape(levels * tracers, LANES)
            total = dot(
                jnp.concatenate(halves(product), axis=1), jnp.concatenate([hot, hot], axis=0)
            )
            out[:, r, :, :] += total.reshape(levels, tracers, cells)
            return carry

        lax.fori_loop(first, first + counts[r], add, 0)
        first = first + counts[r]
        finished(r)


def forcing(step, received, shape, streamed):
    slots = received.shape[0] * CAP
    scratch = [
        pltpu.VMEM((slots, 2 * LANES), BF16),
        pltpu.VMEM((slots // LANES * shape[1], LANES), F32),
        pltpu.VMEM((1, slots), F32),
        pltpu.VMEM((slots + shape[1] * LANES, LANES), F32),
    ]
    if streamed:
        scratch = [resident(*shape), *scratch, pltpu.SemaphoreType.DMA((shape[1],))]
    return pl.pallas_call(
        functools.partial(streamed_forcing_kernel if streamed else forcing_kernel, step),
        out_shape=pltpu.HBM(shape, F32) if streamed else resident(*shape),
        in_specs=[vmem()],
        out_specs=hbm() if streamed else vmem(),
        scratch_shapes=scratch,
        compiler_params=params(16 if streamed else 12),
        name="forcing",
    )(held(received))


def shift_matrix(inner, cells):
    shape = (2 * cells, cells)
    source = lax.broadcasted_iota(jnp.int32, shape, 0)
    target = lax.broadcasted_iota(jnp.int32, shape, 1) + inner
    picks = [jnp.where(source == target + k, 1.0, 0.0).astype(BF16) for k in range(2)]
    return jnp.concatenate(picks, axis=1)


def shifted(low, high, matrix):
    row = jnp.concatenate([low, high], axis=1)
    first, rest = row.astype(BF16), None
    rest = row - first.astype(F32)
    second, third = halves(rest)
    return dot(first, matrix) + dot(second, matrix) + dot(third, matrix)


def spread(x, row, tracers):
    return jnp.broadcast_to(x[row : row + 1, :], (tracers, x.shape[1]))


def eliminate(level, above, carry, rights, ratios):
    below, ratio, values = carry
    if above is None:
        above = jnp.zeros_like(below)
    inverse = 1.0 / (1.0 + below + above + below * ratio)
    lower = below * inverse
    ratio = -above * inverse
    ratios[level] = ratio
    tracers = rights[0].shape[0]
    fresh = [
        spread(inverse, r, tracers) * rights[r] + spread(lower, r, tracers) * values[r]
        for r in range(len(rights))
    ]
    return (above, ratio, fresh)


def substitute(step, ratios, couplings, column, fields, results, done):
    diffused, first, last, polar = fields
    levels, rows, tracers, cells = diffused.shape
    lat = lax.axis_index("lat")
    at_start = lat == 0

    def picked(x):
        return jnp.where(at_start, x[step, 0:1, :], x[step, rows - 1 : rows, :])

    north, south, east = [picked(x) for x in couplings]
    own = jnp.broadcast_to(1.0 - north - south, (tracers, cells))
    side = jnp.broadcast_to(jnp.where(at_start, north, south), (tracers, cells))
    groups = levels // GROUP
    by_tracer = len(polar.shape) == 4
    if by_tracer:
        polar[:, groups, 0, :] = jnp.broadcast_to(east, (tracers, cells))
    else:
        polar[levels] = jnp.broadcast_to(east, (tracers, cells))

    chunks = groups // SPAN

    def polar_copy(at, c):
        if by_tracer:
            source, target = [x.at[:, at] for x in (polar, results[3])]
        else:
            source, target = [x.at[at] for x in (polar, results[3])]
        return pltpu.make_async_copy(source, target, done.at[3, c])

    def copies(c):
        size = SPAN if by_tracer else SPAN * GROUP
        moves = [chunk(fields[k], results[k], done.at[k], c) for k in range(3)]
        return [*moves, polar_copy(pl.ds(c * size, size), c)]

    def send(c):
        for copy in copies(c):
            copy.start()

    weight = polar_copy(pl.ds(groups if by_tracer else levels, 1), chunks)
    weight.start()
    lane = lax.broadcasted_iota(jnp.int32, (tracers, LANES), 1)

    def group(i, solved):
        at = groups - 1 - i
        west = jnp.zeros((tracers, LANES), F32)
        for j in range(GROUP - 1, -1, -1):
            level = at * GROUP + j
            ratio = ratios[level]
            fresh = []
            for r in range(rows):
                value = diffused[level, r] - spread(ratio, r, tracers) * solved[r]
                diffused[level, r] = value
                fresh.append(value)
                lanes = j * rows + r
                moved = pltpu.roll(value[:, :LANES], lanes, 1) if lanes else value[:, :LANES]
                west = jnp.where(lane == lanes, moved, west)
            solved = fresh
            first[level] = solved[0]
            last[level] = solved[rows - 1]
            row = own * jnp.where(at_start, solved[0], solved[rows - 1]) + side * jnp.where(
                at_start, solved[1], solved[rows - 2]
            )
            if by_tracer:
                polar[:, at, j, :] = row
            else:
                polar[level] = row
        column[at] = west
        at_span(at, 0, send)
        return solved

    lax.fori_loop(0, groups, group, [jnp.zeros((tracers, cells), F32)] * rows)
    weight.wait()
    for c in range(chunks):
        for copy in copies(c):
            copy.wait()


def forward_sweep(levels, rows, tracers, cells, diffusion, right_of):
    zero = jnp.zeros((rows, cells), F32)
    carry = (zero, zero, [jnp.zeros((tracers, cells), F32)] * rows)
    groups = levels // GROUP

    def one(g, j, above, carry):
        rights, ratios, store = right_of(g, j, above is None)
        carry = eliminate(g * GROUP + j, above, carry, rights, ratios)
        store(carry[2])
        return carry

    def group(g, carry):
        for j in range(GROUP):
            carry = one(g, j, diffusion(g * GROUP + j), carry)
        return carry

    carry = lax.fori_loop(0, groups - 1, group, carry)
    for j in range(GROUP):
        level = levels - GROUP + j
        carry = one(groups - 1, j, diffusion(level) if level < levels - 1 else None, carry)


def first_kernel(
    step,
    costate,
    diffusion_in,
    north_in,
    south_in,
    east_in,
    result,
    first_out,
    last_out,
    polar_out,
    column,
    staged,
    ratios,
    diffused,
    first,
    last,
    polar,
    diffusion,
    couplings,
    arrived,
    sent,
    ready,
):
    levels, tracers, rows, cells = costate.shape
    small = [pltpu.make_async_copy(diffusion_in.at[step], diffusion, ready.at[0])]
    for k, coupling in enumerate((north_in, south_in, east_in)):
        small.append(pltpu.make_async_copy(coupling, couplings.at[k], ready.at[1 + k]))
    chunk(costate, staged, arrived, 0).start()
    for copy in small:
        copy.start()
    for c in range(1, levels // (GROUP * SPAN)):
        chunk(costate, staged, arrived, c).start()
    for copy in small:
        copy.wait()

    def right_of(g, j, final):
        if j == 0:
            at_span(g, 0, lambda c: chunk(costate, staged, arrived, c).wait())
        level = g * GROUP + j
        rights = [staged[level, :, r, :] for r in range(rows)]

        def store(values):
            for r in range(rows):
                diffused[level, r] = values[r]

        return rights, ratios, store

    forward_sweep(levels, rows, tracers, cells, lambda level: diffusion[level], right_of)
    views = [couplings.at[k] for k in range(3)]
    fields = (diffused, first, last, polar)
    results = (result, first_out, last_out, polar_out)
    substitute(step, ratios, views, column, fields, results, sent)


def meridional(level, row, diffused, after, before, coefs):
    rows = diffused.shape[1]
    own, north, south = coefs
    up = diffused[level, row + 1] if row < rows - 1 else after[level]
    down = diffused[level, row - 1] if row > 0 else before[level]
    return own * diffused[level, row] + north * up + south * down


def borders_kernel(
    step,
    shift,
    column,
    north,
    south,
    after_in,
    before_in,
    polar_in,
    nearby_in,
    edge,
    turned_out,
    south_hops,
    north_hops,
    after,
    before,
    polar,
    nearby,
    turned,
    ready,
):
    rows, cells = north.shape[1:]
    circle = cells * lax.axis_size("lon")
    amounts = [
        lax.rem(shift[step, x] + 2 * circle, circle) for x in (0, shift.shape[1] - 1)
    ]
    south_hops[0, 0] = amounts[0] // cells
    north_hops[0, 0] = amounts[1] // cells
    fetches = [
        pltpu.make_async_copy(source, target, ready.at[2 + k])
        for k, (source, target) in enumerate(((polar_in, polar), (nearby_in, nearby)))
    ]
    sending = pltpu.make_async_copy(turned, turned_out, ready.at[4])
    lat = lax.axis_index("lat")
    last_lat = lax.axis_size("lat") - 1
    at_pole = (lat == 0) | (lat == last_lat)

    @pl.when(at_pole)
    def _():
        for fetch in fetches:
            fetch.start()

    finish = west_column(step, column, north, south, after_in, before_in, edge, after, before, ready)

    @pl.when(at_pole)
    def _():
        for fetch in fetches:
            fetch.wait()
        levels = turned.shape[0]
        amount = jnp.where(lat == 0, amounts[0], amounts[1])
        matrix = shift_matrix(lax.rem(amount, cells), cells)
        tracers = turned.shape[1]
        weight = shifted(polar[levels], nearby[levels], matrix)[:1, :cells]
        size = 3 * GROUP
        for i in range(levels // size):
            at = slice(i * size, (i + 1) * size)
            low, high = [x[at].reshape(size * tracers, cells) for x in (polar, nearby)]
            row = shifted(low, high, matrix)
            row = row[:, :cells] + weight * (row[:, cells:] - row[:, :cells])
            turned[at] = row.reshape(size, tracers, cells)
        sending.start()

    finish()

    @pl.when(at_pole)
    def _():
        sending.wait()


def edge_kernel(
    step, column, north, south, after_in, before_in, edge, after, before, ready
):
    west_column(step, column, north, south, after_in, before_in, edge, after, before, ready)()


def west_column(step, column, north, south, after_in, before_in, edge, after, before, ready):
    groups, tracers, lanes = column.shape
    rows, cells = north.shape[1:]
    tiles = [
        pltpu.make_async_copy(source.at[:, :, pl.ds(0, lanes)], target, ready.at[k])
        for k, (source, target) in enumerate(((after_in, after), (before_in, before)))
    ]
    for tile in tiles:
        tile.start()
    lane = lax.broadcasted_iota(jnp.int32, (tracers, lanes), 1)

    def along_lanes(x):
        shape = (rows, lanes)
        own_lane = (lax.broadcasted_iota(jnp.int32, shape, 1) & (rows - 1)) == (
            lax.broadcasted_iota(jnp.int32, shape, 0)
        )
        picked = jnp.where(own_lane, jnp.broadcast_to(x[step, :, :1], shape), 0.0)
        return jnp.broadcast_to(jnp.sum(picked, axis=0, keepdims=True), (tracers, lanes))

    n, s = along_lanes(north), along_lanes(south)
    own = 1.0 - n - s

    def group(i, carry):
        here = column[i]
        up = pltpu.roll(here, lanes - 1, 1)
        down = pltpu.roll(here, 1, 1)
        for j in range(GROUP):
            level = i * GROUP + j
            bottom, top = j * rows, j * rows + rows - 1
            up = jnp.where(lane == top, pltpu.roll(after[level], top, 1), up)
            moved = before[level]
            moved = pltpu.roll(moved, bottom, 1) if bottom else moved
            down = jnp.where(lane == bottom, moved, down)
        edge[i] = own * here + n * up + s * down
        return carry

    def finish():
        for tile in tiles:
            tile.wait()
        lax.fori_loop(0, groups, group, 0)

    return finish


def rotate_kernel(step, shift, circle_in, out, circle, pairs, turned, ready):
    parts, groups, group, cells = turned.shape
    lat = lax.axis_index("lat")
    last_lat = lax.axis_size("lat") - 1
    rows = shift.shape[1] // lax.axis_size("lat")

    @pl.when((lat == 0) | (lat == last_lat))
    def _():
        fetch = pltpu.make_async_copy(circle_in, circle, ready.at[0])
        fetch.start()
        amount = jnp.where(lat == 0, shift[step, 0], shift[step, rows * last_lat + rows - 1])
        amount = lax.rem(amount + 2 * parts * cells, parts * cells)
        hops = amount // cells
        matrix = shift_matrix(amount - hops * cells, cells)
        fetch.wait()
        height = (groups + 1) * group
        for part in range(parts):
            at = slice(part * height, (part + 1) * height)
            near = lax.rem(part + hops, parts)
            far = lax.rem(part + hops + 1, parts)
            pairs[at, :cells] = circle[near].reshape(height, cells)
            pairs[at, cells:] = circle[far].reshape(height, cells)
        batch = parts // 2
        for i in range(2):
            rows_at = slice(i * batch * height, (i + 1) * batch * height)
            row = shifted(pairs[rows_at, :cells], pairs[rows_at, cells:], matrix)
            row = row.reshape(batch, groups + 1, group, 2 * cells)
            weight = row[:, groups:, :1, :cells]
            row = row[:, :groups]
            row = row[..., :cells] + weight * (row[..., cells:] - row[..., :cells])
            turned[i * batch : (i + 1) * batch] = row
        send = pltpu.make_async_copy(turned, out, ready.at[1])
        send.start()
        send.wait()


def prepare_stencil(step, north, south, east, coefs):
    rows, cells = north.shape[1:]
    tracers = coefs.shape[2]
    for r in range(rows):
        n = north[step, r : r + 1, :]
        s = south[step, r : r + 1, :]
        coefs[0, r] = jnp.broadcast_to(1.0 - n - s, (tracers, cells))
        coefs[1, r] = jnp.broadcast_to(n, (tracers, cells))
        coefs[2, r] = jnp.broadcast_to(s, (tracers, cells))
        coefs[3, r] = jnp.broadcast_to(east[step, r : r + 1, :], (tracers, cells))


def transported(group, lane_at, diffused, after, before, edge_row, coefs, pole):
    level = group * GROUP + lane_at
    rows, tracers, cells = diffused.shape[1:]
    lat = lax.axis_index("lat")
    last = lax.broadcasted_iota(jnp.int32, (tracers, cells), 1) == cells - 1
    result = []
    for r in range(rows):
        mer = meridional(level, r, diffused, after, before, [coefs[k, r] for k in range(3)])
        arrived = pltpu.roll(edge_row, LANES - 1 - (lane_at * rows + r), 1)
        arrived = jnp.concatenate([arrived] * (cells // LANES), axis=1)
        following = jnp.where(last, arrived, pltpu.roll(mer, cells - 1, 1))
        result.append(mer + coefs[3, r] * (following - mer))
    polar = pole[:, group, lane_at, :] if len(pole.shape) == 4 else pole[level]
    result[0] = jnp.where(lat == 0, polar, result[0])
    result[rows - 1] = jnp.where(lat == lax.axis_size("lat") - 1, polar, result[rows - 1])
    return result


def streams(sources, targets, poles, pole, done):
    lat = lax.axis_index("lat")
    last_lat = lax.axis_size("lat") - 1
    last = len(sources)

    def polar_copy(source, c):
        if len(pole.shape) == 4:
            at = pl.ds(c * SPAN, SPAN)
            return pltpu.make_async_copy(source.at[:, at], pole.at[:, at], done.at[last, c])
        return chunk(source, pole, done.at[last], c)

    for g in range(targets[0].shape[0] // (GROUP * SPAN)):
        for k, (source, target) in enumerate(zip(sources, targets)):
            chunk(source, target, done.at[k], g).start()

        @pl.when(lat == 0)
        def _():
            polar_copy(poles[0], g).start()

        @pl.when(lat == last_lat)
        def _():
            polar_copy(poles[-1], g).start()

    def wait(g):
        for k, (source, target) in enumerate(zip(sources, targets)):
            chunk(source, target, done.at[k], g).wait()

        @pl.when((lat == 0) | (lat == last_lat))
        def _():
            polar_copy(poles[0], g).wait()

    return wait


def middle_kernel(
    step,
    before_step,
    forced,
    after_in,
    before_in,
    south_pole,
    north_pole,
    edge,
    diffusion,
    north,
    south,
    east,
    result,
    first_out,
    last_out,
    polar_out,
    column,
    surface,
    coefs,
    ratios,
    diffused,
    after,
    before,
    pole,
    solved,
    first,
    last,
    polar,
    arrived,
    sent,
):
    levels, rows, tracers, cells = diffused.shape
    wait = streams(
        (before_step, after_in, before_in),
        (diffused, after, before),
        (south_pole, north_pole),
        pole,
        arrived,
    )
    prepare_stencil(step, north, south, east, coefs)

    def right_of(g, j, final):
        if j == 0:
            at_span(g, 0, wait)
        level = g * GROUP + j
        rights = transported(g, j, diffused, after, before, edge[g], coefs, pole)
        rights = [rights[r] + forced[level, r] for r in range(rows)]
        if final:
            for r in range(rows):
                surface[r] = rights[r]

        def store(values):
            for r in range(rows):
                solved[level, r] = values[r]

        return rights, ratios, store

    forward_sweep(
        levels, rows, tracers, cells, lambda level: diffusion[step - 1, level], right_of
    )
    couplings = (north, south, east)
    fields = (solved, first, last, polar)
    results = (result, first_out, last_out, polar_out)
    substitute(step - 1, ratios, couplings, column, fields, results, sent)


def last_kernel(
    step,
    before_step,
    forcing_in,
    after_in,
    before_in,
    pole_in,
    edge,
    north,
    south,
    east,
    surface,
    state,
    gradient,
    coefs,
    diffused,
    forced,
    after,
    before,
    pole,
    staged,
    arrived,
    sent,
):
    levels, rows, tracers, cells = diffused.shape
    wait = streams(
        (before_step, forcing_in, after_in, before_in),
        (diffused, forced, after, before),
        (pole_in,),
        pole,
        arrived,
    )
    prepare_stencil(step, north, south, east, coefs)

    def group(g, carry):
        at_span(g, 0, wait)
        edge_row = edge[g]
        for j in range(GROUP):
            level = g * GROUP + j
            values = transported(g, j, diffused, after, before, edge_row, coefs, pole)
            for r in range(rows):
                staged[level, :, r, :] = values[r] + forced[level, r]
        at_span(g, SPAN - 1, lambda c: chunk(staged, state, sent, c).start())
        return carry

    lax.fori_loop(0, levels // GROUP, group, 0)
    for r in range(rows):
        gradient[:, r, :] = surface[r] + staged[levels - 1, :, r, :]
    for c in range(levels // (GROUP * SPAN)):
        chunk(staged, state, sent, c).wait()


def boundary_rows(first, last):
    up = [(i, i + 1) for i in range(lax.axis_size("lat") - 1)]
    down = [(j, i) for i, j in up]
    return lax.ppermute(first, "lat", down), lax.ppermute(last, "lat", up)


def circles(lats, hops):
    lat_count = lax.axis_size("lat")
    lon_count = lax.axis_size("lon")
    return [
        (((j + hops) % lon_count) * lat_count + lat, j * lat_count + lat)
        for lat in lats
        for j in range(lon_count)
    ]


def westward(edge):
    count = lax.axis_size("lon")
    return held(lax.ppermute(edge, "lon", [(i, (i - 1) % count) for i in range(count)]))


def first_exchange(step, after, before, nearby, polar, column, north, south, shift):
    poles = (0, lax.axis_size("lat") - 1)
    levels, tracers, cells = after.shape
    edge, turned, *hops = pl.pallas_call(
        functools.partial(borders_kernel, step),
        out_shape=[
            resident(*column.shape),
            pltpu.HBM((levels, tracers, cells), F32),
            jax.ShapeDtypeStruct((1, 1), jnp.int32),
            jax.ShapeDtypeStruct((1, 1), jnp.int32),
        ],
        in_specs=[smem()] + [vmem()] * 3 + [anywhere()] * 4,
        out_specs=[vmem(), hbm(), smem(), smem()],
        scratch_shapes=[
            pltpu.VMEM((levels, tracers, LANES), F32),
            pltpu.VMEM((levels, tracers, LANES), F32),
            pltpu.VMEM(polar.shape, F32),
            pltpu.VMEM(polar.shape, F32),
            pltpu.VMEM((levels, tracers, cells), F32),
            pltpu.SemaphoreType.DMA((5,)),
        ],
        compiler_params=params(8),
        name="borders",
    )(shift, column, north, south, after, before, pinned(polar), nearby)
    edge = westward(edge)
    moved = []
    for lat, hop in zip(poles, hops):
        moved.append(
            lax.switch(
                hop.reshape(()),
                [
                    functools.partial(
                        lambda k, lat, x: lax.ppermute(x, AXES, circles((lat,), k)), k, lat
                    )
                    for k in range(lax.axis_size("lon"))
                ],
                turned,
            )
        )
    return after, before, pinned(moved[0]), pinned(moved[1]), edge


def last_exchange(step, after, before, circle, column, north, south, shift):
    levels, tracers, cells = after.shape
    parts, groups, group = circle.shape[:3]
    shape = (parts, groups - 1, group, cells)
    turned = pl.pallas_call(
        functools.partial(rotate_kernel, step),
        out_shape=pltpu.HBM(shape, F32),
        in_specs=[smem(), anywhere()],
        out_specs=hbm(),
        scratch_shapes=[
            pltpu.VMEM(circle.shape, F32),
            pltpu.VMEM((parts * groups * group, 2 * cells), F32),
            pltpu.VMEM(shape, F32),
            pltpu.SemaphoreType.DMA((2,)),
        ],
        compiler_params=params(14),
        name="rotate",
    )(shift, circle)
    pole = lax.all_to_all(turned, "lon", 0, 0, tiled=True)
    edge = pl.pallas_call(
        functools.partial(edge_kernel, step),
        out_shape=resident(*column.shape),
        in_specs=[vmem()] * 3 + [anywhere()] * 2,
        out_specs=vmem(),
        scratch_shapes=[
            pltpu.VMEM((levels, tracers, LANES), F32),
            pltpu.VMEM((levels, tracers, LANES), F32),
            pltpu.SemaphoreType.DMA((2,)),
        ],
        compiler_params=params(4),
        name="edge",
    )(column, north, south, after, before)
    return after, before, pole, westward(edge)


def per_device(
    costate,
    diffusion,
    east_courant,
    north_courant,
    south_courant,
    polar_shift,
    owners,
    columns,
    sounding_counts,
    kernels,
    misfits,
):
    levels, tracers, rows, cells = costate.shape
    owner_rows = owners.reshape(owners.shape[0], 1, owners.shape[1])
    couplings = (north_courant, south_courant, east_courant)
    groups = levels // GROUP

    solved_shapes = [
        pltpu.HBM((levels, rows, tracers, cells), F32),
        pltpu.HBM((levels, tracers, cells), F32),
        pltpu.HBM((levels, tracers, cells), F32),
        pltpu.HBM((levels + 1, tracers, cells), F32),
        resident(groups, tracers, LANES),
    ]
    ratios = pltpu.VMEM((levels, rows, cells), F32)
    coefs = pltpu.VMEM((4, rows, tracers, cells), F32)
    field = pltpu.VMEM((levels, rows, tracers, cells), F32)
    line = pltpu.VMEM((levels, tracers, cells), F32)
    solved_scratch = [field, line, line, pltpu.VMEM((levels + 1, tracers, cells), F32)]
    solved_specs = [hbm()] * 4 + [vmem()]
    leaving = pltpu.SemaphoreType.DMA((4, groups // SPAN + 1))
    output = pltpu.VMEM(costate.shape, F32)
    semaphores = pltpu.SemaphoreType.DMA((groups // SPAN,))
    diffused, first, last, polar, column = pl.pallas_call(
        functools.partial(first_kernel, 1),
        out_shape=solved_shapes,
        in_specs=[hbm()] * 5,
        out_specs=solved_specs,
        scratch_shapes=[
            output,
            ratios,
            *solved_scratch,
            pltpu.VMEM(diffusion.shape[1:], F32),
            pltpu.VMEM((3,) + east_courant.shape, F32),
            semaphores,
            leaving,
            pltpu.SemaphoreType.DMA((4,)),
        ],
        compiler_params=params(16),
        name="first",
    )(*[pinned(x) for x in (costate, diffusion, *couplings)])
    couplings = [held(x) for x in couplings]
    diffusion = held(diffusion)
    counts, column = lax.optimization_barrier((sounding_counts, column))
    nearby = lax.ppermute(polar, AXES, circles((0, lax.axis_size("lat") - 1), 1))
    around = (*boundary_rows(first, last), nearby)
    sent = packed(counts, owner_rows, columns, kernels, misfits)
    sent, *around = lax.optimization_barrier((sent, *around))
    around = [pinned(x) for x in around]
    got = lax.all_to_all(sent, AXES, 0, 0, tiled=True)
    shape = (levels, rows, tracers, cells)
    forced = forcing(1, got, shape, False)
    around = first_exchange(1, *around, polar, column, *couplings[:2], polar_shift)
    scratch = [field, line, line]
    transfers = pltpu.SemaphoreType.DMA((4, groups // SPAN))
    solved, first, last, polar, column, surface = pl.pallas_call(
        functools.partial(middle_kernel, 1),
        out_shape=[
            *solved_shapes[:3],
            pltpu.HBM((tracers, groups + 1, GROUP, cells), F32),
            solved_shapes[4],
            resident(rows, tracers, cells),
        ],
        in_specs=[hbm(), vmem()] + [anywhere()] * 2 + [hbm()] * 2 + [vmem()] * 5,
        out_specs=solved_specs + [vmem()],
        scratch_shapes=[
            coefs,
            ratios,
            *scratch,
            line,
            *solved_scratch[:3],
            pltpu.VMEM((tracers, groups + 1, GROUP, cells), F32),
            transfers,
            leaving,
        ],
        compiler_params=params(20),
        name="middle",
    )(pinned(diffused), forced, *around, diffusion, *couplings)
    around = (*boundary_rows(first, last), lax.all_to_all(polar, "lon", 0, 0, tiled=True))
    got, column = lax.optimization_barrier((got, column))
    forced = forcing(0, got, shape, True)
    forced, *around = lax.optimization_barrier((forced, *around))
    around = last_exchange(0, *around, column, *couplings[:2], polar_shift)
    return tuple(
        pl.pallas_call(
            functools.partial(last_kernel, 0),
            out_shape=[
                pltpu.HBM(costate.shape, F32),
                jax.ShapeDtypeStruct((tracers, rows, cells), F32),
            ],
            in_specs=[hbm()] * 2 + [anywhere()] * 3 + [vmem()] * 5,
            out_specs=[hbm(), vmem()],
            scratch_shapes=[
                coefs,
                field,
                *scratch,
                pltpu.VMEM((tracers, groups, GROUP, cells), F32),
                output,
                pltpu.SemaphoreType.DMA((5, groups // SPAN)),
                semaphores,
            ],
            compiler_params=params(22),
            name="last",
        )(pinned(solved), pinned(forced), *around, *couplings, surface)
    )


def solution(mesh):
    return jax.shard_map(
        per_device,
        mesh=mesh,
        in_specs=(
            P(None, None, "lat", "lon"),
            P(None, None, "lat", "lon"),
            P(None, "lat", "lon"),
            P(None, "lat", "lon"),
            P(None, "lat", "lon"),
            P(),
            P(None, ("lon", "lat"), None),
            P(None, ("lon", "lat")),
            P(None, ("lon", "lat")),
            P(None, None, ("lon", "lat")),
            P(None, None, ("lon", "lat")),
        ),
        out_specs=(P(None, None, "lat", "lon"), P(None, "lat", "lon")),
        check_vma=False,
    )
```

```python
import functools

import jax
import jax.numpy as jnp
from jax import lax
from jax.experimental import pallas as pl
from jax.experimental.pallas import tpu as pltpu
from jax.sharding import PartitionSpec as P

AXES = ("lon", "lat")
LANES = 128
CAP = 16
GROUP = 8
SPAN = 3
F32 = jnp.float32
BF16 = jnp.bfloat16
MIB = 1024 * 1024


def vmem():
    return pl.BlockSpec(memory_space=pltpu.VMEM)


def smem():
    return pl.BlockSpec(memory_space=pltpu.SMEM)


def hbm():
    return pl.BlockSpec(memory_space=pltpu.HBM)


def params(limit):
    return pltpu.CompilerParams(vmem_limit_bytes=limit * MIB)


def held(x):
    return pltpu.with_memory_space_constraint(x, pltpu.VMEM)


def anywhere():
    return pl.BlockSpec(memory_space=pl.ANY)


def pinned(x):
    return pltpu.with_memory_space_constraint(x, pltpu.HBM)


def resident(*shape):
    return pltpu.VMEM(shape, F32)


def chunk(source, target, done, c):
    at = pl.ds(c * GROUP * SPAN, GROUP * SPAN)
    return pltpu.make_async_copy(source.at[at], target.at[at], done.at[c])


def at_span(g, place, act):
    if isinstance(g, int):
        if g % SPAN == place:
            act(g // SPAN)
    else:
        pl.when(lax.rem(g, SPAN) == place)(lambda: act(lax.div(g, SPAN)))


def dot(a, b, contract=((1,), (0,))):
    return lax.dot_general(a, b, (contract, ((), ())), preferred_element_type=F32)


def halves(x):
    high = x.astype(BF16)
    return high, (x - high.astype(F32)).astype(BF16)


def spare_lane(levels, tracers):
    return levels + tracers + 8


def pack_kernel(
    counts, owners, columns, kernels, misfits, out, payload, target, staged, done
):
    steps, levels, held = kernels.shape
    tracers = misfits.shape[1]
    shape = (LANES, LANES)
    half = CAP // 2
    device = lax.broadcasted_iota(jnp.int32, shape, 0)
    table = counting_table()
    for step in range(steps):
        owner = owners[step]
        live = lax.broadcasted_iota(jnp.int32, owner.shape, 1) < counts[step, 0]
        owner = jnp.where(live, owner, -1)
        seen = jnp.zeros(shape, F32)
        for start in range(0, held, LANES):
            here = owner[:, start : start + LANES]
            hot = device == here
            counted = dot(jnp.where(hot, 1.0, 0.0).astype(BF16), table)
            rank = jnp.sum(
                jnp.where(hot, counted[:, :LANES] + seen, 0.0), axis=0, keepdims=True
            )
            seen = seen + counted[:, LANES:]
            target[step : step + 1, start : start + LANES] = jnp.where(
                here >= 0, here * CAP + rank.astype(jnp.int32), -1
            )
    spare = spare_lane(levels, tracers)
    main = LANES - spare

    def fill(k, part, pieces):
        rows = jnp.concatenate(
            [jnp.zeros((x, held), F32) if isinstance(x, int) else x for x in pieces], axis=0
        )
        high, low = halves(rows)
        payload[k, :LANES, part * held : (part + 1) * held] = high
        payload[k, LANES:, part * held : (part + 1) * held] = low

    def column(step):
        x = columns[step : step + 1, :].astype(F32) + 1.0
        return jnp.where(lax.broadcasted_iota(jnp.int32, (8, held), 0) == 0, x, 0.0)

    rest = [kernels[0, main:, :], misfits[0], column(0)]
    used = levels - main + tracers + 8
    fill(0, 0, [kernels[1], misfits[1], column(1), main])
    fill(0, 1, [spare, kernels[0, :main, :]])
    fill(1, 0, [*rest, LANES - used])
    fill(1, 1, [LANES // 2, *rest, LANES // 2 - used])
    slot = target[0:1, :] & (CAP - 1)
    owner = target[0:1, :] >> (CAP.bit_length() - 1)
    lower = jnp.where((target[0:1, :] >= 0) & (slot < half), owner * half + slot, -1)
    upper = jnp.where((target[0:1, :] >= 0) & (slot >= half), owner * half + slot - half, -1)
    owned = 512 // CAP
    tiles = out.shape[0] // owned

    def copy(i):
        at = pl.ds(i * owned, owned)
        return pltpu.make_async_copy(staged.at[at], out.at[at], done.at[i])

    def place(i, carry):
        for k, ats, size, rows in (
            (0, (target[1:2, :], target[0:1, :]), owned * CAP, slice(0, CAP)),
            (1, (lower, upper), owned * half, slice(CAP, CAP + half)),
        ):
            hot = jnp.concatenate([tall_one_hot(at - i * size, size) for at in ats], axis=1)
            both = dot(hot, payload[k], ((1,), (1,)))
            both = both[:, :LANES] + both[:, LANES:]
            staged[pl.ds(i * owned, owned), rows, :] = both.reshape(owned, -1, LANES)
        copy(i).start()
        return carry

    lax.fori_loop(0, tiles, place, 0)
    for i in range(tiles):
        copy(i).wait()


def one_hot(at, size):
    at = jnp.where((at >= 0) & (at < size), at, -1).astype(F32).astype(BF16)
    shape = (size, at.shape[1])
    row = lax.broadcasted_iota(jnp.int32, shape, 0).astype(F32).astype(BF16)
    return jnp.where(row == at, jnp.ones(shape, BF16), jnp.zeros(shape, BF16))


def tall_one_hot(at, size):
    parts = [one_hot(at - start, 256) for start in range(0, size, 256)]
    return parts[0] if len(parts) == 1 else jnp.concatenate(parts, axis=0)


def counting_table():
    shape = (LANES, LANES)
    earlier = lax.broadcasted_iota(jnp.int32, shape, 0) < lax.broadcasted_iota(
        jnp.int32, shape, 1
    )
    return jnp.concatenate(
        [jnp.where(earlier, 1.0, 0.0), jnp.ones(shape, F32)], axis=1
    ).astype(BF16)


def packed(counts, owners, columns, kernels, misfits):
    steps, slots = columns.shape
    devices = lax.axis_size("lon") * lax.axis_size("lat")
    return pl.pallas_call(
        pack_kernel,
        out_shape=pltpu.HBM((devices, CAP + CAP // 2, LANES), F32),
        in_specs=[smem()] + [vmem()] * 4,
        out_specs=hbm(),
        scratch_shapes=[
            pltpu.VMEM((2, 2 * LANES, 2 * slots), BF16),
            pltpu.VMEM((steps, slots), jnp.int32),
            pltpu.VMEM((devices, CAP + CAP // 2, LANES), F32),
            pltpu.SemaphoreType.DMA((devices * CAP // 512,)),
        ],
        compiler_params=params(20),
        name="pack",
    )(counts, held(owners), held(columns), held(kernels), held(misfits))


def streamed_forcing_kernel(step, received, result, out, *scratch):
    done = scratch[-1]

    def copy(r):
        return pltpu.make_async_copy(out.at[:, r], result.at[:, r], done.at[r])

    forcing_kernel(step, received, out, *scratch[:-1], finished=lambda r: copy(r).start())
    for r in range(out.shape[1]):
        copy(r).wait()


def forcing_kernel(
    step, received, out, fields, hots, place, ordered, finished=lambda r: None
):
    levels, rows, tracers, cells = out.shape
    sources = received.shape[0]
    slots = sources * CAP
    blocks = slots // LANES
    spare = spare_lane(levels, tracers)
    data = received[:, :CAP, :].reshape(slots, LANES)
    if step == 1:
        at_column = levels + tracers

        def profile(turned):
            return turned[:levels]

    else:
        at_column = levels - (LANES - spare) + tracers
        extra = received[:, CAP:, :]
        other = pltpu.roll(extra.reshape(slots // 2, LANES), LANES // 2, 1)
        extra = jnp.concatenate([extra, other.reshape(extra.shape)], axis=1)
        lane = lax.broadcasted_iota(jnp.int32, (slots, LANES), 1)
        data = jnp.where(lane < LANES // 2, extra.reshape(slots, LANES), data)

        def profile(turned):
            return jnp.concatenate([turned[spare:], turned[: at_column - tracers]], axis=0)

    high, low = halves(data)
    fields[:, :LANES] = high
    fields[:, LANES:] = low
    shape = (8, 2 * LANES)
    pick = (lax.broadcasted_iota(jnp.int32, shape, 1) & (LANES - 1)) == at_column
    column = dot(jnp.where(pick, 1.0, 0.0).astype(BF16), fields[...], ((1,), (1,)))
    cell_row = (column.astype(jnp.int32) - 1) >> (cells.bit_length() - 1)
    sub = lax.broadcasted_iota(jnp.int32, (rows, LANES), 0)
    for b in range(blocks):
        row = cell_row[:, b * LANES : (b + 1) * LANES]
        hots[b * rows : (b + 1) * rows, :] = jnp.where(sub == row, 1.0, 0.0)
    counted = dot(hots[...].astype(BF16), counting_table())
    run = jnp.zeros((rows, LANES), F32)
    runs = []
    for b in range(blocks):
        runs.append(run)
        run = run + counted[b * rows : (b + 1) * rows, LANES:]
    filled = jnp.floor((run + (LANES - 1.0)) * (1.0 / LANES))
    start = jnp.zeros((rows, LANES), F32)
    for j in range(1, rows):
        start = start + jnp.where(sub >= j, pltpu.roll(filled, j, 0), 0.0)
    for b in range(blocks):
        hot = hots[b * rows : (b + 1) * rows, :]
        at = counted[b * rows : (b + 1) * rows, :LANES] + runs[b] + start * float(LANES)
        at = jnp.sum(hot * at, axis=0, keepdims=True)
        live = jnp.sum(hot, axis=0, keepdims=True) > 0.0
        place[:, b * LANES : (b + 1) * LANES] = jnp.where(live, at, -1.0)
    counts = [jnp.max(filled[r : r + 1, :]).astype(jnp.int32) for r in range(rows)]
    used = sum(counts)
    wide = 2 * LANES

    def sort(i, carry):
        hot = one_hot(place[...] - (i * wide).astype(F32), wide)
        both = dot(hot, fields[...])
        ordered[pl.ds(pl.multiple_of(i * wide, wide), wide), :] = both[:, :LANES] + both[:, LANES:]
        return carry

    lax.fori_loop(0, (used + 1) // 2, sort, 0)
    out[...] = jnp.zeros_like(out)
    name = lax.broadcasted_iota(jnp.int32, (LANES, cells), 1).astype(F32)
    first = jnp.int32(0)
    for r in range(rows):

        def add(p, carry):
            block = ordered[pl.ds(pl.multiple_of(p * LANES, LANES), LANES), :]
            own = jnp.broadcast_to(
                block[:, at_column : at_column + 1] - (r * cells + 1.0), (LANES, cells)
            )
            hot = jnp.where(name == own, 1.0, 0.0).astype(BF16)
            turned = block.T
            product = profile(turned)[:, None, :] * turned[at_column - tracers : at_column][None]
            product = product.reshape(levels * tracers, LANES)
            total = dot(
                jnp.concatenate(halves(product), axis=1), jnp.concatenate([hot, hot], axis=0)
            )
            out[:, r, :, :] += total.reshape(levels, tracers, cells)
            return carry

        lax.fori_loop(first, first + counts[r], add, 0)
        first = first + counts[r]
        finished(r)


def forcing(step, received, shape, streamed):
    slots = received.shape[0] * CAP
    scratch = [
        pltpu.VMEM((slots, 2 * LANES), BF16),
        pltpu.VMEM((slots // LANES * shape[1], LANES), F32),
        pltpu.VMEM((1, slots), F32),
        pltpu.VMEM((slots + shape[1] * LANES, LANES), F32),
    ]
    if streamed:
        scratch = [resident(*shape), *scratch, pltpu.SemaphoreType.DMA((shape[1],))]
    return pl.pallas_call(
        functools.partial(streamed_forcing_kernel if streamed else forcing_kernel, step),
        out_shape=pltpu.HBM(shape, F32) if streamed else resident(*shape),
        in_specs=[vmem()],
        out_specs=hbm() if streamed else vmem(),
        scratch_shapes=scratch,
        compiler_params=params(16 if streamed else 12),
        name="forcing",
    )(held(received))


def shift_matrix(inner, cells):
    shape = (2 * cells, cells)
    source = lax.broadcasted_iota(jnp.int32, shape, 0)
    target = lax.broadcasted_iota(jnp.int32, shape, 1) + inner
    picks = [jnp.where(source == target + k, 1.0, 0.0).astype(BF16) for k in range(2)]
    return jnp.concatenate(picks, axis=1)


def shifted(low, high, matrix):
    row = jnp.concatenate([low, high], axis=1)
    first, rest = row.astype(BF16), None
    rest = row - first.astype(F32)
    second, third = halves(rest)
    return dot(first, matrix) + dot(second, matrix) + dot(third, matrix)


def spread(x, row, tracers):
    return jnp.broadcast_to(x[row : row + 1, :], (tracers, x.shape[1]))


def eliminate(level, above, carry, rights, ratios):
    below, ratio, values = carry
    if above is None:
        above = jnp.zeros_like(below)
    inverse = 1.0 / (1.0 + below + above + below * ratio)
    lower = below * inverse
    ratio = -above * inverse
    ratios[level] = ratio
    tracers = rights[0].shape[0]
    fresh = [
        spread(inverse, r, tracers) * rights[r] + spread(lower, r, tracers) * values[r]
        for r in range(len(rights))
    ]
    return (above, ratio, fresh)


def substitute(step, ratios, couplings, column, fields, results, done):
    diffused, first, last, polar = fields
    levels, rows, tracers, cells = diffused.shape
    lat = lax.axis_index("lat")
    at_start = lat == 0

    def picked(x):
        return jnp.where(at_start, x[step, 0:1, :], x[step, rows - 1 : rows, :])

    north, south, east = [picked(x) for x in couplings]
    own = jnp.broadcast_to(1.0 - north - south, (tracers, cells))
    side = jnp.broadcast_to(jnp.where(at_start, north, south), (tracers, cells))
    groups = levels // GROUP
    by_tracer = len(polar.shape) == 4
    if by_tracer:
        polar[:, groups, 0, :] = jnp.broadcast_to(east, (tracers, cells))
    else:
        polar[levels] = jnp.broadcast_to(east, (tracers, cells))

    chunks = groups // SPAN

    def polar_copy(at, c):
        if by_tracer:
            source, target = [x.at[:, at] for x in (polar, results[3])]
        else:
            source, target = [x.at[at] for x in (polar, results[3])]
        return pltpu.make_async_copy(source, target, done.at[3, c])

    def copies(c):
        size = SPAN if by_tracer else SPAN * GROUP
        moves = [chunk(fields[k], results[k], done.at[k], c) for k in range(3)]
        return [*moves, polar_copy(pl.ds(c * size, size), c)]

    def send(c):
        for copy in copies(c):
            copy.start()

    weight = polar_copy(pl.ds(groups if by_tracer else levels, 1), chunks)
    weight.start()
    lane = lax.broadcasted_iota(jnp.int32, (tracers, LANES), 1)

    def group(i, solved):
        at = groups - 1 - i
        west = jnp.zeros((tracers, LANES), F32)
        for j in range(GROUP - 1, -1, -1):
            level = at * GROUP + j
            ratio = ratios[level]
            fresh = []
            for r in range(rows):
                value = diffused[level, r] - spread(ratio, r, tracers) * solved[r]
                diffused[level, r] = value
                fresh.append(value)
                lanes = j * rows + r
                moved = pltpu.roll(value[:, :LANES], lanes, 1) if lanes else value[:, :LANES]
                west = jnp.where(lane == lanes, moved, west)
            solved = fresh
            first[level] = solved[0]
            last[level] = solved[rows - 1]
            row = own * jnp.where(at_start, solved[0], solved[rows - 1]) + side * jnp.where(
                at_start, solved[1], solved[rows - 2]
            )
            if by_tracer:
                polar[:, at, j, :] = row
            else:
                polar[level] = row
        column[at] = west
        at_span(at, 0, send)
        return solved

    lax.fori_loop(0, groups, group, [jnp.zeros((tracers, cells), F32)] * rows)
    weight.wait()
    for c in range(chunks):
        for copy in copies(c):
            copy.wait()


def forward_sweep(levels, rows, tracers, cells, diffusion, right_of):
    zero = jnp.zeros((rows, cells), F32)
    carry = (zero, zero, [jnp.zeros((tracers, cells), F32)] * rows)
    groups = levels // GROUP

    def one(g, j, above, carry):
        rights, ratios, store = right_of(g, j, above is None)
        carry = eliminate(g * GROUP + j, above, carry, rights, ratios)
        store(carry[2])
        return carry

    def group(g, carry):
        for j in range(GROUP):
            carry = one(g, j, diffusion(g * GROUP + j), carry)
        return carry

    carry = lax.fori_loop(0, groups - 1, group, carry)
    for j in range(GROUP):
        level = levels - GROUP + j
        carry = one(groups - 1, j, diffusion(level) if level < levels - 1 else None, carry)


def first_kernel(
    step,
    costate,
    diffusion_in,
    north_in,
    south_in,
    east_in,
    result,
    first_out,
    last_out,
    polar_out,
    column,
    staged,
    ratios,
    diffused,
    first,
    last,
    polar,
    diffusion,
    couplings,
    arrived,
    sent,
    ready,
):
    levels, tracers, rows, cells = costate.shape
    small = [pltpu.make_async_copy(diffusion_in.at[step], diffusion, ready.at[0])]
    for k, coupling in enumerate((north_in, south_in, east_in)):
        small.append(pltpu.make_async_copy(coupling, couplings.at[k], ready.at[1 + k]))
    chunk(costate, staged, arrived, 0).start()
    for copy in small:
        copy.start()
    for c in range(1, levels // (GROUP * SPAN)):
        chunk(costate, staged, arrived, c).start()
    for copy in small:
        copy.wait()

    def right_of(g, j, final):
        if j == 0:
            at_span(g, 0, lambda c: chunk(costate, staged, arrived, c).wait())
        level = g * GROUP + j
        rights = [staged[level, :, r, :] for r in range(rows)]

        def store(values):
            for r in range(rows):
                diffused[level, r] = values[r]

        return rights, ratios, store

    forward_sweep(levels, rows, tracers, cells, lambda level: diffusion[level], right_of)
    views = [couplings.at[k] for k in range(3)]
    fields = (diffused, first, last, polar)
    results = (result, first_out, last_out, polar_out)
    substitute(step, ratios, views, column, fields, results, sent)


def meridional(level, row, diffused, after, before, coefs):
    rows = diffused.shape[1]
    own, north, south = coefs
    up = diffused[level, row + 1] if row < rows - 1 else after[level]
    down = diffused[level, row - 1] if row > 0 else before[level]
    return own * diffused[level, row] + north * up + south * down


def turn_kernel(
    step,
    shift,
    polar_in,
    nearby_in,
    turned_out,
    south_hops,
    north_hops,
    polar,
    nearby,
    turned,
    ready,
):
    levels, tracers, cells = turned.shape
    circle = cells * lax.axis_size("lon")
    amounts = [
        lax.rem(shift[step, x] + 2 * circle, circle) for x in (0, shift.shape[1] - 1)
    ]
    south_hops[0, 0] = amounts[0] // cells
    north_hops[0, 0] = amounts[1] // cells
    lat = lax.axis_index("lat")

    @pl.when((lat == 0) | (lat == lax.axis_size("lat") - 1))
    def _():
        fetches = [
            pltpu.make_async_copy(polar_in, polar, ready.at[0]),
            pltpu.make_async_copy(nearby_in, nearby, ready.at[1]),
        ]
        for fetch in fetches:
            fetch.start()
        amount = jnp.where(lat == 0, amounts[0], amounts[1])
        matrix = shift_matrix(lax.rem(amount, cells), cells)
        for fetch in fetches:
            fetch.wait()
        weight = shifted(polar[levels], nearby[levels], matrix)[:1, :cells]
        size = 3 * GROUP
        for i in range(levels // size):
            at = slice(i * size, (i + 1) * size)
            low, high = [x[at].reshape(size * tracers, cells) for x in (polar, nearby)]
            row = shifted(low, high, matrix)
            row = row[:, :cells] + weight * (row[:, cells:] - row[:, :cells])
            turned[at] = row.reshape(size, tracers, cells)
        send = pltpu.make_async_copy(turned, turned_out, ready.at[2])
        send.start()
        send.wait()


def edge_kernel(
    step, column, north, south, after_in, before_in, edge, after, before, ready
):
    west_column(step, column, north, south, after_in, before_in, edge, after, before, ready)()


def west_column(step, column, north, south, after_in, before_in, edge, after, before, ready):
    groups, tracers, lanes = column.shape
    rows, cells = north.shape[1:]
    tiles = [
        pltpu.make_async_copy(source.at[:, :, pl.ds(0, lanes)], target, ready.at[k])
        for k, (source, target) in enumerate(((after_in, after), (before_in, before)))
    ]
    for tile in tiles:
        tile.start()
    lane = lax.broadcasted_iota(jnp.int32, (tracers, lanes), 1)

    def along_lanes(x):
        shape = (rows, lanes)
        own_lane = (lax.broadcasted_iota(jnp.int32, shape, 1) & (rows - 1)) == (
            lax.broadcasted_iota(jnp.int32, shape, 0)
        )
        picked = jnp.where(own_lane, jnp.broadcast_to(x[step, :, :1], shape), 0.0)
        return jnp.broadcast_to(jnp.sum(picked, axis=0, keepdims=True), (tracers, lanes))

    n, s = along_lanes(north), along_lanes(south)
    own = 1.0 - n - s

    def group(i, carry):
        here = column[i]
        up = pltpu.roll(here, lanes - 1, 1)
        down = pltpu.roll(here, 1, 1)
        for j in range(GROUP):
            level = i * GROUP + j
            bottom, top = j * rows, j * rows + rows - 1
            up = jnp.where(lane == top, pltpu.roll(after[level], top, 1), up)
            moved = before[level]
            moved = pltpu.roll(moved, bottom, 1) if bottom else moved
            down = jnp.where(lane == bottom, moved, down)
        edge[i] = own * here + n * up + s * down
        return carry

    def finish():
        for tile in tiles:
            tile.wait()
        lax.fori_loop(0, groups, group, 0)

    return finish


def rotate_kernel(step, shift, circle_in, out, circle, pairs, turned, ready):
    parts, groups, group, cells = turned.shape
    lat = lax.axis_index("lat")
    last_lat = lax.axis_size("lat") - 1
    rows = shift.shape[1] // lax.axis_size("lat")

    @pl.when((lat == 0) | (lat == last_lat))
    def _():
        fetch = pltpu.make_async_copy(circle_in, circle, ready.at[0])
        fetch.start()
        amount = jnp.where(lat == 0, shift[step, 0], shift[step, rows * last_lat + rows - 1])
        amount = lax.rem(amount + 2 * parts * cells, parts * cells)
        hops = amount // cells
        matrix = shift_matrix(amount - hops * cells, cells)
        fetch.wait()
        height = (groups + 1) * group
        for part in range(parts):
            at = slice(part * height, (part + 1) * height)
            near = lax.rem(part + hops, parts)
            far = lax.rem(part + hops + 1, parts)
            pairs[at, :cells] = circle[near].reshape(height, cells)
            pairs[at, cells:] = circle[far].reshape(height, cells)
        batch = parts // 2
        for i in range(2):
            rows_at = slice(i * batch * height, (i + 1) * batch * height)
            row = shifted(pairs[rows_at, :cells], pairs[rows_at, cells:], matrix)
            row = row.reshape(batch, groups + 1, group, 2 * cells)
            weight = row[:, groups:, :1, :cells]
            row = row[:, :groups]
            row = row[..., :cells] + weight * (row[..., cells:] - row[..., :cells])
            turned[i * batch : (i + 1) * batch] = row
        send = pltpu.make_async_copy(turned, out, ready.at[1])
        send.start()
        send.wait()


def prepare_stencil(step, north, south, east, coefs):
    rows, cells = north.shape[1:]
    tracers = coefs.shape[2]
    for r in range(rows):
        n = north[step, r : r + 1, :]
        s = south[step, r : r + 1, :]
        coefs[0, r] = jnp.broadcast_to(1.0 - n - s, (tracers, cells))
        coefs[1, r] = jnp.broadcast_to(n, (tracers, cells))
        coefs[2, r] = jnp.broadcast_to(s, (tracers, cells))
        coefs[3, r] = jnp.broadcast_to(east[step, r : r + 1, :], (tracers, cells))


def transported(group, lane_at, diffused, after, before, edge_row, coefs, pole):
    level = group * GROUP + lane_at
    rows, tracers, cells = diffused.shape[1:]
    lat = lax.axis_index("lat")
    last = lax.broadcasted_iota(jnp.int32, (tracers, cells), 1) == cells - 1
    result = []
    for r in range(rows):
        mer = meridional(level, r, diffused, after, before, [coefs[k, r] for k in range(3)])
        arrived = pltpu.roll(edge_row, LANES - 1 - (lane_at * rows + r), 1)
        arrived = jnp.concatenate([arrived] * (cells // LANES), axis=1)
        following = jnp.where(last, arrived, pltpu.roll(mer, cells - 1, 1))
        result.append(mer + coefs[3, r] * (following - mer))
    polar = pole[:, group, lane_at, :] if len(pole.shape) == 4 else pole[level]
    result[0] = jnp.where(lat == 0, polar, result[0])
    result[rows - 1] = jnp.where(lat == lax.axis_size("lat") - 1, polar, result[rows - 1])
    return result


def streams(sources, targets, poles, pole, done):
    lat = lax.axis_index("lat")
    last_lat = lax.axis_size("lat") - 1
    last = len(sources)

    def polar_copy(source, c):
        if len(pole.shape) == 4:
            at = pl.ds(c * SPAN, SPAN)
            return pltpu.make_async_copy(source.at[:, at], pole.at[:, at], done.at[last, c])
        return chunk(source, pole, done.at[last], c)

    for g in range(targets[0].shape[0] // (GROUP * SPAN)):
        for k, (source, target) in enumerate(zip(sources, targets)):
            chunk(source, target, done.at[k], g).start()

        @pl.when(lat == 0)
        def _():
            polar_copy(poles[0], g).start()

        @pl.when(lat == last_lat)
        def _():
            polar_copy(poles[-1], g).start()

    def wait(g):
        for k, (source, target) in enumerate(zip(sources, targets)):
            chunk(source, target, done.at[k], g).wait()

        @pl.when((lat == 0) | (lat == last_lat))
        def _():
            polar_copy(poles[0], g).wait()

    return wait


def middle_kernel(
    step,
    before_step,
    forced,
    after_in,
    before_in,
    south_pole,
    north_pole,
    edge,
    diffusion,
    north,
    south,
    east,
    result,
    first_out,
    last_out,
    polar_out,
    column,
    surface,
    coefs,
    ratios,
    diffused,
    after,
    before,
    pole,
    solved,
    first,
    last,
    polar,
    arrived,
    sent,
):
    levels, rows, tracers, cells = diffused.shape
    wait = streams(
        (before_step, after_in, before_in),
        (diffused, after, before),
        (south_pole, north_pole),
        pole,
        arrived,
    )
    prepare_stencil(step, north, south, east, coefs)

    def right_of(g, j, final):
        if j == 0:
            at_span(g, 0, wait)
        level = g * GROUP + j
        rights = transported(g, j, diffused, after, before, edge[g], coefs, pole)
        rights = [rights[r] + forced[level, r] for r in range(rows)]
        if final:
            for r in range(rows):
                surface[r] = rights[r]

        def store(values):
            for r in range(rows):
                solved[level, r] = values[r]

        return rights, ratios, store

    forward_sweep(
        levels, rows, tracers, cells, lambda level: diffusion[step - 1, level], right_of
    )
    couplings = (north, south, east)
    fields = (solved, first, last, polar)
    results = (result, first_out, last_out, polar_out)
    substitute(step - 1, ratios, couplings, column, fields, results, sent)


def last_kernel(
    step,
    before_step,
    forcing_in,
    after_in,
    before_in,
    pole_in,
    edge,
    north,
    south,
    east,
    surface,
    state,
    gradient,
    coefs,
    diffused,
    forced,
    after,
    before,
    pole,
    staged,
    arrived,
    sent,
):
    levels, rows, tracers, cells = diffused.shape
    wait = streams(
        (before_step, forcing_in, after_in, before_in),
        (diffused, forced, after, before),
        (pole_in,),
        pole,
        arrived,
    )
    prepare_stencil(step, north, south, east, coefs)

    def group(g, carry):
        at_span(g, 0, wait)
        edge_row = edge[g]
        for j in range(GROUP):
            level = g * GROUP + j
            values = transported(g, j, diffused, after, before, edge_row, coefs, pole)
            for r in range(rows):
                staged[level, :, r, :] = values[r] + forced[level, r]
        at_span(g, SPAN - 1, lambda c: chunk(staged, state, sent, c).start())
        return carry

    lax.fori_loop(0, levels // GROUP, group, 0)
    for r in range(rows):
        gradient[:, r, :] = surface[r] + staged[levels - 1, :, r, :]
    for c in range(levels // (GROUP * SPAN)):
        chunk(staged, state, sent, c).wait()


def boundary_rows(first, last):
    up = [(i, i + 1) for i in range(lax.axis_size("lat") - 1)]
    down = [(j, i) for i, j in up]
    return lax.ppermute(first, "lat", down), lax.ppermute(last, "lat", up)


def circles(lats, hops):
    lat_count = lax.axis_size("lat")
    lon_count = lax.axis_size("lon")
    return [
        (((j + hops) % lon_count) * lat_count + lat, j * lat_count + lat)
        for lat in lats
        for j in range(lon_count)
    ]


def west_edge(step, column, north, south, after, before):
    levels, tracers, cells = after.shape
    edge = pl.pallas_call(
        functools.partial(edge_kernel, step),
        out_shape=resident(*column.shape),
        in_specs=[vmem()] * 3 + [anywhere()] * 2,
        out_specs=vmem(),
        scratch_shapes=[
            pltpu.VMEM((levels, tracers, LANES), F32),
            pltpu.VMEM((levels, tracers, LANES), F32),
            pltpu.SemaphoreType.DMA((2,)),
        ],
        compiler_params=params(4),
        name="edge",
    )(column, north, south, after, before)
    count = lax.axis_size("lon")
    return held(lax.ppermute(edge, "lon", [(i, (i - 1) % count) for i in range(count)]))


def first_exchange(step, first, last, nearby, polar, column, north, south, shift):
    poles = (0, lax.axis_size("lat") - 1)
    levels, tracers, cells = first.shape
    after, before = boundary_rows(first, last)
    turned, *hops = pl.pallas_call(
        functools.partial(turn_kernel, step),
        out_shape=[
            pltpu.HBM((levels, tracers, cells), F32),
            jax.ShapeDtypeStruct((1, 1), jnp.int32),
            jax.ShapeDtypeStruct((1, 1), jnp.int32),
        ],
        in_specs=[smem()] + [anywhere()] * 2,
        out_specs=[hbm(), smem(), smem()],
        scratch_shapes=[
            pltpu.VMEM(polar.shape, F32),
            pltpu.VMEM(polar.shape, F32),
            pltpu.VMEM((levels, tracers, cells), F32),
            pltpu.SemaphoreType.DMA((3,)),
        ],
        compiler_params=params(8),
        name="turn",
    )(shift, pinned(polar), nearby)
    moved = []
    for lat, hop in zip(poles, hops):
        moved.append(
            lax.switch(
                hop.reshape(()),
                [
                    functools.partial(
                        lambda k, lat, x: lax.ppermute(x, AXES, circles((lat,), k)), k, lat
                    )
                    for k in range(lax.axis_size("lon"))
                ],
                turned,
            )
        )
    after, before, *moved = lax.optimization_barrier((after, before, *moved))
    edge = west_edge(step, column, north, south, after, before)
    return after, before, pinned(moved[0]), pinned(moved[1]), edge


def last_exchange(step, after, before, circle, column, north, south, shift):
    levels, tracers, cells = after.shape
    parts, groups, group = circle.shape[:3]
    shape = (parts, groups - 1, group, cells)
    turned = pl.pallas_call(
        functools.partial(rotate_kernel, step),
        out_shape=pltpu.HBM(shape, F32),
        in_specs=[smem(), anywhere()],
        out_specs=hbm(),
        scratch_shapes=[
            pltpu.VMEM(circle.shape, F32),
            pltpu.VMEM((parts * groups * group, 2 * cells), F32),
            pltpu.VMEM(shape, F32),
            pltpu.SemaphoreType.DMA((2,)),
        ],
        compiler_params=params(14),
        name="rotate",
    )(shift, circle)
    pole = lax.all_to_all(turned, "lon", 0, 0, tiled=True)
    return after, before, pole, west_edge(step, column, north, south, after, before)


def per_device(
    costate,
    diffusion,
    east_courant,
    north_courant,
    south_courant,
    polar_shift,
    owners,
    columns,
    sounding_counts,
    kernels,
    misfits,
):
    levels, tracers, rows, cells = costate.shape
    owner_rows = owners.reshape(owners.shape[0], 1, owners.shape[1])
    couplings = (north_courant, south_courant, east_courant)
    groups = levels // GROUP

    solved_shapes = [
        pltpu.HBM((levels, rows, tracers, cells), F32),
        pltpu.HBM((levels, tracers, cells), F32),
        pltpu.HBM((levels, tracers, cells), F32),
        pltpu.HBM((levels + 1, tracers, cells), F32),
        resident(groups, tracers, LANES),
    ]
    ratios = pltpu.VMEM((levels, rows, cells), F32)
    coefs = pltpu.VMEM((4, rows, tracers, cells), F32)
    field = pltpu.VMEM((levels, rows, tracers, cells), F32)
    line = pltpu.VMEM((levels, tracers, cells), F32)
    solved_scratch = [field, line, line, pltpu.VMEM((levels + 1, tracers, cells), F32)]
    solved_specs = [hbm()] * 4 + [vmem()]
    leaving = pltpu.SemaphoreType.DMA((4, groups // SPAN + 1))
    output = pltpu.VMEM(costate.shape, F32)
    semaphores = pltpu.SemaphoreType.DMA((groups // SPAN,))
    diffused, first, last, polar, column = pl.pallas_call(
        functools.partial(first_kernel, 1),
        out_shape=solved_shapes,
        in_specs=[hbm()] * 5,
        out_specs=solved_specs,
        scratch_shapes=[
            output,
            ratios,
            *solved_scratch,
            pltpu.VMEM(diffusion.shape[1:], F32),
            pltpu.VMEM((3,) + east_courant.shape, F32),
            semaphores,
            leaving,
            pltpu.SemaphoreType.DMA((4,)),
        ],
        compiler_params=params(16),
        name="first",
    )(*[pinned(x) for x in (costate, diffusion, *couplings)])
    couplings = [held(x) for x in couplings]
    diffusion = held(diffusion)
    counts, column = lax.optimization_barrier((sounding_counts, column))
    nearby = lax.ppermute(polar, AXES, circles((0, lax.axis_size("lat") - 1), 1))
    sent = packed(counts, owner_rows, columns, kernels, misfits)
    sent, nearby = lax.optimization_barrier((sent, nearby))
    nearby = pinned(nearby)
    got = lax.all_to_all(sent, AXES, 0, 0, tiled=True)
    shape = (levels, rows, tracers, cells)
    forced = forcing(1, got, shape, False)
    around = first_exchange(
        1, first, last, nearby, polar, column, *couplings[:2], polar_shift
    )
    scratch = [field, line, line]
    transfers = pltpu.SemaphoreType.DMA((4, groups // SPAN))
    solved, first, last, polar, column, surface = pl.pallas_call(
        functools.partial(middle_kernel, 1),
        out_shape=[
            *solved_shapes[:3],
            pltpu.HBM((tracers, groups + 1, GROUP, cells), F32),
            solved_shapes[4],
            resident(rows, tracers, cells),
        ],
        in_specs=[hbm(), vmem()] + [anywhere()] * 2 + [hbm()] * 2 + [vmem()] * 5,
        out_specs=solved_specs + [vmem()],
        scratch_shapes=[
            coefs,
            ratios,
            *scratch,
            line,
            *solved_scratch[:3],
            pltpu.VMEM((tracers, groups + 1, GROUP, cells), F32),
            transfers,
            leaving,
        ],
        compiler_params=params(20),
        name="middle",
    )(pinned(diffused), forced, *around, diffusion, *couplings)
    circle = lax.all_to_all(polar, "lon", 0, 0, tiled=True)
    got, column = lax.optimization_barrier((got, column))
    forced = forcing(0, got, shape, True)
    forced, first, last = lax.optimization_barrier((forced, first, last))
    around = last_exchange(
        0, *boundary_rows(first, last), circle, column, *couplings[:2], polar_shift
    )
    return tuple(
        pl.pallas_call(
            functools.partial(last_kernel, 0),
            out_shape=[
                pltpu.HBM(costate.shape, F32),
                jax.ShapeDtypeStruct((tracers, rows, cells), F32),
            ],
            in_specs=[hbm()] * 2 + [anywhere()] * 3 + [vmem()] * 5,
            out_specs=[hbm(), vmem()],
            scratch_shapes=[
                coefs,
                field,
                *scratch,
                pltpu.VMEM((tracers, groups, GROUP, cells), F32),
                output,
                pltpu.SemaphoreType.DMA((5, groups // SPAN)),
                semaphores,
            ],
            compiler_params=params(22),
            name="last",
        )(pinned(solved), pinned(forced), *around, *couplings, surface)
    )


def solution(mesh):
    return jax.shard_map(
        per_device,
        mesh=mesh,
        in_specs=(
            P(None, None, "lat", "lon"),
            P(None, None, "lat", "lon"),
            P(None, "lat", "lon"),
            P(None, "lat", "lon"),
            P(None, "lat", "lon"),
            P(),
            P(None, ("lon", "lat"), None),
            P(None, ("lon", "lat")),
            P(None, ("lon", "lat")),
            P(None, None, ("lon", "lat")),
            P(None, None, ("lon", "lat")),
        ),
        out_specs=(P(None, None, "lat", "lon"), P(None, "lat", "lon")),
        check_vma=False,
    )
```

```python
import functools

import jax
import jax.numpy as jnp
from jax import lax
from jax.experimental import pallas as pl
from jax.experimental.pallas import tpu as pltpu
from jax.sharding import PartitionSpec as P

AXES = ("lon", "lat")
LANES = 128
CAP = 16
GROUP = 8
SPAN = 3
F32 = jnp.float32
BF16 = jnp.bfloat16
MIB = 1024 * 1024


def vmem():
    return pl.BlockSpec(memory_space=pltpu.VMEM)


def smem():
    return pl.BlockSpec(memory_space=pltpu.SMEM)


def hbm():
    return pl.BlockSpec(memory_space=pltpu.HBM)


def params(limit):
    return pltpu.CompilerParams(vmem_limit_bytes=limit * MIB)


def held(x):
    return pltpu.with_memory_space_constraint(x, pltpu.VMEM)


def anywhere():
    return pl.BlockSpec(memory_space=pl.ANY)


def pinned(x):
    return pltpu.with_memory_space_constraint(x, pltpu.HBM)


def resident(*shape):
    return pltpu.VMEM(shape, F32)


def chunk(source, target, done, c):
    at = pl.ds(c * GROUP * SPAN, GROUP * SPAN)
    return pltpu.make_async_copy(source.at[at], target.at[at], done.at[c])


def at_span(g, place, act):
    if isinstance(g, int):
        if g % SPAN == place:
            act(g // SPAN)
    else:
        pl.when(lax.rem(g, SPAN) == place)(lambda: act(lax.div(g, SPAN)))


def dot(a, b, contract=((1,), (0,))):
    return lax.dot_general(a, b, (contract, ((), ())), preferred_element_type=F32)


def halves(x):
    high = x.astype(BF16)
    return high, (x - high.astype(F32)).astype(BF16)


def spare_lane(levels, tracers):
    return levels + tracers + 8


def pack_kernel(
    counts, owners, columns, kernels, misfits, out, payload, target, staged, done
):
    steps, levels, held = kernels.shape
    tracers = misfits.shape[1]
    shape = (LANES, LANES)
    half = CAP // 2
    device = lax.broadcasted_iota(jnp.int32, shape, 0)
    table = counting_table()
    for step in range(steps):
        owner = owners[step]
        live = lax.broadcasted_iota(jnp.int32, owner.shape, 1) < counts[step, 0]
        owner = jnp.where(live, owner, -1)
        seen = jnp.zeros(shape, F32)
        for start in range(0, held, LANES):
            here = owner[:, start : start + LANES]
            hot = device == here
            counted = dot(jnp.where(hot, 1.0, 0.0).astype(BF16), table)
            rank = jnp.sum(
                jnp.where(hot, counted[:, :LANES] + seen, 0.0), axis=0, keepdims=True
            )
            seen = seen + counted[:, LANES:]
            target[step : step + 1, start : start + LANES] = jnp.where(
                here >= 0, here * CAP + rank.astype(jnp.int32), -1
            )
    spare = spare_lane(levels, tracers)
    main = LANES - spare

    def fill(k, part, pieces):
        rows = jnp.concatenate(
            [jnp.zeros((x, held), F32) if isinstance(x, int) else x for x in pieces], axis=0
        )
        high, low = halves(rows)
        payload[k, :LANES, part * held : (part + 1) * held] = high
        payload[k, LANES:, part * held : (part + 1) * held] = low

    def column(step):
        x = columns[step : step + 1, :].astype(F32) + 1.0
        return jnp.where(lax.broadcasted_iota(jnp.int32, (8, held), 0) == 0, x, 0.0)

    rest = [kernels[0, main:, :], misfits[0], column(0)]
    used = levels - main + tracers + 8
    fill(0, 0, [kernels[1], misfits[1], column(1), main])
    fill(0, 1, [spare, kernels[0, :main, :]])
    fill(1, 0, [*rest, LANES - used])
    fill(1, 1, [LANES // 2, *rest, LANES // 2 - used])
    slot = target[0:1, :] & (CAP - 1)
    owner = target[0:1, :] >> (CAP.bit_length() - 1)
    lower = jnp.where((target[0:1, :] >= 0) & (slot < half), owner * half + slot, -1)
    upper = jnp.where((target[0:1, :] >= 0) & (slot >= half), owner * half + slot - half, -1)
    owned = 512 // CAP
    tiles = out.shape[0] // owned

    def copy(i):
        at = pl.ds(i * owned, owned)
        return pltpu.make_async_copy(staged.at[at], out.at[at], done.at[i])

    def place(i, carry):
        for k, ats, size, rows in (
            (0, (target[1:2, :], target[0:1, :]), owned * CAP, slice(0, CAP)),
            (1, (lower, upper), owned * half, slice(CAP, CAP + half)),
        ):
            hot = jnp.concatenate([tall_one_hot(at - i * size, size) for at in ats], axis=1)
            both = dot(hot, payload[k], ((1,), (1,)))
            both = both[:, :LANES] + both[:, LANES:]
            staged[pl.ds(i * owned, owned), rows, :] = both.reshape(owned, -1, LANES)
        copy(i).start()
        return carry

    lax.fori_loop(0, tiles, place, 0)
    for i in range(tiles):
        copy(i).wait()


def one_hot(at, size):
    at = jnp.where((at >= 0) & (at < size), at, -1).astype(F32).astype(BF16)
    shape = (size, at.shape[1])
    row = lax.broadcasted_iota(jnp.int32, shape, 0).astype(F32).astype(BF16)
    return jnp.where(row == at, jnp.ones(shape, BF16), jnp.zeros(shape, BF16))


def tall_one_hot(at, size):
    parts = [one_hot(at - start, 256) for start in range(0, size, 256)]
    return parts[0] if len(parts) == 1 else jnp.concatenate(parts, axis=0)


def counting_table():
    shape = (LANES, LANES)
    earlier = lax.broadcasted_iota(jnp.int32, shape, 0) < lax.broadcasted_iota(
        jnp.int32, shape, 1
    )
    return jnp.concatenate(
        [jnp.where(earlier, 1.0, 0.0), jnp.ones(shape, F32)], axis=1
    ).astype(BF16)


def packed(counts, owners, columns, kernels, misfits):
    steps, slots = columns.shape
    devices = lax.axis_size("lon") * lax.axis_size("lat")
    return pl.pallas_call(
        pack_kernel,
        out_shape=pltpu.HBM((devices, CAP + CAP // 2, LANES), F32),
        in_specs=[smem()] + [vmem()] * 4,
        out_specs=hbm(),
        scratch_shapes=[
            pltpu.VMEM((2, 2 * LANES, 2 * slots), BF16),
            pltpu.VMEM((steps, slots), jnp.int32),
            pltpu.VMEM((devices, CAP + CAP // 2, LANES), F32),
            pltpu.SemaphoreType.DMA((devices * CAP // 512,)),
        ],
        compiler_params=params(20),
        name="pack",
    )(counts, held(owners), held(columns), held(kernels), held(misfits))


def streamed_forcing_kernel(step, received, result, out, *scratch):
    done = scratch[-1]

    def copy(r):
        return pltpu.make_async_copy(out.at[:, r], result.at[:, r], done.at[r])

    forcing_kernel(step, received, out, *scratch[:-1], finished=lambda r: copy(r).start())
    for r in range(out.shape[1]):
        copy(r).wait()


def forcing_kernel(
    step, received, out, fields, hots, place, ordered, finished=lambda r: None
):
    levels, rows, tracers, cells = out.shape
    sources = received.shape[0]
    slots = sources * CAP
    blocks = slots // LANES
    spare = spare_lane(levels, tracers)
    data = received[:, :CAP, :].reshape(slots, LANES)
    if step == 1:
        at_column = levels + tracers

        def profile(turned):
            return turned[:levels]

    else:
        at_column = levels - (LANES - spare) + tracers
        extra = received[:, CAP:, :]
        other = pltpu.roll(extra.reshape(slots // 2, LANES), LANES // 2, 1)
        extra = jnp.concatenate([extra, other.reshape(extra.shape)], axis=1)
        lane = lax.broadcasted_iota(jnp.int32, (slots, LANES), 1)
        data = jnp.where(lane < LANES // 2, extra.reshape(slots, LANES), data)

        def profile(turned):
            return jnp.concatenate([turned[spare:], turned[: at_column - tracers]], axis=0)

    high, low = halves(data)
    fields[:, :LANES] = high
    fields[:, LANES:] = low
    shape = (8, 2 * LANES)
    pick = (lax.broadcasted_iota(jnp.int32, shape, 1) & (LANES - 1)) == at_column
    column = dot(jnp.where(pick, 1.0, 0.0).astype(BF16), fields[...], ((1,), (1,)))
    cell_row = (column.astype(jnp.int32) - 1) >> (cells.bit_length() - 1)
    sub = lax.broadcasted_iota(jnp.int32, (rows, LANES), 0)
    for b in range(blocks):
        row = cell_row[:, b * LANES : (b + 1) * LANES]
        hots[b * rows : (b + 1) * rows, :] = jnp.where(sub == row, 1.0, 0.0)
    counted = dot(hots[...].astype(BF16), counting_table())
    run = jnp.zeros((rows, LANES), F32)
    runs = []
    for b in range(blocks):
        runs.append(run)
        run = run + counted[b * rows : (b + 1) * rows, LANES:]
    filled = jnp.floor((run + (LANES - 1.0)) * (1.0 / LANES))
    start = jnp.zeros((rows, LANES), F32)
    for j in range(1, rows):
        start = start + jnp.where(sub >= j, pltpu.roll(filled, j, 0), 0.0)
    for b in range(blocks):
        hot = hots[b * rows : (b + 1) * rows, :]
        at = counted[b * rows : (b + 1) * rows, :LANES] + runs[b] + start * float(LANES)
        at = jnp.sum(hot * at, axis=0, keepdims=True)
        live = jnp.sum(hot, axis=0, keepdims=True) > 0.0
        place[:, b * LANES : (b + 1) * LANES] = jnp.where(live, at, -1.0)
    counts = [jnp.max(filled[r : r + 1, :]).astype(jnp.int32) for r in range(rows)]
    used = sum(counts)
    wide = 4 * LANES

    def sort(i, carry):
        hot = tall_one_hot(place[...] - (i * wide).astype(F32), wide)
        both = dot(hot, fields[...])
        ordered[pl.ds(pl.multiple_of(i * wide, wide), wide), :] = both[:, :LANES] + both[:, LANES:]
        return carry

    lax.fori_loop(0, (used + 3) // 4, sort, 0)
    out[...] = jnp.zeros_like(out)
    name = lax.broadcasted_iota(jnp.int32, (LANES, cells), 1).astype(F32)
    first = jnp.int32(0)
    for r in range(rows):

        def add(p, carry):
            block = ordered[pl.ds(pl.multiple_of(p * LANES, LANES), LANES), :]
            own = jnp.broadcast_to(
                block[:, at_column : at_column + 1] - (r * cells + 1.0), (LANES, cells)
            )
            hot = jnp.where(name == own, 1.0, 0.0).astype(BF16)
            turned = block.T
            product = profile(turned)[:, None, :] * turned[at_column - tracers : at_column][None]
            product = product.reshape(levels * tracers, LANES)
            total = dot(
                jnp.concatenate(halves(product), axis=1), jnp.concatenate([hot, hot], axis=0)
            )
            out[:, r, :, :] += total.reshape(levels, tracers, cells)
            return carry

        lax.fori_loop(first, first + counts[r], add, 0)
        first = first + counts[r]
        finished(r)


def forcing(step, received, shape, streamed):
    slots = received.shape[0] * CAP
    scratch = [
        pltpu.VMEM((slots, 2 * LANES), BF16),
        pltpu.VMEM((slots // LANES * shape[1], LANES), F32),
        pltpu.VMEM((1, slots), F32),
        pltpu.VMEM((slots + shape[1] * LANES, LANES), F32),
    ]
    if streamed:
        scratch = [resident(*shape), *scratch, pltpu.SemaphoreType.DMA((shape[1],))]
    return pl.pallas_call(
        functools.partial(streamed_forcing_kernel if streamed else forcing_kernel, step),
        out_shape=pltpu.HBM(shape, F32) if streamed else resident(*shape),
        in_specs=[vmem()],
        out_specs=hbm() if streamed else vmem(),
        scratch_shapes=scratch,
        compiler_params=params(20 if streamed else 16),
        name="forcing",
    )(held(received))


def shift_matrix(inner, cells):
    shape = (2 * cells, cells)
    source = lax.broadcasted_iota(jnp.int32, shape, 0)
    target = lax.broadcasted_iota(jnp.int32, shape, 1) + inner
    picks = [jnp.where(source == target + k, 1.0, 0.0).astype(BF16) for k in range(2)]
    return jnp.concatenate(picks, axis=1)


def shifted(low, high, matrix):
    row = jnp.concatenate([low, high], axis=1)
    first, rest = row.astype(BF16), None
    rest = row - first.astype(F32)
    second, third = halves(rest)
    return dot(first, matrix) + dot(second, matrix) + dot(third, matrix)


def spread(x, row, tracers):
    return jnp.broadcast_to(x[row : row + 1, :], (tracers, x.shape[1]))


def eliminate(level, above, carry, rights, ratios):
    below, ratio, values = carry
    if above is None:
        above = jnp.zeros_like(below)
    inverse = 1.0 / (1.0 + below + above + below * ratio)
    lower = below * inverse
    ratio = -above * inverse
    ratios[level] = ratio
    tracers = rights[0].shape[0]
    fresh = [
        spread(inverse, r, tracers) * rights[r] + spread(lower, r, tracers) * values[r]
        for r in range(len(rights))
    ]
    return (above, ratio, fresh)


def substitute(step, ratios, couplings, column, fields, results, done):
    diffused, first, last, polar = fields
    levels, rows, tracers, cells = diffused.shape
    lat = lax.axis_index("lat")
    at_start = lat == 0

    def picked(x):
        return jnp.where(at_start, x[step, 0:1, :], x[step, rows - 1 : rows, :])

    north, south, east = [picked(x) for x in couplings]
    own = jnp.broadcast_to(1.0 - north - south, (tracers, cells))
    side = jnp.broadcast_to(jnp.where(at_start, north, south), (tracers, cells))
    groups = levels // GROUP
    by_tracer = len(polar.shape) == 4
    if by_tracer:
        polar[:, groups, 0, :] = jnp.broadcast_to(east, (tracers, cells))
    else:
        polar[levels] = jnp.broadcast_to(east, (tracers, cells))

    chunks = groups // SPAN

    def polar_copy(at, c):
        if by_tracer:
            source, target = [x.at[:, at] for x in (polar, results[3])]
        else:
            source, target = [x.at[at] for x in (polar, results[3])]
        return pltpu.make_async_copy(source, target, done.at[3, c])

    def copies(c):
        size = SPAN if by_tracer else SPAN * GROUP
        moves = [chunk(fields[k], results[k], done.at[k], c) for k in range(3)]
        return [*moves, polar_copy(pl.ds(c * size, size), c)]

    def send(c):
        for copy in copies(c):
            copy.start()

    weight = polar_copy(pl.ds(groups if by_tracer else levels, 1), chunks)
    weight.start()
    lane = lax.broadcasted_iota(jnp.int32, (tracers, LANES), 1)

    def group(i, solved):
        at = groups - 1 - i
        west = jnp.zeros((tracers, LANES), F32)
        for j in range(GROUP - 1, -1, -1):
            level = at * GROUP + j
            ratio = ratios[level]
            fresh = []
            for r in range(rows):
                value = diffused[level, r] - spread(ratio, r, tracers) * solved[r]
                diffused[level, r] = value
                fresh.append(value)
                lanes = j * rows + r
                moved = pltpu.roll(value[:, :LANES], lanes, 1) if lanes else value[:, :LANES]
                west = jnp.where(lane == lanes, moved, west)
            solved = fresh
            first[level] = solved[0]
            last[level] = solved[rows - 1]
            row = own * jnp.where(at_start, solved[0], solved[rows - 1]) + side * jnp.where(
                at_start, solved[1], solved[rows - 2]
            )
            if by_tracer:
                polar[:, at, j, :] = row
            else:
                polar[level] = row
        column[at] = west
        at_span(at, 0, send)
        return solved

    lax.fori_loop(0, groups, group, [jnp.zeros((tracers, cells), F32)] * rows)
    weight.wait()
    for c in range(chunks):
        for copy in copies(c):
            copy.wait()


def forward_sweep(levels, rows, tracers, cells, diffusion, right_of):
    zero = jnp.zeros((rows, cells), F32)
    carry = (zero, zero, [jnp.zeros((tracers, cells), F32)] * rows)
    groups = levels // GROUP

    def one(g, j, above, carry):
        rights, ratios, store = right_of(g, j, above is None)
        carry = eliminate(g * GROUP + j, above, carry, rights, ratios)
        store(carry[2])
        return carry

    def group(g, carry):
        for j in range(GROUP):
            carry = one(g, j, diffusion(g * GROUP + j), carry)
        return carry

    carry = lax.fori_loop(0, groups - 1, group, carry)
    for j in range(GROUP):
        level = levels - GROUP + j
        carry = one(groups - 1, j, diffusion(level) if level < levels - 1 else None, carry)


def first_kernel(
    step,
    costate,
    diffusion_in,
    north_in,
    south_in,
    east_in,
    result,
    first_out,
    last_out,
    polar_out,
    column,
    staged,
    ratios,
    diffused,
    first,
    last,
    polar,
    diffusion,
    couplings,
    arrived,
    sent,
    ready,
):
    levels, tracers, rows, cells = costate.shape
    small = [pltpu.make_async_copy(diffusion_in.at[step], diffusion, ready.at[0])]
    for k, coupling in enumerate((north_in, south_in, east_in)):
        small.append(pltpu.make_async_copy(coupling, couplings.at[k], ready.at[1 + k]))
    chunk(costate, staged, arrived, 0).start()
    for copy in small:
        copy.start()
    for c in range(1, levels // (GROUP * SPAN)):
        chunk(costate, staged, arrived, c).start()
    for copy in small:
        copy.wait()

    def right_of(g, j, final):
        if j == 0:
            at_span(g, 0, lambda c: chunk(costate, staged, arrived, c).wait())
        level = g * GROUP + j
        rights = [staged[level, :, r, :] for r in range(rows)]

        def store(values):
            for r in range(rows):
                diffused[level, r] = values[r]

        return rights, ratios, store

    forward_sweep(levels, rows, tracers, cells, lambda level: diffusion[level], right_of)
    views = [couplings.at[k] for k in range(3)]
    fields = (diffused, first, last, polar)
    results = (result, first_out, last_out, polar_out)
    substitute(step, ratios, views, column, fields, results, sent)


def meridional(level, row, diffused, after, before, coefs):
    rows = diffused.shape[1]
    own, north, south = coefs
    up = diffused[level, row + 1] if row < rows - 1 else after[level]
    down = diffused[level, row - 1] if row > 0 else before[level]
    return own * diffused[level, row] + north * up + south * down


def borders_kernel(
    step,
    shift,
    column,
    north,
    south,
    after_in,
    before_in,
    polar_in,
    nearby_in,
    edge,
    turned_out,
    south_hops,
    north_hops,
    after,
    before,
    polar,
    nearby,
    turned,
    ready,
):
    rows, cells = north.shape[1:]
    circle = cells * lax.axis_size("lon")
    amounts = [
        lax.rem(shift[step, x] + 2 * circle, circle) for x in (0, shift.shape[1] - 1)
    ]
    south_hops[0, 0] = amounts[0] // cells
    north_hops[0, 0] = amounts[1] // cells
    fetches = [
        pltpu.make_async_copy(source, target, ready.at[2 + k])
        for k, (source, target) in enumerate(((polar_in, polar), (nearby_in, nearby)))
    ]
    sending = pltpu.make_async_copy(turned, turned_out, ready.at[4])
    lat = lax.axis_index("lat")
    last_lat = lax.axis_size("lat") - 1
    at_pole = (lat == 0) | (lat == last_lat)

    @pl.when(at_pole)
    def _():
        for fetch in fetches:
            fetch.start()

    finish = west_column(step, column, north, south, after_in, before_in, edge, after, before, ready)

    @pl.when(at_pole)
    def _():
        for fetch in fetches:
            fetch.wait()
        levels = turned.shape[0]
        amount = jnp.where(lat == 0, amounts[0], amounts[1])
        matrix = shift_matrix(lax.rem(amount, cells), cells)
        tracers = turned.shape[1]
        weight = shifted(polar[levels], nearby[levels], matrix)[:1, :cells]
        size = 3 * GROUP
        for i in range(levels // size):
            at = slice(i * size, (i + 1) * size)
            low, high = [x[at].reshape(size * tracers, cells) for x in (polar, nearby)]
            row = shifted(low, high, matrix)
            row = row[:, :cells] + weight * (row[:, cells:] - row[:, :cells])
            turned[at] = row.reshape(size, tracers, cells)
        sending.start()

    finish()

    @pl.when(at_pole)
    def _():
        sending.wait()


def edge_kernel(
    step, column, north, south, after_in, before_in, edge, after, before, ready
):
    west_column(step, column, north, south, after_in, before_in, edge, after, before, ready)()


def west_column(step, column, north, south, after_in, before_in, edge, after, before, ready):
    groups, tracers, lanes = column.shape
    rows, cells = north.shape[1:]
    tiles = [
        pltpu.make_async_copy(source.at[:, :, pl.ds(0, lanes)], target, ready.at[k])
        for k, (source, target) in enumerate(((after_in, after), (before_in, before)))
    ]
    for tile in tiles:
        tile.start()
    lane = lax.broadcasted_iota(jnp.int32, (tracers, lanes), 1)

    def along_lanes(x):
        shape = (rows, lanes)
        own_lane = (lax.broadcasted_iota(jnp.int32, shape, 1) & (rows - 1)) == (
            lax.broadcasted_iota(jnp.int32, shape, 0)
        )
        picked = jnp.where(own_lane, jnp.broadcast_to(x[step, :, :1], shape), 0.0)
        return jnp.broadcast_to(jnp.sum(picked, axis=0, keepdims=True), (tracers, lanes))

    n, s = along_lanes(north), along_lanes(south)
    own = 1.0 - n - s

    def group(i, carry):
        here = column[i]
        up = pltpu.roll(here, lanes - 1, 1)
        down = pltpu.roll(here, 1, 1)
        for j in range(GROUP):
            level = i * GROUP + j
            bottom, top = j * rows, j * rows + rows - 1
            up = jnp.where(lane == top, pltpu.roll(after[level], top, 1), up)
            moved = before[level]
            moved = pltpu.roll(moved, bottom, 1) if bottom else moved
            down = jnp.where(lane == bottom, moved, down)
        edge[i] = own * here + n * up + s * down
        return carry

    def finish():
        for tile in tiles:
            tile.wait()
        lax.fori_loop(0, groups, group, 0)

    return finish


def rotate_kernel(step, shift, circle_in, out, circle, pairs, turned, ready):
    parts, groups, group, cells = turned.shape
    lat = lax.axis_index("lat")
    last_lat = lax.axis_size("lat") - 1
    rows = shift.shape[1] // lax.axis_size("lat")

    @pl.when((lat == 0) | (lat == last_lat))
    def _():
        fetch = pltpu.make_async_copy(circle_in, circle, ready.at[0])
        fetch.start()
        amount = jnp.where(lat == 0, shift[step, 0], shift[step, rows * last_lat + rows - 1])
        amount = lax.rem(amount + 2 * parts * cells, parts * cells)
        hops = amount // cells
        matrix = shift_matrix(amount - hops * cells, cells)
        fetch.wait()
        height = (groups + 1) * group
        for part in range(parts):
            at = slice(part * height, (part + 1) * height)
            near = lax.rem(part + hops, parts)
            far = lax.rem(part + hops + 1, parts)
            pairs[at, :cells] = circle[near].reshape(height, cells)
            pairs[at, cells:] = circle[far].reshape(height, cells)
        batch = parts // 2
        for i in range(2):
            rows_at = slice(i * batch * height, (i + 1) * batch * height)
            row = shifted(pairs[rows_at, :cells], pairs[rows_at, cells:], matrix)
            row = row.reshape(batch, groups + 1, group, 2 * cells)
            weight = row[:, groups:, :1, :cells]
            row = row[:, :groups]
            row = row[..., :cells] + weight * (row[..., cells:] - row[..., :cells])
            turned[i * batch : (i + 1) * batch] = row
        send = pltpu.make_async_copy(turned, out, ready.at[1])
        send.start()
        send.wait()


def prepare_stencil(step, north, south, east, coefs):
    rows, cells = north.shape[1:]
    tracers = coefs.shape[2]
    for r in range(rows):
        n = north[step, r : r + 1, :]
        s = south[step, r : r + 1, :]
        coefs[0, r] = jnp.broadcast_to(1.0 - n - s, (tracers, cells))
        coefs[1, r] = jnp.broadcast_to(n, (tracers, cells))
        coefs[2, r] = jnp.broadcast_to(s, (tracers, cells))
        coefs[3, r] = jnp.broadcast_to(east[step, r : r + 1, :], (tracers, cells))


def transported(group, lane_at, diffused, after, before, edge_row, coefs, pole):
    level = group * GROUP + lane_at
    rows, tracers, cells = diffused.shape[1:]
    lat = lax.axis_index("lat")
    last = lax.broadcasted_iota(jnp.int32, (tracers, cells), 1) == cells - 1
    result = []
    for r in range(rows):
        mer = meridional(level, r, diffused, after, before, [coefs[k, r] for k in range(3)])
        arrived = pltpu.roll(edge_row, LANES - 1 - (lane_at * rows + r), 1)
        arrived = jnp.concatenate([arrived] * (cells // LANES), axis=1)
        following = jnp.where(last, arrived, pltpu.roll(mer, cells - 1, 1))
        result.append(mer + coefs[3, r] * (following - mer))
    polar = pole[:, group, lane_at, :] if len(pole.shape) == 4 else pole[level]
    result[0] = jnp.where(lat == 0, polar, result[0])
    result[rows - 1] = jnp.where(lat == lax.axis_size("lat") - 1, polar, result[rows - 1])
    return result


def streams(sources, targets, poles, pole, done):
    lat = lax.axis_index("lat")
    last_lat = lax.axis_size("lat") - 1
    last = len(sources)

    def polar_copy(source, c):
        if len(pole.shape) == 4:
            at = pl.ds(c * SPAN, SPAN)
            return pltpu.make_async_copy(source.at[:, at], pole.at[:, at], done.at[last, c])
        return chunk(source, pole, done.at[last], c)

    for g in range(targets[0].shape[0] // (GROUP * SPAN)):
        for k, (source, target) in enumerate(zip(sources, targets)):
            chunk(source, target, done.at[k], g).start()

        @pl.when(lat == 0)
        def _():
            polar_copy(poles[0], g).start()

        @pl.when(lat == last_lat)
        def _():
            polar_copy(poles[-1], g).start()

    def wait(g):
        for k, (source, target) in enumerate(zip(sources, targets)):
            chunk(source, target, done.at[k], g).wait()

        @pl.when((lat == 0) | (lat == last_lat))
        def _():
            polar_copy(poles[0], g).wait()

    return wait


def middle_kernel(
    step,
    before_step,
    forced,
    after_in,
    before_in,
    south_pole,
    north_pole,
    edge,
    diffusion,
    north,
    south,
    east,
    result,
    first_out,
    last_out,
    polar_out,
    column,
    surface,
    coefs,
    ratios,
    diffused,
    after,
    before,
    pole,
    solved,
    first,
    last,
    polar,
    arrived,
    sent,
):
    levels, rows, tracers, cells = diffused.shape
    wait = streams(
        (before_step, after_in, before_in),
        (diffused, after, before),
        (south_pole, north_pole),
        pole,
        arrived,
    )
    prepare_stencil(step, north, south, east, coefs)

    def right_of(g, j, final):
        if j == 0:
            at_span(g, 0, wait)
        level = g * GROUP + j
        rights = transported(g, j, diffused, after, before, edge[g], coefs, pole)
        rights = [rights[r] + forced[level, r] for r in range(rows)]
        if final:
            for r in range(rows):
                surface[r] = rights[r]

        def store(values):
            for r in range(rows):
                solved[level, r] = values[r]

        return rights, ratios, store

    forward_sweep(
        levels, rows, tracers, cells, lambda level: diffusion[step - 1, level], right_of
    )
    couplings = (north, south, east)
    fields = (solved, first, last, polar)
    results = (result, first_out, last_out, polar_out)
    substitute(step - 1, ratios, couplings, column, fields, results, sent)


def last_kernel(
    step,
    before_step,
    forcing_in,
    after_in,
    before_in,
    pole_in,
    edge,
    north,
    south,
    east,
    surface,
    state,
    gradient,
    coefs,
    diffused,
    forced,
    after,
    before,
    pole,
    staged,
    arrived,
    sent,
):
    levels, rows, tracers, cells = diffused.shape
    wait = streams(
        (before_step, forcing_in, after_in, before_in),
        (diffused, forced, after, before),
        (pole_in,),
        pole,
        arrived,
    )
    prepare_stencil(step, north, south, east, coefs)

    def group(g, carry):
        at_span(g, 0, wait)
        edge_row = edge[g]
        for j in range(GROUP):
            level = g * GROUP + j
            values = transported(g, j, diffused, after, before, edge_row, coefs, pole)
            for r in range(rows):
                staged[level, :, r, :] = values[r] + forced[level, r]
        at_span(g, SPAN - 1, lambda c: chunk(staged, state, sent, c).start())
        return carry

    lax.fori_loop(0, levels // GROUP, group, 0)
    for r in range(rows):
        gradient[:, r, :] = surface[r] + staged[levels - 1, :, r, :]
    for c in range(levels // (GROUP * SPAN)):
        chunk(staged, state, sent, c).wait()


def boundary_rows(first, last):
    up = [(i, i + 1) for i in range(lax.axis_size("lat") - 1)]
    down = [(j, i) for i, j in up]
    return lax.ppermute(first, "lat", down), lax.ppermute(last, "lat", up)


def circles(lats, hops):
    lat_count = lax.axis_size("lat")
    lon_count = lax.axis_size("lon")
    return [
        (((j + hops) % lon_count) * lat_count + lat, j * lat_count + lat)
        for lat in lats
        for j in range(lon_count)
    ]


def westward(edge):
    count = lax.axis_size("lon")
    return held(lax.ppermute(edge, "lon", [(i, (i - 1) % count) for i in range(count)]))


def first_exchange(step, after, before, nearby, polar, column, north, south, shift):
    poles = (0, lax.axis_size("lat") - 1)
    levels, tracers, cells = after.shape
    edge, turned, *hops = pl.pallas_call(
        functools.partial(borders_kernel, step),
        out_shape=[
            resident(*column.shape),
            pltpu.HBM((levels, tracers, cells), F32),
            jax.ShapeDtypeStruct((1, 1), jnp.int32),
            jax.ShapeDtypeStruct((1, 1), jnp.int32),
        ],
        in_specs=[smem()] + [vmem()] * 3 + [anywhere()] * 4,
        out_specs=[vmem(), hbm(), smem(), smem()],
        scratch_shapes=[
            pltpu.VMEM((levels, tracers, LANES), F32),
            pltpu.VMEM((levels, tracers, LANES), F32),
            pltpu.VMEM(polar.shape, F32),
            pltpu.VMEM(polar.shape, F32),
            pltpu.VMEM((levels, tracers, cells), F32),
            pltpu.SemaphoreType.DMA((5,)),
        ],
        compiler_params=params(8),
        name="borders",
    )(shift, column, north, south, after, before, pinned(polar), nearby)
    edge = westward(edge)
    moved = []
    for lat, hop in zip(poles, hops):
        moved.append(
            lax.switch(
                hop.reshape(()),
                [
                    functools.partial(
                        lambda k, lat, x: lax.ppermute(x, AXES, circles((lat,), k)), k, lat
                    )
                    for k in range(lax.axis_size("lon"))
                ],
                turned,
            )
        )
    return after, before, pinned(moved[0]), pinned(moved[1]), edge


def last_exchange(step, after, before, circle, column, north, south, shift):
    levels, tracers, cells = after.shape
    parts, groups, group = circle.shape[:3]
    shape = (parts, groups - 1, group, cells)
    turned = pl.pallas_call(
        functools.partial(rotate_kernel, step),
        out_shape=pltpu.HBM(shape, F32),
        in_specs=[smem(), anywhere()],
        out_specs=hbm(),
        scratch_shapes=[
            pltpu.VMEM(circle.shape, F32),
            pltpu.VMEM((parts * groups * group, 2 * cells), F32),
            pltpu.VMEM(shape, F32),
            pltpu.SemaphoreType.DMA((2,)),
        ],
        compiler_params=params(14),
        name="rotate",
    )(shift, circle)
    pole = lax.all_to_all(turned, "lon", 0, 0, tiled=True)
    edge = pl.pallas_call(
        functools.partial(edge_kernel, step),
        out_shape=resident(*column.shape),
        in_specs=[vmem()] * 3 + [anywhere()] * 2,
        out_specs=vmem(),
        scratch_shapes=[
            pltpu.VMEM((levels, tracers, LANES), F32),
            pltpu.VMEM((levels, tracers, LANES), F32),
            pltpu.SemaphoreType.DMA((2,)),
        ],
        compiler_params=params(4),
        name="edge",
    )(column, north, south, after, before)
    return after, before, pole, westward(edge)


def per_device(
    costate,
    diffusion,
    east_courant,
    north_courant,
    south_courant,
    polar_shift,
    owners,
    columns,
    sounding_counts,
    kernels,
    misfits,
):
    levels, tracers, rows, cells = costate.shape
    owner_rows = owners.reshape(owners.shape[0], 1, owners.shape[1])
    couplings = (north_courant, south_courant, east_courant)
    groups = levels // GROUP

    solved_shapes = [
        pltpu.HBM((levels, rows, tracers, cells), F32),
        pltpu.HBM((levels, tracers, cells), F32),
        pltpu.HBM((levels, tracers, cells), F32),
        pltpu.HBM((levels + 1, tracers, cells), F32),
        resident(groups, tracers, LANES),
    ]
    ratios = pltpu.VMEM((levels, rows, cells), F32)
    coefs = pltpu.VMEM((4, rows, tracers, cells), F32)
    field = pltpu.VMEM((levels, rows, tracers, cells), F32)
    line = pltpu.VMEM((levels, tracers, cells), F32)
    solved_scratch = [field, line, line, pltpu.VMEM((levels + 1, tracers, cells), F32)]
    solved_specs = [hbm()] * 4 + [vmem()]
    leaving = pltpu.SemaphoreType.DMA((4, groups // SPAN + 1))
    output = pltpu.VMEM(costate.shape, F32)
    semaphores = pltpu.SemaphoreType.DMA((groups // SPAN,))
    diffused, first, last, polar, column = pl.pallas_call(
        functools.partial(first_kernel, 1),
        out_shape=solved_shapes,
        in_specs=[hbm()] * 5,
        out_specs=solved_specs,
        scratch_shapes=[
            output,
            ratios,
            *solved_scratch,
            pltpu.VMEM(diffusion.shape[1:], F32),
            pltpu.VMEM((3,) + east_courant.shape, F32),
            semaphores,
            leaving,
            pltpu.SemaphoreType.DMA((4,)),
        ],
        compiler_params=params(16),
        name="first",
    )(*[pinned(x) for x in (costate, diffusion, *couplings)])
    couplings = [held(x) for x in couplings]
    diffusion = held(diffusion)
    counts, column = lax.optimization_barrier((sounding_counts, column))
    nearby = lax.ppermute(polar, AXES, circles((0, lax.axis_size("lat") - 1), 1))
    around = (*boundary_rows(first, last), nearby)
    sent = packed(counts, owner_rows, columns, kernels, misfits)
    sent, *around = lax.optimization_barrier((sent, *around))
    around = [pinned(x) for x in around]
    got = lax.all_to_all(sent, AXES, 0, 0, tiled=True)
    shape = (levels, rows, tracers, cells)
    forced = forcing(1, got, shape, False)
    around = first_exchange(1, *around, polar, column, *couplings[:2], polar_shift)
    scratch = [field, line, line]
    transfers = pltpu.SemaphoreType.DMA((4, groups // SPAN))
    solved, first, last, polar, column, surface = pl.pallas_call(
        functools.partial(middle_kernel, 1),
        out_shape=[
            *solved_shapes[:3],
            pltpu.HBM((tracers, groups + 1, GROUP, cells), F32),
            solved_shapes[4],
            resident(rows, tracers, cells),
        ],
        in_specs=[hbm(), vmem()] + [anywhere()] * 2 + [hbm()] * 2 + [vmem()] * 5,
        out_specs=solved_specs + [vmem()],
        scratch_shapes=[
            coefs,
            ratios,
            *scratch,
            line,
            *solved_scratch[:3],
            pltpu.VMEM((tracers, groups + 1, GROUP, cells), F32),
            transfers,
            leaving,
        ],
        compiler_params=params(20),
        name="middle",
    )(pinned(diffused), forced, *around, diffusion, *couplings)
    circle = lax.all_to_all(polar, "lon", 0, 0, tiled=True)
    got, column = lax.optimization_barrier((got, column))
    forced = forcing(0, got, shape, True)
    forced, first, last = lax.optimization_barrier((forced, first, last))
    around = last_exchange(
        0, *boundary_rows(first, last), circle, column, *couplings[:2], polar_shift
    )
    return tuple(
        pl.pallas_call(
            functools.partial(last_kernel, 0),
            out_shape=[
                pltpu.HBM(costate.shape, F32),
                jax.ShapeDtypeStruct((tracers, rows, cells), F32),
            ],
            in_specs=[hbm()] * 2 + [anywhere()] * 3 + [vmem()] * 5,
            out_specs=[hbm(), vmem()],
            scratch_shapes=[
                coefs,
                field,
                *scratch,
                pltpu.VMEM((tracers, groups, GROUP, cells), F32),
                output,
                pltpu.SemaphoreType.DMA((5, groups // SPAN)),
                semaphores,
            ],
            compiler_params=params(22),
            name="last",
        )(pinned(solved), pinned(forced), *around, *couplings, surface)
    )


def solution(mesh):
    return jax.shard_map(
        per_device,
        mesh=mesh,
        in_specs=(
            P(None, None, "lat", "lon"),
            P(None, None, "lat", "lon"),
            P(None, "lat", "lon"),
            P(None, "lat", "lon"),
            P(None, "lat", "lon"),
            P(),
            P(None, ("lon", "lat"), None),
            P(None, ("lon", "lat")),
            P(None, ("lon", "lat")),
            P(None, None, ("lon", "lat")),
            P(None, None, ("lon", "lat")),
        ),
        out_specs=(P(None, None, "lat", "lon"), P(None, "lat", "lon")),
        check_vma=False,
    )
```

```python
import functools

import jax
import jax.numpy as jnp
from jax import lax
from jax.experimental import pallas as pl
from jax.experimental.pallas import tpu as pltpu
from jax.sharding import PartitionSpec as P

AXES = ("lon", "lat")
LANES = 128
CAP = 16
GROUP = 8
SPAN = 3
F32 = jnp.float32
BF16 = jnp.bfloat16
MIB = 1024 * 1024


def vmem():
    return pl.BlockSpec(memory_space=pltpu.VMEM)


def smem():
    return pl.BlockSpec(memory_space=pltpu.SMEM)


def hbm():
    return pl.BlockSpec(memory_space=pltpu.HBM)


def params(limit):
    return pltpu.CompilerParams(vmem_limit_bytes=limit * MIB)


def held(x):
    return pltpu.with_memory_space_constraint(x, pltpu.VMEM)


def anywhere():
    return pl.BlockSpec(memory_space=pl.ANY)


def pinned(x):
    return pltpu.with_memory_space_constraint(x, pltpu.HBM)


def resident(*shape):
    return pltpu.VMEM(shape, F32)


def chunk(source, target, done, c):
    at = pl.ds(c * GROUP * SPAN, GROUP * SPAN)
    return pltpu.make_async_copy(source.at[at], target.at[at], done.at[c])


def at_span(g, place, act):
    if isinstance(g, int):
        if g % SPAN == place:
            act(g // SPAN)
    else:
        pl.when(lax.rem(g, SPAN) == place)(lambda: act(lax.div(g, SPAN)))


def dot(a, b, contract=((1,), (0,))):
    return lax.dot_general(a, b, (contract, ((), ())), preferred_element_type=F32)


def halves(x):
    high = x.astype(BF16)
    return high, (x - high.astype(F32)).astype(BF16)


def spare_lane(levels, tracers):
    return levels + tracers + 8


def pack_kernel(
    counts, owners, columns, kernels, misfits, out, payload, target, staged, done
):
    steps, levels, held = kernels.shape
    tracers = misfits.shape[1]
    shape = (LANES, LANES)
    half = CAP // 2
    device = lax.broadcasted_iota(jnp.int32, shape, 0)
    table = counting_table()
    for step in range(steps):
        owner = owners[step]
        live = lax.broadcasted_iota(jnp.int32, owner.shape, 1) < counts[step, 0]
        owner = jnp.where(live, owner, -1)
        seen = jnp.zeros(shape, F32)
        for start in range(0, held, LANES):
            here = owner[:, start : start + LANES]
            hot = device == here
            counted = dot(jnp.where(hot, 1.0, 0.0).astype(BF16), table)
            rank = jnp.sum(
                jnp.where(hot, counted[:, :LANES] + seen, 0.0), axis=0, keepdims=True
            )
            seen = seen + counted[:, LANES:]
            target[step : step + 1, start : start + LANES] = jnp.where(
                here >= 0, here * CAP + rank.astype(jnp.int32), -1
            )
    spare = spare_lane(levels, tracers)
    main = LANES - spare

    def fill(k, part, pieces):
        rows = jnp.concatenate(
            [jnp.zeros((x, held), F32) if isinstance(x, int) else x for x in pieces], axis=0
        )
        high, low = halves(rows)
        payload[k, :LANES, part * held : (part + 1) * held] = high
        payload[k, LANES:, part * held : (part + 1) * held] = low

    def column(step):
        x = columns[step : step + 1, :].astype(F32) + 1.0
        return jnp.where(lax.broadcasted_iota(jnp.int32, (8, held), 0) == 0, x, 0.0)

    rest = [kernels[0, main:, :], misfits[0], column(0)]
    used = levels - main + tracers + 8
    fill(0, 0, [kernels[1], misfits[1], column(1), main])
    fill(0, 1, [spare, kernels[0, :main, :]])
    fill(1, 0, [*rest, LANES - used])
    fill(1, 1, [LANES // 2, *rest, LANES // 2 - used])
    slot = target[0:1, :] & (CAP - 1)
    owner = target[0:1, :] >> (CAP.bit_length() - 1)
    lower = jnp.where((target[0:1, :] >= 0) & (slot < half), owner * half + slot, -1)
    upper = jnp.where((target[0:1, :] >= 0) & (slot >= half), owner * half + slot - half, -1)
    owned = 512 // CAP
    tiles = out.shape[0] // owned

    def copy(i):
        at = pl.ds(i * owned, owned)
        return pltpu.make_async_copy(staged.at[at], out.at[at], done.at[i])

    def place(i, carry):
        for k, ats, size, rows in (
            (0, (target[1:2, :], target[0:1, :]), owned * CAP, slice(0, CAP)),
            (1, (lower, upper), owned * half, slice(CAP, CAP + half)),
        ):
            hot = jnp.concatenate([tall_one_hot(at - i * size, size) for at in ats], axis=1)
            both = dot(hot, payload[k], ((1,), (1,)))
            both = both[:, :LANES] + both[:, LANES:]
            staged[pl.ds(i * owned, owned), rows, :] = both.reshape(owned, -1, LANES)
        copy(i).start()
        return carry

    lax.fori_loop(0, tiles, place, 0)
    for i in range(tiles):
        copy(i).wait()


def one_hot(at, size):
    at = jnp.where((at >= 0) & (at < size), at, -1).astype(F32).astype(BF16)
    shape = (size, at.shape[1])
    row = lax.broadcasted_iota(jnp.int32, shape, 0).astype(F32).astype(BF16)
    return jnp.where(row == at, jnp.ones(shape, BF16), jnp.zeros(shape, BF16))


def tall_one_hot(at, size):
    parts = [one_hot(at - start, 256) for start in range(0, size, 256)]
    return parts[0] if len(parts) == 1 else jnp.concatenate(parts, axis=0)


def counting_table():
    shape = (LANES, LANES)
    earlier = lax.broadcasted_iota(jnp.int32, shape, 0) < lax.broadcasted_iota(
        jnp.int32, shape, 1
    )
    return jnp.concatenate(
        [jnp.where(earlier, 1.0, 0.0), jnp.ones(shape, F32)], axis=1
    ).astype(BF16)


def packed(counts, owners, columns, kernels, misfits):
    steps, slots = columns.shape
    devices = lax.axis_size("lon") * lax.axis_size("lat")
    return pl.pallas_call(
        pack_kernel,
        out_shape=pltpu.HBM((devices, CAP + CAP // 2, LANES), F32),
        in_specs=[smem()] + [vmem()] * 4,
        out_specs=hbm(),
        scratch_shapes=[
            pltpu.VMEM((2, 2 * LANES, 2 * slots), BF16),
            pltpu.VMEM((steps, slots), jnp.int32),
            pltpu.VMEM((devices, CAP + CAP // 2, LANES), F32),
            pltpu.SemaphoreType.DMA((devices * CAP // 512,)),
        ],
        compiler_params=params(20),
        name="pack",
    )(counts, held(owners), held(columns), held(kernels), held(misfits))


def streamed_forcing_kernel(step, received, result, out, *scratch):
    done = scratch[-1]

    def copy(r):
        return pltpu.make_async_copy(out.at[:, r], result.at[:, r], done.at[r])

    forcing_kernel(step, received, out, *scratch[:-1], finished=lambda r: copy(r).start())
    for r in range(out.shape[1]):
        copy(r).wait()


def forcing_kernel(
    step, received, out, fields, hots, place, ordered, finished=lambda r: None
):
    levels, rows, tracers, cells = out.shape
    sources = received.shape[0]
    slots = sources * CAP
    blocks = slots // LANES
    spare = spare_lane(levels, tracers)
    data = received[:, :CAP, :].reshape(slots, LANES)
    if step == 1:
        at_column = levels + tracers

        def profile(turned):
            return turned[:levels]

    else:
        at_column = levels - (LANES - spare) + tracers
        extra = received[:, CAP:, :]
        other = pltpu.roll(extra.reshape(slots // 2, LANES), LANES // 2, 1)
        extra = jnp.concatenate([extra, other.reshape(extra.shape)], axis=1)
        lane = lax.broadcasted_iota(jnp.int32, (slots, LANES), 1)
        data = jnp.where(lane < LANES // 2, extra.reshape(slots, LANES), data)

        def profile(turned):
            return jnp.concatenate([turned[spare:], turned[: at_column - tracers]], axis=0)

    high, low = halves(data)
    fields[:, :LANES] = high
    fields[:, LANES:] = low
    shape = (8, 2 * LANES)
    pick = (lax.broadcasted_iota(jnp.int32, shape, 1) & (LANES - 1)) == at_column
    column = dot(jnp.where(pick, 1.0, 0.0).astype(BF16), fields[...], ((1,), (1,)))
    cell_row = (column.astype(jnp.int32) - 1) >> (cells.bit_length() - 1)
    sub = lax.broadcasted_iota(jnp.int32, (rows, LANES), 0)
    for b in range(blocks):
        row = cell_row[:, b * LANES : (b + 1) * LANES]
        hots[b * rows : (b + 1) * rows, :] = jnp.where(sub == row, 1.0, 0.0)
    counted = dot(hots[...].astype(BF16), counting_table())
    run = jnp.zeros((rows, LANES), F32)
    runs = []
    for b in range(blocks):
        runs.append(run)
        run = run + counted[b * rows : (b + 1) * rows, LANES:]
    filled = jnp.floor((run + (LANES - 1.0)) * (1.0 / LANES))
    start = jnp.zeros((rows, LANES), F32)
    for j in range(1, rows):
        start = start + jnp.where(sub >= j, pltpu.roll(filled, j, 0), 0.0)
    for b in range(blocks):
        hot = hots[b * rows : (b + 1) * rows, :]
        at = counted[b * rows : (b + 1) * rows, :LANES] + runs[b] + start * float(LANES)
        at = jnp.sum(hot * at, axis=0, keepdims=True)
        live = jnp.sum(hot, axis=0, keepdims=True) > 0.0
        place[:, b * LANES : (b + 1) * LANES] = jnp.where(live, at, -1.0)
    counts = [jnp.max(filled[r : r + 1, :]).astype(jnp.int32) for r in range(rows)]
    used = sum(counts)
    wide = 4 * LANES

    def sort(i, carry):
        hot = tall_one_hot(place[...] - (i * wide).astype(F32), wide)
        both = dot(hot, fields[...])
        ordered[pl.ds(pl.multiple_of(i * wide, wide), wide), :] = both[:, :LANES] + both[:, LANES:]
        return carry

    lax.fori_loop(0, (used + 3) // 4, sort, 0)
    out[...] = jnp.zeros_like(out)
    name = lax.broadcasted_iota(jnp.int32, (LANES, cells), 1).astype(F32)
    first = jnp.int32(0)
    for r in range(rows):

        def add(p, carry):
            block = ordered[pl.ds(pl.multiple_of(p * LANES, LANES), LANES), :]
            own = jnp.broadcast_to(
                block[:, at_column : at_column + 1] - (r * cells + 1.0), (LANES, cells)
            )
            hot = jnp.where(name == own, 1.0, 0.0).astype(BF16)
            turned = block.T
            product = profile(turned)[:, None, :] * turned[at_column - tracers : at_column][None]
            product = product.reshape(levels * tracers, LANES)
            total = dot(
                jnp.concatenate(halves(product), axis=1), jnp.concatenate([hot, hot], axis=0)
            )
            out[:, r, :, :] += total.reshape(levels, tracers, cells)
            return carry

        lax.fori_loop(first, first + counts[r], add, 0)
        first = first + counts[r]
        finished(r)


def forcing(step, received, shape, streamed):
    slots = received.shape[0] * CAP
    scratch = [
        pltpu.VMEM((slots, 2 * LANES), BF16),
        pltpu.VMEM((slots // LANES * shape[1], LANES), F32),
        pltpu.VMEM((1, slots), F32),
        pltpu.VMEM((slots + shape[1] * LANES, LANES), F32),
    ]
    if streamed:
        scratch = [resident(*shape), *scratch, pltpu.SemaphoreType.DMA((shape[1],))]
    return pl.pallas_call(
        functools.partial(streamed_forcing_kernel if streamed else forcing_kernel, step),
        out_shape=pltpu.HBM(shape, F32) if streamed else resident(*shape),
        in_specs=[vmem()],
        out_specs=hbm() if streamed else vmem(),
        scratch_shapes=scratch,
        compiler_params=params(20 if streamed else 16),
        name="forcing",
    )(held(received))


def shift_matrix(inner, cells):
    shape = (2 * cells, cells)
    source = lax.broadcasted_iota(jnp.int32, shape, 0)
    target = lax.broadcasted_iota(jnp.int32, shape, 1) + inner
    picks = [jnp.where(source == target + k, 1.0, 0.0).astype(BF16) for k in range(2)]
    return jnp.concatenate(picks, axis=1)


def shifted(low, high, matrix):
    row = jnp.concatenate([low, high], axis=1)
    first, rest = row.astype(BF16), None
    rest = row - first.astype(F32)
    second, third = halves(rest)
    return dot(first, matrix) + dot(second, matrix) + dot(third, matrix)


def spread(x, row, tracers):
    return jnp.broadcast_to(x[row : row + 1, :], (tracers, x.shape[1]))


def eliminate(level, above, carry, rights, ratios):
    below, ratio, values = carry
    if above is None:
        above = jnp.zeros_like(below)
    inverse = 1.0 / (1.0 + below + above + below * ratio)
    lower = below * inverse
    ratio = -above * inverse
    ratios[level] = ratio
    tracers = rights[0].shape[0]
    fresh = [
        spread(inverse, r, tracers) * rights[r] + spread(lower, r, tracers) * values[r]
        for r in range(len(rights))
    ]
    return (above, ratio, fresh)


def substitute(step, ratios, couplings, column, fields, results, done):
    diffused, first, last, polar = fields
    levels, rows, tracers, cells = diffused.shape
    lat = lax.axis_index("lat")
    at_start = lat == 0

    def picked(x):
        return jnp.where(at_start, x[step, 0:1, :], x[step, rows - 1 : rows, :])

    north, south, east = [picked(x) for x in couplings]
    own = jnp.broadcast_to(1.0 - north - south, (tracers, cells))
    side = jnp.broadcast_to(jnp.where(at_start, north, south), (tracers, cells))
    groups = levels // GROUP
    by_tracer = len(polar.shape) == 4
    if by_tracer:
        polar[:, groups, 0, :] = jnp.broadcast_to(east, (tracers, cells))
    else:
        polar[levels] = jnp.broadcast_to(east, (tracers, cells))

    chunks = groups // SPAN

    def polar_copy(at, c):
        if by_tracer:
            source, target = [x.at[:, at] for x in (polar, results[3])]
        else:
            source, target = [x.at[at] for x in (polar, results[3])]
        return pltpu.make_async_copy(source, target, done.at[3, c])

    def copies(c):
        size = SPAN if by_tracer else SPAN * GROUP
        moves = [chunk(fields[k], results[k], done.at[k], c) for k in range(3)]
        return [*moves, polar_copy(pl.ds(c * size, size), c)]

    def send(c):
        for copy in copies(c):
            copy.start()

    weight = polar_copy(pl.ds(groups if by_tracer else levels, 1), chunks)
    weight.start()
    lane = lax.broadcasted_iota(jnp.int32, (tracers, LANES), 1)

    def group(i, solved):
        at = groups - 1 - i
        west = jnp.zeros((tracers, LANES), F32)
        for j in range(GROUP - 1, -1, -1):
            level = at * GROUP + j
            ratio = ratios[level]
            fresh = []
            for r in range(rows):
                value = diffused[level, r] - spread(ratio, r, tracers) * solved[r]
                diffused[level, r] = value
                fresh.append(value)
                lanes = j * rows + r
                moved = pltpu.roll(value[:, :LANES], lanes, 1) if lanes else value[:, :LANES]
                west = jnp.where(lane == lanes, moved, west)
            solved = fresh
            first[level] = solved[0]
            last[level] = solved[rows - 1]
            row = own * jnp.where(at_start, solved[0], solved[rows - 1]) + side * jnp.where(
                at_start, solved[1], solved[rows - 2]
            )
            if by_tracer:
                polar[:, at, j, :] = row
            else:
                polar[level] = row
        column[at] = west
        at_span(at, 0, send)
        return solved

    lax.fori_loop(0, groups, group, [jnp.zeros((tracers, cells), F32)] * rows)
    weight.wait()
    for c in range(chunks):
        for copy in copies(c):
            copy.wait()


def forward_sweep(levels, rows, tracers, cells, diffusion, right_of):
    zero = jnp.zeros((rows, cells), F32)
    carry = (zero, zero, [jnp.zeros((tracers, cells), F32)] * rows)
    groups = levels // GROUP

    def one(g, j, above, carry):
        rights, ratios, store = right_of(g, j, above is None)
        carry = eliminate(g * GROUP + j, above, carry, rights, ratios)
        store(carry[2])
        return carry

    def group(g, carry):
        for j in range(GROUP):
            carry = one(g, j, diffusion(g * GROUP + j), carry)
        return carry

    carry = lax.fori_loop(0, groups - 1, group, carry)
    for j in range(GROUP):
        level = levels - GROUP + j
        carry = one(groups - 1, j, diffusion(level) if level < levels - 1 else None, carry)


def first_kernel(
    step,
    costate,
    diffusion_in,
    north_in,
    south_in,
    east_in,
    result,
    first_out,
    last_out,
    polar_out,
    column,
    staged,
    ratios,
    diffused,
    first,
    last,
    polar,
    diffusion,
    couplings,
    arrived,
    sent,
    ready,
):
    levels, tracers, rows, cells = costate.shape
    small = [pltpu.make_async_copy(diffusion_in.at[step], diffusion, ready.at[0])]
    for k, coupling in enumerate((north_in, south_in, east_in)):
        small.append(pltpu.make_async_copy(coupling, couplings.at[k], ready.at[1 + k]))
    chunk(costate, staged, arrived, 0).start()
    for copy in small:
        copy.start()
    for c in range(1, levels // (GROUP * SPAN)):
        chunk(costate, staged, arrived, c).start()
    for copy in small:
        copy.wait()

    def right_of(g, j, final):
        if j == 0:
            at_span(g, 0, lambda c: chunk(costate, staged, arrived, c).wait())
        level = g * GROUP + j
        rights = [staged[level, :, r, :] for r in range(rows)]

        def store(values):
            for r in range(rows):
                diffused[level, r] = values[r]

        return rights, ratios, store

    forward_sweep(levels, rows, tracers, cells, lambda level: diffusion[level], right_of)
    views = [couplings.at[k] for k in range(3)]
    fields = (diffused, first, last, polar)
    results = (result, first_out, last_out, polar_out)
    substitute(step, ratios, views, column, fields, results, sent)


def meridional(level, row, diffused, after, before, coefs):
    rows = diffused.shape[1]
    own, north, south = coefs
    up = diffused[level, row + 1] if row < rows - 1 else after[level]
    down = diffused[level, row - 1] if row > 0 else before[level]
    return own * diffused[level, row] + north * up + south * down


def borders_kernel(
    step,
    shift,
    column,
    north,
    south,
    after_in,
    before_in,
    polar_in,
    nearby_in,
    edge,
    turned_out,
    south_hops,
    north_hops,
    after,
    before,
    polar,
    nearby,
    turned,
    ready,
):
    rows, cells = north.shape[1:]
    circle = cells * lax.axis_size("lon")
    amounts = [
        lax.rem(shift[step, x] + 2 * circle, circle) for x in (0, shift.shape[1] - 1)
    ]
    south_hops[0, 0] = amounts[0] // cells
    north_hops[0, 0] = amounts[1] // cells
    fetches = [
        pltpu.make_async_copy(source, target, ready.at[2 + k])
        for k, (source, target) in enumerate(((polar_in, polar), (nearby_in, nearby)))
    ]
    sending = pltpu.make_async_copy(turned, turned_out, ready.at[4])
    lat = lax.axis_index("lat")
    last_lat = lax.axis_size("lat") - 1
    at_pole = (lat == 0) | (lat == last_lat)

    @pl.when(at_pole)
    def _():
        for fetch in fetches:
            fetch.start()

    finish = west_column(step, column, north, south, after_in, before_in, edge, after, before, ready)

    @pl.when(at_pole)
    def _():
        for fetch in fetches:
            fetch.wait()
        levels = turned.shape[0]
        amount = jnp.where(lat == 0, amounts[0], amounts[1])
        matrix = shift_matrix(lax.rem(amount, cells), cells)
        tracers = turned.shape[1]
        weight = shifted(polar[levels], nearby[levels], matrix)[:1, :cells]
        size = 3 * GROUP
        for i in range(levels // size):
            at = slice(i * size, (i + 1) * size)
            low, high = [x[at].reshape(size * tracers, cells) for x in (polar, nearby)]
            row = shifted(low, high, matrix)
            row = row[:, :cells] + weight * (row[:, cells:] - row[:, :cells])
            turned[at] = row.reshape(size, tracers, cells)
        sending.start()

    finish()

    @pl.when(at_pole)
    def _():
        sending.wait()


def edge_kernel(
    step, column, north, south, after_in, before_in, edge, after, before, ready
):
    west_column(step, column, north, south, after_in, before_in, edge, after, before, ready)()


def west_column(step, column, north, south, after_in, before_in, edge, after, before, ready):
    groups, tracers, lanes = column.shape
    rows, cells = north.shape[1:]
    tiles = [
        pltpu.make_async_copy(source.at[:, :, pl.ds(0, lanes)], target, ready.at[k])
        for k, (source, target) in enumerate(((after_in, after), (before_in, before)))
    ]
    for tile in tiles:
        tile.start()
    lane = lax.broadcasted_iota(jnp.int32, (tracers, lanes), 1)

    def along_lanes(x):
        shape = (rows, lanes)
        own_lane = (lax.broadcasted_iota(jnp.int32, shape, 1) & (rows - 1)) == (
            lax.broadcasted_iota(jnp.int32, shape, 0)
        )
        picked = jnp.where(own_lane, jnp.broadcast_to(x[step, :, :1], shape), 0.0)
        return jnp.broadcast_to(jnp.sum(picked, axis=0, keepdims=True), (tracers, lanes))

    n, s = along_lanes(north), along_lanes(south)
    own = 1.0 - n - s

    def group(i, carry):
        here = column[i]
        up = pltpu.roll(here, lanes - 1, 1)
        down = pltpu.roll(here, 1, 1)
        for j in range(GROUP):
            level = i * GROUP + j
            bottom, top = j * rows, j * rows + rows - 1
            up = jnp.where(lane == top, pltpu.roll(after[level], top, 1), up)
            moved = before[level]
            moved = pltpu.roll(moved, bottom, 1) if bottom else moved
            down = jnp.where(lane == bottom, moved, down)
        edge[i] = own * here + n * up + s * down
        return carry

    def finish():
        for tile in tiles:
            tile.wait()
        lax.fori_loop(0, groups, group, 0)

    return finish


def rotate_kernel(step, shift, circle_in, out, circle, pairs, turned, ready):
    parts, groups, group, cells = turned.shape
    lat = lax.axis_index("lat")
    last_lat = lax.axis_size("lat") - 1
    rows = shift.shape[1] // lax.axis_size("lat")

    @pl.when((lat == 0) | (lat == last_lat))
    def _():
        fetch = pltpu.make_async_copy(circle_in, circle, ready.at[0])
        fetch.start()
        amount = jnp.where(lat == 0, shift[step, 0], shift[step, rows * last_lat + rows - 1])
        amount = lax.rem(amount + 2 * parts * cells, parts * cells)
        hops = amount // cells
        matrix = shift_matrix(amount - hops * cells, cells)
        fetch.wait()
        height = (groups + 1) * group
        for part in range(parts):
            at = slice(part * height, (part + 1) * height)
            near = lax.rem(part + hops, parts)
            far = lax.rem(part + hops + 1, parts)
            pairs[at, :cells] = circle[near].reshape(height, cells)
            pairs[at, cells:] = circle[far].reshape(height, cells)
        batch = parts // 2
        for i in range(2):
            rows_at = slice(i * batch * height, (i + 1) * batch * height)
            row = shifted(pairs[rows_at, :cells], pairs[rows_at, cells:], matrix)
            row = row.reshape(batch, groups + 1, group, 2 * cells)
            weight = row[:, groups:, :1, :cells]
            row = row[:, :groups]
            row = row[..., :cells] + weight * (row[..., cells:] - row[..., :cells])
            turned[i * batch : (i + 1) * batch] = row
        send = pltpu.make_async_copy(turned, out, ready.at[1])
        send.start()
        send.wait()


def prepare_stencil(step, north, south, east, coefs):
    rows, cells = north.shape[1:]
    tracers = coefs.shape[2]
    for r in range(rows):
        n = north[step, r : r + 1, :]
        s = south[step, r : r + 1, :]
        coefs[0, r] = jnp.broadcast_to(1.0 - n - s, (tracers, cells))
        coefs[1, r] = jnp.broadcast_to(n, (tracers, cells))
        coefs[2, r] = jnp.broadcast_to(s, (tracers, cells))
        coefs[3, r] = jnp.broadcast_to(east[step, r : r + 1, :], (tracers, cells))


def transported(group, lane_at, diffused, after, before, edge_row, coefs, pole):
    level = group * GROUP + lane_at
    rows, tracers, cells = diffused.shape[1:]
    lat = lax.axis_index("lat")
    last = lax.broadcasted_iota(jnp.int32, (tracers, cells), 1) == cells - 1
    result = []
    for r in range(rows):
        mer = meridional(level, r, diffused, after, before, [coefs[k, r] for k in range(3)])
        arrived = pltpu.roll(edge_row, LANES - 1 - (lane_at * rows + r), 1)
        arrived = jnp.concatenate([arrived] * (cells // LANES), axis=1)
        following = jnp.where(last, arrived, pltpu.roll(mer, cells - 1, 1))
        result.append(mer + coefs[3, r] * (following - mer))
    polar = pole[:, group, lane_at, :] if len(pole.shape) == 4 else pole[level]
    result[0] = jnp.where(lat == 0, polar, result[0])
    result[rows - 1] = jnp.where(lat == lax.axis_size("lat") - 1, polar, result[rows - 1])
    return result


def streams(sources, targets, poles, pole, done):
    lat = lax.axis_index("lat")
    last_lat = lax.axis_size("lat") - 1
    last = len(sources)

    def polar_copy(source, c):
        if len(pole.shape) == 4:
            at = pl.ds(c * SPAN, SPAN)
            return pltpu.make_async_copy(source.at[:, at], pole.at[:, at], done.at[last, c])
        return chunk(source, pole, done.at[last], c)

    for g in range(targets[0].shape[0] // (GROUP * SPAN)):
        for k, (source, target) in enumerate(zip(sources, targets)):
            chunk(source, target, done.at[k], g).start()

        @pl.when(lat == 0)
        def _():
            polar_copy(poles[0], g).start()

        @pl.when(lat == last_lat)
        def _():
            polar_copy(poles[-1], g).start()

    def wait(g):
        for k, (source, target) in enumerate(zip(sources, targets)):
            chunk(source, target, done.at[k], g).wait()

        @pl.when((lat == 0) | (lat == last_lat))
        def _():
            polar_copy(poles[0], g).wait()

    return wait


def middle_kernel(
    step,
    before_step,
    forced,
    after_in,
    before_in,
    south_pole,
    north_pole,
    edge,
    diffusion,
    north,
    south,
    east,
    result,
    first_out,
    last_out,
    polar_out,
    column,
    surface,
    coefs,
    ratios,
    diffused,
    after,
    before,
    pole,
    solved,
    first,
    last,
    polar,
    arrived,
    sent,
):
    levels, rows, tracers, cells = diffused.shape
    wait = streams(
        (before_step, after_in, before_in),
        (diffused, after, before),
        (south_pole, north_pole),
        pole,
        arrived,
    )
    prepare_stencil(step, north, south, east, coefs)

    def right_of(g, j, final):
        if j == 0:
            at_span(g, 0, wait)
        level = g * GROUP + j
        rights = transported(g, j, diffused, after, before, edge[g], coefs, pole)
        rights = [rights[r] + forced[level, r] for r in range(rows)]
        if final:
            for r in range(rows):
                surface[r] = rights[r]

        def store(values):
            for r in range(rows):
                solved[level, r] = values[r]

        return rights, ratios, store

    forward_sweep(
        levels, rows, tracers, cells, lambda level: diffusion[step - 1, level], right_of
    )
    couplings = (north, south, east)
    fields = (solved, first, last, polar)
    results = (result, first_out, last_out, polar_out)
    substitute(step - 1, ratios, couplings, column, fields, results, sent)


def last_kernel(
    step,
    before_step,
    forcing_in,
    after_in,
    before_in,
    pole_in,
    edge,
    north,
    south,
    east,
    surface,
    state,
    gradient,
    coefs,
    diffused,
    forced,
    after,
    before,
    pole,
    staged,
    arrived,
    sent,
):
    levels, rows, tracers, cells = diffused.shape
    wait = streams(
        (before_step, forcing_in, after_in, before_in),
        (diffused, forced, after, before),
        (pole_in,),
        pole,
        arrived,
    )
    prepare_stencil(step, north, south, east, coefs)

    def group(g, carry):
        at_span(g, 0, wait)
        edge_row = edge[g]
        for j in range(GROUP):
            level = g * GROUP + j
            values = transported(g, j, diffused, after, before, edge_row, coefs, pole)
            for r in range(rows):
                staged[level, :, r, :] = values[r] + forced[level, r]
        at_span(g, SPAN - 1, lambda c: chunk(staged, state, sent, c).start())
        return carry

    lax.fori_loop(0, levels // GROUP, group, 0)
    for r in range(rows):
        gradient[:, r, :] = surface[r] + staged[levels - 1, :, r, :]
    for c in range(levels // (GROUP * SPAN)):
        chunk(staged, state, sent, c).wait()


def boundary_rows(first, last):
    up = [(i, i + 1) for i in range(lax.axis_size("lat") - 1)]
    down = [(j, i) for i, j in up]
    return lax.ppermute(first, "lat", down), lax.ppermute(last, "lat", up)


def circles(lats, hops):
    lat_count = lax.axis_size("lat")
    lon_count = lax.axis_size("lon")
    return [
        (((j + hops) % lon_count) * lat_count + lat, j * lat_count + lat)
        for lat in lats
        for j in range(lon_count)
    ]


def westward(edge):
    count = lax.axis_size("lon")
    return held(lax.ppermute(edge, "lon", [(i, (i - 1) % count) for i in range(count)]))


def first_exchange(step, after, before, nearby, polar, column, north, south, shift):
    poles = (0, lax.axis_size("lat") - 1)
    levels, tracers, cells = after.shape
    edge, turned, *hops = pl.pallas_call(
        functools.partial(borders_kernel, step),
        out_shape=[
            resident(*column.shape),
            pltpu.HBM((levels, tracers, cells), F32),
            jax.ShapeDtypeStruct((1, 1), jnp.int32),
            jax.ShapeDtypeStruct((1, 1), jnp.int32),
        ],
        in_specs=[smem()] + [vmem()] * 3 + [anywhere()] * 4,
        out_specs=[vmem(), hbm(), smem(), smem()],
        scratch_shapes=[
            pltpu.VMEM((levels, tracers, LANES), F32),
            pltpu.VMEM((levels, tracers, LANES), F32),
            pltpu.VMEM(polar.shape, F32),
            pltpu.VMEM(polar.shape, F32),
            pltpu.VMEM((levels, tracers, cells), F32),
            pltpu.SemaphoreType.DMA((5,)),
        ],
        compiler_params=params(8),
        name="borders",
    )(shift, column, north, south, after, before, pinned(polar), nearby)
    moved = []
    for lat, hop in zip(poles, hops):
        moved.append(
            lax.switch(
                hop.reshape(()),
                [
                    functools.partial(
                        lambda k, lat, x: lax.ppermute(x, AXES, circles((lat,), k)), k, lat
                    )
                    for k in range(lax.axis_size("lon"))
                ],
                turned,
            )
        )
    edge, *moved = lax.optimization_barrier((edge, *moved))
    return after, before, pinned(moved[0]), pinned(moved[1]), westward(edge)


def last_exchange(step, after, before, circle, column, north, south, shift):
    levels, tracers, cells = after.shape
    parts, groups, group = circle.shape[:3]
    shape = (parts, groups - 1, group, cells)
    turned = pl.pallas_call(
        functools.partial(rotate_kernel, step),
        out_shape=pltpu.HBM(shape, F32),
        in_specs=[smem(), anywhere()],
        out_specs=hbm(),
        scratch_shapes=[
            pltpu.VMEM(circle.shape, F32),
            pltpu.VMEM((parts * groups * group, 2 * cells), F32),
            pltpu.VMEM(shape, F32),
            pltpu.SemaphoreType.DMA((2,)),
        ],
        compiler_params=params(14),
        name="rotate",
    )(shift, circle)
    pole = lax.all_to_all(turned, "lon", 0, 0, tiled=True)
    edge = pl.pallas_call(
        functools.partial(edge_kernel, step),
        out_shape=resident(*column.shape),
        in_specs=[vmem()] * 3 + [anywhere()] * 2,
        out_specs=vmem(),
        scratch_shapes=[
            pltpu.VMEM((levels, tracers, LANES), F32),
            pltpu.VMEM((levels, tracers, LANES), F32),
            pltpu.SemaphoreType.DMA((2,)),
        ],
        compiler_params=params(4),
        name="edge",
    )(column, north, south, after, before)
    return after, before, pole, westward(edge)


def per_device(
    costate,
    diffusion,
    east_courant,
    north_courant,
    south_courant,
    polar_shift,
    owners,
    columns,
    sounding_counts,
    kernels,
    misfits,
):
    levels, tracers, rows, cells = costate.shape
    owner_rows = owners.reshape(owners.shape[0], 1, owners.shape[1])
    couplings = (north_courant, south_courant, east_courant)
    groups = levels // GROUP

    solved_shapes = [
        pltpu.HBM((levels, rows, tracers, cells), F32),
        pltpu.HBM((levels, tracers, cells), F32),
        pltpu.HBM((levels, tracers, cells), F32),
        pltpu.HBM((levels + 1, tracers, cells), F32),
        resident(groups, tracers, LANES),
    ]
    ratios = pltpu.VMEM((levels, rows, cells), F32)
    coefs = pltpu.VMEM((4, rows, tracers, cells), F32)
    field = pltpu.VMEM((levels, rows, tracers, cells), F32)
    line = pltpu.VMEM((levels, tracers, cells), F32)
    solved_scratch = [field, line, line, pltpu.VMEM((levels + 1, tracers, cells), F32)]
    solved_specs = [hbm()] * 4 + [vmem()]
    leaving = pltpu.SemaphoreType.DMA((4, groups // SPAN + 1))
    output = pltpu.VMEM(costate.shape, F32)
    semaphores = pltpu.SemaphoreType.DMA((groups // SPAN,))
    diffused, first, last, polar, column = pl.pallas_call(
        functools.partial(first_kernel, 1),
        out_shape=solved_shapes,
        in_specs=[hbm()] * 5,
        out_specs=solved_specs,
        scratch_shapes=[
            output,
            ratios,
            *solved_scratch,
            pltpu.VMEM(diffusion.shape[1:], F32),
            pltpu.VMEM((3,) + east_courant.shape, F32),
            semaphores,
            leaving,
            pltpu.SemaphoreType.DMA((4,)),
        ],
        compiler_params=params(16),
        name="first",
    )(*[pinned(x) for x in (costate, diffusion, *couplings)])
    couplings = [held(x) for x in couplings]
    diffusion = held(diffusion)
    counts, column = lax.optimization_barrier((sounding_counts, column))
    nearby = lax.ppermute(polar, AXES, circles((0, lax.axis_size("lat") - 1), 1))
    around = (*boundary_rows(first, last), nearby)
    sent = packed(counts, owner_rows, columns, kernels, misfits)
    sent, *around = lax.optimization_barrier((sent, *around))
    around = [pinned(x) for x in around]
    got = lax.all_to_all(sent, AXES, 0, 0, tiled=True)
    shape = (levels, rows, tracers, cells)
    forced = forcing(1, got, shape, False)
    around = first_exchange(1, *around, polar, column, *couplings[:2], polar_shift)
    scratch = [field, line, line]
    transfers = pltpu.SemaphoreType.DMA((4, groups // SPAN))
    solved, first, last, polar, column, surface = pl.pallas_call(
        functools.partial(middle_kernel, 1),
        out_shape=[
            *solved_shapes[:3],
            pltpu.HBM((tracers, groups + 1, GROUP, cells), F32),
            solved_shapes[4],
            resident(rows, tracers, cells),
        ],
        in_specs=[hbm(), vmem()] + [anywhere()] * 2 + [hbm()] * 2 + [vmem()] * 5,
        out_specs=solved_specs + [vmem()],
        scratch_shapes=[
            coefs,
            ratios,
            *scratch,
            line,
            *solved_scratch[:3],
            pltpu.VMEM((tracers, groups + 1, GROUP, cells), F32),
            transfers,
            leaving,
        ],
        compiler_params=params(20),
        name="middle",
    )(pinned(diffused), forced, *around, diffusion, *couplings)
    circle = lax.all_to_all(polar, "lon", 0, 0, tiled=True)
    got, column = lax.optimization_barrier((got, column))
    forced = forcing(0, got, shape, True)
    forced, first, last = lax.optimization_barrier((forced, first, last))
    around = last_exchange(
        0, *boundary_rows(first, last), circle, column, *couplings[:2], polar_shift
    )
    return tuple(
        pl.pallas_call(
            functools.partial(last_kernel, 0),
            out_shape=[
                pltpu.HBM(costate.shape, F32),
                jax.ShapeDtypeStruct((tracers, rows, cells), F32),
            ],
            in_specs=[hbm()] * 2 + [anywhere()] * 3 + [vmem()] * 5,
            out_specs=[hbm(), vmem()],
            scratch_shapes=[
                coefs,
                field,
                *scratch,
                pltpu.VMEM((tracers, groups, GROUP, cells), F32),
                output,
                pltpu.SemaphoreType.DMA((5, groups // SPAN)),
                semaphores,
            ],
            compiler_params=params(22),
            name="last",
        )(pinned(solved), pinned(forced), *around, *couplings, surface)
    )


def solution(mesh):
    return jax.shard_map(
        per_device,
        mesh=mesh,
        in_specs=(
            P(None, None, "lat", "lon"),
            P(None, None, "lat", "lon"),
            P(None, "lat", "lon"),
            P(None, "lat", "lon"),
            P(None, "lat", "lon"),
            P(),
            P(None, ("lon", "lat"), None),
            P(None, ("lon", "lat")),
            P(None, ("lon", "lat")),
            P(None, None, ("lon", "lat")),
            P(None, None, ("lon", "lat")),
        ),
        out_specs=(P(None, None, "lat", "lon"), P(None, "lat", "lon")),
        check_vma=False,
    )
```

```python
import functools

import jax
import jax.numpy as jnp
from jax import lax
from jax.experimental import pallas as pl
from jax.experimental.pallas import tpu as pltpu
from jax.sharding import PartitionSpec as P

AXES = ("lon", "lat")
LANES = 128
CAP = 16
GROUP = 8
SPAN = 3
F32 = jnp.float32
BF16 = jnp.bfloat16
MIB = 1024 * 1024


def vmem():
    return pl.BlockSpec(memory_space=pltpu.VMEM)


def smem():
    return pl.BlockSpec(memory_space=pltpu.SMEM)


def hbm():
    return pl.BlockSpec(memory_space=pltpu.HBM)


def params(limit):
    return pltpu.CompilerParams(vmem_limit_bytes=limit * MIB)


def held(x):
    return pltpu.with_memory_space_constraint(x, pltpu.VMEM)


def anywhere():
    return pl.BlockSpec(memory_space=pl.ANY)


def pinned(x):
    return pltpu.with_memory_space_constraint(x, pltpu.HBM)


def resident(*shape):
    return pltpu.VMEM(shape, F32)


def chunk(source, target, done, c):
    at = pl.ds(c * GROUP * SPAN, GROUP * SPAN)
    return pltpu.make_async_copy(source.at[at], target.at[at], done.at[c])


def at_span(g, place, act):
    if isinstance(g, int):
        if g % SPAN == place:
            act(g // SPAN)
    else:
        pl.when(lax.rem(g, SPAN) == place)(lambda: act(lax.div(g, SPAN)))


def dot(a, b, contract=((1,), (0,))):
    return lax.dot_general(a, b, (contract, ((), ())), preferred_element_type=F32)


def halves(x):
    high = x.astype(BF16)
    return high, (x - high.astype(F32)).astype(BF16)


def spare_lane(levels, tracers):
    return levels + tracers + 8


def pack_kernel(
    counts, owners, columns, kernels, misfits, out, payload, target, staged, done
):
    steps, levels, held = kernels.shape
    tracers = misfits.shape[1]
    shape = (LANES, LANES)
    half = CAP // 2
    device = lax.broadcasted_iota(jnp.int32, shape, 0)
    table = counting_table()
    for step in range(steps):
        owner = owners[step]
        live = lax.broadcasted_iota(jnp.int32, owner.shape, 1) < counts[step, 0]
        owner = jnp.where(live, owner, -1)
        seen = jnp.zeros(shape, F32)
        for start in range(0, held, LANES):
            here = owner[:, start : start + LANES]
            hot = device == here
            counted = dot(jnp.where(hot, 1.0, 0.0).astype(BF16), table)
            rank = jnp.sum(
                jnp.where(hot, counted[:, :LANES] + seen, 0.0), axis=0, keepdims=True
            )
            seen = seen + counted[:, LANES:]
            target[step : step + 1, start : start + LANES] = jnp.where(
                here >= 0, here * CAP + rank.astype(jnp.int32), -1
            )
    spare = spare_lane(levels, tracers)
    main = LANES - spare

    def fill(k, part, pieces):
        rows = jnp.concatenate(
            [jnp.zeros((x, held), F32) if isinstance(x, int) else x for x in pieces], axis=0
        )
        high, low = halves(rows)
        payload[k, :LANES, part * held : (part + 1) * held] = high
        payload[k, LANES:, part * held : (part + 1) * held] = low

    def column(step):
        x = columns[step : step + 1, :].astype(F32) + 1.0
        return jnp.where(lax.broadcasted_iota(jnp.int32, (8, held), 0) == 0, x, 0.0)

    rest = [kernels[0, main:, :], misfits[0], column(0)]
    used = levels - main + tracers + 8
    fill(0, 0, [kernels[1], misfits[1], column(1), main])
    fill(0, 1, [spare, kernels[0, :main, :]])
    fill(1, 0, [*rest, LANES - used])
    fill(1, 1, [LANES // 2, *rest, LANES // 2 - used])
    slot = target[0:1, :] & (CAP - 1)
    owner = target[0:1, :] >> (CAP.bit_length() - 1)
    lower = jnp.where((target[0:1, :] >= 0) & (slot < half), owner * half + slot, -1)
    upper = jnp.where((target[0:1, :] >= 0) & (slot >= half), owner * half + slot - half, -1)
    owned = 512 // CAP
    tiles = out.shape[0] // owned

    def copy(i):
        at = pl.ds(i * owned, owned)
        return pltpu.make_async_copy(staged.at[at], out.at[at], done.at[i])

    def place(i, carry):
        for k, ats, size, rows in (
            (0, (target[1:2, :], target[0:1, :]), owned * CAP, slice(0, CAP)),
            (1, (lower, upper), owned * half, slice(CAP, CAP + half)),
        ):
            hot = jnp.concatenate([tall_one_hot(at - i * size, size) for at in ats], axis=1)
            both = dot(hot, payload[k], ((1,), (1,)))
            both = both[:, :LANES] + both[:, LANES:]
            staged[pl.ds(i * owned, owned), rows, :] = both.reshape(owned, -1, LANES)
        copy(i).start()
        return carry

    lax.fori_loop(0, tiles, place, 0)
    for i in range(tiles):
        copy(i).wait()


def one_hot(at, size):
    at = jnp.where((at >= 0) & (at < size), at, -1).astype(F32).astype(BF16)
    shape = (size, at.shape[1])
    row = lax.broadcasted_iota(jnp.int32, shape, 0).astype(F32).astype(BF16)
    return jnp.where(row == at, jnp.ones(shape, BF16), jnp.zeros(shape, BF16))


def tall_one_hot(at, size):
    parts = [one_hot(at - start, 256) for start in range(0, size, 256)]
    return parts[0] if len(parts) == 1 else jnp.concatenate(parts, axis=0)


def counting_table():
    shape = (LANES, LANES)
    earlier = lax.broadcasted_iota(jnp.int32, shape, 0) < lax.broadcasted_iota(
        jnp.int32, shape, 1
    )
    return jnp.concatenate(
        [jnp.where(earlier, 1.0, 0.0), jnp.ones(shape, F32)], axis=1
    ).astype(BF16)


def packed(counts, owners, columns, kernels, misfits):
    steps, slots = columns.shape
    devices = lax.axis_size("lon") * lax.axis_size("lat")
    return pl.pallas_call(
        pack_kernel,
        out_shape=pltpu.HBM((devices, CAP + CAP // 2, LANES), F32),
        in_specs=[smem()] + [vmem()] * 4,
        out_specs=hbm(),
        scratch_shapes=[
            pltpu.VMEM((2, 2 * LANES, 2 * slots), BF16),
            pltpu.VMEM((steps, slots), jnp.int32),
            pltpu.VMEM((devices, CAP + CAP // 2, LANES), F32),
            pltpu.SemaphoreType.DMA((devices * CAP // 512,)),
        ],
        compiler_params=params(20),
        name="pack",
    )(counts, held(owners), held(columns), held(kernels), held(misfits))


def streamed_forcing_kernel(step, received, result, out, *scratch):
    done = scratch[-1]

    def copy(r):
        return pltpu.make_async_copy(out.at[:, r], result.at[:, r], done.at[r])

    forcing_kernel(step, received, out, *scratch[:-1], finished=lambda r: copy(r).start())
    for r in range(out.shape[1]):
        copy(r).wait()


def forcing_kernel(
    step, received, out, fields, hots, place, ordered, finished=lambda r: None
):
    levels, rows, tracers, cells = out.shape
    sources = received.shape[0]
    slots = sources * CAP
    blocks = slots // LANES
    spare = spare_lane(levels, tracers)
    data = received[:, :CAP, :].reshape(slots, LANES)
    if step == 1:
        at_column = levels + tracers

        def profile(turned):
            return turned[:levels]

    else:
        at_column = levels - (LANES - spare) + tracers
        extra = received[:, CAP:, :]
        other = pltpu.roll(extra.reshape(slots // 2, LANES), LANES // 2, 1)
        extra = jnp.concatenate([extra, other.reshape(extra.shape)], axis=1)
        lane = lax.broadcasted_iota(jnp.int32, (slots, LANES), 1)
        data = jnp.where(lane < LANES // 2, extra.reshape(slots, LANES), data)

        def profile(turned):
            return jnp.concatenate([turned[spare:], turned[: at_column - tracers]], axis=0)

    high, low = halves(data)
    fields[:, :LANES] = high
    fields[:, LANES:] = low
    shape = (8, 2 * LANES)
    pick = (lax.broadcasted_iota(jnp.int32, shape, 1) & (LANES - 1)) == at_column
    column = dot(jnp.where(pick, 1.0, 0.0).astype(BF16), fields[...], ((1,), (1,)))
    cell_row = (column.astype(jnp.int32) - 1) >> (cells.bit_length() - 1)
    sub = lax.broadcasted_iota(jnp.int32, (rows, LANES), 0)
    for b in range(blocks):
        row = cell_row[:, b * LANES : (b + 1) * LANES]
        hots[b * rows : (b + 1) * rows, :] = jnp.where(sub == row, 1.0, 0.0)
    counted = dot(hots[...].astype(BF16), counting_table())
    run = jnp.zeros((rows, LANES), F32)
    runs = []
    for b in range(blocks):
        runs.append(run)
        run = run + counted[b * rows : (b + 1) * rows, LANES:]
    filled = jnp.floor((run + (LANES - 1.0)) * (1.0 / LANES))
    start = jnp.zeros((rows, LANES), F32)
    for j in range(1, rows):
        start = start + jnp.where(sub >= j, pltpu.roll(filled, j, 0), 0.0)
    for b in range(blocks):
        hot = hots[b * rows : (b + 1) * rows, :]
        at = counted[b * rows : (b + 1) * rows, :LANES] + runs[b] + start * float(LANES)
        at = jnp.sum(hot * at, axis=0, keepdims=True)
        live = jnp.sum(hot, axis=0, keepdims=True) > 0.0
        place[:, b * LANES : (b + 1) * LANES] = jnp.where(live, at, -1.0)
    counts = [jnp.max(filled[r : r + 1, :]).astype(jnp.int32) for r in range(rows)]
    used = sum(counts)
    wide = 4 * LANES

    def sort(i, carry):
        hot = tall_one_hot(place[...] - (i * wide).astype(F32), wide)
        both = dot(hot, fields[...])
        ordered[pl.ds(pl.multiple_of(i * wide, wide), wide), :] = both[:, :LANES] + both[:, LANES:]
        return carry

    lax.fori_loop(0, (used + 3) // 4, sort, 0)
    out[...] = jnp.zeros_like(out)
    name = lax.broadcasted_iota(jnp.int32, (LANES, cells), 1).astype(F32)
    first = jnp.int32(0)
    for r in range(rows):

        def add(p, carry):
            block = ordered[pl.ds(pl.multiple_of(p * LANES, LANES), LANES), :]
            own = jnp.broadcast_to(
                block[:, at_column : at_column + 1] - (r * cells + 1.0), (LANES, cells)
            )
            hot = jnp.where(name == own, 1.0, 0.0).astype(BF16)
            turned = block.T
            product = profile(turned)[:, None, :] * turned[at_column - tracers : at_column][None]
            product = product.reshape(levels * tracers, LANES)
            total = dot(
                jnp.concatenate(halves(product), axis=1), jnp.concatenate([hot, hot], axis=0)
            )
            out[:, r, :, :] += total.reshape(levels, tracers, cells)
            return carry

        lax.fori_loop(first, first + counts[r], add, 0)
        first = first + counts[r]
        finished(r)


def forcing(step, received, shape, streamed):
    slots = received.shape[0] * CAP
    scratch = [
        pltpu.VMEM((slots, 2 * LANES), BF16),
        pltpu.VMEM((slots // LANES * shape[1], LANES), F32),
        pltpu.VMEM((1, slots), F32),
        pltpu.VMEM((slots + shape[1] * LANES, LANES), F32),
    ]
    if streamed:
        scratch = [resident(*shape), *scratch, pltpu.SemaphoreType.DMA((shape[1],))]
    return pl.pallas_call(
        functools.partial(streamed_forcing_kernel if streamed else forcing_kernel, step),
        out_shape=pltpu.HBM(shape, F32) if streamed else resident(*shape),
        in_specs=[vmem()],
        out_specs=hbm() if streamed else vmem(),
        scratch_shapes=scratch,
        compiler_params=params(20 if streamed else 16),
        name="forcing",
    )(held(received))


def shift_matrix(inner, cells):
    shape = (2 * cells, cells)
    source = lax.broadcasted_iota(jnp.int32, shape, 0)
    target = lax.broadcasted_iota(jnp.int32, shape, 1) + inner
    picks = [jnp.where(source == target + k, 1.0, 0.0).astype(BF16) for k in range(2)]
    return jnp.concatenate(picks, axis=1)


def shifted(low, high, matrix):
    row = jnp.concatenate([low, high], axis=1)
    first, rest = row.astype(BF16), None
    rest = row - first.astype(F32)
    second, third = halves(rest)
    return dot(first, matrix) + dot(second, matrix) + dot(third, matrix)


def spread(x, row, tracers):
    return jnp.broadcast_to(x[row : row + 1, :], (tracers, x.shape[1]))


def eliminate(level, above, carry, rights, ratios):
    below, ratio, values = carry
    if above is None:
        above = jnp.zeros_like(below)
    inverse = 1.0 / (1.0 + below + above + below * ratio)
    lower = below * inverse
    ratio = -above * inverse
    ratios[level] = ratio
    tracers = rights[0].shape[0]
    fresh = [
        spread(inverse, r, tracers) * rights[r] + spread(lower, r, tracers) * values[r]
        for r in range(len(rights))
    ]
    return (above, ratio, fresh)


def substitute(step, ratios, couplings, column, fields, results, done):
    diffused, first, last, polar = fields
    levels, rows, tracers, cells = diffused.shape
    lat = lax.axis_index("lat")
    at_start = lat == 0

    def picked(x):
        return jnp.where(at_start, x[step, 0:1, :], x[step, rows - 1 : rows, :])

    north, south, east = [picked(x) for x in couplings]
    own = jnp.broadcast_to(1.0 - north - south, (tracers, cells))
    side = jnp.broadcast_to(jnp.where(at_start, north, south), (tracers, cells))
    groups = levels // GROUP
    by_tracer = len(polar.shape) == 4
    if by_tracer:
        polar[:, groups, 0, :] = jnp.broadcast_to(east, (tracers, cells))
    else:
        polar[levels] = jnp.broadcast_to(east, (tracers, cells))

    chunks = groups // SPAN

    def polar_copy(at, c):
        if by_tracer:
            source, target = [x.at[:, at] for x in (polar, results[3])]
        else:
            source, target = [x.at[at] for x in (polar, results[3])]
        return pltpu.make_async_copy(source, target, done.at[3, c])

    def copies(c):
        size = SPAN if by_tracer else SPAN * GROUP
        moves = [chunk(fields[k], results[k], done.at[k], c) for k in range(3)]
        return [*moves, polar_copy(pl.ds(c * size, size), c)]

    def send(c):
        for copy in copies(c):
            copy.start()

    weight = polar_copy(pl.ds(groups if by_tracer else levels, 1), chunks)
    weight.start()
    lane = lax.broadcasted_iota(jnp.int32, (tracers, LANES), 1)

    def group(i, solved):
        at = groups - 1 - i
        west = jnp.zeros((tracers, LANES), F32)
        for j in range(GROUP - 1, -1, -1):
            level = at * GROUP + j
            ratio = ratios[level]
            fresh = []
            for r in range(rows):
                value = diffused[level, r] - spread(ratio, r, tracers) * solved[r]
                diffused[level, r] = value
                fresh.append(value)
                lanes = j * rows + r
                moved = pltpu.roll(value[:, :LANES], lanes, 1) if lanes else value[:, :LANES]
                west = jnp.where(lane == lanes, moved, west)
            solved = fresh
            first[level] = solved[0]
            last[level] = solved[rows - 1]
            row = own * jnp.where(at_start, solved[0], solved[rows - 1]) + side * jnp.where(
                at_start, solved[1], solved[rows - 2]
            )
            if by_tracer:
                polar[:, at, j, :] = row
            else:
                polar[level] = row
        column[at] = west
        at_span(at, 0, send)
        return solved

    lax.fori_loop(0, groups, group, [jnp.zeros((tracers, cells), F32)] * rows)
    weight.wait()
    for c in range(chunks):
        for copy in copies(c):
            copy.wait()


def forward_sweep(levels, rows, tracers, cells, diffusion, right_of):
    zero = jnp.zeros((rows, cells), F32)
    carry = (zero, zero, [jnp.zeros((tracers, cells), F32)] * rows)
    groups = levels // GROUP

    def one(g, j, above, carry):
        rights, ratios, store = right_of(g, j, above is None)
        carry = eliminate(g * GROUP + j, above, carry, rights, ratios)
        store(carry[2])
        return carry

    def group(g, carry):
        for j in range(GROUP):
            carry = one(g, j, diffusion(g * GROUP + j), carry)
        return carry

    carry = lax.fori_loop(0, groups - 1, group, carry)
    for j in range(GROUP):
        level = levels - GROUP + j
        carry = one(groups - 1, j, diffusion(level) if level < levels - 1 else None, carry)


def first_kernel(
    step,
    costate,
    diffusion_in,
    north_in,
    south_in,
    east_in,
    result,
    first_out,
    last_out,
    polar_out,
    column,
    staged,
    ratios,
    diffused,
    first,
    last,
    polar,
    diffusion,
    couplings,
    arrived,
    sent,
    ready,
):
    levels, tracers, rows, cells = costate.shape
    small = [pltpu.make_async_copy(diffusion_in.at[step], diffusion, ready.at[0])]
    for k, coupling in enumerate((north_in, south_in, east_in)):
        small.append(pltpu.make_async_copy(coupling, couplings.at[k], ready.at[1 + k]))
    chunk(costate, staged, arrived, 0).start()
    for copy in small:
        copy.start()
    for c in range(1, levels // (GROUP * SPAN)):
        chunk(costate, staged, arrived, c).start()
    for copy in small:
        copy.wait()

    def right_of(g, j, final):
        if j == 0:
            at_span(g, 0, lambda c: chunk(costate, staged, arrived, c).wait())
        level = g * GROUP + j
        rights = [staged[level, :, r, :] for r in range(rows)]

        def store(values):
            for r in range(rows):
                diffused[level, r] = values[r]

        return rights, ratios, store

    forward_sweep(levels, rows, tracers, cells, lambda level: diffusion[level], right_of)
    views = [couplings.at[k] for k in range(3)]
    fields = (diffused, first, last, polar)
    results = (result, first_out, last_out, polar_out)
    substitute(step, ratios, views, column, fields, results, sent)


def meridional(level, row, diffused, after, before, coefs):
    rows = diffused.shape[1]
    own, north, south = coefs
    up = diffused[level, row + 1] if row < rows - 1 else after[level]
    down = diffused[level, row - 1] if row > 0 else before[level]
    return own * diffused[level, row] + north * up + south * down


def borders_kernel(
    step,
    shift,
    column,
    north,
    south,
    after_in,
    before_in,
    polar_in,
    nearby_in,
    edge,
    turned_out,
    south_hops,
    north_hops,
    after,
    before,
    polar,
    nearby,
    turned,
    ready,
):
    rows, cells = north.shape[1:]
    circle = cells * lax.axis_size("lon")
    amounts = [
        lax.rem(shift[step, x] + 2 * circle, circle) for x in (0, shift.shape[1] - 1)
    ]
    south_hops[0, 0] = amounts[0] // cells
    north_hops[0, 0] = amounts[1] // cells
    fetches = [
        pltpu.make_async_copy(source, target, ready.at[2 + k])
        for k, (source, target) in enumerate(((polar_in, polar), (nearby_in, nearby)))
    ]
    sending = pltpu.make_async_copy(turned, turned_out, ready.at[4])
    lat = lax.axis_index("lat")
    last_lat = lax.axis_size("lat") - 1
    at_pole = (lat == 0) | (lat == last_lat)

    @pl.when(at_pole)
    def _():
        for fetch in fetches:
            fetch.start()

    finish = west_column(step, column, north, south, after_in, before_in, edge, after, before, ready)

    @pl.when(at_pole)
    def _():
        for fetch in fetches:
            fetch.wait()
        levels = turned.shape[0]
        amount = jnp.where(lat == 0, amounts[0], amounts[1])
        matrix = shift_matrix(lax.rem(amount, cells), cells)
        tracers = turned.shape[1]
        weight = shifted(polar[levels], nearby[levels], matrix)[:1, :cells]
        low, high = [x[:levels].reshape(levels * tracers, cells) for x in (polar, nearby)]
        row = shifted(low, high, matrix)
        row = row[:, :cells] + weight * (row[:, cells:] - row[:, :cells])
        turned[...] = row.reshape(levels, tracers, cells)
        sending.start()

    finish()

    @pl.when(at_pole)
    def _():
        sending.wait()


def edge_kernel(
    step, column, north, south, after_in, before_in, edge, after, before, ready
):
    west_column(step, column, north, south, after_in, before_in, edge, after, before, ready)()


def west_column(step, column, north, south, after_in, before_in, edge, after, before, ready):
    groups, tracers, lanes = column.shape
    rows, cells = north.shape[1:]
    tiles = [
        pltpu.make_async_copy(source.at[:, :, pl.ds(0, lanes)], target, ready.at[k])
        for k, (source, target) in enumerate(((after_in, after), (before_in, before)))
    ]
    for tile in tiles:
        tile.start()
    lane = lax.broadcasted_iota(jnp.int32, (tracers, lanes), 1)

    def along_lanes(x):
        shape = (rows, lanes)
        own_lane = (lax.broadcasted_iota(jnp.int32, shape, 1) & (rows - 1)) == (
            lax.broadcasted_iota(jnp.int32, shape, 0)
        )
        picked = jnp.where(own_lane, jnp.broadcast_to(x[step, :, :1], shape), 0.0)
        return jnp.broadcast_to(jnp.sum(picked, axis=0, keepdims=True), (tracers, lanes))

    n, s = along_lanes(north), along_lanes(south)
    own = 1.0 - n - s

    def group(i, carry):
        here = column[i]
        up = pltpu.roll(here, lanes - 1, 1)
        down = pltpu.roll(here, 1, 1)
        for j in range(GROUP):
            level = i * GROUP + j
            bottom, top = j * rows, j * rows + rows - 1
            up = jnp.where(lane == top, pltpu.roll(after[level], top, 1), up)
            moved = before[level]
            moved = pltpu.roll(moved, bottom, 1) if bottom else moved
            down = jnp.where(lane == bottom, moved, down)
        edge[i] = own * here + n * up + s * down
        return carry

    def finish():
        for tile in tiles:
            tile.wait()
        lax.fori_loop(0, groups, group, 0)

    return finish


def rotate_kernel(step, shift, circle_in, out, circle, pairs, turned, ready):
    parts, groups, group, cells = turned.shape
    lat = lax.axis_index("lat")
    last_lat = lax.axis_size("lat") - 1
    rows = shift.shape[1] // lax.axis_size("lat")

    @pl.when((lat == 0) | (lat == last_lat))
    def _():
        fetch = pltpu.make_async_copy(circle_in, circle, ready.at[0])
        fetch.start()
        amount = jnp.where(lat == 0, shift[step, 0], shift[step, rows * last_lat + rows - 1])
        amount = lax.rem(amount + 2 * parts * cells, parts * cells)
        hops = amount // cells
        matrix = shift_matrix(amount - hops * cells, cells)
        fetch.wait()
        height = (groups + 1) * group
        for part in range(parts):
            at = slice(part * height, (part + 1) * height)
            near = lax.rem(part + hops, parts)
            far = lax.rem(part + hops + 1, parts)
            pairs[at, :cells] = circle[near].reshape(height, cells)
            pairs[at, cells:] = circle[far].reshape(height, cells)
        row = shifted(pairs[:, :cells], pairs[:, cells:], matrix)
        row = row.reshape(parts, groups + 1, group, 2 * cells)
        weight = row[:, groups:, :1, :cells]
        row = row[:, :groups]
        turned[...] = row[..., :cells] + weight * (row[..., cells:] - row[..., :cells])
        send = pltpu.make_async_copy(turned, out, ready.at[1])
        send.start()
        send.wait()


def prepare_stencil(step, north, south, east, coefs):
    rows, cells = north.shape[1:]
    tracers = coefs.shape[2]
    for r in range(rows):
        n = north[step, r : r + 1, :]
        s = south[step, r : r + 1, :]
        coefs[0, r] = jnp.broadcast_to(1.0 - n - s, (tracers, cells))
        coefs[1, r] = jnp.broadcast_to(n, (tracers, cells))
        coefs[2, r] = jnp.broadcast_to(s, (tracers, cells))
        coefs[3, r] = jnp.broadcast_to(east[step, r : r + 1, :], (tracers, cells))


def transported(group, lane_at, diffused, after, before, edge_row, coefs, pole):
    level = group * GROUP + lane_at
    rows, tracers, cells = diffused.shape[1:]
    lat = lax.axis_index("lat")
    last = lax.broadcasted_iota(jnp.int32, (tracers, cells), 1) == cells - 1
    result = []
    for r in range(rows):
        mer = meridional(level, r, diffused, after, before, [coefs[k, r] for k in range(3)])
        arrived = pltpu.roll(edge_row, LANES - 1 - (lane_at * rows + r), 1)
        arrived = jnp.concatenate([arrived] * (cells // LANES), axis=1)
        following = jnp.where(last, arrived, pltpu.roll(mer, cells - 1, 1))
        result.append(mer + coefs[3, r] * (following - mer))
    polar = pole[:, group, lane_at, :] if len(pole.shape) == 4 else pole[level]
    result[0] = jnp.where(lat == 0, polar, result[0])
    result[rows - 1] = jnp.where(lat == lax.axis_size("lat") - 1, polar, result[rows - 1])
    return result


def streams(sources, targets, poles, pole, done):
    lat = lax.axis_index("lat")
    last_lat = lax.axis_size("lat") - 1
    last = len(sources)

    def polar_copy(source, c):
        if len(pole.shape) == 4:
            at = pl.ds(c * SPAN, SPAN)
            return pltpu.make_async_copy(source.at[:, at], pole.at[:, at], done.at[last, c])
        return chunk(source, pole, done.at[last], c)

    for g in range(targets[0].shape[0] // (GROUP * SPAN)):
        for k, (source, target) in enumerate(zip(sources, targets)):
            chunk(source, target, done.at[k], g).start()

        @pl.when(lat == 0)
        def _():
            polar_copy(poles[0], g).start()

        @pl.when(lat == last_lat)
        def _():
            polar_copy(poles[-1], g).start()

    def wait(g):
        for k, (source, target) in enumerate(zip(sources, targets)):
            chunk(source, target, done.at[k], g).wait()

        @pl.when((lat == 0) | (lat == last_lat))
        def _():
            polar_copy(poles[0], g).wait()

    return wait


def middle_kernel(
    step,
    before_step,
    forced,
    after_in,
    before_in,
    south_pole,
    north_pole,
    edge,
    diffusion,
    north,
    south,
    east,
    result,
    first_out,
    last_out,
    polar_out,
    column,
    surface,
    coefs,
    ratios,
    diffused,
    after,
    before,
    pole,
    solved,
    first,
    last,
    polar,
    arrived,
    sent,
):
    levels, rows, tracers, cells = diffused.shape
    wait = streams(
        (before_step, after_in, before_in),
        (diffused, after, before),
        (south_pole, north_pole),
        pole,
        arrived,
    )
    prepare_stencil(step, north, south, east, coefs)

    def right_of(g, j, final):
        if j == 0:
            at_span(g, 0, wait)
        level = g * GROUP + j
        rights = transported(g, j, diffused, after, before, edge[g], coefs, pole)
        rights = [rights[r] + forced[level, r] for r in range(rows)]
        if final:
            for r in range(rows):
                surface[r] = rights[r]

        def store(values):
            for r in range(rows):
                solved[level, r] = values[r]

        return rights, ratios, store

    forward_sweep(
        levels, rows, tracers, cells, lambda level: diffusion[step - 1, level], right_of
    )
    couplings = (north, south, east)
    fields = (solved, first, last, polar)
    results = (result, first_out, last_out, polar_out)
    substitute(step - 1, ratios, couplings, column, fields, results, sent)


def last_kernel(
    step,
    before_step,
    forcing_in,
    after_in,
    before_in,
    pole_in,
    edge,
    north,
    south,
    east,
    surface,
    state,
    gradient,
    coefs,
    diffused,
    forced,
    after,
    before,
    pole,
    staged,
    arrived,
    sent,
):
    levels, rows, tracers, cells = diffused.shape
    wait = streams(
        (before_step, forcing_in, after_in, before_in),
        (diffused, forced, after, before),
        (pole_in,),
        pole,
        arrived,
    )
    prepare_stencil(step, north, south, east, coefs)

    def group(g, carry):
        at_span(g, 0, wait)
        edge_row = edge[g]
        for j in range(GROUP):
            level = g * GROUP + j
            values = transported(g, j, diffused, after, before, edge_row, coefs, pole)
            for r in range(rows):
                staged[level, :, r, :] = values[r] + forced[level, r]
        at_span(g, SPAN - 1, lambda c: chunk(staged, state, sent, c).start())
        return carry

    lax.fori_loop(0, levels // GROUP, group, 0)
    for r in range(rows):
        gradient[:, r, :] = surface[r] + staged[levels - 1, :, r, :]
    for c in range(levels // (GROUP * SPAN)):
        chunk(staged, state, sent, c).wait()


def boundary_rows(first, last):
    up = [(i, i + 1) for i in range(lax.axis_size("lat") - 1)]
    down = [(j, i) for i, j in up]
    return lax.ppermute(first, "lat", down), lax.ppermute(last, "lat", up)


def circles(lats, hops):
    lat_count = lax.axis_size("lat")
    lon_count = lax.axis_size("lon")
    return [
        (((j + hops) % lon_count) * lat_count + lat, j * lat_count + lat)
        for lat in lats
        for j in range(lon_count)
    ]


def westward(edge):
    count = lax.axis_size("lon")
    return held(lax.ppermute(edge, "lon", [(i, (i - 1) % count) for i in range(count)]))


def first_exchange(step, after, before, nearby, polar, column, north, south, shift):
    poles = (0, lax.axis_size("lat") - 1)
    levels, tracers, cells = after.shape
    edge, turned, *hops = pl.pallas_call(
        functools.partial(borders_kernel, step),
        out_shape=[
            resident(*column.shape),
            pltpu.HBM((levels, tracers, cells), F32),
            jax.ShapeDtypeStruct((1, 1), jnp.int32),
            jax.ShapeDtypeStruct((1, 1), jnp.int32),
        ],
        in_specs=[smem()] + [vmem()] * 3 + [anywhere()] * 4,
        out_specs=[vmem(), hbm(), smem(), smem()],
        scratch_shapes=[
            pltpu.VMEM((levels, tracers, LANES), F32),
            pltpu.VMEM((levels, tracers, LANES), F32),
            pltpu.VMEM(polar.shape, F32),
            pltpu.VMEM(polar.shape, F32),
            pltpu.VMEM((levels, tracers, cells), F32),
            pltpu.SemaphoreType.DMA((5,)),
        ],
        compiler_params=params(14),
        name="borders",
    )(shift, column, north, south, after, before, pinned(polar), nearby)
    moved = []
    for lat, hop in zip(poles, hops):
        moved.append(
            lax.switch(
                hop.reshape(()),
                [
                    functools.partial(
                        lambda k, lat, x: lax.ppermute(x, AXES, circles((lat,), k)), k, lat
                    )
                    for k in range(lax.axis_size("lon"))
                ],
                turned,
            )
        )
    edge, *moved = lax.optimization_barrier((edge, *moved))
    return after, before, pinned(moved[0]), pinned(moved[1]), westward(edge)


def last_exchange(step, after, before, circle, column, north, south, shift):
    levels, tracers, cells = after.shape
    parts, groups, group = circle.shape[:3]
    shape = (parts, groups - 1, group, cells)
    turned = pl.pallas_call(
        functools.partial(rotate_kernel, step),
        out_shape=pltpu.HBM(shape, F32),
        in_specs=[smem(), anywhere()],
        out_specs=hbm(),
        scratch_shapes=[
            pltpu.VMEM(circle.shape, F32),
            pltpu.VMEM((parts * groups * group, 2 * cells), F32),
            pltpu.VMEM(shape, F32),
            pltpu.SemaphoreType.DMA((2,)),
        ],
        compiler_params=params(18),
        name="rotate",
    )(shift, circle)
    pole = lax.all_to_all(turned, "lon", 0, 0, tiled=True)
    edge = pl.pallas_call(
        functools.partial(edge_kernel, step),
        out_shape=resident(*column.shape),
        in_specs=[vmem()] * 3 + [anywhere()] * 2,
        out_specs=vmem(),
        scratch_shapes=[
            pltpu.VMEM((levels, tracers, LANES), F32),
            pltpu.VMEM((levels, tracers, LANES), F32),
            pltpu.SemaphoreType.DMA((2,)),
        ],
        compiler_params=params(4),
        name="edge",
    )(column, north, south, after, before)
    return after, before, pole, westward(edge)


def per_device(
    costate,
    diffusion,
    east_courant,
    north_courant,
    south_courant,
    polar_shift,
    owners,
    columns,
    sounding_counts,
    kernels,
    misfits,
):
    levels, tracers, rows, cells = costate.shape
    owner_rows = owners.reshape(owners.shape[0], 1, owners.shape[1])
    couplings = (north_courant, south_courant, east_courant)
    groups = levels // GROUP

    solved_shapes = [
        pltpu.HBM((levels, rows, tracers, cells), F32),
        pltpu.HBM((levels, tracers, cells), F32),
        pltpu.HBM((levels, tracers, cells), F32),
        pltpu.HBM((levels + 1, tracers, cells), F32),
        resident(groups, tracers, LANES),
    ]
    ratios = pltpu.VMEM((levels, rows, cells), F32)
    coefs = pltpu.VMEM((4, rows, tracers, cells), F32)
    field = pltpu.VMEM((levels, rows, tracers, cells), F32)
    line = pltpu.VMEM((levels, tracers, cells), F32)
    solved_scratch = [field, line, line, pltpu.VMEM((levels + 1, tracers, cells), F32)]
    solved_specs = [hbm()] * 4 + [vmem()]
    leaving = pltpu.SemaphoreType.DMA((4, groups // SPAN + 1))
    output = pltpu.VMEM(costate.shape, F32)
    semaphores = pltpu.SemaphoreType.DMA((groups // SPAN,))
    diffused, first, last, polar, column = pl.pallas_call(
        functools.partial(first_kernel, 1),
        out_shape=solved_shapes,
        in_specs=[hbm()] * 5,
        out_specs=solved_specs,
        scratch_shapes=[
            output,
            ratios,
            *solved_scratch,
            pltpu.VMEM(diffusion.shape[1:], F32),
            pltpu.VMEM((3,) + east_courant.shape, F32),
            semaphores,
            leaving,
            pltpu.SemaphoreType.DMA((4,)),
        ],
        compiler_params=params(16),
        name="first",
    )(*[pinned(x) for x in (costate, diffusion, *couplings)])
    couplings = [held(x) for x in couplings]
    diffusion = held(diffusion)
    counts, column = lax.optimization_barrier((sounding_counts, column))
    nearby = lax.ppermute(polar, AXES, circles((0, lax.axis_size("lat") - 1), 1))
    around = (*boundary_rows(first, last), nearby)
    sent = packed(counts, owner_rows, columns, kernels, misfits)
    sent, *around = lax.optimization_barrier((sent, *around))
    around = [pinned(x) for x in around]
    got = lax.all_to_all(sent, AXES, 0, 0, tiled=True)
    shape = (levels, rows, tracers, cells)
    forced = forcing(1, got, shape, False)
    around = first_exchange(1, *around, polar, column, *couplings[:2], polar_shift)
    scratch = [field, line, line]
    transfers = pltpu.SemaphoreType.DMA((4, groups // SPAN))
    solved, first, last, polar, column, surface = pl.pallas_call(
        functools.partial(middle_kernel, 1),
        out_shape=[
            *solved_shapes[:3],
            pltpu.HBM((tracers, groups + 1, GROUP, cells), F32),
            solved_shapes[4],
            resident(rows, tracers, cells),
        ],
        in_specs=[hbm(), vmem()] + [anywhere()] * 2 + [hbm()] * 2 + [vmem()] * 5,
        out_specs=solved_specs + [vmem()],
        scratch_shapes=[
            coefs,
            ratios,
            *scratch,
            line,
            *solved_scratch[:3],
            pltpu.VMEM((tracers, groups + 1, GROUP, cells), F32),
            transfers,
            leaving,
        ],
        compiler_params=params(20),
        name="middle",
    )(pinned(diffused), forced, *around, diffusion, *couplings)
    circle = lax.all_to_all(polar, "lon", 0, 0, tiled=True)
    got, column = lax.optimization_barrier((got, column))
    forced = forcing(0, got, shape, True)
    forced, first, last = lax.optimization_barrier((forced, first, last))
    around = last_exchange(
        0, *boundary_rows(first, last), circle, column, *couplings[:2], polar_shift
    )
    return tuple(
        pl.pallas_call(
            functools.partial(last_kernel, 0),
            out_shape=[
                pltpu.HBM(costate.shape, F32),
                jax.ShapeDtypeStruct((tracers, rows, cells), F32),
            ],
            in_specs=[hbm()] * 2 + [anywhere()] * 3 + [vmem()] * 5,
            out_specs=[hbm(), vmem()],
            scratch_shapes=[
                coefs,
                field,
                *scratch,
                pltpu.VMEM((tracers, groups, GROUP, cells), F32),
                output,
                pltpu.SemaphoreType.DMA((5, groups // SPAN)),
                semaphores,
            ],
            compiler_params=params(22),
            name="last",
        )(pinned(solved), pinned(forced), *around, *couplings, surface)
    )


def solution(mesh):
    return jax.shard_map(
        per_device,
        mesh=mesh,
        in_specs=(
            P(None, None, "lat", "lon"),
            P(None, None, "lat", "lon"),
            P(None, "lat", "lon"),
            P(None, "lat", "lon"),
            P(None, "lat", "lon"),
            P(),
            P(None, ("lon", "lat"), None),
            P(None, ("lon", "lat")),
            P(None, ("lon", "lat")),
            P(None, None, ("lon", "lat")),
            P(None, None, ("lon", "lat")),
        ),
        out_specs=(P(None, None, "lat", "lon"), P(None, "lat", "lon")),
        check_vma=False,
    )
```

```python
import functools

import jax
import jax.numpy as jnp
from jax import lax
from jax.experimental import pallas as pl
from jax.experimental.pallas import tpu as pltpu
from jax.sharding import PartitionSpec as P

AXES = ("lon", "lat")
LANES = 128
CAP = 16
GROUP = 8
SPAN = 3
F32 = jnp.float32
BF16 = jnp.bfloat16
MIB = 1024 * 1024


def vmem():
    return pl.BlockSpec(memory_space=pltpu.VMEM)


def smem():
    return pl.BlockSpec(memory_space=pltpu.SMEM)


def hbm():
    return pl.BlockSpec(memory_space=pltpu.HBM)


def params(limit):
    return pltpu.CompilerParams(vmem_limit_bytes=limit * MIB)


def held(x):
    return pltpu.with_memory_space_constraint(x, pltpu.VMEM)


def anywhere():
    return pl.BlockSpec(memory_space=pl.ANY)


def pinned(x):
    return pltpu.with_memory_space_constraint(x, pltpu.HBM)


def resident(*shape):
    return pltpu.VMEM(shape, F32)


def chunk(source, target, done, c):
    at = pl.ds(c * GROUP * SPAN, GROUP * SPAN)
    return pltpu.make_async_copy(source.at[at], target.at[at], done.at[c])


def at_span(g, place, act):
    if isinstance(g, int):
        if g % SPAN == place:
            act(g // SPAN)
    else:
        pl.when(lax.rem(g, SPAN) == place)(lambda: act(lax.div(g, SPAN)))


def dot(a, b, contract=((1,), (0,))):
    return lax.dot_general(a, b, (contract, ((), ())), preferred_element_type=F32)


def halves(x):
    high = x.astype(BF16)
    return high, (x - high.astype(F32)).astype(BF16)


def spare_lane(levels, tracers):
    return levels + tracers + 8


def pack_kernel(
    counts, owners, columns, kernels, misfits, out, payload, target, staged, done
):
    steps, levels, held = kernels.shape
    tracers = misfits.shape[1]
    shape = (LANES, LANES)
    half = CAP // 2
    device = lax.broadcasted_iota(jnp.int32, shape, 0)
    table = counting_table()
    for step in range(steps):
        owner = owners[step]
        live = lax.broadcasted_iota(jnp.int32, owner.shape, 1) < counts[step, 0]
        owner = jnp.where(live, owner, -1)
        seen = jnp.zeros(shape, F32)
        for start in range(0, held, LANES):
            here = owner[:, start : start + LANES]
            hot = device == here
            counted = dot(jnp.where(hot, 1.0, 0.0).astype(BF16), table)
            rank = jnp.sum(
                jnp.where(hot, counted[:, :LANES] + seen, 0.0), axis=0, keepdims=True
            )
            seen = seen + counted[:, LANES:]
            target[step : step + 1, start : start + LANES] = jnp.where(
                here >= 0, here * CAP + rank.astype(jnp.int32), -1
            )
    spare = spare_lane(levels, tracers)
    main = LANES - spare

    def fill(k, part, pieces):
        rows = jnp.concatenate(
            [jnp.zeros((x, held), F32) if isinstance(x, int) else x for x in pieces], axis=0
        )
        high, low = halves(rows)
        payload[k, :LANES, part * held : (part + 1) * held] = high
        payload[k, LANES:, part * held : (part + 1) * held] = low

    def column(step):
        x = columns[step : step + 1, :].astype(F32) + 1.0
        return jnp.where(lax.broadcasted_iota(jnp.int32, (8, held), 0) == 0, x, 0.0)

    rest = [kernels[0, main:, :], misfits[0], column(0)]
    used = levels - main + tracers + 8
    fill(0, 0, [kernels[1], misfits[1], column(1), main])
    fill(0, 1, [spare, kernels[0, :main, :]])
    fill(1, 0, [*rest, LANES - used])
    fill(1, 1, [LANES // 2, *rest, LANES // 2 - used])
    slot = target[0:1, :] & (CAP - 1)
    owner = target[0:1, :] >> (CAP.bit_length() - 1)
    lower = jnp.where((target[0:1, :] >= 0) & (slot < half), owner * half + slot, -1)
    upper = jnp.where((target[0:1, :] >= 0) & (slot >= half), owner * half + slot - half, -1)
    owned = 1024 // CAP
    tiles = out.shape[0] // owned

    def copy(i):
        at = pl.ds(i * owned, owned)
        return pltpu.make_async_copy(staged.at[at], out.at[at], done.at[i])

    def place(i, carry):
        for k, ats, size, rows in (
            (0, (target[1:2, :], target[0:1, :]), owned * CAP, slice(0, CAP)),
            (1, (lower, upper), owned * half, slice(CAP, CAP + half)),
        ):
            hot = jnp.concatenate([tall_one_hot(at - i * size, size) for at in ats], axis=1)
            both = dot(hot, payload[k], ((1,), (1,)))
            both = both[:, :LANES] + both[:, LANES:]
            staged[pl.ds(i * owned, owned), rows, :] = both.reshape(owned, -1, LANES)
        copy(i).start()
        return carry

    lax.fori_loop(0, tiles, place, 0)
    for i in range(tiles):
        copy(i).wait()


def one_hot(at, size):
    at = jnp.where((at >= 0) & (at < size), at, -1).astype(F32).astype(BF16)
    shape = (size, at.shape[1])
    row = lax.broadcasted_iota(jnp.int32, shape, 0).astype(F32).astype(BF16)
    return jnp.where(row == at, jnp.ones(shape, BF16), jnp.zeros(shape, BF16))


def tall_one_hot(at, size):
    parts = [one_hot(at - start, 256) for start in range(0, size, 256)]
    return parts[0] if len(parts) == 1 else jnp.concatenate(parts, axis=0)


def counting_table():
    shape = (LANES, LANES)
    earlier = lax.broadcasted_iota(jnp.int32, shape, 0) < lax.broadcasted_iota(
        jnp.int32, shape, 1
    )
    return jnp.concatenate(
        [jnp.where(earlier, 1.0, 0.0), jnp.ones(shape, F32)], axis=1
    ).astype(BF16)


def packed(counts, owners, columns, kernels, misfits):
    steps, slots = columns.shape
    devices = lax.axis_size("lon") * lax.axis_size("lat")
    return pl.pallas_call(
        pack_kernel,
        out_shape=pltpu.HBM((devices, CAP + CAP // 2, LANES), F32),
        in_specs=[smem()] + [vmem()] * 4,
        out_specs=hbm(),
        scratch_shapes=[
            pltpu.VMEM((2, 2 * LANES, 2 * slots), BF16),
            pltpu.VMEM((steps, slots), jnp.int32),
            pltpu.VMEM((devices, CAP + CAP // 2, LANES), F32),
            pltpu.SemaphoreType.DMA((devices * CAP // 1024,)),
        ],
        compiler_params=params(32),
        name="pack",
    )(counts, held(owners), held(columns), held(kernels), held(misfits))


def streamed_forcing_kernel(step, received, result, out, *scratch):
    done = scratch[-1]

    def copy(r):
        return pltpu.make_async_copy(out.at[:, r], result.at[:, r], done.at[r])

    forcing_kernel(step, received, out, *scratch[:-1], finished=lambda r: copy(r).start())
    for r in range(out.shape[1]):
        copy(r).wait()


def forcing_kernel(
    step, received, out, fields, hots, place, ordered, finished=lambda r: None
):
    levels, rows, tracers, cells = out.shape
    sources = received.shape[0]
    slots = sources * CAP
    blocks = slots // LANES
    spare = spare_lane(levels, tracers)
    data = received[:, :CAP, :].reshape(slots, LANES)
    if step == 1:
        at_column = levels + tracers

        def profile(turned):
            return turned[:levels]

    else:
        at_column = levels - (LANES - spare) + tracers
        extra = received[:, CAP:, :]
        other = pltpu.roll(extra.reshape(slots // 2, LANES), LANES // 2, 1)
        extra = jnp.concatenate([extra, other.reshape(extra.shape)], axis=1)
        lane = lax.broadcasted_iota(jnp.int32, (slots, LANES), 1)
        data = jnp.where(lane < LANES // 2, extra.reshape(slots, LANES), data)

        def profile(turned):
            return jnp.concatenate([turned[spare:], turned[: at_column - tracers]], axis=0)

    high, low = halves(data)
    fields[:, :LANES] = high
    fields[:, LANES:] = low
    shape = (8, 2 * LANES)
    pick = (lax.broadcasted_iota(jnp.int32, shape, 1) & (LANES - 1)) == at_column
    column = dot(jnp.where(pick, 1.0, 0.0).astype(BF16), fields[...], ((1,), (1,)))
    cell_row = (column.astype(jnp.int32) - 1) >> (cells.bit_length() - 1)
    sub = lax.broadcasted_iota(jnp.int32, (rows, LANES), 0)
    for b in range(blocks):
        row = cell_row[:, b * LANES : (b + 1) * LANES]
        hots[b * rows : (b + 1) * rows, :] = jnp.where(sub == row, 1.0, 0.0)
    counted = dot(hots[...].astype(BF16), counting_table())
    run = jnp.zeros((rows, LANES), F32)
    runs = []
    for b in range(blocks):
        runs.append(run)
        run = run + counted[b * rows : (b + 1) * rows, LANES:]
    filled = jnp.floor((run + (LANES - 1.0)) * (1.0 / LANES))
    start = jnp.zeros((rows, LANES), F32)
    for j in range(1, rows):
        start = start + jnp.where(sub >= j, pltpu.roll(filled, j, 0), 0.0)
    for b in range(blocks):
        hot = hots[b * rows : (b + 1) * rows, :]
        at = counted[b * rows : (b + 1) * rows, :LANES] + runs[b] + start * float(LANES)
        at = jnp.sum(hot * at, axis=0, keepdims=True)
        live = jnp.sum(hot, axis=0, keepdims=True) > 0.0
        place[:, b * LANES : (b + 1) * LANES] = jnp.where(live, at, -1.0)
    counts = [jnp.max(filled[r : r + 1, :]).astype(jnp.int32) for r in range(rows)]
    used = sum(counts)
    wide = 4 * LANES

    def sort(i, carry):
        hot = tall_one_hot(place[...] - (i * wide).astype(F32), wide)
        both = dot(hot, fields[...])
        ordered[pl.ds(pl.multiple_of(i * wide, wide), wide), :] = both[:, :LANES] + both[:, LANES:]
        return carry

    lax.fori_loop(0, (used + 3) // 4, sort, 0)
    out[...] = jnp.zeros_like(out)
    name = lax.broadcasted_iota(jnp.int32, (LANES, cells), 1).astype(F32)
    first = jnp.int32(0)
    for r in range(rows):

        def add(p, carry):
            block = ordered[pl.ds(pl.multiple_of(p * LANES, LANES), LANES), :]
            own = jnp.broadcast_to(
                block[:, at_column : at_column + 1] - (r * cells + 1.0), (LANES, cells)
            )
            hot = jnp.where(name == own, 1.0, 0.0).astype(BF16)
            turned = block.T
            product = profile(turned)[:, None, :] * turned[at_column - tracers : at_column][None]
            product = product.reshape(levels * tracers, LANES)
            total = dot(
                jnp.concatenate(halves(product), axis=1), jnp.concatenate([hot, hot], axis=0)
            )
            out[:, r, :, :] += total.reshape(levels, tracers, cells)
            return carry

        lax.fori_loop(first, first + counts[r], add, 0)
        first = first + counts[r]
        finished(r)


def forcing(step, received, shape, streamed):
    slots = received.shape[0] * CAP
    scratch = [
        pltpu.VMEM((slots, 2 * LANES), BF16),
        pltpu.VMEM((slots // LANES * shape[1], LANES), F32),
        pltpu.VMEM((1, slots), F32),
        pltpu.VMEM((slots + shape[1] * LANES, LANES), F32),
    ]
    if streamed:
        scratch = [resident(*shape), *scratch, pltpu.SemaphoreType.DMA((shape[1],))]
    return pl.pallas_call(
        functools.partial(streamed_forcing_kernel if streamed else forcing_kernel, step),
        out_shape=pltpu.HBM(shape, F32) if streamed else resident(*shape),
        in_specs=[vmem()],
        out_specs=hbm() if streamed else vmem(),
        scratch_shapes=scratch,
        compiler_params=params(20 if streamed else 16),
        name="forcing",
    )(held(received))


def shift_matrix(inner, cells):
    shape = (2 * cells, cells)
    source = lax.broadcasted_iota(jnp.int32, shape, 0)
    target = lax.broadcasted_iota(jnp.int32, shape, 1) + inner
    picks = [jnp.where(source == target + k, 1.0, 0.0).astype(BF16) for k in range(2)]
    return jnp.concatenate(picks, axis=1)


def shifted(low, high, matrix):
    row = jnp.concatenate([low, high], axis=1)
    first, rest = row.astype(BF16), None
    rest = row - first.astype(F32)
    second, third = halves(rest)
    return dot(first, matrix) + dot(second, matrix) + dot(third, matrix)


def spread(x, row, tracers):
    return jnp.broadcast_to(x[row : row + 1, :], (tracers, x.shape[1]))


def eliminate(level, above, carry, rights, ratios):
    below, ratio, values = carry
    if above is None:
        above = jnp.zeros_like(below)
    inverse = 1.0 / (1.0 + below + above + below * ratio)
    lower = below * inverse
    ratio = -above * inverse
    ratios[level] = ratio
    tracers = rights[0].shape[0]
    fresh = [
        spread(inverse, r, tracers) * rights[r] + spread(lower, r, tracers) * values[r]
        for r in range(len(rights))
    ]
    return (above, ratio, fresh)


def substitute(step, ratios, couplings, column, fields, results, done):
    diffused, first, last, polar = fields
    levels, rows, tracers, cells = diffused.shape
    lat = lax.axis_index("lat")
    at_start = lat == 0

    def picked(x):
        return jnp.where(at_start, x[step, 0:1, :], x[step, rows - 1 : rows, :])

    north, south, east = [picked(x) for x in couplings]
    own = jnp.broadcast_to(1.0 - north - south, (tracers, cells))
    side = jnp.broadcast_to(jnp.where(at_start, north, south), (tracers, cells))
    groups = levels // GROUP
    by_tracer = len(polar.shape) == 4
    if by_tracer:
        polar[:, groups, 0, :] = jnp.broadcast_to(east, (tracers, cells))
    else:
        polar[levels] = jnp.broadcast_to(east, (tracers, cells))

    chunks = groups // SPAN

    def polar_copy(at, c):
        if by_tracer:
            source, target = [x.at[:, at] for x in (polar, results[3])]
        else:
            source, target = [x.at[at] for x in (polar, results[3])]
        return pltpu.make_async_copy(source, target, done.at[3, c])

    def copies(c):
        size = SPAN if by_tracer else SPAN * GROUP
        moves = [chunk(fields[k], results[k], done.at[k], c) for k in range(3)]
        return [*moves, polar_copy(pl.ds(c * size, size), c)]

    def send(c):
        for copy in copies(c):
            copy.start()

    weight = polar_copy(pl.ds(groups if by_tracer else levels, 1), chunks)
    weight.start()
    lane = lax.broadcasted_iota(jnp.int32, (tracers, LANES), 1)

    def group(i, solved):
        at = groups - 1 - i
        west = jnp.zeros((tracers, LANES), F32)
        for j in range(GROUP - 1, -1, -1):
            level = at * GROUP + j
            ratio = ratios[level]
            fresh = []
            for r in range(rows):
                value = diffused[level, r] - spread(ratio, r, tracers) * solved[r]
                diffused[level, r] = value
                fresh.append(value)
                lanes = j * rows + r
                moved = pltpu.roll(value[:, :LANES], lanes, 1) if lanes else value[:, :LANES]
                west = jnp.where(lane == lanes, moved, west)
            solved = fresh
            first[level] = solved[0]
            last[level] = solved[rows - 1]
            row = own * jnp.where(at_start, solved[0], solved[rows - 1]) + side * jnp.where(
                at_start, solved[1], solved[rows - 2]
            )
            if by_tracer:
                polar[:, at, j, :] = row
            else:
                polar[level] = row
        column[at] = west
        at_span(at, 0, send)
        return solved

    lax.fori_loop(0, groups, group, [jnp.zeros((tracers, cells), F32)] * rows)
    weight.wait()
    for c in range(chunks):
        for copy in copies(c):
            copy.wait()


def forward_sweep(levels, rows, tracers, cells, diffusion, right_of):
    zero = jnp.zeros((rows, cells), F32)
    carry = (zero, zero, [jnp.zeros((tracers, cells), F32)] * rows)
    groups = levels // GROUP

    def one(g, j, above, carry):
        rights, ratios, store = right_of(g, j, above is None)
        carry = eliminate(g * GROUP + j, above, carry, rights, ratios)
        store(carry[2])
        return carry

    def group(g, carry):
        for j in range(GROUP):
            carry = one(g, j, diffusion(g * GROUP + j), carry)
        return carry

    carry = lax.fori_loop(0, groups - 1, group, carry)
    for j in range(GROUP):
        level = levels - GROUP + j
        carry = one(groups - 1, j, diffusion(level) if level < levels - 1 else None, carry)


def first_kernel(
    step,
    costate,
    diffusion_in,
    north_in,
    south_in,
    east_in,
    result,
    first_out,
    last_out,
    polar_out,
    column,
    staged,
    ratios,
    diffused,
    first,
    last,
    polar,
    diffusion,
    couplings,
    arrived,
    sent,
    ready,
):
    levels, tracers, rows, cells = costate.shape
    small = [pltpu.make_async_copy(diffusion_in.at[step], diffusion, ready.at[0])]
    for k, coupling in enumerate((north_in, south_in, east_in)):
        small.append(pltpu.make_async_copy(coupling, couplings.at[k], ready.at[1 + k]))
    chunk(costate, staged, arrived, 0).start()
    for copy in small:
        copy.start()
    for c in range(1, levels // (GROUP * SPAN)):
        chunk(costate, staged, arrived, c).start()
    for copy in small:
        copy.wait()

    def right_of(g, j, final):
        if j == 0:
            at_span(g, 0, lambda c: chunk(costate, staged, arrived, c).wait())
        level = g * GROUP + j
        rights = [staged[level, :, r, :] for r in range(rows)]

        def store(values):
            for r in range(rows):
                diffused[level, r] = values[r]

        return rights, ratios, store

    forward_sweep(levels, rows, tracers, cells, lambda level: diffusion[level], right_of)
    views = [couplings.at[k] for k in range(3)]
    fields = (diffused, first, last, polar)
    results = (result, first_out, last_out, polar_out)
    substitute(step, ratios, views, column, fields, results, sent)


def meridional(level, row, diffused, after, before, coefs):
    rows = diffused.shape[1]
    own, north, south = coefs
    up = diffused[level, row + 1] if row < rows - 1 else after[level]
    down = diffused[level, row - 1] if row > 0 else before[level]
    return own * diffused[level, row] + north * up + south * down


def borders_kernel(
    step,
    shift,
    column,
    north,
    south,
    after_in,
    before_in,
    polar_in,
    nearby_in,
    edge,
    turned_out,
    south_hops,
    north_hops,
    after,
    before,
    polar,
    nearby,
    turned,
    ready,
):
    rows, cells = north.shape[1:]
    circle = cells * lax.axis_size("lon")
    amounts = [
        lax.rem(shift[step, x] + 2 * circle, circle) for x in (0, shift.shape[1] - 1)
    ]
    south_hops[0, 0] = amounts[0] // cells
    north_hops[0, 0] = amounts[1] // cells
    fetches = [
        pltpu.make_async_copy(source, target, ready.at[2 + k])
        for k, (source, target) in enumerate(((polar_in, polar), (nearby_in, nearby)))
    ]
    sending = pltpu.make_async_copy(turned, turned_out, ready.at[4])
    lat = lax.axis_index("lat")
    last_lat = lax.axis_size("lat") - 1
    at_pole = (lat == 0) | (lat == last_lat)

    @pl.when(at_pole)
    def _():
        for fetch in fetches:
            fetch.start()

    finish = west_column(step, column, north, south, after_in, before_in, edge, after, before, ready)

    @pl.when(at_pole)
    def _():
        for fetch in fetches:
            fetch.wait()
        levels = turned.shape[0]
        amount = jnp.where(lat == 0, amounts[0], amounts[1])
        matrix = shift_matrix(lax.rem(amount, cells), cells)
        tracers = turned.shape[1]
        weight = shifted(polar[levels], nearby[levels], matrix)[:1, :cells]
        size = 3 * GROUP
        for i in range(levels // size):
            at = slice(i * size, (i + 1) * size)
            low, high = [x[at].reshape(size * tracers, cells) for x in (polar, nearby)]
            row = shifted(low, high, matrix)
            row = row[:, :cells] + weight * (row[:, cells:] - row[:, :cells])
            turned[at] = row.reshape(size, tracers, cells)
        sending.start()

    finish()

    @pl.when(at_pole)
    def _():
        sending.wait()


def edge_kernel(
    step, column, north, south, after_in, before_in, edge, after, before, ready
):
    west_column(step, column, north, south, after_in, before_in, edge, after, before, ready)()


def west_column(step, column, north, south, after_in, before_in, edge, after, before, ready):
    groups, tracers, lanes = column.shape
    rows, cells = north.shape[1:]
    tiles = [
        pltpu.make_async_copy(source.at[:, :, pl.ds(0, lanes)], target, ready.at[k])
        for k, (source, target) in enumerate(((after_in, after), (before_in, before)))
    ]
    for tile in tiles:
        tile.start()
    lane = lax.broadcasted_iota(jnp.int32, (tracers, lanes), 1)

    def along_lanes(x):
        shape = (rows, lanes)
        own_lane = (lax.broadcasted_iota(jnp.int32, shape, 1) & (rows - 1)) == (
            lax.broadcasted_iota(jnp.int32, shape, 0)
        )
        picked = jnp.where(own_lane, jnp.broadcast_to(x[step, :, :1], shape), 0.0)
        return jnp.broadcast_to(jnp.sum(picked, axis=0, keepdims=True), (tracers, lanes))

    n, s = along_lanes(north), along_lanes(south)
    own = 1.0 - n - s

    def group(i, carry):
        here = column[i]
        up = pltpu.roll(here, lanes - 1, 1)
        down = pltpu.roll(here, 1, 1)
        for j in range(GROUP):
            level = i * GROUP + j
            bottom, top = j * rows, j * rows + rows - 1
            up = jnp.where(lane == top, pltpu.roll(after[level], top, 1), up)
            moved = before[level]
            moved = pltpu.roll(moved, bottom, 1) if bottom else moved
            down = jnp.where(lane == bottom, moved, down)
        edge[i] = own * here + n * up + s * down
        return carry

    def finish():
        for tile in tiles:
            tile.wait()
        lax.fori_loop(0, groups, group, 0)

    return finish


def rotate_kernel(step, shift, circle_in, out, circle, pairs, turned, ready):
    parts, groups, group, cells = turned.shape
    lat = lax.axis_index("lat")
    last_lat = lax.axis_size("lat") - 1
    rows = shift.shape[1] // lax.axis_size("lat")

    @pl.when((lat == 0) | (lat == last_lat))
    def _():
        fetch = pltpu.make_async_copy(circle_in, circle, ready.at[0])
        fetch.start()
        amount = jnp.where(lat == 0, shift[step, 0], shift[step, rows * last_lat + rows - 1])
        amount = lax.rem(amount + 2 * parts * cells, parts * cells)
        hops = amount // cells
        matrix = shift_matrix(amount - hops * cells, cells)
        fetch.wait()
        height = (groups + 1) * group
        for part in range(parts):
            at = slice(part * height, (part + 1) * height)
            near = lax.rem(part + hops, parts)
            far = lax.rem(part + hops + 1, parts)
            pairs[at, :cells] = circle[near].reshape(height, cells)
            pairs[at, cells:] = circle[far].reshape(height, cells)
        batch = parts // 2
        for i in range(2):
            rows_at = slice(i * batch * height, (i + 1) * batch * height)
            row = shifted(pairs[rows_at, :cells], pairs[rows_at, cells:], matrix)
            row = row.reshape(batch, groups + 1, group, 2 * cells)
            weight = row[:, groups:, :1, :cells]
            row = row[:, :groups]
            row = row[..., :cells] + weight * (row[..., cells:] - row[..., :cells])
            turned[i * batch : (i + 1) * batch] = row
        send = pltpu.make_async_copy(turned, out, ready.at[1])
        send.start()
        send.wait()


def prepare_stencil(step, north, south, east, coefs):
    rows, cells = north.shape[1:]
    tracers = coefs.shape[2]
    for r in range(rows):
        n = north[step, r : r + 1, :]
        s = south[step, r : r + 1, :]
        coefs[0, r] = jnp.broadcast_to(1.0 - n - s, (tracers, cells))
        coefs[1, r] = jnp.broadcast_to(n, (tracers, cells))
        coefs[2, r] = jnp.broadcast_to(s, (tracers, cells))
        coefs[3, r] = jnp.broadcast_to(east[step, r : r + 1, :], (tracers, cells))


def transported(group, lane_at, diffused, after, before, edge_row, coefs, pole):
    level = group * GROUP + lane_at
    rows, tracers, cells = diffused.shape[1:]
    lat = lax.axis_index("lat")
    last = lax.broadcasted_iota(jnp.int32, (tracers, cells), 1) == cells - 1
    result = []
    for r in range(rows):
        mer = meridional(level, r, diffused, after, before, [coefs[k, r] for k in range(3)])
        arrived = pltpu.roll(edge_row, LANES - 1 - (lane_at * rows + r), 1)
        arrived = jnp.concatenate([arrived] * (cells // LANES), axis=1)
        following = jnp.where(last, arrived, pltpu.roll(mer, cells - 1, 1))
        result.append(mer + coefs[3, r] * (following - mer))
    polar = pole[:, group, lane_at, :] if len(pole.shape) == 4 else pole[level]
    result[0] = jnp.where(lat == 0, polar, result[0])
    result[rows - 1] = jnp.where(lat == lax.axis_size("lat") - 1, polar, result[rows - 1])
    return result


def streams(sources, targets, poles, pole, done):
    lat = lax.axis_index("lat")
    last_lat = lax.axis_size("lat") - 1
    last = len(sources)

    def polar_copy(source, c):
        if len(pole.shape) == 4:
            at = pl.ds(c * SPAN, SPAN)
            return pltpu.make_async_copy(source.at[:, at], pole.at[:, at], done.at[last, c])
        return chunk(source, pole, done.at[last], c)

    for g in range(targets[0].shape[0] // (GROUP * SPAN)):
        for k, (source, target) in enumerate(zip(sources, targets)):
            chunk(source, target, done.at[k], g).start()

        @pl.when(lat == 0)
        def _():
            polar_copy(poles[0], g).start()

        @pl.when(lat == last_lat)
        def _():
            polar_copy(poles[-1], g).start()

    def wait(g):
        for k, (source, target) in enumerate(zip(sources, targets)):
            chunk(source, target, done.at[k], g).wait()

        @pl.when((lat == 0) | (lat == last_lat))
        def _():
            polar_copy(poles[0], g).wait()

    return wait


def middle_kernel(
    step,
    before_step,
    forced,
    after_in,
    before_in,
    south_pole,
    north_pole,
    edge,
    diffusion,
    north,
    south,
    east,
    result,
    first_out,
    last_out,
    polar_out,
    column,
    surface,
    coefs,
    ratios,
    diffused,
    after,
    before,
    pole,
    solved,
    first,
    last,
    polar,
    arrived,
    sent,
):
    levels, rows, tracers, cells = diffused.shape
    wait = streams(
        (before_step, after_in, before_in),
        (diffused, after, before),
        (south_pole, north_pole),
        pole,
        arrived,
    )
    prepare_stencil(step, north, south, east, coefs)

    def right_of(g, j, final):
        if j == 0:
            at_span(g, 0, wait)
        level = g * GROUP + j
        rights = transported(g, j, diffused, after, before, edge[g], coefs, pole)
        rights = [rights[r] + forced[level, r] for r in range(rows)]
        if final:
            for r in range(rows):
                surface[r] = rights[r]

        def store(values):
            for r in range(rows):
                solved[level, r] = values[r]

        return rights, ratios, store

    forward_sweep(
        levels, rows, tracers, cells, lambda level: diffusion[step - 1, level], right_of
    )
    couplings = (north, south, east)
    fields = (solved, first, last, polar)
    results = (result, first_out, last_out, polar_out)
    substitute(step - 1, ratios, couplings, column, fields, results, sent)


def last_kernel(
    step,
    before_step,
    forcing_in,
    after_in,
    before_in,
    pole_in,
    edge,
    north,
    south,
    east,
    surface,
    state,
    gradient,
    coefs,
    diffused,
    forced,
    after,
    before,
    pole,
    staged,
    arrived,
    sent,
):
    levels, rows, tracers, cells = diffused.shape
    wait = streams(
        (before_step, forcing_in, after_in, before_in),
        (diffused, forced, after, before),
        (pole_in,),
        pole,
        arrived,
    )
    prepare_stencil(step, north, south, east, coefs)

    def group(g, carry):
        at_span(g, 0, wait)
        edge_row = edge[g]
        for j in range(GROUP):
            level = g * GROUP + j
            values = transported(g, j, diffused, after, before, edge_row, coefs, pole)
            for r in range(rows):
                staged[level, :, r, :] = values[r] + forced[level, r]
        at_span(g, SPAN - 1, lambda c: chunk(staged, state, sent, c).start())
        return carry

    lax.fori_loop(0, levels // GROUP, group, 0)
    for r in range(rows):
        gradient[:, r, :] = surface[r] + staged[levels - 1, :, r, :]
    for c in range(levels // (GROUP * SPAN)):
        chunk(staged, state, sent, c).wait()


def boundary_rows(first, last):
    up = [(i, i + 1) for i in range(lax.axis_size("lat") - 1)]
    down = [(j, i) for i, j in up]
    return lax.ppermute(first, "lat", down), lax.ppermute(last, "lat", up)


def circles(lats, hops):
    lat_count = lax.axis_size("lat")
    lon_count = lax.axis_size("lon")
    return [
        (((j + hops) % lon_count) * lat_count + lat, j * lat_count + lat)
        for lat in lats
        for j in range(lon_count)
    ]


def westward(edge):
    count = lax.axis_size("lon")
    return held(lax.ppermute(edge, "lon", [(i, (i - 1) % count) for i in range(count)]))


def first_exchange(step, after, before, nearby, polar, column, north, south, shift):
    poles = (0, lax.axis_size("lat") - 1)
    levels, tracers, cells = after.shape
    edge, turned, *hops = pl.pallas_call(
        functools.partial(borders_kernel, step),
        out_shape=[
            resident(*column.shape),
            pltpu.HBM((levels, tracers, cells), F32),
            jax.ShapeDtypeStruct((1, 1), jnp.int32),
            jax.ShapeDtypeStruct((1, 1), jnp.int32),
        ],
        in_specs=[smem()] + [vmem()] * 3 + [anywhere()] * 4,
        out_specs=[vmem(), hbm(), smem(), smem()],
        scratch_shapes=[
            pltpu.VMEM((levels, tracers, LANES), F32),
            pltpu.VMEM((levels, tracers, LANES), F32),
            pltpu.VMEM(polar.shape, F32),
            pltpu.VMEM(polar.shape, F32),
            pltpu.VMEM((levels, tracers, cells), F32),
            pltpu.SemaphoreType.DMA((5,)),
        ],
        compiler_params=params(8),
        name="borders",
    )(shift, column, north, south, after, before, pinned(polar), nearby)
    moved = []
    for lat, hop in zip(poles, hops):
        moved.append(
            lax.switch(
                hop.reshape(()),
                [
                    functools.partial(
                        lambda k, lat, x: lax.ppermute(x, AXES, circles((lat,), k)), k, lat
                    )
                    for k in range(lax.axis_size("lon"))
                ],
                turned,
            )
        )
    edge, *moved = lax.optimization_barrier((edge, *moved))
    return after, before, pinned(moved[0]), pinned(moved[1]), westward(edge)


def last_exchange(step, after, before, circle, column, north, south, shift):
    levels, tracers, cells = after.shape
    parts, groups, group = circle.shape[:3]
    shape = (parts, groups - 1, group, cells)
    turned = pl.pallas_call(
        functools.partial(rotate_kernel, step),
        out_shape=pltpu.HBM(shape, F32),
        in_specs=[smem(), anywhere()],
        out_specs=hbm(),
        scratch_shapes=[
            pltpu.VMEM(circle.shape, F32),
            pltpu.VMEM((parts * groups * group, 2 * cells), F32),
            pltpu.VMEM(shape, F32),
            pltpu.SemaphoreType.DMA((2,)),
        ],
        compiler_params=params(14),
        name="rotate",
    )(shift, circle)
    pole = lax.all_to_all(turned, "lon", 0, 0, tiled=True)
    edge = pl.pallas_call(
        functools.partial(edge_kernel, step),
        out_shape=resident(*column.shape),
        in_specs=[vmem()] * 3 + [anywhere()] * 2,
        out_specs=vmem(),
        scratch_shapes=[
            pltpu.VMEM((levels, tracers, LANES), F32),
            pltpu.VMEM((levels, tracers, LANES), F32),
            pltpu.SemaphoreType.DMA((2,)),
        ],
        compiler_params=params(4),
        name="edge",
    )(column, north, south, after, before)
    return after, before, pole, westward(edge)


def per_device(
    costate,
    diffusion,
    east_courant,
    north_courant,
    south_courant,
    polar_shift,
    owners,
    columns,
    sounding_counts,
    kernels,
    misfits,
):
    levels, tracers, rows, cells = costate.shape
    owner_rows = owners.reshape(owners.shape[0], 1, owners.shape[1])
    couplings = (north_courant, south_courant, east_courant)
    groups = levels // GROUP

    solved_shapes = [
        pltpu.HBM((levels, rows, tracers, cells), F32),
        pltpu.HBM((levels, tracers, cells), F32),
        pltpu.HBM((levels, tracers, cells), F32),
        pltpu.HBM((levels + 1, tracers, cells), F32),
        resident(groups, tracers, LANES),
    ]
    ratios = pltpu.VMEM((levels, rows, cells), F32)
    coefs = pltpu.VMEM((4, rows, tracers, cells), F32)
    field = pltpu.VMEM((levels, rows, tracers, cells), F32)
    line = pltpu.VMEM((levels, tracers, cells), F32)
    solved_scratch = [field, line, line, pltpu.VMEM((levels + 1, tracers, cells), F32)]
    solved_specs = [hbm()] * 4 + [vmem()]
    leaving = pltpu.SemaphoreType.DMA((4, groups // SPAN + 1))
    output = pltpu.VMEM(costate.shape, F32)
    semaphores = pltpu.SemaphoreType.DMA((groups // SPAN,))
    diffused, first, last, polar, column = pl.pallas_call(
        functools.partial(first_kernel, 1),
        out_shape=solved_shapes,
        in_specs=[hbm()] * 5,
        out_specs=solved_specs,
        scratch_shapes=[
            output,
            ratios,
            *solved_scratch,
            pltpu.VMEM(diffusion.shape[1:], F32),
            pltpu.VMEM((3,) + east_courant.shape, F32),
            semaphores,
            leaving,
            pltpu.SemaphoreType.DMA((4,)),
        ],
        compiler_params=params(16),
        name="first",
    )(*[pinned(x) for x in (costate, diffusion, *couplings)])
    couplings = [held(x) for x in couplings]
    diffusion = held(diffusion)
    counts, column = lax.optimization_barrier((sounding_counts, column))
    nearby = lax.ppermute(polar, AXES, circles((0, lax.axis_size("lat") - 1), 1))
    around = (*boundary_rows(first, last), nearby)
    sent = packed(counts, owner_rows, columns, kernels, misfits)
    sent, *around = lax.optimization_barrier((sent, *around))
    around = [pinned(x) for x in around]
    got = lax.all_to_all(sent, AXES, 0, 0, tiled=True)
    shape = (levels, rows, tracers, cells)
    forced = forcing(1, got, shape, False)
    around = first_exchange(1, *around, polar, column, *couplings[:2], polar_shift)
    scratch = [field, line, line]
    transfers = pltpu.SemaphoreType.DMA((4, groups // SPAN))
    solved, first, last, polar, column, surface = pl.pallas_call(
        functools.partial(middle_kernel, 1),
        out_shape=[
            *solved_shapes[:3],
            pltpu.HBM((tracers, groups + 1, GROUP, cells), F32),
            solved_shapes[4],
            resident(rows, tracers, cells),
        ],
        in_specs=[hbm(), vmem()] + [anywhere()] * 2 + [hbm()] * 2 + [vmem()] * 5,
        out_specs=solved_specs + [vmem()],
        scratch_shapes=[
            coefs,
            ratios,
            *scratch,
            line,
            *solved_scratch[:3],
            pltpu.VMEM((tracers, groups + 1, GROUP, cells), F32),
            transfers,
            leaving,
        ],
        compiler_params=params(20),
        name="middle",
    )(pinned(diffused), forced, *around, diffusion, *couplings)
    circle = lax.all_to_all(polar, "lon", 0, 0, tiled=True)
    got, column = lax.optimization_barrier((got, column))
    forced = forcing(0, got, shape, True)
    forced, first, last = lax.optimization_barrier((forced, first, last))
    around = last_exchange(
        0, *boundary_rows(first, last), circle, column, *couplings[:2], polar_shift
    )
    return tuple(
        pl.pallas_call(
            functools.partial(last_kernel, 0),
            out_shape=[
                pltpu.HBM(costate.shape, F32),
                jax.ShapeDtypeStruct((tracers, rows, cells), F32),
            ],
            in_specs=[hbm()] * 2 + [anywhere()] * 3 + [vmem()] * 5,
            out_specs=[hbm(), vmem()],
            scratch_shapes=[
                coefs,
                field,
                *scratch,
                pltpu.VMEM((tracers, groups, GROUP, cells), F32),
                output,
                pltpu.SemaphoreType.DMA((5, groups // SPAN)),
                semaphores,
            ],
            compiler_params=params(22),
            name="last",
        )(pinned(solved), pinned(forced), *around, *couplings, surface)
    )


def solution(mesh):
    return jax.shard_map(
        per_device,
        mesh=mesh,
        in_specs=(
            P(None, None, "lat", "lon"),
            P(None, None, "lat", "lon"),
            P(None, "lat", "lon"),
            P(None, "lat", "lon"),
            P(None, "lat", "lon"),
            P(),
            P(None, ("lon", "lat"), None),
            P(None, ("lon", "lat")),
            P(None, ("lon", "lat")),
            P(None, None, ("lon", "lat")),
            P(None, None, ("lon", "lat")),
        ),
        out_specs=(P(None, None, "lat", "lon"), P(None, "lat", "lon")),
        check_vma=False,
    )
```
